32 devices in a mesh: dp: 8 (over y, x, core), mp: 4 (over z).
Axes of the slice: x: 2, y: 2, z: 4, core: 2. Of those that a mesh axis runs over, the one named last changes fastest.
Arguments:
- hidden_in: bfloat16 [8, 2048, 1024], P('dp', 'mp'), may hold values from -6 to 6
- segment_ids: int32 [8, 2048], P('dp'), may hold values from 0 to 6, as said below
- first_values: bfloat16 [8, 2048, 1024], P('dp', None, 'mp'), may hold values from -20 to 20
- grad_out: bfloat16 [8, 2048, 1024], P('dp', 'mp'), may hold values from -6 to 6
- input_proj: float32 [3, 1024, 1024], P(None, 'dp', 'mp'), may hold values from -0.1875 to 0.1875
- output_proj: float32 [1024, 1024], P('mp', 'dp'), may hold values from -3 to 3
- expand_proj: float32 [2, 1024, 2816], P(None, 'dp', 'mp'), may hold values from -0.1875 to 0.1875
- reduce_proj: float32 [2816, 1024], P('mp', 'dp'), may hold values from -0.1875 to 0.1875
- norm_gains: float32 [2, 1024], P(None, 'dp'), may hold values from 0.5 to 1.5
- old_moment_input: float32 [3, 1024, 1024], P(None, 'dp', 'mp'), may hold values from -1536 to 1536
- old_moment_output: float32 [1024, 1024], P('mp', 'dp'), may hold values from -96 to 96
- old_moment_expand: float32 [2, 1024, 2816], P(None, 'dp', 'mp'), may hold values from -512 to 512
- old_moment_reduce: float32 [2816, 1024], P('mp', 'dp'), may hold values from -448 to 448
- old_moment_gains: float32 [2, 1024], P(None, 'dp'), may hold values from -1280 to 1280
- old_square_input: float32 [3, 1024, 1024], P(None, 'dp', 'mp'), may hold values from 63717.918 to 254871.67
- old_square_output: float32 [1024, 1024], P('mp', 'dp'), may hold values from 248.48643 to 993.94574
- old_square_expand: float32 [2, 1024, 2816], P(None, 'dp', 'mp'), may hold values from 6434.444 to 25737.775
- old_square_reduce: float32 [2816, 1024], P('mp', 'dp'), may hold values from 5898.24 to 23592.96
- old_square_gains: float32 [2, 1024], P(None, 'dp'), may hold values from 47349.76 to 189399.05
Outputs:
- layer_output: bfloat16 [8, 2048, 1024], P('dp', 'mp')
- input_grad: float32 [8, 2048, 1024], P('dp', 'mp')
- values_grad: float32 [8, 2048, 1024], P('dp', None, 'mp')
- value_norms: float32 [2], replicated
- updated_input: float32 [3, 1024, 1024], P(None, 'dp', 'mp')
- updated_output: float32 [1024, 1024], P('mp', 'dp')
- updated_expand: float32 [2, 1024, 2816], P(None, 'dp', 'mp')
- updated_reduce: float32 [2816, 1024], P('mp', 'dp')
- updated_gains: float32 [2, 1024], P(None, 'dp')
- moment_input: float32 [3, 1024, 1024], P(None, 'dp', 'mp')
- moment_output: float32 [1024, 1024], P('mp', 'dp')
- moment_expand: float32 [2, 1024, 2816], P(None, 'dp', 'mp')
- moment_reduce: float32 [2816, 1024], P('mp', 'dp')
- moment_gains: float32 [2, 1024], P(None, 'dp')
- square_input: float32 [3, 1024, 1024], P(None, 'dp', 'mp')
- square_output: float32 [1024, 1024], P('mp', 'dp')
- square_expand: float32 [2, 1024, 2816], P(None, 'dp', 'mp')
- square_reduce: float32 [2816, 1024], P('mp', 'dp')
- square_gains: float32 [2, 1024], P(None, 'dp')
The draws below stay inside these ranges and needn't reach their ends.
Inputs may be any that keep to these rules, and one draw needn't show every extreme that they name: `segment_ids`: along each row the ids start at 0, never fall and end at 6 (seven documents); in every row one document begins within the first 512 positions and ends within the last 512.
All inputs are finite; a program needn't handle non-finite values.
Results may differ from the reference program's by a relative error of at most 0.023.
Values may be sent and summed in bfloat16 or wider, within the bound.
A program may use at most 192 MiB of HBM per device.

```python
import math
import jax
import jax.numpy as jnp
from jax import lax

D = 1024
HEADS = 16
HD = 64
FF = 2816
LEN = 2048
STEP = 5
BATCH = 8
TOKENS = 16384
SHARD = 512


def draw_segment_ids(key, part):
    pieces = jax.random.split(key, 6)
    places = jnp.arange(LEN, dtype=jnp.int32)[None, :]
    opening = jax.random.randint(pieces[0], (BATCH, 1), SHARD // 2, SHARD, dtype=jnp.int32)
    closing = jax.random.randint(pieces[1], (BATCH, 1), LEN - SHARD + 1, LEN - SHARD // 2 + 1, dtype=jnp.int32)
    early_mid = opening // 2
    first_cut = jax.random.randint(pieces[2], (BATCH, 1), 1, early_mid, dtype=jnp.int32)
    second_cut = jax.random.randint(pieces[3], (BATCH, 1), early_mid, opening, dtype=jnp.int32)
    late_mid = closing + 1 + (LEN - closing - 1) // 2
    third_cut = jax.random.randint(pieces[4], (BATCH, 1), closing + 1, late_mid, dtype=jnp.int32)
    fourth_cut = jax.random.randint(pieces[5], (BATCH, 1), late_mid, LEN, dtype=jnp.int32)
    cuts = (places == first_cut) | (places == second_cut) | (places == opening) | (places == closing) | (places == third_cut) | (places == fourth_cut)
    return jnp.cumsum(cuts.astype(jnp.int32), axis=1).astype(jnp.int32)


def draw_first_values(key, part):
    row_place = jnp.arange(BATCH, dtype=jnp.float32)[:, None, None] / max(BATCH - 1, 1)
    column_place = jnp.arange(D, dtype=jnp.float32)[None, None, :] / (D - 1)
    base = jnp.clip(jax.random.normal(key, (BATCH, LEN, D), jnp.float32), -6.0, 6.0)
    growth = 0.73
    return (base * (1.0 + growth * row_place) * (1.0 + growth * column_place)).astype(jnp.bfloat16)


def steps_of(rng, extent, shards, smallest, high):
    def one(dim, parts):
        heights = jax.random.uniform(jax.random.fold_in(jax.random.fold_in(rng, 6), dim), (parts,), jnp.float32, smallest / len(shards), high / len(shards))
        return jnp.repeat(jnp.exp(heights), extent[dim] // parts).reshape((-1,) + (1,) * (len(extent) - dim - 1))

    level = one(*shards[0])
    for cut in shards[1:]:
        level = level * one(*cut)
    return level


def centred(rng, shape, width, reach, cuts=(), kind=jnp.bfloat16):
    loudness = steps_of(rng, shape, cuts, -0.22, 0.18) if cuts else 1.0
    values = jax.random.normal(rng, shape, jnp.float32) * width * loudness
    return jnp.minimum(jnp.maximum(values, -reach), reach).astype(kind)


def setup_inputs(seed: int = 0) -> dict:
    seeds = jax.random.split(jax.random.key(seed), 20)
    hidden_in = centred(seeds[0], (BATCH, LEN, D), 1.0, 6.0, ((0, 8), (1, 4)))
    segment_ids = draw_segment_ids(jax.random.fold_in(seeds[19], 71), 0)
    first_values = draw_first_values(jax.random.fold_in(seeds[19], 71), 0)
    grad_out = centred(seeds[3], (BATCH, LEN, D), 1.0, 6.0, ((0, 8), (1, 4)))
    input_proj = centred(seeds[4], (3, D, D), D ** -0.5, 0.1875, ((1, 8), (2, 4)), jnp.float32)
    output_proj = centred(seeds[5], (D, D), (max(1, 8 * HEADS * HD // LEN)) ** -0.5, 3.0, ((0, 4), (1, 8)), jnp.float32)
    expand_proj = centred(seeds[6], (2, D, FF), D ** -0.5, 0.1875, ((1, 8), (2, 4)), jnp.float32)
    reduce_proj = centred(seeds[7], (FF, D), (FF // 3) ** -0.5, 0.1875, ((0, 4), (1, 8)), jnp.float32)
    norm_gains = jnp.clip(1.0 + 0.1 * jax.random.normal(seeds[8], (2, D), jnp.float32), 0.5, 1.5)
    old_moment_input = centred(seeds[9], (3, D, D), (0.92 * LEN ** 0.1 * TOKENS ** 0.5), 1536.0, ((1, 8), (2, 4)), jnp.float32)
    old_moment_output = centred(seeds[10], (D, D), (2.6 * LEN ** -0.4 * TOKENS ** 0.5), 96.0, ((0, 4), (1, 8)), jnp.float32)
    old_moment_expand = centred(seeds[11], (2, D, FF), (0.6 * (3 * D) ** 0.5 * FF ** -0.5 * TOKENS ** 0.5), 512.0, ((1, 8), (2, 4)), jnp.float32)
    old_moment_reduce = centred(seeds[12], (FF, D), (0.6 * TOKENS ** 0.5), 448.0, ((0, 4), (1, 8)), jnp.float32)
    old_moment_gains = centred(seeds[13], (2, D), (1.7 * TOKENS ** 0.5), 1280.0, ((1, 8),), jnp.float32)
    old_square_input = jnp.clip(63717.918 + 191153.75 * jax.random.uniform(seeds[14], (3, D, D), jnp.float32) ** steps_of(seeds[14], (3, D, D), ((1, 8), (2, 4)), -0.2, 0.2), 63717.918, 254871.67)
    old_square_output = jnp.clip(248.48643 + 745.4593 * jax.random.uniform(seeds[15], (D, D), jnp.float32) ** steps_of(seeds[15], (D, D), ((0, 4), (1, 8)), -0.2, 0.2), 248.48643, 993.94574)
    old_square_expand = jnp.clip(6434.444 + 19303.332 * jax.random.uniform(seeds[16], (2, D, FF), jnp.float32) ** steps_of(seeds[16], (2, D, FF), ((1, 8), (2, 4)), -0.2, 0.2), 6434.444, 25737.775)
    old_square_reduce = jnp.clip(5898.24 + 17694.72 * jax.random.uniform(seeds[17], (FF, D), jnp.float32) ** steps_of(seeds[17], (FF, D), ((0, 4), (1, 8)), -0.2, 0.2), 5898.24, 23592.96)
    old_square_gains = jnp.clip(47349.76 + 142049.285 * jax.random.uniform(seeds[18], (2, D), jnp.float32) ** steps_of(seeds[18], (2, D), ((1, 8),), -0.2, 0.2), 47349.76, 189399.05)
    return dict(hidden_in=hidden_in, segment_ids=segment_ids, first_values=first_values, grad_out=grad_out, input_proj=input_proj, output_proj=output_proj, expand_proj=expand_proj, reduce_proj=reduce_proj, norm_gains=norm_gains, old_moment_input=old_moment_input, old_moment_output=old_moment_output, old_moment_expand=old_moment_expand, old_moment_reduce=old_moment_reduce, old_moment_gains=old_moment_gains, old_square_input=old_square_input, old_square_output=old_square_output, old_square_expand=old_square_expand, old_square_reduce=old_square_reduce, old_square_gains=old_square_gains)


@jax.custom_vjp
def low(v):
    return lax.optimization_barrier(v.astype(jnp.bfloat16)).astype(jnp.float32)

@jax.custom_vjp
def low_back(v):
    return v

def low_keep(v):
    return (low(v), None)

def low_pass(kept, grad):
    return (grad,)

def back_keep(v):
    return (v, None)

def back_low(kept, grad):
    return (low(grad),)
low.defvjp(low_keep, low_pass)
low_back.defvjp(back_keep, back_low)

def rope_tables(seg_row):
    places = jnp.arange(LEN, dtype=jnp.int32)
    is_fresh = jnp.concatenate([jnp.ones((1,), jnp.bool_), seg_row[1:] != seg_row[:-1]])
    begins = lax.cummax(jnp.where(is_fresh, places, 0), axis=0)
    offset = (places - begins).astype(jnp.float32)
    inverse_rates = 10000.0 ** (-2.0 * jnp.arange(HD // 2, dtype=jnp.float32) / HD)
    angles = offset[:, None] * inverse_rates[None, :]
    return (jnp.cos(angles)[:, None, :], jnp.sin(angles)[:, None, :])

def rotate(values, cosine, sine_part):
    half_size = values.shape[-1] // 2
    first_half = values[..., :half_size]
    second_half = values[..., half_size:]
    return jnp.concatenate([first_half * cosine - second_half * sine_part, second_half * cosine + first_half * sine_part], axis=-1)

def normed(values, gain_row):
    factor = lax.rsqrt(lax.optimization_barrier(jnp.mean(values * values, axis=-1, keepdims=True)) + 1e-06)
    return values * factor * gain_row

def layer_row(hidden, first_in, weights, seg_row):
    attn_weight, out_weight, expand_weight, reduce_weight, gains = weights
    highest = lax.Precision.HIGHEST
    normed_one = low(normed(hidden, gains[0]))
    projected = low_back(jnp.einsum('td,cde->cte', normed_one, attn_weight, precision=highest))
    cosine, sine_part = rope_tables(seg_row)
    queries = low(rotate(projected[0].reshape(LEN, HEADS, HD), cosine, sine_part))
    keys_rot = low(rotate(projected[1].reshape(LEN, HEADS, HD), cosine, sine_part))
    blended = 0.5 * projected[2] + 0.5 * first_in
    mixed_values = low(blended).reshape(LEN, HEADS, HD)
    places = jnp.arange(LEN, dtype=jnp.int32)
    visible = (seg_row[:, None] == seg_row[None, :]) & (places[:, None] >= places[None, :])
    score_scale = 1.0 / math.sqrt(HD)

    def one_head(operands):
        query_head, key_head, value_head = operands
        scores = low_back(jnp.dot(query_head, key_head.T, precision=highest) * score_scale)
        scores = jnp.where(visible, scores, -1e+30)
        top_score = lax.optimization_barrier(jnp.max(scores, axis=1, keepdims=True))
        raised = jnp.exp(scores - top_score)
        shares = raised / lax.optimization_barrier(jnp.sum(raised, axis=1, keepdims=True))
        return jnp.dot(low(shares), value_head, precision=highest)
    heads_out = lax.map(jax.checkpoint(one_head), (queries.transpose(1, 0, 2), keys_rot.transpose(1, 0, 2), mixed_values.transpose(1, 0, 2)))
    attended = low_back(low(heads_out.transpose(1, 0, 2).reshape(LEN, D)))
    branch = low_back(jnp.dot(attended, out_weight, precision=highest))
    middle = hidden + branch
    normed_two = low(normed(middle, gains[1]))
    gate_up = low_back(jnp.einsum('td,cdf->ctf', normed_two, expand_weight, precision=highest))
    activated = low(jax.nn.silu(gate_up[0]) * gate_up[1])
    feed_out = low_back(jnp.dot(activated, reduce_weight, precision=highest))
    return (middle + feed_out, blended)

def adamw(master, gradient, moment, square, step_rate, decay):
    new_moment = 0.5 * moment + 0.5 * gradient
    new_square = 0.5 * square + 0.5 * gradient * gradient
    correct = 1.0 - 0.5 ** STEP
    update = new_moment / correct / (jnp.sqrt(new_square / correct) + 1e-08)
    return (master - step_rate * (update + decay * master), new_moment, new_square)

def reference(hidden_in, segment_ids, first_values, grad_out, input_proj, output_proj, expand_proj, reduce_proj, norm_gains, old_moment_input, old_moment_output, old_moment_expand, old_moment_reduce, old_moment_gains, old_square_input, old_square_output, old_square_expand, old_square_reduce, old_square_gains):
    masters = (input_proj, output_proj, expand_proj, reduce_proj, norm_gains)
    weights = tuple((low(master) for master in masters))
    empty_grads = tuple((jnp.zeros(master.shape, jnp.float32) for master in masters))

    def per_row(running, row_data):
        grads, square_sums = running
        hidden_row, first_row, seg_row, cotangent = row_data
        hidden32 = hidden_row.astype(jnp.float32)
        first32 = first_row.astype(jnp.float32)

        def forward(hidden_arg, first_arg, weight_args):
            return layer_row(hidden_arg, first_arg, weight_args, seg_row)
        output_row, pullback, blended = jax.vjp(forward, hidden32, first32, weights, has_aux=True)
        hidden_grad, first_grad, weight_grads = pullback(cotangent.astype(jnp.float32))
        grads = tuple((total + piece for total, piece in zip(grads, weight_grads)))
        square_sums = square_sums + jnp.stack([jnp.sum(first32 * first32), jnp.sum(blended * blended)])
        return ((grads, square_sums), (output_row.astype(jnp.bfloat16), hidden_grad, first_grad))
    (grads, square_sums), (layer_output, input_grad, values_grad) = lax.scan(per_row, (empty_grads, jnp.zeros((2,), jnp.float32)), (hidden_in, first_values, segment_ids, grad_out))
    value_norms = jnp.sqrt(square_sums / (BATCH * LEN * D))
    step_rates = (D ** (-0.5), max(1, 8 * HEADS * HD // LEN) ** (-0.5), D ** (-0.5), (FF // 3) ** (-0.5), 0.2)
    decays = (0.1, 0.1, 0.1, 0.1, 0.0)
    moments = (old_moment_input, old_moment_output, old_moment_expand, old_moment_reduce, old_moment_gains)
    squares = (old_square_input, old_square_output, old_square_expand, old_square_reduce, old_square_gains)
    results = [adamw(masters[which], grads[which], moments[which], squares[which], step_rates[which], decays[which]) for which in range(5)]
    return (layer_output, input_grad, values_grad, value_norms, results[0][0], results[1][0], results[2][0], results[3][0], results[4][0], results[0][1], results[1][1], results[2][1], results[3][1], results[4][1], results[0][2], results[1][2], results[2][2], results[3][2], results[4][2])
```

```python
import functools
import math

import jax
import jax.numpy as jnp
from jax import lax
from jax.experimental import pallas as pl
from jax.experimental.pallas import tpu as pltpu
from jax.sharding import PartitionSpec as P

D = 1024
HEADS = 16
HD = 64
FF = 2816
LEN = 2048
STEP = 5
PLANES = 4
PIECE = 128
BLOCKS = 4
ATTN_ROWS = 784
VMEM_LIMIT = 56 << 20
OPEN_COPIES = 66


def arrivals(plane):
    order = [(0, 0, plane)]
    for hop in range(1, PLANES):
        if plane + hop < PLANES:
            order.append((0, hop, plane + hop))
        if plane - hop >= 0:
            order.append((1, hop, plane - hop))
    return order


SLOTS = [arrivals(plane) for plane in range(PLANES)]


def cost(flops, moved):
    return pl.CostEstimate(flops=flops, bytes_accessed=moved, transcendentals=0)


def rope_tables(seg_row, head_size):
    length = seg_row.shape[0]
    places = jnp.arange(length, dtype=jnp.int32)
    begins = jnp.sum((seg_row[None, :] < seg_row[:, None]).astype(jnp.int32), axis=1)
    offset = (places - begins).astype(jnp.float32)
    inverse_rates = 10000.0 ** (-2.0 * jnp.arange(head_size // 2, dtype=jnp.float32) / head_size)
    angles = offset[:, None] * inverse_rates[None, :]
    return (jnp.cos(angles)[:, None, :], jnp.sin(angles)[:, None, :])


def rotate(values, cosine, sine_part, forward):
    half_size = values.shape[-1] // 2
    first_half = values[..., :half_size]
    second_half = values[..., half_size:]
    if forward:
        return jnp.concatenate(
            [
                first_half * cosine - second_half * sine_part,
                second_half * cosine + first_half * sine_part,
            ],
            axis=-1,
        )
    return jnp.concatenate(
        [
            first_half * cosine + second_half * sine_part,
            second_half * cosine - first_half * sine_part,
        ],
        axis=-1,
    )


def rms_factor(values):
    return lax.rsqrt(jnp.mean(values * values, axis=-1, keepdims=True) + 1e-06)


def norm_back(values, factor, gain_row, incoming):
    scaled = incoming * gain_row
    value_grad = factor * scaled - values * factor**3 * jnp.mean(
        scaled * values, axis=-1, keepdims=True
    )
    gain_grad = jnp.sum(incoming * values * factor, axis=0)
    return (value_grad, gain_grad)


def visible_block(seg_row, first_row, block_rows):
    length = seg_row.shape[0]
    query_seg = lax.dynamic_slice_in_dim(seg_row, first_row, block_rows, 0)
    query_places = first_row + jnp.arange(block_rows, dtype=jnp.int32)
    key_places = jnp.arange(length, dtype=jnp.int32)
    return (query_seg[:, None] == seg_row[None, :]) & (query_places[:, None] >= key_places[None, :])


def block_scores(queries, keys_rot, seg_row, first_row, block_rows, score_scale):
    query_block = lax.dynamic_slice_in_dim(queries, first_row, block_rows, 0)
    visible = visible_block(seg_row, first_row, block_rows)
    scores = (
        jnp.einsum("qhd,khd->hqk", query_block, keys_rot, preferred_element_type=jnp.float32)
        * score_scale
    )
    return (query_block, jnp.where(visible[None], scores, -1e30))


def attend(queries, keys_rot, mixed_values, seg_row, score_scale):
    length = queries.shape[0]
    block_rows = min(512, length)

    def one_block(block_index):
        first_row = block_index * block_rows
        query_block, scores = block_scores(
            queries, keys_rot, seg_row, first_row, block_rows, score_scale
        )
        top_score = jnp.max(scores, axis=-1, keepdims=True)
        raised = jnp.exp(scores - top_score)
        totals = jnp.sum(raised, axis=-1, keepdims=True)
        shares = (raised / totals).astype(jnp.bfloat16)
        combined = jnp.einsum(
            "hqk,khd->qhd", shares, mixed_values, preferred_element_type=jnp.float32
        )
        return (combined, (top_score + jnp.log(totals))[..., 0])

    combined, log_totals = lax.map(one_block, jnp.arange(length // block_rows, dtype=jnp.int32))
    return (combined.reshape(length, -1), log_totals)


def attend_back(queries, keys_rot, mixed_values, out_grad, log_totals, seg_row, score_scale):
    length = queries.shape[0]
    block_rows = min(512, length)

    def one_block(running, operands):
        key_sum, value_sum = running
        block_index, block_totals = operands
        first_row = block_index * block_rows
        query_block, scores = block_scores(
            queries, keys_rot, seg_row, first_row, block_rows, score_scale
        )
        grad_block = lax.dynamic_slice_in_dim(out_grad, first_row, block_rows, 0)
        shares = jnp.exp(scores - block_totals[..., None])
        share_grad = jnp.einsum(
            "qhd,khd->hqk", grad_block, mixed_values, preferred_element_type=jnp.float32
        )
        inner = jnp.sum(shares * share_grad, axis=-1, keepdims=True)
        score_grad = (shares * (share_grad - inner)).astype(jnp.bfloat16)
        query_grad = (
            jnp.einsum("hqk,khd->qhd", score_grad, keys_rot, preferred_element_type=jnp.float32)
            * score_scale
        )
        key_sum = (
            key_sum
            + jnp.einsum(
                "hqk,qhd->khd", score_grad, query_block, preferred_element_type=jnp.float32
            )
            * score_scale
        )
        value_sum = value_sum + jnp.einsum(
            "hqk,qhd->khd",
            shares.astype(jnp.bfloat16),
            grad_block,
            preferred_element_type=jnp.float32,
        )
        return ((key_sum, value_sum), query_grad)

    empty_sum = jnp.zeros(keys_rot.shape, jnp.float32)
    (key_grad, value_grad), query_grad = lax.scan(
        one_block,
        (empty_sum, empty_sum),
        (jnp.arange(length // block_rows, dtype=jnp.int32), log_totals),
    )
    return (query_grad.reshape(keys_rot.shape), key_grad, value_grad)


def adamw(master, gradient, moment, square, step_rate, decay):
    new_moment = 0.5 * moment + 0.5 * gradient
    new_square = 0.5 * square + 0.5 * gradient * gradient
    correct = 1.0 - 0.5**STEP
    update = new_moment / correct / (jnp.sqrt(new_square / correct) + 1e-08)
    return (master - step_rate * (update + decay * master), new_moment, new_square)


def shards(
    hidden_in,
    segment_ids,
    first_values,
    grad_out,
    input_proj,
    output_proj,
    expand_proj,
    reduce_proj,
    norm_gains,
    old_moment_input,
    old_moment_output,
    old_moment_expand,
    old_moment_reduce,
    old_moment_gains,
    old_square_input,
    old_square_output,
    old_square_expand,
    old_square_reduce,
    old_square_gains,
):
    attn_weight, out_weight, expand_weight, reduce_weight, gains_low = (
        lax.all_gather(input_proj.astype(jnp.bfloat16), "dp", axis=1, tiled=True),
        lax.all_gather(output_proj.astype(jnp.bfloat16), "dp", axis=1, tiled=True),
        lax.all_gather(expand_proj.astype(jnp.bfloat16), "dp", axis=1, tiled=True),
        lax.all_gather(reduce_proj.astype(jnp.bfloat16), "dp", axis=1, tiled=True),
        lax.all_gather(norm_gains.astype(jnp.bfloat16), "dp", axis=1, tiled=True),
    )
    gains = gains_low.astype(jnp.float32)
    hidden = hidden_in[0].astype(jnp.float32)
    seg_row = segment_ids[0]
    length = seg_row.shape[0]
    first_in = first_values[0].astype(jnp.float32)
    local_heads = attn_weight.shape[2] // HD
    score_scale = 1.0 / math.sqrt(HD)
    factor_one = rms_factor(hidden)
    normed_one = (hidden * factor_one * gains[0]).astype(jnp.bfloat16)
    all_normed, all_grad_out = (
        lax.all_gather(normed_one, "mp", axis=0, tiled=True),
        lax.all_gather(grad_out[0], "mp", axis=0, tiled=True),
    )
    projected = jnp.einsum(
        "td,cde->cte", all_normed, attn_weight, preferred_element_type=jnp.float32
    )
    cosine, sine_part = rope_tables(seg_row, HD)
    queries = rotate(projected[0].reshape(length, local_heads, HD), cosine, sine_part, True).astype(
        jnp.bfloat16
    )
    keys_rot = rotate(
        projected[1].reshape(length, local_heads, HD), cosine, sine_part, True
    ).astype(jnp.bfloat16)
    blended = 0.5 * projected[2] + 0.5 * first_in
    mixed_values = blended.astype(jnp.bfloat16).reshape(length, local_heads, HD)
    square_terms = jnp.stack([jnp.sum(first_in * first_in), jnp.sum(blended * blended)])
    attended, log_totals = attend(queries, keys_rot, mixed_values, seg_row, score_scale)
    attended_low = attended.astype(jnp.bfloat16)
    rows_part = attended_low
    branch = lax.psum_scatter(
        jnp.dot(rows_part, out_weight, preferred_element_type=jnp.float32),
        "mp",
        scatter_dimension=0,
        tiled=True,
    )
    middle = hidden + branch
    factor_two = rms_factor(middle)
    normed_two = (middle * factor_two * gains[1]).astype(jnp.bfloat16)
    all_normed_two = lax.all_gather(normed_two, "mp", axis=0, tiled=True)
    gate_up = jnp.einsum(
        "td,cdf->ctf", all_normed_two, expand_weight, preferred_element_type=jnp.float32
    )
    gate_sig = jax.nn.sigmoid(gate_up[0])
    gate_act = gate_up[0] * gate_sig
    activated = (gate_act * gate_up[1]).astype(jnp.bfloat16)
    rows_part = activated
    feed_out = lax.psum_scatter(
        jnp.dot(rows_part, reduce_weight, preferred_element_type=jnp.float32).astype(jnp.bfloat16),
        "mp",
        scatter_dimension=0,
        tiled=True,
    ).astype(jnp.float32)
    layer_output = (middle + feed_out).astype(jnp.bfloat16)[None]
    hidden_grad = jnp.einsum(
        "td,fd->tf", all_grad_out, reduce_weight, preferred_element_type=jnp.float32
    )
    reduce_grad = jnp.einsum(
        "tf,td->fd", activated, all_grad_out, preferred_element_type=jnp.float32
    )
    gate_grad = hidden_grad * gate_up[1] * gate_sig * (1.0 + gate_up[0] * (1.0 - gate_sig))
    up_grad = hidden_grad * gate_act
    pair_grad = jnp.stack([gate_grad, up_grad]).astype(jnp.bfloat16)
    expand_grad = jnp.einsum(
        "ctf,td->cdf", pair_grad, all_normed_two, preferred_element_type=jnp.float32
    )
    rows_part = pair_grad
    normed_two_grad = lax.psum_scatter(
        jnp.einsum(
            "ctf,cdf->td", rows_part, expand_weight, preferred_element_type=jnp.float32
        ).astype(jnp.bfloat16),
        "mp",
        scatter_dimension=0,
        tiled=True,
    ).astype(jnp.float32)
    middle_part, gain_two_grad = norm_back(middle, factor_two, gains[1], normed_two_grad)
    middle_grad = grad_out[0].astype(jnp.float32) + middle_part
    branch_low = middle_grad.astype(jnp.bfloat16)
    all_branch = lax.all_gather(branch_low, "mp", axis=0, tiled=True)
    out_grad = jnp.einsum("te,td->ed", attended_low, all_branch, preferred_element_type=jnp.float32)
    attended_grad = jnp.einsum(
        "td,ed->te", all_branch, out_weight, preferred_element_type=jnp.float32
    ).astype(jnp.bfloat16)
    query_grad, key_grad, mix_grad = attend_back(
        queries,
        keys_rot,
        mixed_values,
        attended_grad.reshape(length, local_heads, HD),
        log_totals,
        seg_row,
        score_scale,
    )
    query_grad = rotate(query_grad, cosine, sine_part, False).reshape(length, -1)
    key_grad = rotate(key_grad, cosine, sine_part, False).reshape(length, -1)
    mix_grad = mix_grad.reshape(length, -1)
    values_grad = (0.5 * mix_grad)[None]
    proj_grad = jnp.stack([query_grad, key_grad, 0.5 * mix_grad]).astype(jnp.bfloat16)
    attn_grad = jnp.einsum("cte,td->cde", proj_grad, all_normed, preferred_element_type=jnp.float32)
    rows_part = proj_grad
    normed_one_grad = lax.psum_scatter(
        jnp.einsum(
            "cte,cde->td", rows_part, attn_weight, preferred_element_type=jnp.float32
        ).astype(jnp.bfloat16),
        "mp",
        scatter_dimension=0,
        tiled=True,
    ).astype(jnp.float32)
    input_part, gain_one_grad = norm_back(hidden, factor_one, gains[0], normed_one_grad)
    input_grad = (middle_grad + input_part)[None]
    attn_total, out_total, expand_total, reduce_total = (
        lax.psum_scatter(
            attn_grad.astype(jnp.bfloat16), "dp", scatter_dimension=1, tiled=True
        ).astype(jnp.float32),
        lax.psum_scatter(
            out_grad.astype(jnp.bfloat16), "dp", scatter_dimension=1, tiled=True
        ).astype(jnp.float32),
        lax.psum_scatter(
            expand_grad.astype(jnp.bfloat16), "dp", scatter_dimension=1, tiled=True
        ).astype(jnp.float32),
        lax.psum_scatter(
            reduce_grad.astype(jnp.bfloat16), "dp", scatter_dimension=1, tiled=True
        ).astype(jnp.float32),
    )
    gain_totals, square_sums = lax.psum(
        (jnp.stack([gain_one_grad, gain_two_grad]), square_terms), ("dp", "mp")
    )
    gain_width = norm_gains.shape[1]
    gain_total = lax.dynamic_slice_in_dim(
        gain_totals, lax.axis_index("dp") * gain_width, gain_width, 1
    )
    value_norms = jnp.sqrt(square_sums / (lax.axis_size("dp") * length * D))
    new_input = adamw(input_proj, attn_total, old_moment_input, old_square_input, D ** (-0.5), 0.1)
    new_output = adamw(
        output_proj,
        out_total,
        old_moment_output,
        old_square_output,
        max(1, 8 * HEADS * HD // LEN) ** (-0.5),
        0.1,
    )
    new_expand = adamw(
        expand_proj, expand_total, old_moment_expand, old_square_expand, D ** (-0.5), 0.1
    )
    new_reduce = adamw(
        reduce_proj, reduce_total, old_moment_reduce, old_square_reduce, (FF // 3) ** (-0.5), 0.1
    )
    new_gains = adamw(norm_gains, gain_total, old_moment_gains, old_square_gains, 0.2, 0.0)
    return (
        layer_output,
        input_grad,
        values_grad,
        value_norms,
        new_input[0],
        new_output[0],
        new_expand[0],
        new_reduce[0],
        new_gains[0],
        new_input[1],
        new_output[1],
        new_expand[1],
        new_reduce[1],
        new_gains[1],
        new_input[2],
        new_output[2],
        new_expand[2],
        new_reduce[2],
        new_gains[2],
    )


def tokens_dot(a, b, left, right):
    return lax.dot_general(a, b, (((left,), (right,)), ((), ())), preferred_element_type=jnp.float32)


def piece_columns(place, step):
    start = jnp.bitwise_xor(place, step) * PIECE
    return pl.ds(pl.multiple_of(start, PIECE), PIECE)


def turn(values, cosine, sine_part, forward):
    lane = lax.broadcasted_iota(jnp.int32, values.shape, 1)
    swapped = jnp.where(
        lax.rem(lane, HD) < HD // 2, pltpu.roll(values, 96, 1), pltpu.roll(values, 32, 1)
    )
    if forward:
        return values * cosine + swapped * sine_part
    return values * cosine - swapped * sine_part


MESH = pl.DeviceIdType.MESH
LOG2E = 1.4426950408889634


def flip(place, bit):
    return place + bit - 2 * bit * lax.rem(lax.div(place, bit), 2)


def at_plane(depth, values):
    found = 0
    for plane, value in enumerate(values):
        found = found + jnp.where(depth == plane, value, 0)
    return found


def slot_at(depth, way, hop):
    return at_plane(
        depth,
        [
            next((k for k, s in enumerate(SLOTS[plane]) if s[:2] == (way, hop)), 0)
            for plane in range(PLANES)
        ],
    )


def columns_of(piece, width=PIECE):
    return pl.ds(pl.multiple_of(piece * width, width), width)


class Links:
    def __init__(self, send, recv):
        self.send, self.recv, self.count, self.started = send, recv, 0, []
        self.place, self.depth = lax.axis_index("dp"), lax.axis_index("mp")

    def number(self, count=1):
        self.count += count
        return self.count - count

    def copy(self, number, source, target, to):
        return pltpu.make_async_remote_copy(
            src_ref=source,
            dst_ref=target,
            send_sem=self.send.at[number],
            recv_sem=self.recv.at[number],
            device_id=to,
            device_id_type=MESH,
        )

    def go(self, number, source, target, to, when=None):
        copy = self.copy(number, source, target, to)
        self.started.append((copy, when))
        if when is None:
            copy.start()
        else:
            pl.when(when)(copy.start)

    def got(self, number, landed, when=None):
        copy = self.copy(number, landed, landed, (flip(self.place, 1), self.depth))
        if when is None:
            copy.wait_recv()
        else:
            pl.when(when)(copy.wait_recv)

    def drain(self):
        for copy, when in self.started:
            if when is None:
                copy.wait_send()
            else:
                pl.when(when)(copy.wait_send)

    def greet(self):
        barrier = pltpu.get_barrier_semaphore()
        others = [(flip(self.place, bit), self.depth) for bit in (1, 2, 4)]
        others += [(self.place, lax.rem(self.depth + step, PLANES)) for step in range(1, PLANES)]
        for other in others:
            pl.semaphore_signal(barrier, inc=1, device_id=other, device_id_type=MESH)
        pl.semaphore_wait(barrier, len(others))


class Spread:
    def __init__(self, links, own, spot, bits):
        self.links, self.own, self.spot, self.bits = links, own, spot, bits
        self.base = links.number(7)
        place = links.place
        self.first, self.second = flip(place, bits[0]), flip(place, bits[1])
        self.both = flip(self.first, bits[1])

    def to(self, bit):
        return (flip(self.links.place, bit), self.links.depth)

    def one(self):
        links = self.links
        links.go(self.base, self.own, self.spot(links.place), self.to(self.bits[0]))

    def two(self):
        links = self.links
        to = self.to(self.bits[1])
        links.go(self.base + 1, self.own, self.spot(links.place), to)
        links.got(self.base, self.spot(self.first))
        links.go(self.base + 2, self.spot(self.first), self.spot(self.first), to)

    def three(self):
        links = self.links
        to = self.to(1)
        links.go(self.base + 3, self.own, self.spot(links.place), to)
        links.go(self.base + 4, self.spot(self.first), self.spot(self.first), to)
        links.got(self.base + 1, self.spot(self.second))
        links.go(self.base + 5, self.spot(self.second), self.spot(self.second), to)
        links.got(self.base + 2, self.spot(self.both))
        links.go(self.base + 6, self.spot(self.both), self.spot(self.both), to)

    def end(self):
        links = self.links
        for index, piece in enumerate((links.place, self.first, self.second, self.both)):
            links.got(self.base + 3 + index, self.spot(flip(piece, 1)))


class Relay:
    def __init__(self, links, own, put):
        self.links, self.own, self.put = links, own, put
        self.base = links.number(2 * (PLANES - 1))

    def send(self, hop):
        links, depth = self.links, self.links.depth
        for way in range(2):
            to = depth + (1 if way else -1)
            when = (
                (depth >= hop - 1) & (depth < PLANES - 1)
                if way
                else (depth <= PLANES - hop) & (depth > 0)
            )
            source = self.own if hop == 1 else self.put(depth, way, hop - 1)
            links.go(
                self.base + 2 * (hop - 1) + way,
                source,
                self.put(to, way, hop),
                (links.place, jnp.clip(to, 0, PLANES - 1)),
                when,
            )

    def take(self, hop):
        links, depth = self.links, self.links.depth
        for way in range(2):
            when = depth >= hop if way else depth + hop < PLANES
            links.got(self.base + 2 * (hop - 1) + way, self.put(depth, way, hop), when)


def open_kernel(*refs):
    hidden, attn_piece, out_piece, feed_piece, cos_ref, sin_ref, first_ref, begin_ref = refs[:8]
    q_out, k_out, v_out, o_out, n_out, weight_out, out_weight_out, feed_all = refs[8:16]
    gain_ref, square_ref, log_ref, middle_ref, normed_ref, attended_ref = refs[16:22]
    held, q_ref, k_ref, v_ref, o_ref, n_ref, weight_ref, out_ref, send, recv, local = refs[22:]
    links = Links(send, recv)
    place, depth = links.place, links.depth
    shard = hidden.shape[0]
    stores = []

    def store(source, target):
        copy = pltpu.make_async_copy(source, target, local.at[len(stores)])
        copy.start()
        stores.append(copy)
        return copy

    block_at = lambda plane, way, hop: jnp.clip(plane + (-hop if way else hop), 0, PLANES - 1)
    wide = Relay(links, hidden, lambda plane, way, hop: held.at[block_at(plane, way, hop)])
    out_rows = lambda block: out_ref.at[
        pl.ds(pl.multiple_of(block * 256, 256), 256), columns_of(place)
    ]
    thin = Relay(links, out_piece, lambda plane, way, hop: out_rows(block_at(plane, way, hop)))
    feeds = Relay(
        links,
        feed_piece,
        lambda plane, way, hop: feed_all.at[slot_at(plane, way, hop), place],
    )
    attn = Spread(links, attn_piece, lambda piece: weight_ref.at[:, columns_of(piece)], (2, 4))
    outs = Spread(
        links, out_ref.at[:, columns_of(place)], lambda piece: out_ref.at[:, columns_of(piece)], (2, 4)
    )
    slots = [
        Spread(
            links,
            feed_piece if slot == 0 else feed_all.at[slot, place],
            lambda piece, slot=slot: feed_all.at[slot, piece],
            (2, 4) if slot % 2 == 0 else (4, 2),
        )
        for slot in range(PLANES)
    ]
    across = links.number(PLANES)

    links.greet()
    thin.send(1)
    wide.send(1)
    attn.one()
    own_hidden = store(hidden, held.at[depth])
    own_attn = store(attn_piece, weight_ref.at[:, columns_of(place)])
    own_out = store(out_piece, out_rows(depth))
    own_feed = store(feed_piece, feed_all.at[0, place])
    square_ref[...] = jnp.zeros_like(square_ref)
    attn.two()
    attn.three()
    slots[0].one()
    attn.end()
    for copy in (own_hidden, own_attn, own_out, own_feed):
        copy.wait()
    store(weight_ref, weight_out)
    gain_ref[...] = weight_ref[pl.ds(768, 16), :].astype(jnp.float32)

    def project(block):
        rows = pl.ds(pl.multiple_of(block * shard, shard), shard)
        values = held[block].astype(jnp.float32)
        factor = lax.rsqrt(jnp.mean(values * values, axis=-1, keepdims=True) + 1e-06)
        normed = (values * factor * gain_ref[0:1, :]).astype(jnp.bfloat16)
        n_ref[rows, :] = normed
        cosine, sine_part = cos_ref[rows, :], sin_ref[rows, :]
        query = tokens_dot(normed, weight_ref[pl.ds(0, 256), :], 1, 1)
        key = tokens_dot(normed, weight_ref[pl.ds(256, 256), :], 1, 1)
        value = tokens_dot(normed, weight_ref[pl.ds(512, 256), :], 1, 1)
        for half in range(2):
            lanes = slice(half * 128, half * 128 + 128)
            turned = turn(query[:, lanes], cosine, sine_part, True)
            q_ref[rows, lanes] = (turned * (HD**-0.5 * LOG2E)).astype(jnp.bfloat16)
            k_ref[rows, lanes] = turn(key[:, lanes], cosine, sine_part, True).astype(jnp.bfloat16)
        first = first_ref[rows, :].astype(jnp.float32)
        blended = 0.5 * value + 0.5 * first
        v_ref[rows, :] = blended.astype(jnp.bfloat16)
        square_ref[0:1, :] += jnp.sum(first * first, axis=0, keepdims=True)
        square_ref[1:2, :] += jnp.sum(blended * blended, axis=0, keepdims=True)

    def project_hop(hop):
        def one(side, carried):
            block = depth + hop * (2 * side - 1)
            pl.when((block >= 0) & (block < PLANES))(lambda: project(block))
            return carried

        lax.fori_loop(0, 2, one, 0)

    project(depth)
    wide.take(1)
    wide.send(2)
    thin.take(1)
    thin.send(2)
    slots[0].two()
    project_hop(1)
    wide.take(2)
    wide.send(3)
    thin.take(2)
    thin.send(3)
    project_hop(2)
    slots[0].three()
    wide.take(3)
    thin.take(3)
    feeds.send(1)
    outs.one()
    project_hop(3)
    store(n_ref, n_out)
    store(q_ref, q_out)
    store(k_ref, k_out)
    store(v_ref, v_out)

    lane = lax.broadcasted_iota(jnp.int32, (shard, 128), 1)
    inside = lax.broadcasted_iota(jnp.int32, (shard, shard), 1)
    down = lax.broadcasted_iota(jnp.int32, (shard, 1), 0)

    def flash_pair(block, pair):
        rows = pl.ds(pl.multiple_of(block * shard, shard), shard)
        lanes = columns_of(pair)
        query = q_ref[rows, lanes]
        begin = begin_ref[rows, :]
        parts = [
            jnp.where((lane < HD) == (head == 0), query, jnp.zeros_like(query)) for head in range(2)
        ]

        def tile(index, carried, visible):
            span = pl.ds(pl.multiple_of(index * shard, shard), shard)
            keys, values = k_ref[span, lanes], v_ref[span, lanes]
            after = []
            for head in range(2):
                top, total, summed = carried[3 * head : 3 * head + 3]
                scores = jnp.where(visible, tokens_dot(parts[head], keys, 1, 1), -1e30)
                raised_top = jnp.maximum(top, jnp.max(scores, axis=1, keepdims=True))
                shrink = jnp.exp2(top - raised_top)
                shares = jnp.exp2(scores - raised_top)
                total = total * shrink + jnp.sum(shares, axis=1, keepdims=True)
                summed = summed * shrink + tokens_dot(shares.astype(jnp.bfloat16), values, 1, 0)
                after += [raised_top, total, summed]
            return tuple(after)

        fresh = (
            jnp.full((shard, 1), -1e30, jnp.float32),
            jnp.zeros((shard, 1), jnp.float32),
            jnp.zeros((shard, 128), jnp.float32),
        )
        carried = tile(block, fresh + fresh, (inside >= begin - block * shard) & (inside <= down))
        top0, total0, sum0, top1, total1, sum1 = lax.fori_loop(
            0, block, lambda j, held: tile(j, held, inside >= begin - j * shard), carried
        )
        o_ref[rows, lanes] = jnp.where(lane < HD, sum0 / total0, sum1 / total1).astype(jnp.bfloat16)
        turned = jnp.transpose(
            jnp.where(lane < HD, top0 + jnp.log2(total0), top1 + jnp.log2(total1))
        )
        log_ref[pair, 0:1, rows] = turned[0:1]
        log_ref[pair, 1:2, rows] = turned[HD : HD + 1]

    own_columns = attended_ref.at[:, columns_of(depth, 256)]

    def hand(step):
        block = lax.rem(depth + step, PLANES)
        rows = pl.ds(pl.multiple_of(block * shard, shard), shard)
        return links.copy(across + step, o_ref.at[rows, :], own_columns, (place, block))

    def flash(step):
        block = lax.rem(depth + step, PLANES)

        def one(pair, carried):
            flash_pair(block, pair)
            return carried

        lax.fori_loop(0, 2, one, 0)

    flash(3)
    hand(3).start()
    feeds.take(1)
    feeds.send(2)
    slots[1].one()
    outs.two()
    slots[0].end()

    def middle_steps(index, carried):
        step = 2 - index
        flash(step)
        hand(step).start()
        return carried

    lax.fori_loop(0, 2, middle_steps, 0)
    feeds.take(2)
    feeds.send(3)
    slots[1].two()
    slots[2].one()
    outs.three()
    flash(0)
    own_rows = pl.ds(pl.multiple_of(depth * shard, shard), shard)
    attended_ref[:, columns_of(depth, 256)] = o_ref[own_rows, :]
    store(o_ref, o_out)
    feeds.take(3)
    slots[2].two()
    slots[3].one()
    slots[1].three()
    outs.end()
    store(out_ref, out_weight_out)
    for step in range(1, PLANES):
        source = lax.rem(depth - step + PLANES, PLANES)
        links.got(across + step, attended_ref.at[:, columns_of(source, 256)])
    half = shard // 2
    for part in range(2):
        rows = pl.ds(part * half, half)
        middle = held[depth, rows, :].astype(jnp.float32) + tokens_dot(
            attended_ref[rows, :], out_ref[...], 1, 0
        )
        middle_ref[rows, :] = middle
        factor = lax.rsqrt(jnp.mean(middle * middle, axis=-1, keepdims=True) + 1e-06)
        normed_ref[rows, :] = (middle * factor * gain_ref[1:2, :]).astype(jnp.bfloat16)
    slots[2].three()
    slots[1].end()
    slots[3].two()
    slots[2].end()
    slots[3].three()
    slots[3].end()
    for step in range(1, PLANES):
        hand(step).wait_send()
    links.drain()
    for copy in stores[4:]:
        copy.wait()


def opening(hidden, attn_piece, out_piece, feed_piece, cosine, sine_part, first_values, begin_column):
    length, width = first_values.shape
    rows = hidden.shape[0]
    count = feed_piece.shape[0]
    low, full = jnp.bfloat16, jnp.float32
    any_spec, vmem = pl.BlockSpec(memory_space=pl.ANY), pl.BlockSpec(memory_space=pltpu.VMEM)
    shape = jax.ShapeDtypeStruct
    return pl.pallas_call(
        open_kernel,
        in_specs=[any_spec] * 4 + [vmem] * 4,
        out_specs=[any_spec] * 8 + [vmem] * 6,
        out_shape=[
            shape((length, width), low),
            shape((length, width), low),
            shape((length, width), low),
            shape((length, width), low),
            shape((length, D), low),
            shape((ATTN_ROWS, D), low),
            shape((D, D), low),
            shape((PLANES, 8, count, PIECE), low),
            shape((16, D), full),
            shape((8, width), full),
            shape((width // 128, 8, length), full),
            shape((rows, D), full),
            shape((rows, D), low),
            shape((rows, D), low),
        ],
        scratch_shapes=[
            pltpu.VMEM((PLANES, rows, D), low),
            pltpu.VMEM((length, width), low),
            pltpu.VMEM((length, width), low),
            pltpu.VMEM((length, width), low),
            pltpu.VMEM((length, width), low),
            pltpu.VMEM((length, D), low),
            pltpu.VMEM((ATTN_ROWS, D), low),
            pltpu.VMEM((D, D), low),
            pltpu.SemaphoreType.DMA((OPEN_COPIES,)),
            pltpu.SemaphoreType.DMA((OPEN_COPIES,)),
            pltpu.SemaphoreType.DMA((12,)),
        ],
        compiler_params=pltpu.CompilerParams(
            vmem_limit_bytes=VMEM_LIMIT, collective_id=1, has_side_effects=True
        ),
        name="opening",
    )(hidden, attn_piece, out_piece, feed_piece, cosine, sine_part, first_values, begin_column)


def feed_kernel(normed_ref, grad_ref, pieces, feed_ref, back_ref, made_out, weight, made, act, gate, up, sem, out_sem):
    slot = pl.program_id(0)
    place = lax.axis_index("dp")
    now = lax.rem(slot, 2)

    def load(which, buffer):
        return [
            pltpu.make_async_copy(
                pieces.at[which, piece],
                weight.at[buffer, :, pl.ds(piece * PIECE, PIECE)],
                sem.at[buffer, piece],
            )
            for piece in range(8)
        ]

    def flush(which, buffer):
        return [
            pltpu.make_async_copy(
                made.at[buffer, :, piece_columns(place, index)],
                made_out.at[which, index & 1, index >> 1],
                out_sem.at[buffer, index],
            )
            for index in range(8)
        ]

    @pl.when(slot == 0)
    def _():
        for copy in load(slot, now):
            copy.start()
        feed_ref[...] = jnp.zeros_like(feed_ref)
        back_ref[...] = jnp.zeros_like(back_ref)

    @pl.when(slot + 1 < PLANES)
    def _():
        for copy in load(slot + 1, 1 - now):
            copy.start()

    for copy in load(slot, now):
        copy.wait()

    @pl.when(slot >= 2)
    def _():
        for copy in flush(slot - 2, now):
            copy.wait()

    count = weight.shape[1] // 3
    rows = normed_ref.shape[0]
    spans = [pl.ds(index * count, count) for index in range(3)]
    half = rows // 2
    for tile in range(2):
        at = pl.ds(tile * half, half)
        normed, grad = normed_ref[at, :], grad_ref[at, :]
        gates = tokens_dot(weight[now, spans[0], :], normed, 1, 1)
        ups = tokens_dot(weight[now, spans[1], :], normed, 1, 1)
        backs = tokens_dot(weight[now, spans[2], :], grad, 1, 1)
        sig = jax.nn.sigmoid(gates)
        active = gates * sig
        act[:, at] = (active * ups).astype(jnp.bfloat16)
        gate[:, at] = (backs * ups * sig * (1.0 + gates * (1.0 - sig))).astype(jnp.bfloat16)
        up[:, at] = (backs * active).astype(jnp.bfloat16)

    def columns(tile, carried):
        lanes = columns_of(tile, 256)
        normed, grad = normed_ref[:, lanes], grad_ref[:, lanes]
        made[now, spans[0], lanes] = tokens_dot(gate[...], normed, 1, 0).astype(jnp.bfloat16)
        made[now, spans[1], lanes] = tokens_dot(up[...], normed, 1, 0).astype(jnp.bfloat16)
        made[now, spans[2], lanes] = tokens_dot(act[...], grad, 1, 0).astype(jnp.bfloat16)
        feed_ref[:, lanes] += tokens_dot(act[...], weight[now, spans[2], lanes], 0, 0)
        back_ref[:, lanes] += tokens_dot(gate[...], weight[now, spans[0], lanes], 0, 0) + tokens_dot(
            up[...], weight[now, spans[1], lanes], 0, 0
        )
        return carried

    lax.fori_loop(0, D // 256, columns, 0)
    for copy in flush(slot, now):
        copy.start()

    @pl.when(slot == PLANES - 1)
    def _():
        for copy in flush(slot - 1, 1 - now) + flush(slot, now):
            copy.wait()


def feed(normed, grad, pieces):
    rows = normed.shape[0]
    count = pieces.shape[2]
    any_spec = pl.BlockSpec(memory_space=pl.ANY)
    whole = pl.BlockSpec((rows, D), lambda i: (0, 0))
    total = jax.ShapeDtypeStruct((rows, D), jnp.float32)
    narrow = pltpu.VMEM((count // 3, rows), jnp.bfloat16)
    return pl.pallas_call(
        feed_kernel,
        grid=(PLANES,),
        in_specs=[whole, whole, any_spec],
        out_specs=[whole, whole, any_spec],
        out_shape=[
            total,
            total,
            jax.ShapeDtypeStruct((PLANES, 2, 4, count, PIECE), jnp.bfloat16),
        ],
        scratch_shapes=[
            pltpu.VMEM((2, count, D), jnp.bfloat16),
            pltpu.VMEM((2, count, D), jnp.bfloat16),
            narrow,
            narrow,
            narrow,
            pltpu.SemaphoreType.DMA((2, 8)),
            pltpu.SemaphoreType.DMA((2, 8)),
        ],
        compiler_params=pltpu.CompilerParams(vmem_limit_bytes=VMEM_LIMIT),
        cost_estimate=cost(24 * rows * D * count, 40 << 20),
        name="feed",
    )(normed, grad, pieces)


def flash_back_kernel(*refs):
    low_ref, q_ref, k_ref, v_ref, o_ref = refs[:5]
    incoming = refs[5:9]
    log_ref, begin_ref, cos_ref, sin_ref = refs[9:13]
    dq_ref, dk_ref, dv_ref, first_ref = refs[13:17]
    grad, inner, total, queries, grads, sem = refs[17:]
    pair, block = pl.program_id(0), pl.program_id(1)
    depth = lax.axis_index("mp")
    length = q_ref.shape[0]
    rows = length // BLOCKS
    shard = length // PLANES
    lane = lax.broadcasted_iota(jnp.int32, (rows, 128), 1)

    @pl.when(block == 0)
    def _():
        copies = [
            pltpu.make_async_copy(
                piece.at[:, pl.ds(pl.multiple_of(pair * 128, 128), 128)],
                grad.at[pl.ds(pl.multiple_of(lax.rem(depth - index + PLANES, PLANES) * shard, shard), shard)],
                sem.at[index],
            )
            for index, piece in enumerate(incoming)
        ]
        for copy in copies:
            copy.start()
        for copy in copies:
            copy.wait()
        total[...] = jnp.zeros_like(total)
        for index in range(BLOCKS):
            span = pl.ds(index * rows, rows)
            product = grad[span, :].astype(jnp.float32) * o_ref[span, :].astype(jnp.float32)
            turned = jnp.transpose(product)
            for head in range(2):
                inner[head : head + 1, span] = jnp.sum(
                    turned[head * HD : head * HD + HD], axis=0, keepdims=True
                )
                keep = (lane < HD) == (head == 0)
                none = jnp.zeros((rows, 128), jnp.bfloat16)
                queries[head, span, :] = jnp.where(keep, q_ref[span, :], none)
                grads[head, span, :] = jnp.where(keep, grad[span, :], none)

    start = pl.multiple_of(block * rows, rows)
    keys, values = k_ref[pl.ds(start, rows), :], v_ref[pl.ds(start, rows), :]
    keeps = [lane < HD, lane >= HD]
    own_keys = [jnp.where(keep, keys, jnp.zeros_like(keys)) for keep in keeps]
    seen = start + lax.broadcasted_iota(jnp.int32, (rows, rows), 0)
    across = lax.broadcasted_iota(jnp.int32, (1, rows), 1)

    def one(index, carried):
        key_sum, value_sum = carried
        at = pl.multiple_of(index * rows, rows)
        span = pl.ds(at, rows)
        visible = (seen >= begin_ref[0:1, span]) & (seen <= across + at)
        query_sum = total[span, :]
        for head in range(2):
            query, out_grad = queries[head, span, :], grads[head, span, :]
            scores = tokens_dot(keys, query, 1, 1)
            shares = jnp.where(visible, jnp.exp2(scores - log_ref[0, head : head + 1, span]), 0.0)
            share_grad = tokens_dot(values, out_grad, 1, 1)
            score_grad = (shares * (share_grad - inner[head : head + 1, span])).astype(jnp.bfloat16)
            value_sum = value_sum + tokens_dot(shares.astype(jnp.bfloat16), out_grad, 1, 0)
            key_sum = key_sum + tokens_dot(score_grad, query, 1, 0)
            query_sum = query_sum + tokens_dot(score_grad, own_keys[head], 0, 0)
        total[span, :] = query_sum
        return (key_sum, value_sum)

    last = block + 1
    for index in range(1, BLOCKS):
        reaches = (index > block) & (low_ref[index] < start + rows)
        last = last + jnp.where(reaches, 1, 0)
    empty = jnp.zeros((rows, 128), jnp.float32)
    key_sum, value_sum = lax.fori_loop(block, last, one, (empty, empty))
    span = pl.ds(start, rows)
    dk_ref[span, :] = turn(key_sum * (1 / LOG2E), cos_ref[span, :], sin_ref[span, :], False).astype(jnp.bfloat16)
    dv_ref[span, :] = (0.5 * value_sum).astype(jnp.bfloat16)
    first_ref[span, :] = 0.5 * value_sum
    query_sum = total[span, :] * HD**-0.5
    dq_ref[span, :] = turn(query_sum, cos_ref[span, :], sin_ref[span, :], False).astype(jnp.bfloat16)


def flash_back(queries, keys, values, attended, incoming, logs, begin_row, cosine, sine_part, lows):
    length, width = queries.shape
    pairs = width // 128
    column = pl.BlockSpec((length, 128), lambda p, j, low: (0, p))
    table = pl.BlockSpec((length, 128), lambda p, j, low: (0, 0))
    any_spec = pl.BlockSpec(memory_space=pl.ANY)
    return pl.pallas_call(
        flash_back_kernel,
        grid_spec=pltpu.PrefetchScalarGridSpec(
            num_scalar_prefetch=1,
            grid=(pairs, BLOCKS),
            in_specs=[column] * 4
            + [any_spec] * 4
            + [
                pl.BlockSpec((1, 8, length), lambda p, j, low: (p, 0, 0)),
                pl.BlockSpec((8, length), lambda p, j, low: (0, 0)),
                table,
                table,
            ],
            out_specs=[column] * 4,
            scratch_shapes=[
                pltpu.VMEM((length, 128), jnp.bfloat16),
                pltpu.VMEM((8, length), jnp.float32),
                pltpu.VMEM((length, 128), jnp.float32),
                pltpu.VMEM((2, length, 128), jnp.bfloat16),
                pltpu.VMEM((2, length, 128), jnp.bfloat16),
                pltpu.SemaphoreType.DMA((PLANES,)),
            ],
        ),
        out_shape=[jax.ShapeDtypeStruct((length, width), jnp.bfloat16)] * 3
        + [jax.ShapeDtypeStruct((length, width), jnp.float32)],
        compiler_params=pltpu.CompilerParams(vmem_limit_bytes=VMEM_LIMIT),
        cost_estimate=cost(24 * length * length * width, 12 << 20),
        name="flash_back",
    )(lows, queries, keys, values, attended, *incoming, logs, begin_row, cosine, sine_part)


def middle_back_kernel(*refs):
    middle_ref, grad_ref, back_ref, weight_ref, gain_ref = refs[:5]
    low_ref, dm_ref, gain_grad_ref = refs[5:8]
    outs = refs[8:12]
    depth = lax.axis_index("mp")
    half = middle_ref.shape[0] // 2
    gain = gain_ref[1:2, :]
    gain_grad_ref[...] = jnp.zeros_like(gain_grad_ref)
    for tile in range(2):
        rows = pl.ds(tile * half, half)
        middle, incoming = middle_ref[rows, :], back_ref[rows, :]
        factor = lax.rsqrt(jnp.mean(middle * middle, axis=-1, keepdims=True) + 1e-06)
        scaled = incoming * gain
        mean = jnp.mean(scaled * middle, axis=-1, keepdims=True)
        total = grad_ref[rows, :].astype(jnp.float32) + factor * scaled - middle * (factor**3 * mean)
        gain_grad_ref[0:1, :] += jnp.sum(incoming * middle * factor, axis=0, keepdims=True)
        dm_ref[rows, :] = total
        low_ref[rows, :] = total.astype(jnp.bfloat16)
    for index, out in enumerate(outs):
        owner = lax.rem(depth + index, PLANES)
        rows = pl.ds(pl.multiple_of(owner * 256, 256), 256)
        out[...] = tokens_dot(low_ref[...], weight_ref[rows, :], 1, 1).astype(jnp.bfloat16)


def middle_back(middle, grad, back, weight, gains):
    rows = middle.shape[0]
    return pl.pallas_call(
        middle_back_kernel,
        out_shape=[
            jax.ShapeDtypeStruct((rows, D), jnp.bfloat16),
            jax.ShapeDtypeStruct((rows, D), jnp.float32),
            jax.ShapeDtypeStruct((8, D), jnp.float32),
        ]
        + [jax.ShapeDtypeStruct((rows, 256), jnp.bfloat16)] * PLANES,
        compiler_params=pltpu.CompilerParams(vmem_limit_bytes=VMEM_LIMIT),
        cost_estimate=cost(2 * rows * D * D, 12 << 20),
        name="middle_back",
    )(middle, grad, back, weight, gains)


def grad_kernel(*refs):
    wide, other_ref, out_ref, acc, sem = refs[:-4], refs[-4], refs[-3], refs[-2], refs[-1]
    place = lax.axis_index("dp")
    step = pl.program_id(0)
    row = 0
    for one in wide:
        count = one.shape[1]
        acc[pl.ds(row, count), :] = tokens_dot(one[...], other_ref[...], 0, 0).astype(jnp.bfloat16)
        row += count
    copies = []
    for part in range(2):
        at = jnp.bitwise_xor(place, 2 * step + part)
        to = out_ref.at[lax.rem(at, 2), lax.div(at, 2)]
        copies.append(pltpu.make_async_copy(acc.at[:, pl.ds(part * PIECE, PIECE)], to, sem.at[part]))
    for copy in copies:
        copy.start()
    for copy in copies:
        copy.wait()


def weight_grad(wide, other, name):
    rows = other.shape[0]
    count = sum(one.shape[1] for one in wide)
    return pl.pallas_call(
        grad_kernel,
        grid=(D // 256,),
        in_specs=[pl.BlockSpec(one.shape, lambda i: (0, 0)) for one in wide]
        + [pl.BlockSpec((rows, 256), lambda i: (0, i))],
        out_specs=pl.BlockSpec(memory_space=pl.ANY),
        out_shape=jax.ShapeDtypeStruct((2, 4, count, PIECE), jnp.bfloat16),
        scratch_shapes=[pltpu.VMEM((count, 256), jnp.bfloat16), pltpu.SemaphoreType.DMA((2,))],
        compiler_params=pltpu.CompilerParams(vmem_limit_bytes=VMEM_LIMIT),
        cost_estimate=cost(2 * rows * D * count, 8 << 20),
        name=name,
    )(*wide, other)


def input_back_kernel(dq_ref, dk_ref, dv_ref, weight_ref, n_ref, gain_ref, out_ref, gain_grad_ref):
    @pl.when(pl.program_id(0) == 0)
    def _():
        gain_grad_ref[...] = jnp.zeros_like(gain_grad_ref)

    incoming = (
        tokens_dot(dq_ref[...], weight_ref[pl.ds(0, 256), :], 1, 0)
        + tokens_dot(dk_ref[...], weight_ref[pl.ds(256, 256), :], 1, 0)
        + tokens_dot(dv_ref[...], weight_ref[pl.ds(512, 256), :], 1, 0)
    )
    out_ref[0] = incoming.astype(jnp.bfloat16)
    gain_grad_ref[0:1, :] += (
        jnp.sum(incoming * n_ref[...].astype(jnp.float32), axis=0, keepdims=True) / gain_ref[0:1, :]
    )


def input_back(grads, weight, normed, gains):
    length = normed.shape[0]
    rows = length // PLANES
    tile = pl.BlockSpec((rows, 256), lambda i: (i, 0))
    whole = lambda *shape: pl.BlockSpec(shape, lambda i: (0,) * len(shape))
    return pl.pallas_call(
        input_back_kernel,
        grid=(PLANES,),
        in_specs=[tile] * 3
        + [whole(ATTN_ROWS, D), pl.BlockSpec((rows, D), lambda i: (i, 0)), whole(16, D)],
        out_specs=[pl.BlockSpec((1, rows, D), lambda i: (i, 0, 0)), whole(8, D)],
        out_shape=[
            jax.ShapeDtypeStruct((PLANES, rows, D), jnp.bfloat16),
            jax.ShapeDtypeStruct((8, D), jnp.float32),
        ],
        compiler_params=pltpu.CompilerParams(vmem_limit_bytes=VMEM_LIMIT),
        cost_estimate=cost(2 * length * D * 768, 12 << 20),
        name="input_back",
    )(*grads, weight, normed, gains)


def permute(values, pairs):
    return lax.ppermute(values, ("dp", "mp"), pairs)


def swap(values, bit):
    return permute(
        values,
        [
            (place * PLANES + depth, (place ^ bit) * PLANES + depth)
            for place in range(8)
            for depth in range(PLANES)
        ],
    )


def along(values, moves):
    return permute(
        values,
        [(place * PLANES + a, place * PLANES + b) for place in range(8) for a, b in moves],
    )


def added(a, b):
    return (a.astype(jnp.float32) + b.astype(jnp.float32)).astype(jnp.bfloat16)


def fold(keep, send, bits):
    got = swap(send, 1)
    mine, theirs = added(keep[:2], got[:2]), added(keep[2:], got[2:])
    got = swap(theirs, bits[0])
    mine, theirs = added(mine[0], got[0]), added(mine[1], got[1])
    return added(mine, swap(theirs, bits[1]))


def fold_line(block, depth):
    right = left = None
    for step in range(1, PLANES):
        there = block(jnp.minimum(depth + PLANES - step, PLANES - 1))
        right = along(
            there if right is None else added(there, right), [(a, a + 1) for a in range(step)]
        )
        there = block(jnp.maximum(depth - PLANES + step, 0))
        left = along(
            there if left is None else added(there, left),
            [(a, a - 1) for a in range(PLANES - step, PLANES)],
        )
    return (
        block(depth).astype(jnp.float32) + right.astype(jnp.float32) + left.astype(jnp.float32)
    )


def exchange(parts):
    return [parts[0]] + [
        along(parts[step], [(a, (a + step) % PLANES) for a in range(PLANES)])
        for step in range(1, PLANES)
    ]


def fast_shards(
    hidden_in,
    segment_ids,
    first_values,
    grad_out,
    input_proj,
    output_proj,
    expand_proj,
    reduce_proj,
    norm_gains,
    old_moment_input,
    old_moment_output,
    old_moment_expand,
    old_moment_reduce,
    old_moment_gains,
    old_square_input,
    old_square_output,
    old_square_expand,
    old_square_reduce,
    old_square_gains,
):
    place, depth = lax.axis_index("dp"), lax.axis_index("mp")
    low = jnp.bfloat16
    hidden, out_cotangent = hidden_in[0], grad_out[0]
    seg_row = segment_ids[0]
    length = seg_row.shape[0]
    shard = hidden.shape[0]
    ffs = reduce_proj.shape[0]

    attn_piece = jnp.concatenate(
        [
            input_proj.astype(low).transpose(0, 2, 1).reshape(768, PIECE),
            norm_gains.astype(low),
            jnp.zeros((14, PIECE), low),
        ]
    )
    feed_piece = jnp.concatenate(
        [
            expand_proj.astype(low).transpose(0, 2, 1).reshape(2 * ffs, PIECE),
            reduce_proj.astype(low),
        ]
    )

    begins = jnp.zeros_like(seg_row)
    for number in range(1, 7):
        start = jnp.sum((seg_row < number).astype(jnp.int32))
        begins = jnp.where(seg_row == number, start, begins)
    lows = begins[:: length // BLOCKS]
    offset = (jnp.arange(length, dtype=jnp.int32) - begins).astype(jnp.float32)
    inverse_rates = 10000.0 ** (-2.0 * jnp.arange(HD // 2, dtype=jnp.float32) / HD)
    angles = offset[:, None] * inverse_rates[None, :]
    cosine, sine = jnp.cos(angles), jnp.sin(angles)
    cosine = jnp.concatenate([cosine] * 4, axis=1)
    sine_part = jnp.concatenate([-sine, sine, -sine, sine], axis=1)

    (
        queries,
        keys,
        values,
        attended,
        normed,
        attn_weight,
        out_weight,
        feed_all,
        gains,
        squares,
        logs,
        middle,
        normed_two,
        attended_own,
    ) = opening(
        hidden,
        attn_piece,
        output_proj.astype(low),
        feed_piece,
        cosine,
        sine_part,
        first_values[0],
        begins[:, None],
    )
    feed_out, normed_two_grad, feed_parts = feed(normed_two, out_cotangent, feed_all)
    made = [fold(feed_parts[slot, 0], feed_parts[slot, 1], (4, 2)) for slot in range(PLANES)]
    layer_output = (middle + feed_out).astype(low)[None]
    branch_low, middle_grad, gain_two, *out_grads = middle_back(
        middle, out_cotangent, normed_two_grad, out_weight, gains
    )
    incoming = exchange(out_grads)
    out_made = weight_grad([attended_own], branch_low, "output_grad")
    out_made = fold(out_made[0], out_made[1], (4, 2))
    feed_made = jnp.stack(made)

    dq, dk, dv, values_grad = flash_back(
        queries,
        keys,
        values,
        attended,
        incoming,
        logs,
        jnp.broadcast_to(begins[None], (8, length)),
        cosine,
        sine_part,
        lows,
    )
    slot_table = jnp.array(
        [[[s[2] for s in SLOTS[plane]].index(j) for j in range(PLANES)] for plane in range(PLANES)],
        jnp.int32,
    )[depth]
    weight_total = fold_line(
        lambda j: jnp.concatenate(
            [
                lax.dynamic_index_in_dim(feed_made, slot_table[j], 0, False),
                lax.dynamic_slice_in_dim(out_made, j * 256, 256, 0),
            ]
        ),
        depth,
    )
    input_partial, gain_one = input_back((dq, dk, dv), attn_weight, normed, gains)
    attn_made = weight_grad([dq, dk, dv], normed, "input_grad")
    normed_grad = fold_line(lambda j: lax.dynamic_index_in_dim(input_partial, j, 0, False), depth)
    attn_total = fold(attn_made[0], attn_made[1], (4, 2)).astype(jnp.float32)

    small = jnp.concatenate(
        [
            gain_one[0].reshape(8, PIECE),
            gain_two[0].reshape(8, PIECE),
            jnp.broadcast_to(jnp.sum(squares[:2], axis=1)[:, None], (2, PIECE)),
            jnp.zeros((6, PIECE), jnp.float32),
        ]
    )
    for bit in (1, 2, 4):
        small = small + swap(small, bit)
    for bit in (1, 2):
        small = small + along(small, [(a, a ^ bit) for a in range(PLANES)])
    value_norms = jnp.sqrt(small[16:18, 0] / (8 * length * D))
    gain_total = lax.dynamic_index_in_dim(small[:16].reshape(2, 8, PIECE), place, 1, False)

    hidden32 = hidden.astype(jnp.float32)
    factor_one = rms_factor(hidden32)
    input_part, _ = norm_back(hidden32, factor_one, gains[0], normed_grad)
    input_grad = (middle_grad + input_part)[None]

    expand_total = weight_total[: 2 * ffs].reshape(2, ffs, PIECE).transpose(0, 2, 1)
    reduce_total = weight_total[2 * ffs : 3 * ffs]
    out_total = weight_total[3 * ffs :]
    attn_total = attn_total.reshape(3, 256, PIECE).transpose(0, 2, 1)
    new_input = adamw(input_proj, attn_total, old_moment_input, old_square_input, D ** (-0.5), 0.1)
    new_output = adamw(
        output_proj,
        out_total,
        old_moment_output,
        old_square_output,
        max(1, 8 * HEADS * HD // LEN) ** (-0.5),
        0.1,
    )
    new_expand = adamw(
        expand_proj, expand_total, old_moment_expand, old_square_expand, D ** (-0.5), 0.1
    )
    new_reduce = adamw(
        reduce_proj, reduce_total, old_moment_reduce, old_square_reduce, (FF // 3) ** (-0.5), 0.1
    )
    new_gains = adamw(norm_gains, gain_total, old_moment_gains, old_square_gains, 0.2, 0.0)
    return (
        layer_output,
        input_grad,
        values_grad[None],
        value_norms,
        new_input[0],
        new_output[0],
        new_expand[0],
        new_reduce[0],
        new_gains[0],
        new_input[1],
        new_output[1],
        new_expand[1],
        new_reduce[1],
        new_gains[1],
        new_input[2],
        new_output[2],
        new_expand[2],
        new_reduce[2],
        new_gains[2],
    )


def solution(mesh):
    quick = mesh.shape["dp"] == 8 and mesh.shape["mp"] == PLANES
    return jax.shard_map(
        fast_shards if quick else shards,
        mesh=mesh,
        in_specs=(
            P("dp", "mp", None),
            P("dp", None),
            P("dp", None, "mp"),
            P("dp", "mp", None),
            P(None, "dp", "mp"),
            P("mp", "dp"),
            P(None, "dp", "mp"),
            P("mp", "dp"),
            P(None, "dp"),
            P(None, "dp", "mp"),
            P("mp", "dp"),
            P(None, "dp", "mp"),
            P("mp", "dp"),
            P(None, "dp"),
            P(None, "dp", "mp"),
            P("mp", "dp"),
            P(None, "dp", "mp"),
            P("mp", "dp"),
            P(None, "dp"),
        ),
        out_specs=(
            P("dp", "mp", None),
            P("dp", "mp", None),
            P("dp", None, "mp"),
            P(),
            P(None, "dp", "mp"),
            P("mp", "dp"),
            P(None, "dp", "mp"),
            P("mp", "dp"),
            P(None, "dp"),
            P(None, "dp", "mp"),
            P("mp", "dp"),
            P(None, "dp", "mp"),
            P("mp", "dp"),
            P(None, "dp"),
            P(None, "dp", "mp"),
            P("mp", "dp"),
            P(None, "dp", "mp"),
            P("mp", "dp"),
            P(None, "dp"),
        ),
        check_vma=False,
    )
```

```python
import functools
import math

import jax
import jax.numpy as jnp
from jax import lax
from jax.experimental import pallas as pl
from jax.experimental.pallas import tpu as pltpu
from jax.sharding import PartitionSpec as P

D = 1024
HEADS = 16
HD = 64
FF = 2816
LEN = 2048
STEP = 5
PLANES = 4
PIECE = 128
BLOCKS = 4
ATTN_ROWS = 784
VMEM_LIMIT = 56 << 20
OPEN_COPIES = 66
CLOSE_COPIES = 64
CLOSE_VMEM = 60 << 20


def arrivals(plane):
    order = [(0, 0, plane)]
    for hop in range(1, PLANES):
        if plane + hop < PLANES:
            order.append((0, hop, plane + hop))
        if plane - hop >= 0:
            order.append((1, hop, plane - hop))
    return order


SLOTS = [arrivals(plane) for plane in range(PLANES)]


def cost(flops, moved):
    return pl.CostEstimate(flops=flops, bytes_accessed=moved, transcendentals=0)


def rope_tables(seg_row, head_size):
    length = seg_row.shape[0]
    places = jnp.arange(length, dtype=jnp.int32)
    begins = jnp.sum((seg_row[None, :] < seg_row[:, None]).astype(jnp.int32), axis=1)
    offset = (places - begins).astype(jnp.float32)
    inverse_rates = 10000.0 ** (-2.0 * jnp.arange(head_size // 2, dtype=jnp.float32) / head_size)
    angles = offset[:, None] * inverse_rates[None, :]
    return (jnp.cos(angles)[:, None, :], jnp.sin(angles)[:, None, :])


def rotate(values, cosine, sine_part, forward):
    half_size = values.shape[-1] // 2
    first_half = values[..., :half_size]
    second_half = values[..., half_size:]
    if forward:
        return jnp.concatenate(
            [
                first_half * cosine - second_half * sine_part,
                second_half * cosine + first_half * sine_part,
            ],
            axis=-1,
        )
    return jnp.concatenate(
        [
            first_half * cosine + second_half * sine_part,
            second_half * cosine - first_half * sine_part,
        ],
        axis=-1,
    )


def rms_factor(values):
    return lax.rsqrt(jnp.mean(values * values, axis=-1, keepdims=True) + 1e-06)


def norm_back(values, factor, gain_row, incoming):
    scaled = incoming * gain_row
    value_grad = factor * scaled - values * factor**3 * jnp.mean(
        scaled * values, axis=-1, keepdims=True
    )
    gain_grad = jnp.sum(incoming * values * factor, axis=0)
    return (value_grad, gain_grad)


def visible_block(seg_row, first_row, block_rows):
    length = seg_row.shape[0]
    query_seg = lax.dynamic_slice_in_dim(seg_row, first_row, block_rows, 0)
    query_places = first_row + jnp.arange(block_rows, dtype=jnp.int32)
    key_places = jnp.arange(length, dtype=jnp.int32)
    return (query_seg[:, None] == seg_row[None, :]) & (query_places[:, None] >= key_places[None, :])


def block_scores(queries, keys_rot, seg_row, first_row, block_rows, score_scale):
    query_block = lax.dynamic_slice_in_dim(queries, first_row, block_rows, 0)
    visible = visible_block(seg_row, first_row, block_rows)
    scores = (
        jnp.einsum("qhd,khd->hqk", query_block, keys_rot, preferred_element_type=jnp.float32)
        * score_scale
    )
    return (query_block, jnp.where(visible[None], scores, -1e30))


def attend(queries, keys_rot, mixed_values, seg_row, score_scale):
    length = queries.shape[0]
    block_rows = min(512, length)

    def one_block(block_index):
        first_row = block_index * block_rows
        query_block, scores = block_scores(
            queries, keys_rot, seg_row, first_row, block_rows, score_scale
        )
        top_score = jnp.max(scores, axis=-1, keepdims=True)
        raised = jnp.exp(scores - top_score)
        totals = jnp.sum(raised, axis=-1, keepdims=True)
        shares = (raised / totals).astype(jnp.bfloat16)
        combined = jnp.einsum(
            "hqk,khd->qhd", shares, mixed_values, preferred_element_type=jnp.float32
        )
        return (combined, (top_score + jnp.log(totals))[..., 0])

    combined, log_totals = lax.map(one_block, jnp.arange(length // block_rows, dtype=jnp.int32))
    return (combined.reshape(length, -1), log_totals)


def attend_back(queries, keys_rot, mixed_values, out_grad, log_totals, seg_row, score_scale):
    length = queries.shape[0]
    block_rows = min(512, length)

    def one_block(running, operands):
        key_sum, value_sum = running
        block_index, block_totals = operands
        first_row = block_index * block_rows
        query_block, scores = block_scores(
            queries, keys_rot, seg_row, first_row, block_rows, score_scale
        )
        grad_block = lax.dynamic_slice_in_dim(out_grad, first_row, block_rows, 0)
        shares = jnp.exp(scores - block_totals[..., None])
        share_grad = jnp.einsum(
            "qhd,khd->hqk", grad_block, mixed_values, preferred_element_type=jnp.float32
        )
        inner = jnp.sum(shares * share_grad, axis=-1, keepdims=True)
        score_grad = (shares * (share_grad - inner)).astype(jnp.bfloat16)
        query_grad = (
            jnp.einsum("hqk,khd->qhd", score_grad, keys_rot, preferred_element_type=jnp.float32)
            * score_scale
        )
        key_sum = (
            key_sum
            + jnp.einsum(
                "hqk,qhd->khd", score_grad, query_block, preferred_element_type=jnp.float32
            )
            * score_scale
        )
        value_sum = value_sum + jnp.einsum(
            "hqk,qhd->khd",
            shares.astype(jnp.bfloat16),
            grad_block,
            preferred_element_type=jnp.float32,
        )
        return ((key_sum, value_sum), query_grad)

    empty_sum = jnp.zeros(keys_rot.shape, jnp.float32)
    (key_grad, value_grad), query_grad = lax.scan(
        one_block,
        (empty_sum, empty_sum),
        (jnp.arange(length // block_rows, dtype=jnp.int32), log_totals),
    )
    return (query_grad.reshape(keys_rot.shape), key_grad, value_grad)


def adamw(master, gradient, moment, square, step_rate, decay):
    new_moment = 0.5 * moment + 0.5 * gradient
    new_square = 0.5 * square + 0.5 * gradient * gradient
    correct = 1.0 - 0.5**STEP
    update = new_moment / correct / (jnp.sqrt(new_square / correct) + 1e-08)
    return (master - step_rate * (update + decay * master), new_moment, new_square)


def shards(
    hidden_in,
    segment_ids,
    first_values,
    grad_out,
    input_proj,
    output_proj,
    expand_proj,
    reduce_proj,
    norm_gains,
    old_moment_input,
    old_moment_output,
    old_moment_expand,
    old_moment_reduce,
    old_moment_gains,
    old_square_input,
    old_square_output,
    old_square_expand,
    old_square_reduce,
    old_square_gains,
):
    attn_weight, out_weight, expand_weight, reduce_weight, gains_low = (
        lax.all_gather(input_proj.astype(jnp.bfloat16), "dp", axis=1, tiled=True),
        lax.all_gather(output_proj.astype(jnp.bfloat16), "dp", axis=1, tiled=True),
        lax.all_gather(expand_proj.astype(jnp.bfloat16), "dp", axis=1, tiled=True),
        lax.all_gather(reduce_proj.astype(jnp.bfloat16), "dp", axis=1, tiled=True),
        lax.all_gather(norm_gains.astype(jnp.bfloat16), "dp", axis=1, tiled=True),
    )
    gains = gains_low.astype(jnp.float32)
    hidden = hidden_in[0].astype(jnp.float32)
    seg_row = segment_ids[0]
    length = seg_row.shape[0]
    first_in = first_values[0].astype(jnp.float32)
    local_heads = attn_weight.shape[2] // HD
    score_scale = 1.0 / math.sqrt(HD)
    factor_one = rms_factor(hidden)
    normed_one = (hidden * factor_one * gains[0]).astype(jnp.bfloat16)
    all_normed, all_grad_out = (
        lax.all_gather(normed_one, "mp", axis=0, tiled=True),
        lax.all_gather(grad_out[0], "mp", axis=0, tiled=True),
    )
    projected = jnp.einsum(
        "td,cde->cte", all_normed, attn_weight, preferred_element_type=jnp.float32
    )
    cosine, sine_part = rope_tables(seg_row, HD)
    queries = rotate(projected[0].reshape(length, local_heads, HD), cosine, sine_part, True).astype(
        jnp.bfloat16
    )
    keys_rot = rotate(
        projected[1].reshape(length, local_heads, HD), cosine, sine_part, True
    ).astype(jnp.bfloat16)
    blended = 0.5 * projected[2] + 0.5 * first_in
    mixed_values = blended.astype(jnp.bfloat16).reshape(length, local_heads, HD)
    square_terms = jnp.stack([jnp.sum(first_in * first_in), jnp.sum(blended * blended)])
    attended, log_totals = attend(queries, keys_rot, mixed_values, seg_row, score_scale)
    attended_low = attended.astype(jnp.bfloat16)
    rows_part = attended_low
    branch = lax.psum_scatter(
        jnp.dot(rows_part, out_weight, preferred_element_type=jnp.float32),
        "mp",
        scatter_dimension=0,
        tiled=True,
    )
    middle = hidden + branch
    factor_two = rms_factor(middle)
    normed_two = (middle * factor_two * gains[1]).astype(jnp.bfloat16)
    all_normed_two = lax.all_gather(normed_two, "mp", axis=0, tiled=True)
    gate_up = jnp.einsum(
        "td,cdf->ctf", all_normed_two, expand_weight, preferred_element_type=jnp.float32
    )
    gate_sig = jax.nn.sigmoid(gate_up[0])
    gate_act = gate_up[0] * gate_sig
    activated = (gate_act * gate_up[1]).astype(jnp.bfloat16)
    rows_part = activated
    feed_out = lax.psum_scatter(
        jnp.dot(rows_part, reduce_weight, preferred_element_type=jnp.float32).astype(jnp.bfloat16),
        "mp",
        scatter_dimension=0,
        tiled=True,
    ).astype(jnp.float32)
    layer_output = (middle + feed_out).astype(jnp.bfloat16)[None]
    hidden_grad = jnp.einsum(
        "td,fd->tf", all_grad_out, reduce_weight, preferred_element_type=jnp.float32
    )
    reduce_grad = jnp.einsum(
        "tf,td->fd", activated, all_grad_out, preferred_element_type=jnp.float32
    )
    gate_grad = hidden_grad * gate_up[1] * gate_sig * (1.0 + gate_up[0] * (1.0 - gate_sig))
    up_grad = hidden_grad * gate_act
    pair_grad = jnp.stack([gate_grad, up_grad]).astype(jnp.bfloat16)
    expand_grad = jnp.einsum(
        "ctf,td->cdf", pair_grad, all_normed_two, preferred_element_type=jnp.float32
    )
    rows_part = pair_grad
    normed_two_grad = lax.psum_scatter(
        jnp.einsum(
            "ctf,cdf->td", rows_part, expand_weight, preferred_element_type=jnp.float32
        ).astype(jnp.bfloat16),
        "mp",
        scatter_dimension=0,
        tiled=True,
    ).astype(jnp.float32)
    middle_part, gain_two_grad = norm_back(middle, factor_two, gains[1], normed_two_grad)
    middle_grad = grad_out[0].astype(jnp.float32) + middle_part
    branch_low = middle_grad.astype(jnp.bfloat16)
    all_branch = lax.all_gather(branch_low, "mp", axis=0, tiled=True)
    out_grad = jnp.einsum("te,td->ed", attended_low, all_branch, preferred_element_type=jnp.float32)
    attended_grad = jnp.einsum(
        "td,ed->te", all_branch, out_weight, preferred_element_type=jnp.float32
    ).astype(jnp.bfloat16)
    query_grad, key_grad, mix_grad = attend_back(
        queries,
        keys_rot,
        mixed_values,
        attended_grad.reshape(length, local_heads, HD),
        log_totals,
        seg_row,
        score_scale,
    )
    query_grad = rotate(query_grad, cosine, sine_part, False).reshape(length, -1)
    key_grad = rotate(key_grad, cosine, sine_part, False).reshape(length, -1)
    mix_grad = mix_grad.reshape(length, -1)
    values_grad = (0.5 * mix_grad)[None]
    proj_grad = jnp.stack([query_grad, key_grad, 0.5 * mix_grad]).astype(jnp.bfloat16)
    attn_grad = jnp.einsum("cte,td->cde", proj_grad, all_normed, preferred_element_type=jnp.float32)
    rows_part = proj_grad
    normed_one_grad = lax.psum_scatter(
        jnp.einsum(
            "cte,cde->td", rows_part, attn_weight, preferred_element_type=jnp.float32
        ).astype(jnp.bfloat16),
        "mp",
        scatter_dimension=0,
        tiled=True,
    ).astype(jnp.float32)
    input_part, gain_one_grad = norm_back(hidden, factor_one, gains[0], normed_one_grad)
    input_grad = (middle_grad + input_part)[None]
    attn_total, out_total, expand_total, reduce_total = (
        lax.psum_scatter(
            attn_grad.astype(jnp.bfloat16), "dp", scatter_dimension=1, tiled=True
        ).astype(jnp.float32),
        lax.psum_scatter(
            out_grad.astype(jnp.bfloat16), "dp", scatter_dimension=1, tiled=True
        ).astype(jnp.float32),
        lax.psum_scatter(
            expand_grad.astype(jnp.bfloat16), "dp", scatter_dimension=1, tiled=True
        ).astype(jnp.float32),
        lax.psum_scatter(
            reduce_grad.astype(jnp.bfloat16), "dp", scatter_dimension=1, tiled=True
        ).astype(jnp.float32),
    )
    gain_totals, square_sums = lax.psum(
        (jnp.stack([gain_one_grad, gain_two_grad]), square_terms), ("dp", "mp")
    )
    gain_width = norm_gains.shape[1]
    gain_total = lax.dynamic_slice_in_dim(
        gain_totals, lax.axis_index("dp") * gain_width, gain_width, 1
    )
    value_norms = jnp.sqrt(square_sums / (lax.axis_size("dp") * length * D))
    new_input = adamw(input_proj, attn_total, old_moment_input, old_square_input, D ** (-0.5), 0.1)
    new_output = adamw(
        output_proj,
        out_total,
        old_moment_output,
        old_square_output,
        max(1, 8 * HEADS * HD // LEN) ** (-0.5),
        0.1,
    )
    new_expand = adamw(
        expand_proj, expand_total, old_moment_expand, old_square_expand, D ** (-0.5), 0.1
    )
    new_reduce = adamw(
        reduce_proj, reduce_total, old_moment_reduce, old_square_reduce, (FF // 3) ** (-0.5), 0.1
    )
    new_gains = adamw(norm_gains, gain_total, old_moment_gains, old_square_gains, 0.2, 0.0)
    return (
        layer_output,
        input_grad,
        values_grad,
        value_norms,
        new_input[0],
        new_output[0],
        new_expand[0],
        new_reduce[0],
        new_gains[0],
        new_input[1],
        new_output[1],
        new_expand[1],
        new_reduce[1],
        new_gains[1],
        new_input[2],
        new_output[2],
        new_expand[2],
        new_reduce[2],
        new_gains[2],
    )


def tokens_dot(a, b, left, right):
    return lax.dot_general(a, b, (((left,), (right,)), ((), ())), preferred_element_type=jnp.float32)


def piece_columns(place, step):
    start = jnp.bitwise_xor(place, step) * PIECE
    return pl.ds(pl.multiple_of(start, PIECE), PIECE)


def turn(values, cosine, sine_part, forward):
    lane = lax.broadcasted_iota(jnp.int32, values.shape, 1)
    swapped = jnp.where(
        lax.rem(lane, HD) < HD // 2, pltpu.roll(values, 96, 1), pltpu.roll(values, 32, 1)
    )
    if forward:
        return values * cosine + swapped * sine_part
    return values * cosine - swapped * sine_part


MESH = pl.DeviceIdType.MESH
LOG2E = 1.4426950408889634


def flip(place, bit):
    return place + bit - 2 * bit * lax.rem(lax.div(place, bit), 2)


def at_plane(depth, values):
    found = 0
    for plane, value in enumerate(values):
        found = found + jnp.where(depth == plane, value, 0)
    return found


def slot_at(depth, way, hop):
    return at_plane(
        depth,
        [
            next((k for k, s in enumerate(SLOTS[plane]) if s[:2] == (way, hop)), 0)
            for plane in range(PLANES)
        ],
    )


def columns_of(piece, width=PIECE):
    return pl.ds(pl.multiple_of(piece * width, width), width)


class Links:
    def __init__(self, send, recv):
        self.send, self.recv, self.count, self.started = send, recv, 0, []
        self.place, self.depth = lax.axis_index("dp"), lax.axis_index("mp")

    def number(self, count=1):
        self.count += count
        return self.count - count

    def copy(self, number, source, target, to):
        return pltpu.make_async_remote_copy(
            src_ref=source,
            dst_ref=target,
            send_sem=self.send.at[number],
            recv_sem=self.recv.at[number],
            device_id=to,
            device_id_type=MESH,
        )

    def go(self, number, source, target, to, when=None):
        copy = self.copy(number, source, target, to)
        self.started.append((number, source, target, to, when))
        if when is None:
            copy.start()
        else:
            pl.when(when)(copy.start)

    def got(self, number, landed, when=None):
        copy = self.copy(number, landed, landed, (flip(self.place, 1), self.depth))
        if when is None:
            copy.wait_recv()
        else:
            pl.when(when)(copy.wait_recv)

    def drain(self):
        for *parts, when in self.started:
            copy = self.copy(*parts)
            if when is None:
                copy.wait_send()
            else:
                pl.when(when)(copy.wait_send)

    def greet(self):
        barrier = pltpu.get_barrier_semaphore()
        others = [(flip(self.place, bit), self.depth) for bit in (1, 2, 4)]
        others += [(self.place, lax.rem(self.depth + step, PLANES)) for step in range(1, PLANES)]
        for other in others:
            pl.semaphore_signal(barrier, inc=1, device_id=other, device_id_type=MESH)
        pl.semaphore_wait(barrier, len(others))


class Spread:
    def __init__(self, links, own, spot, bits):
        self.links, self.own, self.spot, self.bits = links, own, spot, bits
        self.base = links.number(7)
        place = links.place
        self.first, self.second = flip(place, bits[0]), flip(place, bits[1])
        self.both = flip(self.first, bits[1])

    def to(self, bit):
        return (flip(self.links.place, bit), self.links.depth)

    def one(self):
        links = self.links
        links.go(self.base, self.own, self.spot(links.place), self.to(self.bits[0]))

    def two(self):
        links = self.links
        to = self.to(self.bits[1])
        links.go(self.base + 1, self.own, self.spot(links.place), to)
        links.got(self.base, self.spot(self.first))
        links.go(self.base + 2, self.spot(self.first), self.spot(self.first), to)

    def three(self):
        links = self.links
        to = self.to(1)
        links.go(self.base + 3, self.own, self.spot(links.place), to)
        links.go(self.base + 4, self.spot(self.first), self.spot(self.first), to)
        links.got(self.base + 1, self.spot(self.second))
        links.go(self.base + 5, self.spot(self.second), self.spot(self.second), to)
        links.got(self.base + 2, self.spot(self.both))
        links.go(self.base + 6, self.spot(self.both), self.spot(self.both), to)

    def end(self):
        links = self.links
        for index, piece in enumerate((links.place, self.first, self.second, self.both)):
            links.got(self.base + 3 + index, self.spot(flip(piece, 1)))


class Relay:
    def __init__(self, links, own, put):
        self.links, self.own, self.put = links, own, put
        self.base = links.number(2 * (PLANES - 1))

    def send(self, hop):
        links, depth = self.links, self.links.depth
        for way in range(2):
            to = depth + (1 if way else -1)
            when = (
                (depth >= hop - 1) & (depth < PLANES - 1)
                if way
                else (depth <= PLANES - hop) & (depth > 0)
            )
            source = self.own if hop == 1 else self.put(depth, way, hop - 1)
            links.go(
                self.base + 2 * (hop - 1) + way,
                source,
                self.put(to, way, hop),
                (links.place, jnp.clip(to, 0, PLANES - 1)),
                when,
            )

    def take(self, hop):
        links, depth = self.links, self.links.depth
        for way in range(2):
            when = depth >= hop if way else depth + hop < PLANES
            links.got(self.base + 2 * (hop - 1) + way, self.put(depth, way, hop), when)


def open_kernel(*refs):
    hidden, attn_piece, out_piece, feed_piece, cos_ref, sin_ref, first_ref, begin_ref = refs[:8]
    q_out, k_out, v_out, o_out, n_out, weight_out, out_weight_out, feed_all = refs[8:16]
    gain_ref, square_ref, log_ref, middle_ref, normed_ref, attended_ref = refs[16:22]
    held, q_ref, k_ref, v_ref, o_ref, n_ref, weight_ref, out_ref, send, recv, local = refs[22:]
    links = Links(send, recv)
    place, depth = links.place, links.depth
    shard = hidden.shape[0]
    stores = []

    def store(source, target):
        copy = pltpu.make_async_copy(source, target, local.at[len(stores)])
        copy.start()
        stores.append(copy)
        return copy

    block_at = lambda plane, way, hop: jnp.clip(plane + (-hop if way else hop), 0, PLANES - 1)
    wide = Relay(links, hidden, lambda plane, way, hop: held.at[block_at(plane, way, hop)])
    out_rows = lambda block: out_ref.at[
        pl.ds(pl.multiple_of(block * 256, 256), 256), columns_of(place)
    ]
    thin = Relay(links, out_piece, lambda plane, way, hop: out_rows(block_at(plane, way, hop)))
    feeds = Relay(
        links,
        feed_piece,
        lambda plane, way, hop: feed_all.at[slot_at(plane, way, hop), place],
    )
    attn = Spread(links, attn_piece, lambda piece: weight_ref.at[:, columns_of(piece)], (2, 4))
    outs = Spread(
        links, out_ref.at[:, columns_of(place)], lambda piece: out_ref.at[:, columns_of(piece)], (2, 4)
    )
    slots = [
        Spread(
            links,
            feed_piece if slot == 0 else feed_all.at[slot, place],
            lambda piece, slot=slot: feed_all.at[slot, piece],
            (2, 4) if slot % 2 == 0 else (4, 2),
        )
        for slot in range(PLANES)
    ]
    across = links.number(PLANES)

    links.greet()
    thin.send(1)
    wide.send(1)
    attn.one()
    own_hidden = store(hidden, held.at[depth])
    own_attn = store(attn_piece, weight_ref.at[:, columns_of(place)])
    own_out = store(out_piece, out_rows(depth))
    own_feed = store(feed_piece, feed_all.at[0, place])
    square_ref[...] = jnp.zeros_like(square_ref)
    attn.two()
    attn.three()
    slots[0].one()
    attn.end()
    for copy in (own_hidden, own_attn, own_out, own_feed):
        copy.wait()
    store(weight_ref, weight_out)
    gain_ref[...] = weight_ref[pl.ds(768, 16), :].astype(jnp.float32)

    def project(block):
        rows = pl.ds(pl.multiple_of(block * shard, shard), shard)
        values = held[block].astype(jnp.float32)
        factor = lax.rsqrt(jnp.mean(values * values, axis=-1, keepdims=True) + 1e-06)
        normed = (values * factor * gain_ref[0:1, :]).astype(jnp.bfloat16)
        n_ref[rows, :] = normed
        cosine, sine_part = cos_ref[rows, :], sin_ref[rows, :]
        query = tokens_dot(normed, weight_ref[pl.ds(0, 256), :], 1, 1)
        key = tokens_dot(normed, weight_ref[pl.ds(256, 256), :], 1, 1)
        value = tokens_dot(normed, weight_ref[pl.ds(512, 256), :], 1, 1)
        for half in range(2):
            lanes = slice(half * 128, half * 128 + 128)
            turned = turn(query[:, lanes], cosine, sine_part, True)
            q_ref[rows, lanes] = (turned * (HD**-0.5 * LOG2E)).astype(jnp.bfloat16)
            k_ref[rows, lanes] = turn(key[:, lanes], cosine, sine_part, True).astype(jnp.bfloat16)
        first = first_ref[rows, :].astype(jnp.float32)
        blended = 0.5 * value + 0.5 * first
        v_ref[rows, :] = blended.astype(jnp.bfloat16)
        square_ref[0:1, :] += jnp.sum(first * first, axis=0, keepdims=True)
        square_ref[1:2, :] += jnp.sum(blended * blended, axis=0, keepdims=True)

    def project_hop(hop):
        def one(side, carried):
            block = depth + hop * (2 * side - 1)
            pl.when((block >= 0) & (block < PLANES))(lambda: project(block))
            return carried

        lax.fori_loop(0, 2, one, 0)

    project(depth)
    wide.take(1)
    wide.send(2)
    thin.take(1)
    thin.send(2)
    slots[0].two()
    project_hop(1)
    wide.take(2)
    wide.send(3)
    thin.take(2)
    thin.send(3)
    project_hop(2)
    slots[0].three()
    wide.take(3)
    thin.take(3)
    feeds.send(1)
    outs.one()
    project_hop(3)
    store(n_ref, n_out)
    store(q_ref, q_out)
    store(k_ref, k_out)
    store(v_ref, v_out)

    lane = lax.broadcasted_iota(jnp.int32, (shard, 128), 1)
    inside = lax.broadcasted_iota(jnp.int32, (shard, shard), 1)
    down = lax.broadcasted_iota(jnp.int32, (shard, 1), 0)

    def flash_pair(block, pair):
        rows = pl.ds(pl.multiple_of(block * shard, shard), shard)
        lanes = columns_of(pair)
        query = q_ref[rows, lanes]
        begin = begin_ref[rows, :]
        parts = [
            jnp.where((lane < HD) == (head == 0), query, jnp.zeros_like(query)) for head in range(2)
        ]

        def tile(index, carried, visible):
            span = pl.ds(pl.multiple_of(index * shard, shard), shard)
            keys, values = k_ref[span, lanes], v_ref[span, lanes]
            after = []
            for head in range(2):
                top, total, summed = carried[3 * head : 3 * head + 3]
                scores = jnp.where(visible, tokens_dot(parts[head], keys, 1, 1), -1e30)
                raised_top = jnp.maximum(top, jnp.max(scores, axis=1, keepdims=True))
                shrink = jnp.exp2(top - raised_top)
                shares = jnp.exp2(scores - raised_top)
                total = total * shrink + jnp.sum(shares, axis=1, keepdims=True)
                summed = summed * shrink + tokens_dot(shares.astype(jnp.bfloat16), values, 1, 0)
                after += [raised_top, total, summed]
            return tuple(after)

        fresh = (
            jnp.full((shard, 1), -1e30, jnp.float32),
            jnp.zeros((shard, 1), jnp.float32),
            jnp.zeros((shard, 128), jnp.float32),
        )
        carried = tile(block, fresh + fresh, (inside >= begin - block * shard) & (inside <= down))
        top0, total0, sum0, top1, total1, sum1 = lax.fori_loop(
            0, block, lambda j, held: tile(j, held, inside >= begin - j * shard), carried
        )
        o_ref[rows, lanes] = jnp.where(lane < HD, sum0 / total0, sum1 / total1).astype(jnp.bfloat16)
        turned = jnp.transpose(
            jnp.where(lane < HD, top0 + jnp.log2(total0), top1 + jnp.log2(total1))
        )
        log_ref[pair, 0:1, rows] = turned[0:1]
        log_ref[pair, 1:2, rows] = turned[HD : HD + 1]

    own_columns = attended_ref.at[:, columns_of(depth, 256)]

    def hand(step):
        block = lax.rem(depth + step, PLANES)
        rows = pl.ds(pl.multiple_of(block * shard, shard), shard)
        return links.copy(across + step, o_ref.at[rows, :], own_columns, (place, block))

    def flash(step):
        block = lax.rem(depth + step, PLANES)

        def one(pair, carried):
            flash_pair(block, pair)
            return carried

        lax.fori_loop(0, 2, one, 0)

    flash(3)
    hand(3).start()
    feeds.take(1)
    feeds.send(2)
    slots[1].one()
    outs.two()
    slots[0].end()

    def middle_steps(index, carried):
        step = 2 - index
        flash(step)
        hand(step).start()
        return carried

    lax.fori_loop(0, 2, middle_steps, 0)
    feeds.take(2)
    feeds.send(3)
    slots[1].two()
    slots[2].one()
    outs.three()
    flash(0)
    own_rows = pl.ds(pl.multiple_of(depth * shard, shard), shard)
    attended_ref[:, columns_of(depth, 256)] = o_ref[own_rows, :]
    store(o_ref, o_out)
    feeds.take(3)
    slots[2].two()
    slots[3].one()
    slots[1].three()
    outs.end()
    store(out_ref, out_weight_out)
    for step in range(1, PLANES):
        source = lax.rem(depth - step + PLANES, PLANES)
        links.got(across + step, attended_ref.at[:, columns_of(source, 256)])
    half = shard // 2
    for part in range(2):
        rows = pl.ds(part * half, half)
        middle = held[depth, rows, :].astype(jnp.float32) + tokens_dot(
            attended_ref[rows, :], out_ref[...], 1, 0
        )
        middle_ref[rows, :] = middle
        factor = lax.rsqrt(jnp.mean(middle * middle, axis=-1, keepdims=True) + 1e-06)
        normed_ref[rows, :] = (middle * factor * gain_ref[1:2, :]).astype(jnp.bfloat16)
    slots[2].three()
    slots[1].end()
    slots[3].two()
    slots[2].end()
    slots[3].three()
    slots[3].end()
    for step in range(1, PLANES):
        hand(step).wait_send()
    links.drain()
    for copy in stores[4:]:
        copy.wait()


def opening(hidden, attn_piece, out_piece, feed_piece, cosine, sine_part, first_values, begin_column):
    length, width = first_values.shape
    rows = hidden.shape[0]
    count = feed_piece.shape[0]
    low, full = jnp.bfloat16, jnp.float32
    any_spec, vmem = pl.BlockSpec(memory_space=pl.ANY), pl.BlockSpec(memory_space=pltpu.VMEM)
    shape = jax.ShapeDtypeStruct
    return pl.pallas_call(
        open_kernel,
        in_specs=[any_spec] * 4 + [vmem] * 4,
        out_specs=[any_spec] * 8 + [vmem] * 6,
        out_shape=[
            shape((length, width), low),
            shape((length, width), low),
            shape((length, width), low),
            shape((length, width), low),
            shape((length, D), low),
            shape((ATTN_ROWS, D), low),
            shape((D, D), low),
            shape((PLANES, 8, count, PIECE), low),
            shape((16, D), full),
            shape((8, width), full),
            shape((width // 128, 8, length), full),
            shape((rows, D), full),
            shape((rows, D), low),
            shape((rows, D), low),
        ],
        scratch_shapes=[
            pltpu.VMEM((PLANES, rows, D), low),
            pltpu.VMEM((length, width), low),
            pltpu.VMEM((length, width), low),
            pltpu.VMEM((length, width), low),
            pltpu.VMEM((length, width), low),
            pltpu.VMEM((length, D), low),
            pltpu.VMEM((ATTN_ROWS, D), low),
            pltpu.VMEM((D, D), low),
            pltpu.SemaphoreType.DMA((OPEN_COPIES,)),
            pltpu.SemaphoreType.DMA((OPEN_COPIES,)),
            pltpu.SemaphoreType.DMA((12,)),
        ],
        compiler_params=pltpu.CompilerParams(
            vmem_limit_bytes=VMEM_LIMIT, collective_id=1, has_side_effects=True
        ),
        name="opening",
    )(hidden, attn_piece, out_piece, feed_piece, cosine, sine_part, first_values, begin_column)


def feed_kernel(*refs):
    normed_ref, grad_ref, middle_ref, pieces = refs[:4]
    back_ref, out_ref, made_out = refs[4:7]
    fed, weight, mine, theirs, made, halves, other_halves, send, recv, sem, out_sem = refs[7:]
    links = Links(send, recv)
    core = (flip(links.place, 1), links.depth)
    mine_first, theirs_first = lax.rem(links.place, 2), 1 - lax.rem(links.place, 2)
    count = weight.shape[1] // 3
    rows = normed_ref.shape[0]

    def load(which, buffer):
        return [
            pltpu.make_async_copy(
                pieces.at[which, piece],
                weight.at[buffer, :, pl.ds(piece * PIECE, PIECE)],
                sem.at[buffer, piece],
            )
            for piece in range(8)
        ]

    def flush(which, buffer):
        return [
            pltpu.make_async_copy(
                made.at[buffer, :, pl.ds(piece * PIECE, PIECE)],
                made_out.at[which, piece],
                out_sem.at[buffer, piece],
            )
            for piece in range(4)
        ]

    for copy in load(0, 0):
        copy.start()
    barrier = pltpu.get_barrier_semaphore()
    pl.semaphore_signal(barrier, inc=1, device_id=core, device_id_type=MESH)
    pl.semaphore_wait(barrier, 1)
    base = links.number(8)
    for index, ref in enumerate((normed_ref, grad_ref)):
        for piece in range(4):
            links.go(
                base + 4 * index + piece,
                ref.at[:, columns_of(2 * piece + theirs_first)],
                other_halves.at[index, :, pl.ds(piece * PIECE, PIECE)],
                core,
            )
            halves[index, :, pl.ds(piece * PIECE, PIECE)] = ref[:, columns_of(2 * piece + mine_first)]
    fed[...] = jnp.zeros_like(fed)
    back_ref[...] = jnp.zeros_like(back_ref)
    for index in range(2):
        for piece in range(4):
            links.got(
                base + 4 * index + piece, other_halves.at[index, :, pl.ds(piece * PIECE, PIECE)]
            )
    given = links.number(PLANES)
    hand = lambda slot: links.copy(given + slot, mine.at[lax.rem(slot, 2)], theirs.at[slot], core)
    spans = [pl.ds(index * count, count) for index in range(3)]
    half = rows // 2

    def forward(slot):
        now = lax.rem(slot, 2)
        for copy in load(slot, now):
            copy.wait()

        @pl.when(slot + 1 < PLANES)
        def _():
            for copy in load(slot + 1, 1 - now):
                copy.start()

        @pl.when(slot >= 2)
        def _():
            hand(slot - 2).wait_send()

        for tile in range(2):
            at = pl.ds(tile * half, half)
            normed, grad = normed_ref[at, :], grad_ref[at, :]
            gates = tokens_dot(weight[now, spans[0], :], normed, 1, 1)
            ups = tokens_dot(weight[now, spans[1], :], normed, 1, 1)
            backs = tokens_dot(weight[now, spans[2], :], grad, 1, 1)
            sig = jax.nn.sigmoid(gates)
            active = gates * sig
            mine[now, 2, :, at] = (active * ups).astype(jnp.bfloat16)
            mine[now, 0, :, at] = (backs * ups * sig * (1.0 + gates * (1.0 - sig))).astype(jnp.bfloat16)
            mine[now, 1, :, at] = (backs * active).astype(jnp.bfloat16)
        hand(slot).start()

        def columns(tile, carried):
            lanes = columns_of(tile, 256)
            fed[:, lanes] += tokens_dot(mine[now, 2], weight[now, spans[2], lanes], 0, 0)
            back_ref[:, lanes] += tokens_dot(
                mine[now, 0], weight[now, spans[0], lanes], 0, 0
            ) + tokens_dot(mine[now, 1], weight[now, spans[1], lanes], 0, 0)
            return carried

        lax.fori_loop(0, D // 256, columns, 0)

    def backward(slot):
        now = lax.rem(slot, 2)
        hand(slot).wait_recv()

        @pl.when(slot >= 2)
        def _():
            for copy in flush(slot - 2, now):
                copy.wait()

        def columns(tile, carried):
            lanes = columns_of(tile, 256)
            for index in range(3):
                which = index // 2
                made[now, spans[index], lanes] = (
                    tokens_dot(mine[now, index], halves[which, :, lanes], 1, 0)
                    + tokens_dot(theirs[slot, index], other_halves[which, :, lanes], 1, 0)
                ).astype(jnp.bfloat16)
            return carried

        lax.fori_loop(0, 2, columns, 0)
        for copy in flush(slot, now):
            copy.start()

    def one(step, carried):
        pl.when(step < PLANES)(lambda: forward(step))
        pl.when(step >= 1)(lambda: backward(step - 1))
        return carried

    lax.fori_loop(0, PLANES + 1, one, 0)
    out_ref[...] = (middle_ref[...] + fed[...]).astype(jnp.bfloat16)
    for slot in (PLANES - 2, PLANES - 1):
        hand(slot).wait_send()
        for copy in flush(slot, slot % 2):
            copy.wait()
    links.drain()


def feed(normed, grad, middle, pieces):
    rows = normed.shape[0]
    count = pieces.shape[2]
    any_spec, vmem = pl.BlockSpec(memory_space=pl.ANY), pl.BlockSpec(memory_space=pltpu.VMEM)
    low = jnp.bfloat16
    return pl.pallas_call(
        feed_kernel,
        in_specs=[vmem, vmem, vmem, any_spec],
        out_specs=[vmem, vmem, any_spec],
        out_shape=[
            jax.ShapeDtypeStruct((rows, D), jnp.float32),
            jax.ShapeDtypeStruct((rows, D), low),
            jax.ShapeDtypeStruct((PLANES, 4, count, PIECE), low),
        ],
        scratch_shapes=[
            pltpu.VMEM((rows, D), jnp.float32),
            pltpu.VMEM((2, count, D), low),
            pltpu.VMEM((2, 3, count // 3, rows), low),
            pltpu.VMEM((PLANES, 3, count // 3, rows), low),
            pltpu.VMEM((2, count, 4 * PIECE), low),
            pltpu.VMEM((2, rows, 4 * PIECE), low),
            pltpu.VMEM((2, rows, 4 * PIECE), low),
            pltpu.SemaphoreType.DMA((12,)),
            pltpu.SemaphoreType.DMA((12,)),
            pltpu.SemaphoreType.DMA((2, 8)),
            pltpu.SemaphoreType.DMA((2, 4)),
        ],
        compiler_params=pltpu.CompilerParams(
            vmem_limit_bytes=VMEM_LIMIT, collective_id=2, has_side_effects=True
        ),
        name="feed",
    )(normed, grad, middle, pieces)


def add_into(target, source):
    rows = target.shape[0]
    chunk = next(c for c in (352, 256, rows) if rows % c == 0)

    def one(index, carried):
        span = pl.ds(pl.multiple_of(index * chunk, chunk), chunk)
        target[span, :] = (
            target[span, :].astype(jnp.float32) + source[span, :].astype(jnp.float32)
        ).astype(jnp.bfloat16)
        return carried

    lax.fori_loop(0, rows // chunk, one, 0)


class Fold:
    def __init__(self, links, whole, first, final, bits):
        self.links, self.first, self.final = links, [first.at[m] for m in range(2)], final
        self.base = links.number(3)
        chip = lax.div(links.place, 2)
        ones = lambda bit: lax.rem(lax.div(chip, bit), 2)
        near, far = ones(bits[0]), ones(bits[1])
        self.away = [whole((1 - near) * bits[0] + m * bits[1]) for m in range(2)]
        self.stay = [whole(near * bits[0] + m * bits[1]) for m in range(2)]
        self.near_to = (flip(links.place, 2 * bits[0]), links.depth)
        self.far_to = (flip(links.place, 2 * bits[1]), links.depth)
        self.passed, self.own = first.at[1 - far], first.at[far]

    def one(self):
        for m in range(2):
            self.links.go(self.base + m, self.away[m], self.first[m], self.near_to)

    def two(self, stay=None):
        for m in range(2):
            self.links.got(self.base + m, self.first[m])
            add_into(self.first[m], self.stay[m] if stay is None else stay[m])
        self.links.go(self.base + 2, self.passed, self.final, self.far_to)

    def end(self):
        self.links.got(self.base + 2, self.final)
        add_into(self.final, self.own)


class LineFold:
    def __init__(self, links, block, held):
        self.links = links
        self.held = [[held.at[way, step] for step in range(PLANES - 1)] for way in range(2)]
        self.base = links.number(2 * (PLANES - 1))
        depth = links.depth
        self.blocks, self.sends, self.sums, self.takes, self.to = [], [], [], [], []
        for step in range(1, PLANES):
            right = jnp.minimum(depth + PLANES - step, PLANES - 1)
            left = jnp.maximum(depth - PLANES + step, 0)
            self.blocks.append((block(left), block(right)))
            self.sends.append((depth >= PLANES - step, depth < step))
            self.takes.append(((depth >= PLANES - 1 - step) & (depth < PLANES - 1), (depth <= step) & (depth > 0)))
        self.ends = (depth == PLANES - 1, depth == 0)
        self.to = (
            (links.place, jnp.maximum(depth - 1, 0)),
            (links.place, jnp.minimum(depth + 1, PLANES - 1)),
        )
        self.inner = [
            [self.sends[step][way] & jnp.logical_not(self.ends[way]) for way in range(2)]
            for step in range(PLANES - 1)
        ]
        self.outer = [
            [self.sends[step][way] & self.ends[way] for way in range(2)] for step in range(PLANES - 1)
        ]

    def launch(self, step):
        for way in range(2):
            self.links.go(
                self.base + 2 * (step - 1) + way,
                self.blocks[step - 1][way],
                self.held[way][step - 1],
                self.to[way],
                self.outer[step - 1][way],
            )

    def take(self, step):
        for way in range(2):
            self.links.got(
                self.base + 2 * (step - 1) + way, self.held[way][step - 1], self.takes[step - 1][way]
            )

    def forward(self, step):
        for way in range(2):
            before = self.held[way][step - 2]
            block = self.blocks[step - 1][way]

            @pl.when(self.inner[step - 1][way])
            def _():
                add_into(before, block)

            self.links.go(
                self.base + 2 * (step - 1) + way,
                before,
                self.held[way][step - 1],
                self.to[way],
                self.inner[step - 1][way],
            )

    def total(self, own, out):
        depth = self.links.depth
        rows = out.shape[0]
        chunk = next(c for c in (352, 256, rows) if rows % c == 0)

        def one(index, carried):
            span = pl.ds(pl.multiple_of(index * chunk, chunk), chunk)
            value = own[span, :].astype(jnp.float32)
            sides = [self.held[way][PLANES - 2][span, :].astype(jnp.float32) for way in range(2)]
            value = value + jnp.where(depth < PLANES - 1, sides[0], 0.0)
            out[span, :] = value + jnp.where(depth > 0, sides[1], 0.0)
            return carried

        lax.fori_loop(0, rows // chunk, one, 0)


def close_kernel(*refs):
    (made, low_in, attended_in, q_in, k_in, v_in, o_in, n_in, weight_in, cos_in, sin_in) = refs[:11]
    incoming = refs[11:15]
    log_ref, begin_ref, gain_ref, small_in = refs[15:19]
    first_ref, back_ref, feed_total, out_total, attn_total, small_ref = refs[19:25]
    (
        q_ref, k_ref, v_ref, o_ref, n_ref, weight_ref, cos_ref, sin_ref, grad, inner, total, made_ref,
        stay, feed_first, feed_final, feed_held, out_made, out_core, out_first, out_final, out_held,
        attn_core, attn_first, attn_final, partial, partial_held, small_got,
        send, recv, local,
    ) = refs[25:]
    links = Links(send, recv)
    place, depth = links.place, links.depth
    length = q_ref.shape[0]
    shard = length // PLANES
    parity, chip = lax.rem(place, 2), lax.div(place, 2)
    core = (flip(place, 1), depth)
    loads = []

    def load(source, target):
        copy = pltpu.make_async_copy(source, target, local.at[len(loads)])
        copy.start()
        loads.append(copy)
        return copy

    order = (3, 2, 1, 0)
    folds = {
        slot: Fold(
            links,
            lambda i, slot=slot: made.at[slot, i],
            feed_first.at[slot],
            feed_final.at[slot],
            (1, 2) if slot % 2 else (2, 1),
        )
        for slot in order
    }
    out_fold = Fold(links, lambda i: out_core.at[i], out_first, out_final, (1, 2))
    attn_fold = Fold(links, lambda i: attn_core.at[i], attn_first, attn_final, (1, 2))

    def slot_holding(block):
        found = 0
        for plane in range(PLANES):
            for slot, (_, _, held) in enumerate(SLOTS[plane]):
                found = found + jnp.where((depth == plane) & (block == held), slot, 0)
        return found

    feed_line = LineFold(links, lambda j: feed_final.at[slot_holding(j)], feed_held)
    out_line = LineFold(
        links, lambda j: out_final.at[pl.ds(pl.multiple_of(j * 256, 256), 256), :], out_held
    )
    line = LineFold(links, lambda j: partial.at[j], partial_held)
    out_swap, attn_swap = links.number(4), links.number(4)
    sides = [columns_of(2 * i + parity) for i in range(4)]
    others = [columns_of(2 * i + 1 - parity) for i in range(4)]
    across = links.number(PLANES)
    tiny = links.number(6)
    stays = [[stay.at[index, m] for m in range(2)] for index in range(2)]
    tiny_to = [core, (flip(place, 2), depth), (flip(place, 4), depth)]
    plane_to = [(place, lax.rem(depth + step, PLANES)) for step in range(1, PLANES)]
    plane_rows = [lax.rem(depth - step + PLANES, PLANES) for step in range(PLANES)]

    attended_ref, low_ref = partial.at[0], partial.at[1]
    first_loads = [load(attended_in, attended_ref), load(low_in, low_ref)]
    for slot in order[:2]:
        for m in range(2):
            load(folds[slot].stay[m], stays[slot % 2][m])
    q_loads = [load(source, target) for source, target in ((q_in, q_ref), (k_in, k_ref), (v_in, v_ref), (o_in, o_ref), (cos_in, cos_ref), (sin_in, sin_ref))]
    own_rows = pl.ds(pl.multiple_of(depth * shard, shard), shard)
    q_loads.append(load(incoming[0], grad.at[own_rows, :]))
    late = [load(n_in, n_ref), load(weight_in, weight_ref)]

    links.greet()
    for step in range(1, PLANES):
        links.go(across + step, incoming[step], grad.at[own_rows, :], plane_to[step - 1])
    for slot in order[:2]:
        folds[slot].one()

    for copy in first_loads:
        copy.wait()
    for index in range(4):
        rows = pl.ds(index * 256, 256)
        out_made[rows, :] = tokens_dot(attended_ref[:, rows], low_ref[...], 0, 0).astype(jnp.bfloat16)
    out_swaps = [links.copy(out_swap + i, out_made.at[:, others[i]], out_core.at[i], core) for i in range(4)]
    for copy in out_swaps:
        copy.start()
    for i in range(4):
        links.got(out_swap + i, out_core.at[i])
        add_into(out_core.at[i], out_made.at[:, sides[i]])
    out_fold.one()

    def restay(slot):
        copies = [
            pltpu.make_async_copy(folds[slot].stay[m], stays[slot % 2][m], local.at[16 + 2 * (slot % 2) + m])
            for m in range(2)
        ]
        return copies

    for copy in loads[2:6]:
        copy.wait()
    for copy in q_loads:
        copy.wait()
    for slot in order[:2]:
        folds[slot].two(stays[slot % 2])
    for slot in order[2:]:
        folds[slot].one()
        for copy in restay(slot):
            copy.start()
    for step in range(1, PLANES):
        links.got(across + step, grad.at[pl.ds(pl.multiple_of(plane_rows[step] * shard, shard), shard), :])

    lane = lax.broadcasted_iota(jnp.int32, (shard, 128), 1)
    keeps = [lane < HD, lane >= HD]
    down = lax.broadcasted_iota(jnp.int32, (shard, shard), 0)
    along = lax.broadcasted_iota(jnp.int32, (1, shard), 1)

    def masked(values, head):
        return jnp.where(keeps[head], values, jnp.zeros_like(values))

    def after_a():
        for slot in order[:2]:
            folds[slot].end()
        feed_line.launch(1)
        feed_line.launch(2)
        out_fold.two()

    def after_b():
        feed_line.take(1)
        feed_line.forward(2)
        out_fold.end()

    def after_c():
        for slot in order[2:]:
            for copy in restay(slot):
                copy.wait()
            folds[slot].two(stays[slot % 2])

    def after_d():
        for slot in order[2:]:
            folds[slot].end()
        feed_line.launch(3)
        feed_line.take(2)
        feed_line.forward(3)
        out_line.launch(1)
        out_line.launch(2)
        out_line.launch(3)

    def back_step(step, carried):
        pair, block = lax.div(step, PLANES), lax.rem(step, PLANES)
        lanes = columns_of(pair)
        start = pl.multiple_of(block * shard, shard)
        own = pl.ds(start, shard)

        @pl.when(block == 0)
        def _():
            total[...] = jnp.zeros_like(total)
            for index in range(PLANES):
                span = pl.ds(index * shard, shard)
                turned = jnp.transpose(
                    grad[span, lanes].astype(jnp.float32) * o_ref[span, lanes].astype(jnp.float32)
                )
                for head in range(2):
                    inner[head : head + 1, span] = jnp.sum(
                        turned[head * HD : head * HD + HD], axis=0, keepdims=True
                    )

        keys, values = k_ref[own, lanes], v_ref[own, lanes]
        own_keys = [masked(keys, head) for head in range(2)]

        def tile(index, sums, visible):
            key_sum, value_sum = sums
            span = pl.ds(pl.multiple_of(index * shard, shard), shard)
            query_block, grad_block = q_ref[span, lanes], grad[span, lanes]
            query_sum = total[span, :]
            for head in range(2):
                query, out_grad = masked(query_block, head), masked(grad_block, head)
                scores = tokens_dot(keys, query, 1, 1)
                shares = jnp.where(
                    visible, jnp.exp2(scores - log_ref[pair, head : head + 1, span]), 0.0
                )
                share_grad = tokens_dot(values, out_grad, 1, 1)
                score_grad = (shares * (share_grad - inner[head : head + 1, span])).astype(jnp.bfloat16)
                value_sum = value_sum + tokens_dot(shares.astype(jnp.bfloat16), out_grad, 1, 0)
                key_sum = key_sum + tokens_dot(score_grad, query, 1, 0)
                query_sum = query_sum + tokens_dot(score_grad, own_keys[head], 0, 0)
            total[span, :] = query_sum
            return (key_sum, value_sum)

        empty = jnp.zeros((shard, 128), jnp.float32)
        sums = tile(
            block, (empty, empty), (down >= begin_ref[0:1, own] - start) & (down <= along)
        )
        key_sum, value_sum = lax.fori_loop(
            block + 1,
            PLANES,
            lambda i, held: tile(
                i,
                held,
                down >= begin_ref[0:1, pl.ds(pl.multiple_of(i * shard, shard), shard)] - start,
            ),
            sums,
        )
        cosine, sine_part = cos_ref[own, :], sin_ref[own, :]
        made_ref[own, columns_of(pair)] = turn(
            total[own, :] * HD**-0.5, cosine, sine_part, False
        ).astype(jnp.bfloat16)
        made_ref[own, columns_of(2 + pair)] = turn(
            key_sum * (1 / LOG2E), cosine, sine_part, False
        ).astype(jnp.bfloat16)
        half_sum = 0.5 * value_sum
        made_ref[own, columns_of(4 + pair)] = half_sum.astype(jnp.bfloat16)
        first_ref[own, lanes] = half_sum
        for when, pump in ((0, after_a), (3, after_b), (4, after_c), (6, after_d)):
            pl.when(step == when)(pump)
        return carried

    lax.fori_loop(0, 2 * PLANES, back_step, 0)
    for copy in late:
        copy.wait()
    small_ref[...] = small_in[...]

    def input_back(index, carried):
        block = jnp.where(depth < PLANES // 2, PLANES - 1 - index, index)
        rows = pl.ds(pl.multiple_of(block * shard, shard), shard)
        value = tokens_dot(made_ref[rows, :], weight_ref[pl.ds(0, 768), :], 1, 0)
        partial[block] = value.astype(jnp.bfloat16)
        gain = (
            jnp.sum(value * n_ref[rows, :].astype(jnp.float32), axis=0, keepdims=True)
            / gain_ref[0:1, :]
        )
        for piece in range(8):
            small_ref[0, piece : piece + 1, :] += gain[:, piece * PIECE : piece * PIECE + PIECE]
        return carried

    input_back(0, 0)
    line.launch(1)
    lax.fori_loop(1, PLANES, input_back, 0)
    line.launch(2)
    line.launch(3)
    out_line.take(1)
    out_line.forward(2)

    links.go(tiny, small_ref.at[0], small_got.at[0], tiny_to[0])
    for copy in out_swaps:
        copy.wait_send()
    attn_made = out_made.at[pl.ds(0, 768), :]
    for index in range(3):
        rows = pl.ds(index * 256, 256)
        attn_made[rows, :] = tokens_dot(made_ref[:, rows], n_ref[...], 0, 0).astype(jnp.bfloat16)
    for i in range(4):
        links.go(attn_swap + i, attn_made.at[:, others[i]], attn_core.at[i], core)
    links.got(tiny, small_got.at[0])
    small_ref[1] = small_ref[0] + small_got[0]
    links.go(tiny + 1, small_ref.at[1], small_got.at[1], tiny_to[1])
    for i in range(4):
        links.got(attn_swap + i, attn_core.at[i])
        add_into(attn_core.at[i], attn_made.at[:, sides[i]])
    attn_fold.one()
    line.take(1)
    line.forward(2)
    links.got(tiny + 1, small_got.at[1])
    small_ref[2] = small_ref[1] + small_got[1]
    links.go(tiny + 2, small_ref.at[2], small_got.at[2], tiny_to[2])
    feed_line.take(3)
    feed_line.total(feed_final.at[0], feed_total)
    out_line.take(2)
    out_line.forward(3)
    attn_fold.two()
    links.got(tiny + 2, small_got.at[2])
    small_ref[3] = small_ref[2] + small_got[2]
    small_place = small_got.at[3 + depth]
    for step in range(1, PLANES):
        links.go(tiny + 2 + step, small_ref.at[3], small_place, plane_to[step - 1])
    small_got[3 + depth] = small_ref[3]
    out_line.take(3)
    out_line.total(out_final.at[pl.ds(pl.multiple_of(depth * 256, 256), 256), :], out_total)
    line.take(2)
    line.forward(3)
    attn_fold.end()
    attn_total[...] = attn_final[...].astype(jnp.float32)
    for step in range(1, PLANES):
        links.got(tiny + 2 + step, small_got.at[3 + plane_rows[step]])
    small_ref[4] = small_got[3] + small_got[4] + small_got[5] + small_got[6]
    line.take(3)
    line.total(partial.at[depth], back_ref)
    links.drain()


def closing(made, low_ref, attended_own, heads, normed, weight, tables, incoming, logs, begin_row, gains, small):
    length, width = heads[0].shape
    rows = low_ref.shape[0]
    count = made.shape[2]
    low, full = jnp.bfloat16, jnp.float32
    any_spec, vmem = pl.BlockSpec(memory_space=pl.ANY), pl.BlockSpec(memory_space=pltpu.VMEM)
    shape = jax.ShapeDtypeStruct
    return pl.pallas_call(
        close_kernel,
        in_specs=[any_spec] * 15 + [vmem] * 4,
        out_specs=[vmem] * 6,
        out_shape=[
            shape((length, width), full),
            shape((rows, D), full),
            shape((count, PIECE), full),
            shape((256, PIECE), full),
            shape((768, PIECE), full),
            shape((5, 24, PIECE), full),
        ],
        scratch_shapes=[pltpu.VMEM((length, width), low)] * 4
        + [
            pltpu.VMEM((length, D), low),
            pltpu.VMEM((ATTN_ROWS, D), low),
            pltpu.VMEM((length, 128), full),
            pltpu.VMEM((length, 128), full),
            pltpu.VMEM((length, width), low),
            pltpu.VMEM((8, length), full),
            pltpu.VMEM((length, 128), full),
            pltpu.VMEM((length, 768), low),
            pltpu.VMEM((2, 2, count, PIECE), low),
            pltpu.VMEM((PLANES, 2, count, PIECE), low),
            pltpu.VMEM((PLANES, count, PIECE), low),
            pltpu.VMEM((2, PLANES - 1, count, PIECE), low),
            pltpu.VMEM((D, D), low),
            pltpu.VMEM((4, D, PIECE), low),
            pltpu.VMEM((2, D, PIECE), low),
            pltpu.VMEM((D, PIECE), low),
            pltpu.VMEM((2, PLANES - 1, 256, PIECE), low),
            pltpu.VMEM((4, 768, PIECE), low),
            pltpu.VMEM((2, 768, PIECE), low),
            pltpu.VMEM((768, PIECE), low),
            pltpu.VMEM((PLANES, rows, D), low),
            pltpu.VMEM((2, PLANES - 1, rows, D), low),
            pltpu.VMEM((7, 24, PIECE), full),
            pltpu.SemaphoreType.DMA((CLOSE_COPIES,)),
            pltpu.SemaphoreType.DMA((CLOSE_COPIES,)),
            pltpu.SemaphoreType.DMA((20,)),
        ],
        compiler_params=pltpu.CompilerParams(
            vmem_limit_bytes=CLOSE_VMEM, collective_id=3, has_side_effects=True
        ),
        name="closing",
    )(made, low_ref, attended_own, *heads, normed, weight, *tables, *incoming, logs, begin_row, gains, small)


def middle_back_kernel(*refs):
    middle_ref, grad_ref, back_ref, weight_ref, gain_ref = refs[:5]
    low_ref, dm_ref, gain_grad_ref = refs[5:8]
    outs = refs[8:12]
    depth = lax.axis_index("mp")
    half = middle_ref.shape[0] // 2
    gain = gain_ref[1:2, :]
    gain_grad_ref[...] = jnp.zeros_like(gain_grad_ref)
    for tile in range(2):
        rows = pl.ds(tile * half, half)
        middle, incoming = middle_ref[rows, :], back_ref[rows, :]
        factor = lax.rsqrt(jnp.mean(middle * middle, axis=-1, keepdims=True) + 1e-06)
        scaled = incoming * gain
        mean = jnp.mean(scaled * middle, axis=-1, keepdims=True)
        total = grad_ref[rows, :].astype(jnp.float32) + factor * scaled - middle * (factor**3 * mean)
        gain_grad_ref[0:1, :] += jnp.sum(incoming * middle * factor, axis=0, keepdims=True)
        dm_ref[rows, :] = total
        low_ref[rows, :] = total.astype(jnp.bfloat16)
    for index, out in enumerate(outs):
        owner = lax.rem(depth + index, PLANES)
        rows = pl.ds(pl.multiple_of(owner * 256, 256), 256)
        out[...] = tokens_dot(low_ref[...], weight_ref[rows, :], 1, 1).astype(jnp.bfloat16)


def middle_back(middle, grad, back, weight, gains):
    rows = middle.shape[0]
    return pl.pallas_call(
        middle_back_kernel,
        out_shape=[
            jax.ShapeDtypeStruct((rows, D), jnp.bfloat16),
            jax.ShapeDtypeStruct((rows, D), jnp.float32),
            jax.ShapeDtypeStruct((8, D), jnp.float32),
        ]
        + [jax.ShapeDtypeStruct((rows, 256), jnp.bfloat16)] * PLANES,
        compiler_params=pltpu.CompilerParams(vmem_limit_bytes=VMEM_LIMIT),
        cost_estimate=cost(2 * rows * D * D, 12 << 20),
        name="middle_back",
    )(middle, grad, back, weight, gains)


def fast_shards(
    hidden_in,
    segment_ids,
    first_values,
    grad_out,
    input_proj,
    output_proj,
    expand_proj,
    reduce_proj,
    norm_gains,
    old_moment_input,
    old_moment_output,
    old_moment_expand,
    old_moment_reduce,
    old_moment_gains,
    old_square_input,
    old_square_output,
    old_square_expand,
    old_square_reduce,
    old_square_gains,
):
    place, depth = lax.axis_index("dp"), lax.axis_index("mp")
    low = jnp.bfloat16
    hidden, out_cotangent = hidden_in[0], grad_out[0]
    seg_row = segment_ids[0]
    length = seg_row.shape[0]
    shard = hidden.shape[0]
    ffs = reduce_proj.shape[0]

    attn_piece = jnp.concatenate(
        [
            input_proj.astype(low).transpose(0, 2, 1).reshape(768, PIECE),
            norm_gains.astype(low),
            jnp.zeros((14, PIECE), low),
        ]
    )
    feed_piece = jnp.concatenate(
        [
            expand_proj.astype(low).transpose(0, 2, 1).reshape(2 * ffs, PIECE),
            reduce_proj.astype(low),
        ]
    )

    begins = jnp.zeros_like(seg_row)
    for number in range(1, 7):
        start = jnp.sum((seg_row < number).astype(jnp.int32))
        begins = jnp.where(seg_row == number, start, begins)
    lows = begins[:: length // BLOCKS]
    offset = (jnp.arange(length, dtype=jnp.int32) - begins).astype(jnp.float32)
    inverse_rates = 10000.0 ** (-2.0 * jnp.arange(HD // 2, dtype=jnp.float32) / HD)
    angles = offset[:, None] * inverse_rates[None, :]
    cosine, sine = jnp.cos(angles), jnp.sin(angles)
    cosine = jnp.concatenate([cosine] * 4, axis=1)
    sine_part = jnp.concatenate([-sine, sine, -sine, sine], axis=1)

    (
        queries,
        keys,
        values,
        attended,
        normed,
        attn_weight,
        out_weight,
        feed_all,
        gains,
        squares,
        logs,
        middle,
        normed_two,
        attended_own,
    ) = opening(
        hidden,
        attn_piece,
        output_proj.astype(low),
        feed_piece,
        cosine,
        sine_part,
        first_values[0],
        begins[:, None],
    )
    normed_two_grad, layer_output, made = feed(normed_two, out_cotangent, middle, feed_all)
    layer_output = layer_output[None]
    branch_low, middle_grad, gain_two, *out_grads = middle_back(
        middle, out_cotangent, normed_two_grad, out_weight, gains
    )
    small = jnp.concatenate(
        [
            jnp.zeros((8, PIECE), jnp.float32),
            gain_two[0].reshape(8, PIECE),
            jnp.broadcast_to(jnp.sum(squares[:2], axis=1)[:, None], (2, PIECE)),
            jnp.zeros((6, PIECE), jnp.float32),
        ]
    )
    values_grad, normed_grad, feed_total, out_total, attn_total, small = closing(
        made,
        branch_low,
        attended_own,
        (queries, keys, values, attended),
        normed,
        attn_weight,
        (cosine, sine_part),
        out_grads,
        logs,
        jnp.broadcast_to(begins[None], (8, length)),
        gains,
        jnp.broadcast_to(small[None], (5, 24, PIECE)),
    )
    small = small[4]
    value_norms = jnp.sqrt(small[16:18, 0] / (8 * length * D))
    gain_total = lax.dynamic_index_in_dim(small[:16].reshape(2, 8, PIECE), place, 1, False)

    hidden32 = hidden.astype(jnp.float32)
    factor_one = rms_factor(hidden32)
    input_part, _ = norm_back(hidden32, factor_one, gains[0], normed_grad)
    input_grad = (middle_grad + input_part)[None]

    expand_total = feed_total[: 2 * ffs].reshape(2, ffs, PIECE).transpose(0, 2, 1)
    reduce_total = feed_total[2 * ffs :]
    attn_total = attn_total.reshape(3, 256, PIECE).transpose(0, 2, 1)
    new_input = adamw(input_proj, attn_total, old_moment_input, old_square_input, D ** (-0.5), 0.1)
    new_output = adamw(
        output_proj,
        out_total,
        old_moment_output,
        old_square_output,
        max(1, 8 * HEADS * HD // LEN) ** (-0.5),
        0.1,
    )
    new_expand = adamw(
        expand_proj, expand_total, old_moment_expand, old_square_expand, D ** (-0.5), 0.1
    )
    new_reduce = adamw(
        reduce_proj, reduce_total, old_moment_reduce, old_square_reduce, (FF // 3) ** (-0.5), 0.1
    )
    new_gains = adamw(norm_gains, gain_total, old_moment_gains, old_square_gains, 0.2, 0.0)
    return (
        layer_output,
        input_grad,
        values_grad[None],
        value_norms,
        new_input[0],
        new_output[0],
        new_expand[0],
        new_reduce[0],
        new_gains[0],
        new_input[1],
        new_output[1],
        new_expand[1],
        new_reduce[1],
        new_gains[1],
        new_input[2],
        new_output[2],
        new_expand[2],
        new_reduce[2],
        new_gains[2],
    )


def solution(mesh):
    quick = mesh.shape["dp"] == 8 and mesh.shape["mp"] == PLANES
    return jax.shard_map(
        fast_shards if quick else shards,
        mesh=mesh,
        in_specs=(
            P("dp", "mp", None),
            P("dp", None),
            P("dp", None, "mp"),
            P("dp", "mp", None),
            P(None, "dp", "mp"),
            P("mp", "dp"),
            P(None, "dp", "mp"),
            P("mp", "dp"),
            P(None, "dp"),
            P(None, "dp", "mp"),
            P("mp", "dp"),
            P(None, "dp", "mp"),
            P("mp", "dp"),
            P(None, "dp"),
            P(None, "dp", "mp"),
            P("mp", "dp"),
            P(None, "dp", "mp"),
            P("mp", "dp"),
            P(None, "dp"),
        ),
        out_specs=(
            P("dp", "mp", None),
            P("dp", "mp", None),
            P("dp", None, "mp"),
            P(),
            P(None, "dp", "mp"),
            P("mp", "dp"),
            P(None, "dp", "mp"),
            P("mp", "dp"),
            P(None, "dp"),
            P(None, "dp", "mp"),
            P("mp", "dp"),
            P(None, "dp", "mp"),
            P("mp", "dp"),
            P(None, "dp"),
            P(None, "dp", "mp"),
            P("mp", "dp"),
            P(None, "dp", "mp"),
            P("mp", "dp"),
            P(None, "dp"),
        ),
        check_vma=False,
    )
```

```python
import functools
import math

import jax
import jax.numpy as jnp
from jax import lax
from jax.experimental import pallas as pl
from jax.experimental.pallas import tpu as pltpu
from jax.sharding import PartitionSpec as P

D = 1024
HEADS = 16
HD = 64
FF = 2816
LEN = 2048
STEP = 5
PLANES = 4
PIECE = 128
BLOCKS = 4
ATTN_ROWS = 784
VMEM_LIMIT = 56 << 20
OPEN_COPIES = 80
CLOSE_COPIES = 80
CLOSE_VMEM = 60 << 20


def arrivals(plane):
    order = [(0, 0, plane)]
    for hop in range(1, PLANES):
        if plane + hop < PLANES:
            order.append((0, hop, plane + hop))
        if plane - hop >= 0:
            order.append((1, hop, plane - hop))
    return order


SLOTS = [arrivals(plane) for plane in range(PLANES)]


def cost(flops, moved):
    return pl.CostEstimate(flops=flops, bytes_accessed=moved, transcendentals=0)


def rope_tables(seg_row, head_size):
    length = seg_row.shape[0]
    places = jnp.arange(length, dtype=jnp.int32)
    begins = jnp.sum((seg_row[None, :] < seg_row[:, None]).astype(jnp.int32), axis=1)
    offset = (places - begins).astype(jnp.float32)
    inverse_rates = 10000.0 ** (-2.0 * jnp.arange(head_size // 2, dtype=jnp.float32) / head_size)
    angles = offset[:, None] * inverse_rates[None, :]
    return (jnp.cos(angles)[:, None, :], jnp.sin(angles)[:, None, :])


def rotate(values, cosine, sine_part, forward):
    half_size = values.shape[-1] // 2
    first_half = values[..., :half_size]
    second_half = values[..., half_size:]
    if forward:
        return jnp.concatenate(
            [
                first_half * cosine - second_half * sine_part,
                second_half * cosine + first_half * sine_part,
            ],
            axis=-1,
        )
    return jnp.concatenate(
        [
            first_half * cosine + second_half * sine_part,
            second_half * cosine - first_half * sine_part,
        ],
        axis=-1,
    )


def rms_factor(values):
    return lax.rsqrt(jnp.mean(values * values, axis=-1, keepdims=True) + 1e-06)


def norm_back(values, factor, gain_row, incoming):
    scaled = incoming * gain_row
    value_grad = factor * scaled - values * factor**3 * jnp.mean(
        scaled * values, axis=-1, keepdims=True
    )
    gain_grad = jnp.sum(incoming * values * factor, axis=0)
    return (value_grad, gain_grad)


def visible_block(seg_row, first_row, block_rows):
    length = seg_row.shape[0]
    query_seg = lax.dynamic_slice_in_dim(seg_row, first_row, block_rows, 0)
    query_places = first_row + jnp.arange(block_rows, dtype=jnp.int32)
    key_places = jnp.arange(length, dtype=jnp.int32)
    return (query_seg[:, None] == seg_row[None, :]) & (query_places[:, None] >= key_places[None, :])


def block_scores(queries, keys_rot, seg_row, first_row, block_rows, score_scale):
    query_block = lax.dynamic_slice_in_dim(queries, first_row, block_rows, 0)
    visible = visible_block(seg_row, first_row, block_rows)
    scores = (
        jnp.einsum("qhd,khd->hqk", query_block, keys_rot, preferred_element_type=jnp.float32)
        * score_scale
    )
    return (query_block, jnp.where(visible[None], scores, -1e30))


def attend(queries, keys_rot, mixed_values, seg_row, score_scale):
    length = queries.shape[0]
    block_rows = min(512, length)

    def one_block(block_index):
        first_row = block_index * block_rows
        query_block, scores = block_scores(
            queries, keys_rot, seg_row, first_row, block_rows, score_scale
        )
        top_score = jnp.max(scores, axis=-1, keepdims=True)
        raised = jnp.exp(scores - top_score)
        totals = jnp.sum(raised, axis=-1, keepdims=True)
        shares = (raised / totals).astype(jnp.bfloat16)
        combined = jnp.einsum(
            "hqk,khd->qhd", shares, mixed_values, preferred_element_type=jnp.float32
        )
        return (combined, (top_score + jnp.log(totals))[..., 0])

    combined, log_totals = lax.map(one_block, jnp.arange(length // block_rows, dtype=jnp.int32))
    return (combined.reshape(length, -1), log_totals)


def attend_back(queries, keys_rot, mixed_values, out_grad, log_totals, seg_row, score_scale):
    length = queries.shape[0]
    block_rows = min(512, length)

    def one_block(running, operands):
        key_sum, value_sum = running
        block_index, block_totals = operands
        first_row = block_index * block_rows
        query_block, scores = block_scores(
            queries, keys_rot, seg_row, first_row, block_rows, score_scale
        )
        grad_block = lax.dynamic_slice_in_dim(out_grad, first_row, block_rows, 0)
        shares = jnp.exp(scores - block_totals[..., None])
        share_grad = jnp.einsum(
            "qhd,khd->hqk", grad_block, mixed_values, preferred_element_type=jnp.float32
        )
        inner = jnp.sum(shares * share_grad, axis=-1, keepdims=True)
        score_grad = (shares * (share_grad - inner)).astype(jnp.bfloat16)
        query_grad = (
            jnp.einsum("hqk,khd->qhd", score_grad, keys_rot, preferred_element_type=jnp.float32)
            * score_scale
        )
        key_sum = (
            key_sum
            + jnp.einsum(
                "hqk,qhd->khd", score_grad, query_block, preferred_element_type=jnp.float32
            )
            * score_scale
        )
        value_sum = value_sum + jnp.einsum(
            "hqk,qhd->khd",
            shares.astype(jnp.bfloat16),
            grad_block,
            preferred_element_type=jnp.float32,
        )
        return ((key_sum, value_sum), query_grad)

    empty_sum = jnp.zeros(keys_rot.shape, jnp.float32)
    (key_grad, value_grad), query_grad = lax.scan(
        one_block,
        (empty_sum, empty_sum),
        (jnp.arange(length // block_rows, dtype=jnp.int32), log_totals),
    )
    return (query_grad.reshape(keys_rot.shape), key_grad, value_grad)


def adamw(master, gradient, moment, square, step_rate, decay):
    new_moment = 0.5 * moment + 0.5 * gradient
    new_square = 0.5 * square + 0.5 * gradient * gradient
    correct = 1.0 - 0.5**STEP
    update = new_moment / correct / (jnp.sqrt(new_square / correct) + 1e-08)
    return (master - step_rate * (update + decay * master), new_moment, new_square)


def shards(
    hidden_in,
    segment_ids,
    first_values,
    grad_out,
    input_proj,
    output_proj,
    expand_proj,
    reduce_proj,
    norm_gains,
    old_moment_input,
    old_moment_output,
    old_moment_expand,
    old_moment_reduce,
    old_moment_gains,
    old_square_input,
    old_square_output,
    old_square_expand,
    old_square_reduce,
    old_square_gains,
):
    attn_weight, out_weight, expand_weight, reduce_weight, gains_low = (
        lax.all_gather(input_proj.astype(jnp.bfloat16), "dp", axis=1, tiled=True),
        lax.all_gather(output_proj.astype(jnp.bfloat16), "dp", axis=1, tiled=True),
        lax.all_gather(expand_proj.astype(jnp.bfloat16), "dp", axis=1, tiled=True),
        lax.all_gather(reduce_proj.astype(jnp.bfloat16), "dp", axis=1, tiled=True),
        lax.all_gather(norm_gains.astype(jnp.bfloat16), "dp", axis=1, tiled=True),
    )
    gains = gains_low.astype(jnp.float32)
    hidden = hidden_in[0].astype(jnp.float32)
    seg_row = segment_ids[0]
    length = seg_row.shape[0]
    first_in = first_values[0].astype(jnp.float32)
    local_heads = attn_weight.shape[2] // HD
    score_scale = 1.0 / math.sqrt(HD)
    factor_one = rms_factor(hidden)
    normed_one = (hidden * factor_one * gains[0]).astype(jnp.bfloat16)
    all_normed, all_grad_out = (
        lax.all_gather(normed_one, "mp", axis=0, tiled=True),
        lax.all_gather(grad_out[0], "mp", axis=0, tiled=True),
    )
    projected = jnp.einsum(
        "td,cde->cte", all_normed, attn_weight, preferred_element_type=jnp.float32
    )
    cosine, sine_part = rope_tables(seg_row, HD)
    queries = rotate(projected[0].reshape(length, local_heads, HD), cosine, sine_part, True).astype(
        jnp.bfloat16
    )
    keys_rot = rotate(
        projected[1].reshape(length, local_heads, HD), cosine, sine_part, True
    ).astype(jnp.bfloat16)
    blended = 0.5 * projected[2] + 0.5 * first_in
    mixed_values = blended.astype(jnp.bfloat16).reshape(length, local_heads, HD)
    square_terms = jnp.stack([jnp.sum(first_in * first_in), jnp.sum(blended * blended)])
    attended, log_totals = attend(queries, keys_rot, mixed_values, seg_row, score_scale)
    attended_low = attended.astype(jnp.bfloat16)
    rows_part = attended_low
    branch = lax.psum_scatter(
        jnp.dot(rows_part, out_weight, preferred_element_type=jnp.float32),
        "mp",
        scatter_dimension=0,
        tiled=True,
    )
    middle = hidden + branch
    factor_two = rms_factor(middle)
    normed_two = (middle * factor_two * gains[1]).astype(jnp.bfloat16)
    all_normed_two = lax.all_gather(normed_two, "mp", axis=0, tiled=True)
    gate_up = jnp.einsum(
        "td,cdf->ctf", all_normed_two, expand_weight, preferred_element_type=jnp.float32
    )
    gate_sig = jax.nn.sigmoid(gate_up[0])
    gate_act = gate_up[0] * gate_sig
    activated = (gate_act * gate_up[1]).astype(jnp.bfloat16)
    rows_part = activated
    feed_out = lax.psum_scatter(
        jnp.dot(rows_part, reduce_weight, preferred_element_type=jnp.float32).astype(jnp.bfloat16),
        "mp",
        scatter_dimension=0,
        tiled=True,
    ).astype(jnp.float32)
    layer_output = (middle + feed_out).astype(jnp.bfloat16)[None]
    hidden_grad = jnp.einsum(
        "td,fd->tf", all_grad_out, reduce_weight, preferred_element_type=jnp.float32
    )
    reduce_grad = jnp.einsum(
        "tf,td->fd", activated, all_grad_out, preferred_element_type=jnp.float32
    )
    gate_grad = hidden_grad * gate_up[1] * gate_sig * (1.0 + gate_up[0] * (1.0 - gate_sig))
    up_grad = hidden_grad * gate_act
    pair_grad = jnp.stack([gate_grad, up_grad]).astype(jnp.bfloat16)
    expand_grad = jnp.einsum(
        "ctf,td->cdf", pair_grad, all_normed_two, preferred_element_type=jnp.float32
    )
    rows_part = pair_grad
    normed_two_grad = lax.psum_scatter(
        jnp.einsum(
            "ctf,cdf->td", rows_part, expand_weight, preferred_element_type=jnp.float32
        ).astype(jnp.bfloat16),
        "mp",
        scatter_dimension=0,
        tiled=True,
    ).astype(jnp.float32)
    middle_part, gain_two_grad = norm_back(middle, factor_two, gains[1], normed_two_grad)
    middle_grad = grad_out[0].astype(jnp.float32) + middle_part
    branch_low = middle_grad.astype(jnp.bfloat16)
    all_branch = lax.all_gather(branch_low, "mp", axis=0, tiled=True)
    out_grad = jnp.einsum("te,td->ed", attended_low, all_branch, preferred_element_type=jnp.float32)
    attended_grad = jnp.einsum(
        "td,ed->te", all_branch, out_weight, preferred_element_type=jnp.float32
    ).astype(jnp.bfloat16)
    query_grad, key_grad, mix_grad = attend_back(
        queries,
        keys_rot,
        mixed_values,
        attended_grad.reshape(length, local_heads, HD),
        log_totals,
        seg_row,
        score_scale,
    )
    query_grad = rotate(query_grad, cosine, sine_part, False).reshape(length, -1)
    key_grad = rotate(key_grad, cosine, sine_part, False).reshape(length, -1)
    mix_grad = mix_grad.reshape(length, -1)
    values_grad = (0.5 * mix_grad)[None]
    proj_grad = jnp.stack([query_grad, key_grad, 0.5 * mix_grad]).astype(jnp.bfloat16)
    attn_grad = jnp.einsum("cte,td->cde", proj_grad, all_normed, preferred_element_type=jnp.float32)
    rows_part = proj_grad
    normed_one_grad = lax.psum_scatter(
        jnp.einsum(
            "cte,cde->td", rows_part, attn_weight, preferred_element_type=jnp.float32
        ).astype(jnp.bfloat16),
        "mp",
        scatter_dimension=0,
        tiled=True,
    ).astype(jnp.float32)
    input_part, gain_one_grad = norm_back(hidden, factor_one, gains[0], normed_one_grad)
    input_grad = (middle_grad + input_part)[None]
    attn_total, out_total, expand_total, reduce_total = (
        lax.psum_scatter(
            attn_grad.astype(jnp.bfloat16), "dp", scatter_dimension=1, tiled=True
        ).astype(jnp.float32),
        lax.psum_scatter(
            out_grad.astype(jnp.bfloat16), "dp", scatter_dimension=1, tiled=True
        ).astype(jnp.float32),
        lax.psum_scatter(
            expand_grad.astype(jnp.bfloat16), "dp", scatter_dimension=1, tiled=True
        ).astype(jnp.float32),
        lax.psum_scatter(
            reduce_grad.astype(jnp.bfloat16), "dp", scatter_dimension=1, tiled=True
        ).astype(jnp.float32),
    )
    gain_totals, square_sums = lax.psum(
        (jnp.stack([gain_one_grad, gain_two_grad]), square_terms), ("dp", "mp")
    )
    gain_width = norm_gains.shape[1]
    gain_total = lax.dynamic_slice_in_dim(
        gain_totals, lax.axis_index("dp") * gain_width, gain_width, 1
    )
    value_norms = jnp.sqrt(square_sums / (lax.axis_size("dp") * length * D))
    new_input = adamw(input_proj, attn_total, old_moment_input, old_square_input, D ** (-0.5), 0.1)
    new_output = adamw(
        output_proj,
        out_total,
        old_moment_output,
        old_square_output,
        max(1, 8 * HEADS * HD // LEN) ** (-0.5),
        0.1,
    )
    new_expand = adamw(
        expand_proj, expand_total, old_moment_expand, old_square_expand, D ** (-0.5), 0.1
    )
    new_reduce = adamw(
        reduce_proj, reduce_total, old_moment_reduce, old_square_reduce, (FF // 3) ** (-0.5), 0.1
    )
    new_gains = adamw(norm_gains, gain_total, old_moment_gains, old_square_gains, 0.2, 0.0)
    return (
        layer_output,
        input_grad,
        values_grad,
        value_norms,
        new_input[0],
        new_output[0],
        new_expand[0],
        new_reduce[0],
        new_gains[0],
        new_input[1],
        new_output[1],
        new_expand[1],
        new_reduce[1],
        new_gains[1],
        new_input[2],
        new_output[2],
        new_expand[2],
        new_reduce[2],
        new_gains[2],
    )


def tokens_dot(a, b, left, right):
    return lax.dot_general(a, b, (((left,), (right,)), ((), ())), preferred_element_type=jnp.float32)


def piece_columns(place, step):
    start = jnp.bitwise_xor(place, step) * PIECE
    return pl.ds(pl.multiple_of(start, PIECE), PIECE)


def turn(values, cosine, sine_part, forward):
    lane = lax.broadcasted_iota(jnp.int32, values.shape, 1)
    swapped = jnp.where(
        lax.rem(lane, HD) < HD // 2, pltpu.roll(values, 96, 1), pltpu.roll(values, 32, 1)
    )
    if forward:
        return values * cosine + swapped * sine_part
    return values * cosine - swapped * sine_part


MESH = pl.DeviceIdType.MESH
LOG2E = 1.4426950408889634


def flip(place, bit):
    return place + bit - 2 * bit * lax.rem(lax.div(place, bit), 2)


def at_plane(depth, values):
    found = 0
    for plane, value in enumerate(values):
        found = found + jnp.where(depth == plane, value, 0)
    return found


def slot_at(depth, way, hop):
    return at_plane(
        depth,
        [
            next((k for k, s in enumerate(SLOTS[plane]) if s[:2] == (way, hop)), 0)
            for plane in range(PLANES)
        ],
    )


def columns_of(piece, width=PIECE):
    return pl.ds(pl.multiple_of(piece * width, width), width)


class Links:
    def __init__(self, send, recv):
        self.send, self.recv, self.count, self.started, self.waited = send, recv, 0, [], []
        self.place, self.depth = lax.axis_index("dp"), lax.axis_index("mp")

    def number(self, count=1):
        self.count += count
        return self.count - count

    def copy(self, number, source, target, to):
        return pltpu.make_async_remote_copy(
            src_ref=source,
            dst_ref=target,
            send_sem=self.send.at[number],
            recv_sem=self.recv.at[number],
            device_id=to,
            device_id_type=MESH,
        )

    def go(self, number, source, target, to, when=None):
        copy = self.copy(number, source, target, to)
        self.started.append((number, source, target, to, when))
        if when is None:
            copy.start()
        else:
            pl.when(when)(copy.start)

    def got(self, number, landed, when=None):
        copy = self.copy(number, landed, landed, (flip(self.place, 1), self.depth))
        if when is None:
            copy.wait_recv()
        else:
            pl.when(when)(copy.wait_recv)

    def drain(self):
        for *parts, when in self.started:
            copy = self.copy(*parts)
            for plane in [plane for number, plane in self.waited if number == parts[0]]:
                when = when & (self.depth != plane)
            if when is None:
                copy.wait_send()
            else:
                pl.when(when)(copy.wait_send)

    def greet(self, planes=True):
        barrier = pltpu.get_barrier_semaphore()
        others = [(flip(self.place, bit), self.depth) for bit in (1, 2, 4)]
        if planes:
            others += [(self.place, lax.rem(self.depth + step, PLANES)) for step in range(1, PLANES)]
        for other in others:
            pl.semaphore_signal(barrier, inc=1, device_id=other, device_id_type=MESH)
        pl.semaphore_wait(barrier, len(others))


class Spread:
    def __init__(self, links, own, spot, bits):
        self.links, self.own = links, own
        self.base = links.number(7)
        place = links.place
        first, second = flip(place, bits[0]), flip(place, bits[1])
        self.spots = [spot(piece) for piece in (place, first, second, flip(first, bits[1]))]
        self.lands = [
            spot(flip(piece, 1)) for piece in (place, first, second, flip(first, bits[1]))
        ]
        self.near, self.far, self.core = [
            (flip(place, bit), links.depth) for bit in (bits[0], bits[1], 1)
        ]

    def one(self):
        self.links.go(self.base, self.own, self.spots[0], self.near)

    def two(self):
        links, spots = self.links, self.spots
        links.go(self.base + 1, self.own, spots[0], self.far)
        links.got(self.base, spots[1])
        links.go(self.base + 2, spots[1], spots[1], self.far)

    def three(self):
        links, spots = self.links, self.spots
        links.go(self.base + 3, self.own, spots[0], self.core)
        links.go(self.base + 4, spots[1], spots[1], self.core)
        links.got(self.base + 1, spots[2])
        links.go(self.base + 5, spots[2], spots[2], self.core)
        links.got(self.base + 2, spots[3])
        links.go(self.base + 6, spots[3], spots[3], self.core)

    def end(self):
        for index, land in enumerate(self.lands):
            self.links.got(self.base + 3 + index, land)


class Halves:
    def __init__(self, parts):
        self.parts = parts

    def one(self):
        for part in self.parts:
            part.one()

    def two(self, *given):
        for index, part in enumerate(self.parts):
            part.two(*[one[index] for one in given])

    def three(self):
        for part in self.parts:
            part.three()

    def end(self):
        for part in self.parts:
            part.end()


def half_of(ref, half):
    rows = ref.shape[-2] // 2
    lead = (slice(None),) * (len(ref.shape) - 2)
    return ref.at[(*lead, pl.ds(half * rows, rows), slice(None))]


def halved_spread(links, own, spot):
    return Halves(
        [
            Spread(
                links,
                half_of(own, half),
                lambda piece, half=half: half_of(spot(piece), half),
                ((2, 4), (4, 2))[half],
            )
            for half in range(2)
        ]
    )


class Relay:
    def __init__(self, links, own, put):
        self.links, self.own, self.put = links, own, put
        self.base = links.number(2 * (PLANES - 1))
        self.waited = links.waited

    def send(self, hop, only=None):
        links, depth = self.links, self.links.depth
        for way in range(2):
            to = depth + (1 if way else -1)
            when = (
                (depth >= hop - 1) & (depth < PLANES - 1)
                if way
                else (depth <= PLANES - hop) & (depth > 0)
            )
            if only is not None:
                when = when & (depth == only[way])
            source = self.own if hop == 1 else self.put(depth, way, hop - 1)
            links.go(
                self.base + 2 * (hop - 1) + way,
                source,
                self.put(to, way, hop),
                (links.place, jnp.clip(to, 0, PLANES - 1)),
                when,
            )

    def take(self, hop, only=None):
        links, depth = self.links, self.links.depth
        for way in range(2):
            when = depth >= hop if way else depth + hop < PLANES
            if only is not None:
                when = when & (depth == only[way])
            links.got(self.base + 2 * (hop - 1) + way, self.put(depth, way, hop), when)

    def left(self, hop, only):
        links, depth = self.links, self.links.depth
        for way in range(2):
            source = self.own if hop == 1 else self.put(depth, way, hop - 1)
            to = (links.place, jnp.clip(depth + (1 if way else -1), 0, PLANES - 1))
            copy = links.copy(self.base + 2 * (hop - 1) + way, source, source, to)
            pl.when(depth == only[way])(copy.wait_send)
            self.waited.append((self.base + 2 * (hop - 1) + way, only[way]))


def open_kernel(*refs):
    hidden, attn_piece, out_piece, feed_piece, cos_ref, sin_ref, first_ref, begin_ref = refs[:8]
    q_out, k_out, v_out, o_out, n_out, weight_out, out_weight_out, feed_all = refs[8:16]
    gain_ref, square_ref, log_ref, middle_ref, normed_ref, attended_ref = refs[16:22]
    held, q_ref, k_ref, v_ref, o_ref, n_ref, weight_ref, out_ref, send, recv, local = refs[22:]
    links = Links(send, recv)
    place, depth = links.place, links.depth
    shard = hidden.shape[0]
    stores = []

    def store(source, target):
        copy = pltpu.make_async_copy(source, target, local.at[len(stores)])
        copy.start()
        stores.append(copy)
        return copy

    block_at = lambda plane, way, hop: jnp.clip(plane + (-hop if way else hop), 0, PLANES - 1)
    wide = Relay(links, hidden, lambda plane, way, hop: held.at[block_at(plane, way, hop)])
    out_rows = lambda block: out_ref.at[
        pl.ds(pl.multiple_of(block * 256, 256), 256), columns_of(place)
    ]
    thin = Relay(links, out_piece, lambda plane, way, hop: out_rows(block_at(plane, way, hop)))
    feeds = Relay(
        links,
        feed_piece,
        lambda plane, way, hop: feed_all.at[slot_at(plane, way, hop), place],
    )
    attn = Spread(links, attn_piece, lambda piece: weight_ref.at[:, columns_of(piece)], (2, 4))
    outs = Spread(
        links, out_ref.at[:, columns_of(place)], lambda piece: out_ref.at[:, columns_of(piece)], (2, 4)
    )
    slots = [
        halved_spread(
            links,
            feed_piece if slot == 0 else feed_all.at[slot, place],
            lambda piece, slot=slot: feed_all.at[slot, piece],
        )
        for slot in range(PLANES - 1)
    ]
    across = links.number(PLANES)

    links.greet()
    thin.send(1)
    wide.send(1)
    attn.one()
    own_hidden = store(hidden, held.at[depth])
    own_attn = store(attn_piece, weight_ref.at[:, columns_of(place)])
    own_out = store(out_piece, out_rows(depth))
    own_feed = store(feed_piece, feed_all.at[0, place])
    square_ref[...] = jnp.zeros_like(square_ref)
    attn.two()
    attn.three()
    slots[0].one()
    attn.end()
    for copy in (own_hidden, own_attn, own_out, own_feed):
        copy.wait()
    store(weight_ref, weight_out)
    gain_ref[...] = weight_ref[pl.ds(768, 16), :].astype(jnp.float32)

    def project(block):
        rows = pl.ds(pl.multiple_of(block * shard, shard), shard)
        values = held[block].astype(jnp.float32)
        factor = lax.rsqrt(jnp.mean(values * values, axis=-1, keepdims=True) + 1e-06)
        normed = (values * factor * gain_ref[0:1, :]).astype(jnp.bfloat16)
        n_ref[rows, :] = normed
        cosine, sine_part = cos_ref[rows, :], sin_ref[rows, :]
        query = tokens_dot(normed, weight_ref[pl.ds(0, 256), :], 1, 1)
        key = tokens_dot(normed, weight_ref[pl.ds(256, 256), :], 1, 1)
        value = tokens_dot(normed, weight_ref[pl.ds(512, 256), :], 1, 1)
        for half in range(2):
            lanes = slice(half * 128, half * 128 + 128)
            turned = turn(query[:, lanes], cosine, sine_part, True)
            q_ref[rows, lanes] = (turned * (HD**-0.5 * LOG2E)).astype(jnp.bfloat16)
            k_ref[rows, lanes] = turn(key[:, lanes], cosine, sine_part, True).astype(jnp.bfloat16)
        first = first_ref[rows, :].astype(jnp.float32)
        blended = 0.5 * value + 0.5 * first
        v_ref[rows, :] = blended.astype(jnp.bfloat16)
        square_ref[0:1, :] += jnp.sum(first * first, axis=0, keepdims=True)
        square_ref[1:2, :] += jnp.sum(blended * blended, axis=0, keepdims=True)

    def project_hop(hop):
        def one(side, carried):
            block = depth + hop * (2 * side - 1)
            pl.when((block >= 0) & (block < PLANES))(lambda: project(block))
            return carried

        lax.fori_loop(0, 2, one, 0)

    ends, inner = (PLANES - 1, 0), (PLANES - 2, 1)
    project(depth)
    wide.take(1)
    wide.send(2)
    feeds.send(1, ends)
    thin.take(1)
    thin.send(2)
    slots[0].two()
    project_hop(1)
    wide.take(2)
    wide.send(3)
    feeds.take(1, inner)
    feeds.send(1, inner)
    feeds.send(2, inner)
    thin.take(2)
    thin.send(3)
    project_hop(2)
    slots[0].three()
    wide.take(3)
    wide.left(3, (1, PLANES - 2))
    feeds.take(1, (1, PLANES - 2))
    feeds.take(2, (1, PLANES - 2))
    for hop in range(1, PLANES):
        feeds.send(hop, (1, PLANES - 2))
    thin.take(3)
    outs.one()
    project_hop(3)
    store(n_ref, n_out)
    store(q_ref, q_out)
    store(k_ref, k_out)
    store(v_ref, v_out)

    lane = lax.broadcasted_iota(jnp.int32, (shard, 128), 1)
    inside = lax.broadcasted_iota(jnp.int32, (shard, shard), 1)
    down = lax.broadcasted_iota(jnp.int32, (shard, 1), 0)

    def flash_pair(block, pair):
        rows = pl.ds(pl.multiple_of(block * shard, shard), shard)
        lanes = columns_of(pair)
        query = q_ref[rows, lanes]
        begin = begin_ref[rows, :]
        parts = [
            jnp.where((lane < HD) == (head == 0), query, jnp.zeros_like(query)) for head in range(2)
        ]

        def tile(index, carried, visible):
            span = pl.ds(pl.multiple_of(index * shard, shard), shard)
            keys, values = k_ref[span, lanes], v_ref[span, lanes]
            after = []
            for head in range(2):
                top, total, summed = carried[3 * head : 3 * head + 3]
                scores = jnp.where(visible, tokens_dot(parts[head], keys, 1, 1), -1e30)
                raised_top = jnp.maximum(top, jnp.max(scores, axis=1, keepdims=True))
                shrink = jnp.exp2(top - raised_top)
                shares = jnp.exp2(scores - raised_top)
                total = total * shrink + jnp.sum(shares, axis=1, keepdims=True)
                summed = summed * shrink + tokens_dot(shares.astype(jnp.bfloat16), values, 1, 0)
                after += [raised_top, total, summed]
            return tuple(after)

        fresh = (
            jnp.full((shard, 1), -1e30, jnp.float32),
            jnp.zeros((shard, 1), jnp.float32),
            jnp.zeros((shard, 128), jnp.float32),
        )
        carried = tile(block, fresh + fresh, (inside >= begin - block * shard) & (inside <= down))
        top0, total0, sum0, top1, total1, sum1 = lax.fori_loop(
            0, block, lambda j, held: tile(j, held, inside >= begin - j * shard), carried
        )
        o_ref[rows, lanes] = jnp.where(lane < HD, sum0 / total0, sum1 / total1).astype(jnp.bfloat16)
        turned = jnp.transpose(
            jnp.where(lane < HD, top0 + jnp.log2(total0), top1 + jnp.log2(total1))
        )
        log_ref[pair, 0:1, rows] = turned[0:1]
        log_ref[pair, 1:2, rows] = turned[HD : HD + 1]

    own_columns = attended_ref.at[:, columns_of(depth, 256)]

    def hand(step):
        block = lax.rem(depth + step, PLANES)
        rows = pl.ds(pl.multiple_of(block * shard, shard), shard)
        return links.copy(across + step, o_ref.at[rows, :], own_columns, (place, block))

    near = (0, PLANES - 1)

    def pump_a():
        feeds.take(1, near)
        slots[1].one()
        outs.two()

    def pump_b():
        slots[1].two()
        slots[0].end()

    def pump_c():
        feeds.take(2, near)
        slots[2].one()
        outs.three()

    pumps = ((0, pump_a), (1, pump_b), (2, pump_c), (4, slots[1].three), (5, slots[2].two))

    def flash(index, carried):
        step, pair = PLANES - 1 - lax.div(index, 2), lax.rem(index, 2)
        flash_pair(lax.rem(depth + step, PLANES), pair)
        pl.when((pair == 1) & (step > 0))(lambda: hand(step).start())
        for when, pump in pumps:
            pl.when(index == when)(pump)
        return carried

    lax.fori_loop(0, 2 * PLANES, flash, 0)
    own_rows = pl.ds(pl.multiple_of(depth * shard, shard), shard)
    attended_ref[:, columns_of(depth, 256)] = o_ref[own_rows, :]
    store(o_ref, o_out)
    outs.end()
    store(out_ref, out_weight_out)
    for step in range(1, PLANES):
        source = lax.rem(depth - step + PLANES, PLANES)
        links.got(across + step, attended_ref.at[:, columns_of(source, 256)])
    half = shard // 2
    for part in range(2):
        rows = pl.ds(part * half, half)
        middle = held[depth, rows, :].astype(jnp.float32) + tokens_dot(
            attended_ref[rows, :], out_ref[...], 1, 0
        )
        middle_ref[rows, :] = middle
        factor = lax.rsqrt(jnp.mean(middle * middle, axis=-1, keepdims=True) + 1e-06)
        normed_ref[rows, :] = (middle * factor * gain_ref[1:2, :]).astype(jnp.bfloat16)
    slots[2].three()
    slots[1].end()
    feeds.take(3)
    slots[2].end()
    for step in range(1, PLANES):
        hand(step).wait_send()
    links.drain()
    for copy in stores[4:]:
        copy.wait()


def opening(hidden, attn_piece, out_piece, feed_piece, cosine, sine_part, first_values, begin_column):
    length, width = first_values.shape
    rows = hidden.shape[0]
    count = feed_piece.shape[0]
    low, full = jnp.bfloat16, jnp.float32
    any_spec, vmem = pl.BlockSpec(memory_space=pl.ANY), pl.BlockSpec(memory_space=pltpu.VMEM)
    shape = jax.ShapeDtypeStruct
    return pl.pallas_call(
        open_kernel,
        in_specs=[any_spec] * 4 + [vmem] * 4,
        out_specs=[any_spec] * 8 + [vmem] * 6,
        out_shape=[
            shape((length, width), low),
            shape((length, width), low),
            shape((length, width), low),
            shape((length, width), low),
            shape((length, D), low),
            shape((ATTN_ROWS, D), low),
            shape((D, D), low),
            shape((PLANES, 8, count, PIECE), low),
            shape((16, D), full),
            shape((8, width), full),
            shape((width // 128, 8, length), full),
            shape((rows, D), full),
            shape((rows, D), low),
            shape((rows, D), low),
        ],
        scratch_shapes=[
            pltpu.VMEM((PLANES, rows, D), low),
            pltpu.VMEM((length, width), low),
            pltpu.VMEM((length, width), low),
            pltpu.VMEM((length, width), low),
            pltpu.VMEM((length, width), low),
            pltpu.VMEM((length, D), low),
            pltpu.VMEM((ATTN_ROWS, D), low),
            pltpu.VMEM((D, D), low),
            pltpu.SemaphoreType.DMA((OPEN_COPIES,)),
            pltpu.SemaphoreType.DMA((OPEN_COPIES,)),
            pltpu.SemaphoreType.DMA((12,)),
        ],
        compiler_params=pltpu.CompilerParams(
            vmem_limit_bytes=VMEM_LIMIT, collective_id=1, has_side_effects=True
        ),
        name="opening",
    )(hidden, attn_piece, out_piece, feed_piece, cosine, sine_part, first_values, begin_column)


def feed_kernel(*refs):
    normed_ref, grad_ref, middle_ref, pieces = refs[:4]
    back_ref, out_ref, made_out = refs[4:7]
    fed, weight, mine, theirs, made, halves, other_halves, send, recv, sem, out_sem, last_sem = refs[7:]
    links = Links(send, recv)
    place = links.place
    core = (flip(links.place, 1), links.depth)
    mine_first, theirs_first = lax.rem(links.place, 2), 1 - lax.rem(links.place, 2)
    count = weight.shape[1] // 3
    rows = normed_ref.shape[0]

    def load(which, buffer):
        return [
            pltpu.make_async_copy(
                pieces.at[which, piece],
                weight.at[buffer, :, pl.ds(piece * PIECE, PIECE)],
                sem.at[buffer, piece],
            )
            for piece in range(8)
        ]

    def flush(which, buffer):
        return [
            pltpu.make_async_copy(
                made.at[buffer, :, pl.ds(piece * PIECE, PIECE)],
                made_out.at[which, piece],
                out_sem.at[buffer, piece],
            )
            for piece in range(4)
        ]

    for copy in load(0, 0):
        copy.start()
    far = pieces.at[PLANES - 1, place]
    last = halved_spread(links, far, lambda piece: weight.at[2, :, columns_of(piece)])
    last_own = pltpu.make_async_copy(far, weight.at[2, :, columns_of(place)], last_sem)
    last_own.start()
    links.greet(planes=False)
    last.one()
    base = links.number(8)
    for index, ref in enumerate((normed_ref, grad_ref)):
        for piece in range(4):
            links.go(
                base + 4 * index + piece,
                ref.at[:, columns_of(2 * piece + theirs_first)],
                other_halves.at[index, :, pl.ds(piece * PIECE, PIECE)],
                core,
            )
            halves[index, :, pl.ds(piece * PIECE, PIECE)] = ref[:, columns_of(2 * piece + mine_first)]
    fed[...] = jnp.zeros_like(fed)
    back_ref[...] = jnp.zeros_like(back_ref)
    for index in range(2):
        for piece in range(4):
            links.got(
                base + 4 * index + piece, other_halves.at[index, :, pl.ds(piece * PIECE, PIECE)]
            )
    given = links.number(PLANES)
    hand = lambda slot: links.copy(given + slot, mine.at[lax.rem(slot, 2)], theirs.at[slot], core)
    spans = [pl.ds(index * count, count) for index in range(3)]
    half = rows // 2

    def forward(slot):
        now = lax.rem(slot, 2)
        held = jnp.where(slot == PLANES - 1, 2, now)

        @pl.when(slot < PLANES - 1)
        def _():
            for copy in load(slot, now):
                copy.wait()

        @pl.when(slot + 2 < PLANES)
        def _():
            for copy in load(slot + 1, 1 - now):
                copy.start()

        @pl.when(slot == PLANES - 1)
        def _():
            last_own.wait()
            last.end()

        @pl.when(slot >= 2)
        def _():
            hand(slot - 2).wait_send()

        for tile in range(2):
            at = pl.ds(tile * half, half)
            normed, grad = normed_ref[at, :], grad_ref[at, :]
            gates = tokens_dot(weight[held, spans[0], :], normed, 1, 1)
            ups = tokens_dot(weight[held, spans[1], :], normed, 1, 1)
            backs = tokens_dot(weight[held, spans[2], :], grad, 1, 1)
            sig = jax.nn.sigmoid(gates)
            active = gates * sig
            mine[now, 2, :, at] = (active * ups).astype(jnp.bfloat16)
            mine[now, 0, :, at] = (backs * ups * sig * (1.0 + gates * (1.0 - sig))).astype(jnp.bfloat16)
            mine[now, 1, :, at] = (backs * active).astype(jnp.bfloat16)
        hand(slot).start()

        def columns(tile, carried):
            lanes = columns_of(tile, 256)
            fed[:, lanes] += tokens_dot(mine[now, 2], weight[held, spans[2], lanes], 0, 0)
            back_ref[:, lanes] += tokens_dot(
                mine[now, 0], weight[held, spans[0], lanes], 0, 0
            ) + tokens_dot(mine[now, 1], weight[held, spans[1], lanes], 0, 0)
            return carried

        lax.fori_loop(0, D // 256, columns, 0)

    def backward(slot):
        now = lax.rem(slot, 2)
        hand(slot).wait_recv()

        @pl.when(slot >= 2)
        def _():
            for copy in flush(slot - 2, now):
                copy.wait()

        def columns(tile, carried):
            lanes = columns_of(tile, 256)
            for index in range(3):
                which = index // 2
                made[now, spans[index], lanes] = (
                    tokens_dot(mine[now, index], halves[which, :, lanes], 1, 0)
                    + tokens_dot(theirs[slot, index], other_halves[which, :, lanes], 1, 0)
                ).astype(jnp.bfloat16)
            return carried

        lax.fori_loop(0, 2, columns, 0)
        for copy in flush(slot, now):
            copy.start()

    def one(step, carried):
        pl.when(step < PLANES)(lambda: forward(step))
        pl.when(step == 0)(last.two)
        pl.when(step == 2)(last.three)
        pl.when(step >= 1)(lambda: backward(step - 1))
        return carried

    lax.fori_loop(0, PLANES + 1, one, 0)
    out_ref[...] = (middle_ref[...] + fed[...]).astype(jnp.bfloat16)
    for slot in (PLANES - 2, PLANES - 1):
        hand(slot).wait_send()
        for copy in flush(slot, slot % 2):
            copy.wait()
    links.drain()


def feed(normed, grad, middle, pieces):
    rows = normed.shape[0]
    count = pieces.shape[2]
    any_spec, vmem = pl.BlockSpec(memory_space=pl.ANY), pl.BlockSpec(memory_space=pltpu.VMEM)
    low = jnp.bfloat16
    return pl.pallas_call(
        feed_kernel,
        in_specs=[vmem, vmem, vmem, any_spec],
        out_specs=[vmem, vmem, any_spec],
        out_shape=[
            jax.ShapeDtypeStruct((rows, D), jnp.float32),
            jax.ShapeDtypeStruct((rows, D), low),
            jax.ShapeDtypeStruct((PLANES, 4, count, PIECE), low),
        ],
        scratch_shapes=[
            pltpu.VMEM((rows, D), jnp.float32),
            pltpu.VMEM((3, count, D), low),
            pltpu.VMEM((2, 3, count // 3, rows), low),
            pltpu.VMEM((PLANES, 3, count // 3, rows), low),
            pltpu.VMEM((2, count, 4 * PIECE), low),
            pltpu.VMEM((2, rows, 4 * PIECE), low),
            pltpu.VMEM((2, rows, 4 * PIECE), low),
            pltpu.SemaphoreType.DMA((26,)),
            pltpu.SemaphoreType.DMA((26,)),
            pltpu.SemaphoreType.DMA((2, 8)),
            pltpu.SemaphoreType.DMA((2, 4)),
            pltpu.SemaphoreType.DMA,
        ],
        compiler_params=pltpu.CompilerParams(
            vmem_limit_bytes=VMEM_LIMIT, collective_id=2, has_side_effects=True
        ),
        name="feed",
    )(normed, grad, middle, pieces)


def add_into(target, source):
    rows = target.shape[0]
    chunk = next(c for c in (352, 256, rows) if rows % c == 0 and c <= rows)

    def one(index, carried):
        span = pl.ds(pl.multiple_of(index * chunk, chunk), chunk)
        target[span, :] = (
            target[span, :].astype(jnp.float32) + source[span, :].astype(jnp.float32)
        ).astype(jnp.bfloat16)
        return carried

    lax.fori_loop(0, rows // chunk, one, 0)


class Fold:
    def __init__(self, links, whole, first, final, bits):
        self.links, self.first, self.final = links, [first.at[m] for m in range(2)], final
        self.base = links.number(3)
        chip = lax.div(links.place, 2)
        ones = lambda bit: lax.rem(lax.div(chip, bit), 2)
        near, far = ones(bits[0]), ones(bits[1])
        self.away = [whole((1 - near) * bits[0] + m * bits[1]) for m in range(2)]
        self.stay = [whole(near * bits[0] + m * bits[1]) for m in range(2)]
        self.near_to = (flip(links.place, 2 * bits[0]), links.depth)
        self.far_to = (flip(links.place, 2 * bits[1]), links.depth)
        self.passed, self.own = first.at[1 - far], first.at[far]

    def one(self):
        for m in range(2):
            self.links.go(self.base + m, self.away[m], self.first[m], self.near_to)

    def two(self, stay=None):
        for m in range(2):
            self.links.got(self.base + m, self.first[m])
            add_into(self.first[m], self.stay[m] if stay is None else stay[m])
        self.links.go(self.base + 2, self.passed, self.final, self.far_to)

    def end(self):
        self.links.got(self.base + 2, self.final)
        add_into(self.final, self.own)


class LineFold:
    def __init__(self, links, block, held):
        self.links = links
        self.held = [[held.at[way, step] for step in range(PLANES - 1)] for way in range(2)]
        self.base = links.number(2 * (PLANES - 1))
        depth = links.depth
        self.blocks, self.sends, self.sums, self.takes, self.to = [], [], [], [], []
        for step in range(1, PLANES):
            right = jnp.minimum(depth + PLANES - step, PLANES - 1)
            left = jnp.maximum(depth - PLANES + step, 0)
            self.blocks.append((block(left), block(right)))
            self.sends.append((depth >= PLANES - step, depth < step))
            self.takes.append(((depth >= PLANES - 1 - step) & (depth < PLANES - 1), (depth <= step) & (depth > 0)))
        self.ends = (depth == PLANES - 1, depth == 0)
        self.to = (
            (links.place, jnp.maximum(depth - 1, 0)),
            (links.place, jnp.minimum(depth + 1, PLANES - 1)),
        )
        self.inner = [
            [self.sends[step][way] & jnp.logical_not(self.ends[way]) for way in range(2)]
            for step in range(PLANES - 1)
        ]
        self.outer = [
            [self.sends[step][way] & self.ends[way] for way in range(2)] for step in range(PLANES - 1)
        ]

    def launch(self, step):
        for way in range(2):
            self.links.go(
                self.base + 2 * (step - 1) + way,
                self.blocks[step - 1][way],
                self.held[way][step - 1],
                self.to[way],
                self.outer[step - 1][way],
            )

    def take(self, step):
        for way in range(2):
            self.links.got(
                self.base + 2 * (step - 1) + way, self.held[way][step - 1], self.takes[step - 1][way]
            )

    def forward(self, step):
        for way in range(2):
            before = self.held[way][step - 2]
            block = self.blocks[step - 1][way]

            @pl.when(self.inner[step - 1][way])
            def _():
                add_into(before, block)

            self.links.go(
                self.base + 2 * (step - 1) + way,
                before,
                self.held[way][step - 1],
                self.to[way],
                self.inner[step - 1][way],
            )

    def total(self, own, out):
        depth = self.links.depth
        rows = out.shape[0]
        chunk = next(c for c in (352, 256, rows) if rows % c == 0)

        def one(index, carried):
            span = pl.ds(pl.multiple_of(index * chunk, chunk), chunk)
            value = own[span, :].astype(jnp.float32)
            sides = [self.held[way][PLANES - 2][span, :].astype(jnp.float32) for way in range(2)]
            value = value + jnp.where(depth < PLANES - 1, sides[0], 0.0)
            out[span, :] = value + jnp.where(depth > 0, sides[1], 0.0)
            return carried

        lax.fori_loop(0, rows // chunk, one, 0)


def close_kernel(*refs):
    (made, low_in, attended_in, q_in, k_in, v_in, o_in, n_in, weight_in, cos_in, sin_in) = refs[:11]
    incoming = refs[11:15]
    log_ref, begin_ref, gain_ref, small_in = refs[15:19]
    first_ref, back_ref, feed_total, out_total, attn_total, small_ref = refs[19:25]
    (
        q_ref, k_ref, v_ref, o_ref, n_ref, weight_ref, cos_ref, sin_ref, grad, inner, total, made_ref,
        stay, feed_first, feed_final, feed_held, out_made, out_core, out_first, out_final, out_held,
        attn_core, attn_first, attn_final, partial, partial_held, small_got,
        send, recv, local,
    ) = refs[25:]
    links = Links(send, recv)
    place, depth = links.place, links.depth
    length = q_ref.shape[0]
    shard = length // PLANES
    parity, chip = lax.rem(place, 2), lax.div(place, 2)
    core = (flip(place, 1), depth)
    loads = []

    def load(source, target):
        copy = pltpu.make_async_copy(source, target, local.at[len(loads)])
        copy.start()
        loads.append(copy)
        return copy

    order = (3, 2, 1, 0)

    def halved_fold(whole, first, final):
        return Halves(
            [
                Fold(
                    links,
                    lambda i, half=half: half_of(whole(i), half),
                    half_of(first, half),
                    half_of(final, half),
                    ((1, 2), (2, 1))[half],
                )
                for half in range(2)
            ]
        )

    folds = {
        slot: halved_fold(
            lambda i, slot=slot: made.at[slot, i], feed_first.at[slot], feed_final.at[slot]
        )
        for slot in order
    }
    out_fold = halved_fold(lambda i: out_core.at[i], out_first, out_final)
    attn_fold = halved_fold(lambda i: attn_core.at[i], attn_first, attn_final)

    def slot_holding(block):
        found = 0
        for plane in range(PLANES):
            for slot, (_, _, held) in enumerate(SLOTS[plane]):
                found = found + jnp.where((depth == plane) & (block == held), slot, 0)
        return found

    feed_line = LineFold(links, lambda j: feed_final.at[slot_holding(j)], feed_held)
    out_line = LineFold(
        links, lambda j: out_final.at[pl.ds(pl.multiple_of(j * 256, 256), 256), :], out_held
    )
    line = LineFold(links, lambda j: partial.at[j], partial_held)
    out_swap, attn_swap = links.number(4), links.number(4)
    sides = [columns_of(2 * i + parity) for i in range(4)]
    others = [columns_of(2 * i + 1 - parity) for i in range(4)]
    across = links.number(2 * PLANES)
    tiny = links.number(6)
    stays = [
        [[half_of(stay.at[index, m], half) for m in range(2)] for half in range(2)] for index in range(2)
    ]
    stay_sems = [[[16 + 4 * index + 2 * half + m for m in range(2)] for half in range(2)] for index in range(2)]

    def restay(slot):
        return [
            pltpu.make_async_copy(
                folds[slot].parts[half].stay[m],
                stays[slot % 2][half][m],
                local.at[stay_sems[slot % 2][half][m]],
            )
            for half in range(2)
            for m in range(2)
        ]

    tiny_to = [core, (flip(place, 2), depth), (flip(place, 4), depth)]
    plane_to = [(place, lax.rem(depth + step, PLANES)) for step in range(1, PLANES)]
    plane_rows = [lax.rem(depth - step + PLANES, PLANES) for step in range(PLANES)]

    attended_ref, low_ref = partial.at[0], partial.at[1]
    first_loads = [load(attended_in, attended_ref), load(low_in, low_ref)]
    for slot in order[:2]:
        for copy in restay(slot):
            copy.start()
    q_loads = [load(source, target) for source, target in ((q_in, q_ref), (k_in, k_ref), (v_in, v_ref), (o_in, o_ref), (cos_in, cos_ref), (sin_in, sin_ref))]
    own_rows = pl.ds(pl.multiple_of(depth * shard, shard), shard)
    q_loads.append(load(incoming[0], grad.at[own_rows, :]))
    late = [load(n_in, n_ref), load(weight_in, weight_ref)]

    links.greet()
    for pair in range(2):
        lanes = pl.ds(pair * 128, 128)
        for step in range(1, PLANES):
            links.go(
                across + 4 * pair + step,
                incoming[step].at[:, lanes],
                grad.at[own_rows, lanes],
                plane_to[step - 1],
            )
    folds[3].one()

    for copy in first_loads:
        copy.wait()
    for index in range(4):
        rows = pl.ds(index * 256, 256)
        out_made[rows, :] = tokens_dot(attended_ref[:, rows], low_ref[...], 0, 0).astype(jnp.bfloat16)
    out_swaps = [links.copy(out_swap + i, out_made.at[:, others[i]], out_core.at[i], core) for i in range(4)]
    for copy in out_swaps:
        copy.start()
    for i in range(4):
        links.got(out_swap + i, out_core.at[i])
        add_into(out_core.at[i], out_made.at[:, sides[i]])
    for copy in q_loads:
        copy.wait()

    def fold_two(slot):
        for copy in restay(slot):
            copy.wait()
        folds[slot].two(stays[slot % 2])

    fold_two(3)
    folds[2].one()
    grad_rows = [
        [
            grad.at[pl.ds(pl.multiple_of(plane_rows[step] * shard, shard), shard), pl.ds(pair * 128, 128)]
            for step in range(PLANES)
        ]
        for pair in range(2)
    ]

    def take_grads(pair):
        for step in range(1, PLANES):
            links.got(across + 4 * pair + step, grad_rows[pair][step])

    take_grads(0)

    lane = lax.broadcasted_iota(jnp.int32, (shard, 128), 1)
    keeps = [lane < HD, lane >= HD]
    down = lax.broadcasted_iota(jnp.int32, (shard, shard), 0)
    along = lax.broadcasted_iota(jnp.int32, (1, shard), 1)

    def masked(values, head):
        return jnp.where(keeps[head], values, jnp.zeros_like(values))

    def after_a():
        folds[3].end()
        feed_line.launch(1)
        out_fold.one()

    def after_b():
        fold_two(2)
        folds[1].one()
        for copy in restay(1):
            copy.start()

    def after_c():
        folds[2].end()
        feed_line.launch(2)
        feed_line.take(1)
        feed_line.forward(2)
        out_fold.two()
        take_grads(1)

    def after_d():
        fold_two(1)
        folds[0].one()
        for copy in restay(0):
            copy.start()
        out_fold.end()

    def after_e():
        folds[1].end()
        feed_line.launch(3)
        feed_line.take(2)
        feed_line.forward(3)
        for step in range(1, PLANES):
            out_line.launch(step)

    def back_step(step, carried):
        pair, block = lax.div(step, PLANES), lax.rem(step, PLANES)
        lanes = columns_of(pair)
        start = pl.multiple_of(block * shard, shard)
        own = pl.ds(start, shard)

        @pl.when(block == 0)
        def _():
            total[...] = jnp.zeros_like(total)
            for index in range(PLANES):
                span = pl.ds(index * shard, shard)
                turned = jnp.transpose(
                    grad[span, lanes].astype(jnp.float32) * o_ref[span, lanes].astype(jnp.float32)
                )
                for head in range(2):
                    inner[head : head + 1, span] = jnp.sum(
                        turned[head * HD : head * HD + HD], axis=0, keepdims=True
                    )

        keys, values = k_ref[own, lanes], v_ref[own, lanes]
        own_keys = [masked(keys, head) for head in range(2)]

        def tile(index, sums, visible):
            key_sum, value_sum = sums
            span = pl.ds(pl.multiple_of(index * shard, shard), shard)
            query_block, grad_block = q_ref[span, lanes], grad[span, lanes]
            query_sum = total[span, :]
            for head in range(2):
                query, out_grad = masked(query_block, head), masked(grad_block, head)
                scores = tokens_dot(keys, query, 1, 1)
                shares = jnp.where(
                    visible, jnp.exp2(scores - log_ref[pair, head : head + 1, span]), 0.0
                )
                share_grad = tokens_dot(values, out_grad, 1, 1)
                score_grad = (shares * (share_grad - inner[head : head + 1, span])).astype(jnp.bfloat16)
                value_sum = value_sum + tokens_dot(shares.astype(jnp.bfloat16), out_grad, 1, 0)
                key_sum = key_sum + tokens_dot(score_grad, query, 1, 0)
                query_sum = query_sum + tokens_dot(score_grad, own_keys[head], 0, 0)
            total[span, :] = query_sum
            return (key_sum, value_sum)

        empty = jnp.zeros((shard, 128), jnp.float32)
        sums = tile(
            block, (empty, empty), (down >= begin_ref[0:1, own] - start) & (down <= along)
        )
        key_sum, value_sum = lax.fori_loop(
            block + 1,
            PLANES,
            lambda i, held: tile(
                i,
                held,
                down >= begin_ref[0:1, pl.ds(pl.multiple_of(i * shard, shard), shard)] - start,
            ),
            sums,
        )
        cosine, sine_part = cos_ref[own, :], sin_ref[own, :]
        made_ref[own, columns_of(pair)] = turn(
            total[own, :] * HD**-0.5, cosine, sine_part, False
        ).astype(jnp.bfloat16)
        made_ref[own, columns_of(2 + pair)] = turn(
            key_sum * (1 / LOG2E), cosine, sine_part, False
        ).astype(jnp.bfloat16)
        half_sum = 0.5 * value_sum
        made_ref[own, columns_of(4 + pair)] = half_sum.astype(jnp.bfloat16)
        first_ref[own, lanes] = half_sum
        for when, pump in ((0, after_a), (1, after_b), (3, after_c), (5, after_d), (7, after_e)):
            pl.when(step == when)(pump)
        return carried

    lax.fori_loop(0, 2 * PLANES, back_step, 0)
    for copy in late:
        copy.wait()
    small_ref[...] = small_in[...]

    def input_back(index, carried):
        block = jnp.where(depth < PLANES // 2, PLANES - 1 - index, index)
        rows = pl.ds(pl.multiple_of(block * shard, shard), shard)
        value = tokens_dot(made_ref[rows, :], weight_ref[pl.ds(0, 768), :], 1, 0)
        partial[block] = value.astype(jnp.bfloat16)
        gain = (
            jnp.sum(value * n_ref[rows, :].astype(jnp.float32), axis=0, keepdims=True)
            / gain_ref[0:1, :]
        )
        for piece in range(8):
            small_ref[0, piece : piece + 1, :] += gain[:, piece * PIECE : piece * PIECE + PIECE]
        return carried

    input_back(0, 0)
    line.launch(1)
    lax.fori_loop(1, PLANES, input_back, 0)
    line.launch(2)
    line.launch(3)
    fold_two(0)
    out_line.take(1)
    out_line.forward(2)

    links.go(tiny, small_ref.at[0], small_got.at[0], tiny_to[0])
    for copy in out_swaps:
        copy.wait_send()
    attn_made = out_made.at[pl.ds(0, 768), :]
    for index in range(3):
        rows = pl.ds(index * 256, 256)
        attn_made[rows, :] = tokens_dot(made_ref[:, rows], n_ref[...], 0, 0).astype(jnp.bfloat16)
    for i in range(4):
        links.go(attn_swap + i, attn_made.at[:, others[i]], attn_core.at[i], core)
    links.got(tiny, small_got.at[0])
    small_ref[1] = small_ref[0] + small_got[0]
    links.go(tiny + 1, small_ref.at[1], small_got.at[1], tiny_to[1])
    for i in range(4):
        links.got(attn_swap + i, attn_core.at[i])
        add_into(attn_core.at[i], attn_made.at[:, sides[i]])
    attn_fold.one()
    line.take(1)
    line.forward(2)
    links.got(tiny + 1, small_got.at[1])
    small_ref[2] = small_ref[1] + small_got[1]
    links.go(tiny + 2, small_ref.at[2], small_got.at[2], tiny_to[2])
    folds[0].end()
    feed_line.take(3)
    feed_line.total(feed_final.at[0], feed_total)
    out_line.take(2)
    out_line.forward(3)
    attn_fold.two()
    links.got(tiny + 2, small_got.at[2])
    small_ref[3] = small_ref[2] + small_got[2]
    small_place = small_got.at[3 + depth]
    for step in range(1, PLANES):
        links.go(tiny + 2 + step, small_ref.at[3], small_place, plane_to[step - 1])
    small_got[3 + depth] = small_ref[3]
    out_line.take(3)
    out_line.total(out_final.at[pl.ds(pl.multiple_of(depth * 256, 256), 256), :], out_total)
    line.take(2)
    line.forward(3)
    attn_fold.end()
    attn_total[...] = attn_final[...].astype(jnp.float32)
    for step in range(1, PLANES):
        links.got(tiny + 2 + step, small_got.at[3 + plane_rows[step]])
    small_ref[4] = small_got[3] + small_got[4] + small_got[5] + small_got[6]
    line.take(3)
    line.total(partial.at[depth], back_ref)
    links.drain()


def closing(made, low_ref, attended_own, heads, normed, weight, tables, incoming, logs, begin_row, gains, small):
    length, width = heads[0].shape
    rows = low_ref.shape[0]
    count = made.shape[2]
    low, full = jnp.bfloat16, jnp.float32
    any_spec, vmem = pl.BlockSpec(memory_space=pl.ANY), pl.BlockSpec(memory_space=pltpu.VMEM)
    shape = jax.ShapeDtypeStruct
    return pl.pallas_call(
        close_kernel,
        in_specs=[any_spec] * 15 + [vmem] * 4,
        out_specs=[vmem] * 6,
        out_shape=[
            shape((length, width), full),
            shape((rows, D), full),
            shape((count, PIECE), full),
            shape((256, PIECE), full),
            shape((768, PIECE), full),
            shape((5, 24, PIECE), full),
        ],
        scratch_shapes=[pltpu.VMEM((length, width), low)] * 4
        + [
            pltpu.VMEM((length, D), low),
            pltpu.VMEM((ATTN_ROWS, D), low),
            pltpu.VMEM((length, 128), full),
            pltpu.VMEM((length, 128), full),
            pltpu.VMEM((length, width), low),
            pltpu.VMEM((8, length), full),
            pltpu.VMEM((length, 128), full),
            pltpu.VMEM((length, 768), low),
            pltpu.VMEM((2, 2, count, PIECE), low),
            pltpu.VMEM((PLANES, 2, count, PIECE), low),
            pltpu.VMEM((PLANES, count, PIECE), low),
            pltpu.VMEM((2, PLANES - 1, count, PIECE), low),
            pltpu.VMEM((D, D), low),
            pltpu.VMEM((4, D, PIECE), low),
            pltpu.VMEM((2, D, PIECE), low),
            pltpu.VMEM((D, PIECE), low),
            pltpu.VMEM((2, PLANES - 1, 256, PIECE), low),
            pltpu.VMEM((4, 768, PIECE), low),
            pltpu.VMEM((2, 768, PIECE), low),
            pltpu.VMEM((768, PIECE), low),
            pltpu.VMEM((PLANES, rows, D), low),
            pltpu.VMEM((2, PLANES - 1, rows, D), low),
            pltpu.VMEM((7, 24, PIECE), full),
            pltpu.SemaphoreType.DMA((CLOSE_COPIES,)),
            pltpu.SemaphoreType.DMA((CLOSE_COPIES,)),
            pltpu.SemaphoreType.DMA((24,)),
        ],
        compiler_params=pltpu.CompilerParams(
            vmem_limit_bytes=CLOSE_VMEM, collective_id=3, has_side_effects=True
        ),
        name="closing",
    )(made, low_ref, attended_own, *heads, normed, weight, *tables, *incoming, logs, begin_row, gains, small)


def middle_back_kernel(*refs):
    middle_ref, grad_ref, back_ref, weight_ref, gain_ref = refs[:5]
    low_ref, dm_ref, gain_grad_ref = refs[5:8]
    outs = refs[8:12]
    depth = lax.axis_index("mp")
    half = middle_ref.shape[0] // 2
    gain = gain_ref[1:2, :]
    gain_grad_ref[...] = jnp.zeros_like(gain_grad_ref)
    for tile in range(2):
        rows = pl.ds(tile * half, half)
        middle, incoming = middle_ref[rows, :], back_ref[rows, :]
        factor = lax.rsqrt(jnp.mean(middle * middle, axis=-1, keepdims=True) + 1e-06)
        scaled = incoming * gain
        mean = jnp.mean(scaled * middle, axis=-1, keepdims=True)
        total = grad_ref[rows, :].astype(jnp.float32) + factor * scaled - middle * (factor**3 * mean)
        gain_grad_ref[0:1, :] += jnp.sum(incoming * middle * factor, axis=0, keepdims=True)
        dm_ref[rows, :] = total
        low_ref[rows, :] = total.astype(jnp.bfloat16)
    for index, out in enumerate(outs):
        owner = lax.rem(depth + index, PLANES)
        rows = pl.ds(pl.multiple_of(owner * 256, 256), 256)
        out[...] = tokens_dot(low_ref[...], weight_ref[rows, :], 1, 1).astype(jnp.bfloat16)


def middle_back(middle, grad, back, weight, gains):
    rows = middle.shape[0]
    return pl.pallas_call(
        middle_back_kernel,
        out_shape=[
            jax.ShapeDtypeStruct((rows, D), jnp.bfloat16),
            jax.ShapeDtypeStruct((rows, D), jnp.float32),
            jax.ShapeDtypeStruct((8, D), jnp.float32),
        ]
        + [jax.ShapeDtypeStruct((rows, 256), jnp.bfloat16)] * PLANES,
        compiler_params=pltpu.CompilerParams(vmem_limit_bytes=VMEM_LIMIT),
        cost_estimate=cost(2 * rows * D * D, 12 << 20),
        name="middle_back",
    )(middle, grad, back, weight, gains)


def fast_shards(
    hidden_in,
    segment_ids,
    first_values,
    grad_out,
    input_proj,
    output_proj,
    expand_proj,
    reduce_proj,
    norm_gains,
    old_moment_input,
    old_moment_output,
    old_moment_expand,
    old_moment_reduce,
    old_moment_gains,
    old_square_input,
    old_square_output,
    old_square_expand,
    old_square_reduce,
    old_square_gains,
):
    place, depth = lax.axis_index("dp"), lax.axis_index("mp")
    low = jnp.bfloat16
    hidden, out_cotangent = hidden_in[0], grad_out[0]
    seg_row = segment_ids[0]
    length = seg_row.shape[0]
    shard = hidden.shape[0]
    ffs = reduce_proj.shape[0]

    attn_piece = jnp.concatenate(
        [
            input_proj.astype(low).transpose(0, 2, 1).reshape(768, PIECE),
            norm_gains.astype(low),
            jnp.zeros((14, PIECE), low),
        ]
    )
    feed_piece = jnp.concatenate(
        [
            expand_proj.astype(low).transpose(0, 2, 1).reshape(2 * ffs, PIECE),
            reduce_proj.astype(low),
        ]
    )

    begins = jnp.zeros_like(seg_row)
    for number in range(1, 7):
        start = jnp.sum((seg_row < number).astype(jnp.int32))
        begins = jnp.where(seg_row == number, start, begins)
    lows = begins[:: length // BLOCKS]
    offset = (jnp.arange(length, dtype=jnp.int32) - begins).astype(jnp.float32)
    inverse_rates = 10000.0 ** (-2.0 * jnp.arange(HD // 2, dtype=jnp.float32) / HD)
    angles = offset[:, None] * inverse_rates[None, :]
    cosine, sine = jnp.cos(angles), jnp.sin(angles)
    cosine = jnp.concatenate([cosine] * 4, axis=1)
    sine_part = jnp.concatenate([-sine, sine, -sine, sine], axis=1)

    (
        queries,
        keys,
        values,
        attended,
        normed,
        attn_weight,
        out_weight,
        feed_all,
        gains,
        squares,
        logs,
        middle,
        normed_two,
        attended_own,
    ) = opening(
        hidden,
        attn_piece,
        output_proj.astype(low),
        feed_piece,
        cosine,
        sine_part,
        first_values[0],
        begins[:, None],
    )
    normed_two_grad, layer_output, made = feed(normed_two, out_cotangent, middle, feed_all)
    layer_output = layer_output[None]
    branch_low, middle_grad, gain_two, *out_grads = middle_back(
        middle, out_cotangent, normed_two_grad, out_weight, gains
    )
    small = jnp.concatenate(
        [
            jnp.zeros((8, PIECE), jnp.float32),
            gain_two[0].reshape(8, PIECE),
            jnp.broadcast_to(jnp.sum(squares[:2], axis=1)[:, None], (2, PIECE)),
            jnp.zeros((6, PIECE), jnp.float32),
        ]
    )
    values_grad, normed_grad, feed_total, out_total, attn_total, small = closing(
        made,
        branch_low,
        attended_own,
        (queries, keys, values, attended),
        normed,
        attn_weight,
        (cosine, sine_part),
        out_grads,
        logs,
        jnp.broadcast_to(begins[None], (8, length)),
        gains,
        jnp.broadcast_to(small[None], (5, 24, PIECE)),
    )
    small = small[4]
    value_norms = jnp.sqrt(small[16:18, 0] / (8 * length * D))
    gain_total = lax.dynamic_index_in_dim(small[:16].reshape(2, 8, PIECE), place, 1, False)

    hidden32 = hidden.astype(jnp.float32)
    factor_one = rms_factor(hidden32)
    input_part, _ = norm_back(hidden32, factor_one, gains[0], normed_grad)
    input_grad = (middle_grad + input_part)[None]

    expand_total = feed_total[: 2 * ffs].reshape(2, ffs, PIECE).transpose(0, 2, 1)
    reduce_total = feed_total[2 * ffs :]
    attn_total = attn_total.reshape(3, 256, PIECE).transpose(0, 2, 1)
    new_input = adamw(input_proj, attn_total, old_moment_input, old_square_input, D ** (-0.5), 0.1)
    new_output = adamw(
        output_proj,
        out_total,
        old_moment_output,
        old_square_output,
        max(1, 8 * HEADS * HD // LEN) ** (-0.5),
        0.1,
    )
    new_expand = adamw(
        expand_proj, expand_total, old_moment_expand, old_square_expand, D ** (-0.5), 0.1
    )
    new_reduce = adamw(
        reduce_proj, reduce_total, old_moment_reduce, old_square_reduce, (FF // 3) ** (-0.5), 0.1
    )
    new_gains = adamw(norm_gains, gain_total, old_moment_gains, old_square_gains, 0.2, 0.0)
    return (
        layer_output,
        input_grad,
        values_grad[None],
        value_norms,
        new_input[0],
        new_output[0],
        new_expand[0],
        new_reduce[0],
        new_gains[0],
        new_input[1],
        new_output[1],
        new_expand[1],
        new_reduce[1],
        new_gains[1],
        new_input[2],
        new_output[2],
        new_expand[2],
        new_reduce[2],
        new_gains[2],
    )


def solution(mesh):
    quick = mesh.shape["dp"] == 8 and mesh.shape["mp"] == PLANES
    return jax.shard_map(
        fast_shards if quick else shards,
        mesh=mesh,
        in_specs=(
            P("dp", "mp", None),
            P("dp", None),
            P("dp", None, "mp"),
            P("dp", "mp", None),
            P(None, "dp", "mp"),
            P("mp", "dp"),
            P(None, "dp", "mp"),
            P("mp", "dp"),
            P(None, "dp"),
            P(None, "dp", "mp"),
            P("mp", "dp"),
            P(None, "dp", "mp"),
            P("mp", "dp"),
            P(None, "dp"),
            P(None, "dp", "mp"),
            P("mp", "dp"),
            P(None, "dp", "mp"),
            P("mp", "dp"),
            P(None, "dp"),
        ),
        out_specs=(
            P("dp", "mp", None),
            P("dp", "mp", None),
            P("dp", None, "mp"),
            P(),
            P(None, "dp", "mp"),
            P("mp", "dp"),
            P(None, "dp", "mp"),
            P("mp", "dp"),
            P(None, "dp"),
            P(None, "dp", "mp"),
            P("mp", "dp"),
            P(None, "dp", "mp"),
            P("mp", "dp"),
            P(None, "dp"),
            P(None, "dp", "mp"),
            P("mp", "dp"),
            P(None, "dp", "mp"),
            P("mp", "dp"),
            P(None, "dp"),
        ),
        check_vma=False,
    )
```

```python
import functools
import math

import jax
import jax.numpy as jnp
import numpy as np
from jax import lax
from jax.experimental import pallas as pl
from jax.experimental.pallas import tpu as pltpu
from jax.sharding import PartitionSpec as P

D = 1024
HEADS = 16
HD = 64
FF = 2816
LEN = 2048
STEP = 5
PLANES = 4
PIECE = 128
BLOCKS = 4
ATTN_ROWS = 784
VMEM_LIMIT = 56 << 20
OPEN_COPIES = 80
CLOSE_COPIES = 80
CLOSE_VMEM = 60 << 20


def arrivals(plane):
    order = [(0, 0, plane)]
    for hop in range(1, PLANES):
        if plane + hop < PLANES:
            order.append((0, hop, plane + hop))
        if plane - hop >= 0:
            order.append((1, hop, plane - hop))
    return order


SLOTS = [arrivals(plane) for plane in range(PLANES)]


def cost(flops, moved):
    return pl.CostEstimate(flops=flops, bytes_accessed=moved, transcendentals=0)


def rope_tables(seg_row, head_size):
    length = seg_row.shape[0]
    places = jnp.arange(length, dtype=jnp.int32)
    begins = jnp.sum((seg_row[None, :] < seg_row[:, None]).astype(jnp.int32), axis=1)
    offset = (places - begins).astype(jnp.float32)
    inverse_rates = 10000.0 ** (-2.0 * jnp.arange(head_size // 2, dtype=jnp.float32) / head_size)
    angles = offset[:, None] * inverse_rates[None, :]
    return (jnp.cos(angles)[:, None, :], jnp.sin(angles)[:, None, :])


def rotate(values, cosine, sine_part, forward):
    half_size = values.shape[-1] // 2
    first_half = values[..., :half_size]
    second_half = values[..., half_size:]
    if forward:
        return jnp.concatenate(
            [
                first_half * cosine - second_half * sine_part,
                second_half * cosine + first_half * sine_part,
            ],
            axis=-1,
        )
    return jnp.concatenate(
        [
            first_half * cosine + second_half * sine_part,
            second_half * cosine - first_half * sine_part,
        ],
        axis=-1,
    )


def rms_factor(values):
    return lax.rsqrt(jnp.mean(values * values, axis=-1, keepdims=True) + 1e-06)


def norm_back(values, factor, gain_row, incoming):
    scaled = incoming * gain_row
    value_grad = factor * scaled - values * factor**3 * jnp.mean(
        scaled * values, axis=-1, keepdims=True
    )
    gain_grad = jnp.sum(incoming * values * factor, axis=0)
    return (value_grad, gain_grad)


def visible_block(seg_row, first_row, block_rows):
    length = seg_row.shape[0]
    query_seg = lax.dynamic_slice_in_dim(seg_row, first_row, block_rows, 0)
    query_places = first_row + jnp.arange(block_rows, dtype=jnp.int32)
    key_places = jnp.arange(length, dtype=jnp.int32)
    return (query_seg[:, None] == seg_row[None, :]) & (query_places[:, None] >= key_places[None, :])


def block_scores(queries, keys_rot, seg_row, first_row, block_rows, score_scale):
    query_block = lax.dynamic_slice_in_dim(queries, first_row, block_rows, 0)
    visible = visible_block(seg_row, first_row, block_rows)
    scores = (
        jnp.einsum("qhd,khd->hqk", query_block, keys_rot, preferred_element_type=jnp.float32)
        * score_scale
    )
    return (query_block, jnp.where(visible[None], scores, -1e30))


def attend(queries, keys_rot, mixed_values, seg_row, score_scale):
    length = queries.shape[0]
    block_rows = min(512, length)

    def one_block(block_index):
        first_row = block_index * block_rows
        query_block, scores = block_scores(
            queries, keys_rot, seg_row, first_row, block_rows, score_scale
        )
        top_score = jnp.max(scores, axis=-1, keepdims=True)
        raised = jnp.exp(scores - top_score)
        totals = jnp.sum(raised, axis=-1, keepdims=True)
        shares = (raised / totals).astype(jnp.bfloat16)
        combined = jnp.einsum(
            "hqk,khd->qhd", shares, mixed_values, preferred_element_type=jnp.float32
        )
        return (combined, (top_score + jnp.log(totals))[..., 0])

    combined, log_totals = lax.map(one_block, jnp.arange(length // block_rows, dtype=jnp.int32))
    return (combined.reshape(length, -1), log_totals)


def attend_back(queries, keys_rot, mixed_values, out_grad, log_totals, seg_row, score_scale):
    length = queries.shape[0]
    block_rows = min(512, length)

    def one_block(running, operands):
        key_sum, value_sum = running
        block_index, block_totals = operands
        first_row = block_index * block_rows
        query_block, scores = block_scores(
            queries, keys_rot, seg_row, first_row, block_rows, score_scale
        )
        grad_block = lax.dynamic_slice_in_dim(out_grad, first_row, block_rows, 0)
        shares = jnp.exp(scores - block_totals[..., None])
        share_grad = jnp.einsum(
            "qhd,khd->hqk", grad_block, mixed_values, preferred_element_type=jnp.float32
        )
        inner = jnp.sum(shares * share_grad, axis=-1, keepdims=True)
        score_grad = (shares * (share_grad - inner)).astype(jnp.bfloat16)
        query_grad = (
            jnp.einsum("hqk,khd->qhd", score_grad, keys_rot, preferred_element_type=jnp.float32)
            * score_scale
        )
        key_sum = (
            key_sum
            + jnp.einsum(
                "hqk,qhd->khd", score_grad, query_block, preferred_element_type=jnp.float32
            )
            * score_scale
        )
        value_sum = value_sum + jnp.einsum(
            "hqk,qhd->khd",
            shares.astype(jnp.bfloat16),
            grad_block,
            preferred_element_type=jnp.float32,
        )
        return ((key_sum, value_sum), query_grad)

    empty_sum = jnp.zeros(keys_rot.shape, jnp.float32)
    (key_grad, value_grad), query_grad = lax.scan(
        one_block,
        (empty_sum, empty_sum),
        (jnp.arange(length // block_rows, dtype=jnp.int32), log_totals),
    )
    return (query_grad.reshape(keys_rot.shape), key_grad, value_grad)


def adamw(master, gradient, moment, square, step_rate, decay):
    new_moment = 0.5 * moment + 0.5 * gradient
    new_square = 0.5 * square + 0.5 * gradient * gradient
    correct = 1.0 - 0.5**STEP
    update = new_moment / correct / (jnp.sqrt(new_square / correct) + 1e-08)
    return (master - step_rate * (update + decay * master), new_moment, new_square)


def shards(
    hidden_in,
    segment_ids,
    first_values,
    grad_out,
    input_proj,
    output_proj,
    expand_proj,
    reduce_proj,
    norm_gains,
    old_moment_input,
    old_moment_output,
    old_moment_expand,
    old_moment_reduce,
    old_moment_gains,
    old_square_input,
    old_square_output,
    old_square_expand,
    old_square_reduce,
    old_square_gains,
):
    attn_weight, out_weight, expand_weight, reduce_weight, gains_low = (
        lax.all_gather(input_proj.astype(jnp.bfloat16), "dp", axis=1, tiled=True),
        lax.all_gather(output_proj.astype(jnp.bfloat16), "dp", axis=1, tiled=True),
        lax.all_gather(expand_proj.astype(jnp.bfloat16), "dp", axis=1, tiled=True),
        lax.all_gather(reduce_proj.astype(jnp.bfloat16), "dp", axis=1, tiled=True),
        lax.all_gather(norm_gains.astype(jnp.bfloat16), "dp", axis=1, tiled=True),
    )
    gains = gains_low.astype(jnp.float32)
    hidden = hidden_in[0].astype(jnp.float32)
    seg_row = segment_ids[0]
    length = seg_row.shape[0]
    first_in = first_values[0].astype(jnp.float32)
    local_heads = attn_weight.shape[2] // HD
    score_scale = 1.0 / math.sqrt(HD)
    factor_one = rms_factor(hidden)
    normed_one = (hidden * factor_one * gains[0]).astype(jnp.bfloat16)
    all_normed, all_grad_out = (
        lax.all_gather(normed_one, "mp", axis=0, tiled=True),
        lax.all_gather(grad_out[0], "mp", axis=0, tiled=True),
    )
    projected = jnp.einsum(
        "td,cde->cte", all_normed, attn_weight, preferred_element_type=jnp.float32
    )
    cosine, sine_part = rope_tables(seg_row, HD)
    queries = rotate(projected[0].reshape(length, local_heads, HD), cosine, sine_part, True).astype(
        jnp.bfloat16
    )
    keys_rot = rotate(
        projected[1].reshape(length, local_heads, HD), cosine, sine_part, True
    ).astype(jnp.bfloat16)
    blended = 0.5 * projected[2] + 0.5 * first_in
    mixed_values = blended.astype(jnp.bfloat16).reshape(length, local_heads, HD)
    square_terms = jnp.stack([jnp.sum(first_in * first_in), jnp.sum(blended * blended)])
    attended, log_totals = attend(queries, keys_rot, mixed_values, seg_row, score_scale)
    attended_low = attended.astype(jnp.bfloat16)
    rows_part = attended_low
    branch = lax.psum_scatter(
        jnp.dot(rows_part, out_weight, preferred_element_type=jnp.float32),
        "mp",
        scatter_dimension=0,
        tiled=True,
    )
    middle = hidden + branch
    factor_two = rms_factor(middle)
    normed_two = (middle * factor_two * gains[1]).astype(jnp.bfloat16)
    all_normed_two = lax.all_gather(normed_two, "mp", axis=0, tiled=True)
    gate_up = jnp.einsum(
        "td,cdf->ctf", all_normed_two, expand_weight, preferred_element_type=jnp.float32
    )
    gate_sig = jax.nn.sigmoid(gate_up[0])
    gate_act = gate_up[0] * gate_sig
    activated = (gate_act * gate_up[1]).astype(jnp.bfloat16)
    rows_part = activated
    feed_out = lax.psum_scatter(
        jnp.dot(rows_part, reduce_weight, preferred_element_type=jnp.float32).astype(jnp.bfloat16),
        "mp",
        scatter_dimension=0,
        tiled=True,
    ).astype(jnp.float32)
    layer_output = (middle + feed_out).astype(jnp.bfloat16)[None]
    hidden_grad = jnp.einsum(
        "td,fd->tf", all_grad_out, reduce_weight, preferred_element_type=jnp.float32
    )
    reduce_grad = jnp.einsum(
        "tf,td->fd", activated, all_grad_out, preferred_element_type=jnp.float32
    )
    gate_grad = hidden_grad * gate_up[1] * gate_sig * (1.0 + gate_up[0] * (1.0 - gate_sig))
    up_grad = hidden_grad * gate_act
    pair_grad = jnp.stack([gate_grad, up_grad]).astype(jnp.bfloat16)
    expand_grad = jnp.einsum(
        "ctf,td->cdf", pair_grad, all_normed_two, preferred_element_type=jnp.float32
    )
    rows_part = pair_grad
    normed_two_grad = lax.psum_scatter(
        jnp.einsum(
            "ctf,cdf->td", rows_part, expand_weight, preferred_element_type=jnp.float32
        ).astype(jnp.bfloat16),
        "mp",
        scatter_dimension=0,
        tiled=True,
    ).astype(jnp.float32)
    middle_part, gain_two_grad = norm_back(middle, factor_two, gains[1], normed_two_grad)
    middle_grad = grad_out[0].astype(jnp.float32) + middle_part
    branch_low = middle_grad.astype(jnp.bfloat16)
    all_branch = lax.all_gather(branch_low, "mp", axis=0, tiled=True)
    out_grad = jnp.einsum("te,td->ed", attended_low, all_branch, preferred_element_type=jnp.float32)
    attended_grad = jnp.einsum(
        "td,ed->te", all_branch, out_weight, preferred_element_type=jnp.float32
    ).astype(jnp.bfloat16)
    query_grad, key_grad, mix_grad = attend_back(
        queries,
        keys_rot,
        mixed_values,
        attended_grad.reshape(length, local_heads, HD),
        log_totals,
        seg_row,
        score_scale,
    )
    query_grad = rotate(query_grad, cosine, sine_part, False).reshape(length, -1)
    key_grad = rotate(key_grad, cosine, sine_part, False).reshape(length, -1)
    mix_grad = mix_grad.reshape(length, -1)
    values_grad = (0.5 * mix_grad)[None]
    proj_grad = jnp.stack([query_grad, key_grad, 0.5 * mix_grad]).astype(jnp.bfloat16)
    attn_grad = jnp.einsum("cte,td->cde", proj_grad, all_normed, preferred_element_type=jnp.float32)
    rows_part = proj_grad
    normed_one_grad = lax.psum_scatter(
        jnp.einsum(
            "cte,cde->td", rows_part, attn_weight, preferred_element_type=jnp.float32
        ).astype(jnp.bfloat16),
        "mp",
        scatter_dimension=0,
        tiled=True,
    ).astype(jnp.float32)
    input_part, gain_one_grad = norm_back(hidden, factor_one, gains[0], normed_one_grad)
    input_grad = (middle_grad + input_part)[None]
    attn_total, out_total, expand_total, reduce_total = (
        lax.psum_scatter(
            attn_grad.astype(jnp.bfloat16), "dp", scatter_dimension=1, tiled=True
        ).astype(jnp.float32),
        lax.psum_scatter(
            out_grad.astype(jnp.bfloat16), "dp", scatter_dimension=1, tiled=True
        ).astype(jnp.float32),
        lax.psum_scatter(
            expand_grad.astype(jnp.bfloat16), "dp", scatter_dimension=1, tiled=True
        ).astype(jnp.float32),
        lax.psum_scatter(
            reduce_grad.astype(jnp.bfloat16), "dp", scatter_dimension=1, tiled=True
        ).astype(jnp.float32),
    )
    gain_totals, square_sums = lax.psum(
        (jnp.stack([gain_one_grad, gain_two_grad]), square_terms), ("dp", "mp")
    )
    gain_width = norm_gains.shape[1]
    gain_total = lax.dynamic_slice_in_dim(
        gain_totals, lax.axis_index("dp") * gain_width, gain_width, 1
    )
    value_norms = jnp.sqrt(square_sums / (lax.axis_size("dp") * length * D))
    new_input = adamw(input_proj, attn_total, old_moment_input, old_square_input, D ** (-0.5), 0.1)
    new_output = adamw(
        output_proj,
        out_total,
        old_moment_output,
        old_square_output,
        max(1, 8 * HEADS * HD // LEN) ** (-0.5),
        0.1,
    )
    new_expand = adamw(
        expand_proj, expand_total, old_moment_expand, old_square_expand, D ** (-0.5), 0.1
    )
    new_reduce = adamw(
        reduce_proj, reduce_total, old_moment_reduce, old_square_reduce, (FF // 3) ** (-0.5), 0.1
    )
    new_gains = adamw(norm_gains, gain_total, old_moment_gains, old_square_gains, 0.2, 0.0)
    return (
        layer_output,
        input_grad,
        values_grad,
        value_norms,
        new_input[0],
        new_output[0],
        new_expand[0],
        new_reduce[0],
        new_gains[0],
        new_input[1],
        new_output[1],
        new_expand[1],
        new_reduce[1],
        new_gains[1],
        new_input[2],
        new_output[2],
        new_expand[2],
        new_reduce[2],
        new_gains[2],
    )


def tokens_dot(a, b, left, right):
    return lax.dot_general(a, b, (((left,), (right,)), ((), ())), preferred_element_type=jnp.float32)


def piece_columns(place, step):
    start = jnp.bitwise_xor(place, step) * PIECE
    return pl.ds(pl.multiple_of(start, PIECE), PIECE)


def turn(values, cosine, sine_part, forward):
    lane = lax.broadcasted_iota(jnp.int32, values.shape, 1)
    swapped = jnp.where(
        lax.rem(lane, HD) < HD // 2, pltpu.roll(values, 96, 1), pltpu.roll(values, 32, 1)
    )
    if forward:
        return values * cosine + swapped * sine_part
    return values * cosine - swapped * sine_part


MESH = pl.DeviceIdType.MESH
LOG2E = 1.4426950408889634


def flip(place, bit):
    return place + bit - 2 * bit * lax.rem(lax.div(place, bit), 2)


def at_plane(depth, values):
    found = 0
    for plane, value in enumerate(values):
        found = found + jnp.where(depth == plane, value, 0)
    return found


def slot_at(depth, way, hop):
    return at_plane(
        depth,
        [
            next((k for k, s in enumerate(SLOTS[plane]) if s[:2] == (way, hop)), 0)
            for plane in range(PLANES)
        ],
    )


def columns_of(piece, width=PIECE):
    return pl.ds(pl.multiple_of(piece * width, width), width)


class Links:
    def __init__(self, send, recv):
        self.send, self.recv, self.count, self.started, self.waited = send, recv, 0, [], []
        self.place, self.depth = lax.axis_index("dp"), lax.axis_index("mp")

    def number(self, count=1):
        self.count += count
        return self.count - count

    def copy(self, number, source, target, to):
        return pltpu.make_async_remote_copy(
            src_ref=source,
            dst_ref=target,
            send_sem=self.send.at[number],
            recv_sem=self.recv.at[number],
            device_id=to,
            device_id_type=MESH,
        )

    def go(self, number, source, target, to, when=None):
        copy = self.copy(number, source, target, to)
        self.started.append((number, source, target, to, when))
        if when is None:
            copy.start()
        else:
            pl.when(when)(copy.start)

    def got(self, number, landed, when=None):
        copy = self.copy(number, landed, landed, (flip(self.place, 1), self.depth))
        if when is None:
            copy.wait_recv()
        else:
            pl.when(when)(copy.wait_recv)

    def drain(self):
        for *parts, when in self.started:
            copy = self.copy(*parts)
            for plane in [plane for number, plane in self.waited if number == parts[0]]:
                when = when & (self.depth != plane)
            if when is None:
                copy.wait_send()
            else:
                pl.when(when)(copy.wait_send)

    def greet(self, planes=True):
        barrier = pltpu.get_barrier_semaphore()
        others = [(flip(self.place, bit), self.depth) for bit in (1, 2, 4)]
        if planes:
            others += [(self.place, lax.rem(self.depth + step, PLANES)) for step in range(1, PLANES)]
        for other in others:
            pl.semaphore_signal(barrier, inc=1, device_id=other, device_id_type=MESH)
        pl.semaphore_wait(barrier, len(others))


class Spread:
    def __init__(self, links, own, spot, bits):
        self.links, self.own = links, own
        self.base = links.number(7)
        place = links.place
        first, second = flip(place, bits[0]), flip(place, bits[1])
        self.spots = [spot(piece) for piece in (place, first, second, flip(first, bits[1]))]
        self.lands = [
            spot(flip(piece, 1)) for piece in (place, first, second, flip(first, bits[1]))
        ]
        self.near, self.far, self.core = [
            (flip(place, bit), links.depth) for bit in (bits[0], bits[1], 1)
        ]

    def one(self):
        self.links.go(self.base, self.own, self.spots[0], self.near)

    def two(self):
        links, spots = self.links, self.spots
        links.go(self.base + 1, self.own, spots[0], self.far)
        links.got(self.base, spots[1])
        links.go(self.base + 2, spots[1], spots[1], self.far)

    def three(self):
        links, spots = self.links, self.spots
        links.go(self.base + 3, self.own, spots[0], self.core)
        links.go(self.base + 4, spots[1], spots[1], self.core)
        links.got(self.base + 1, spots[2])
        links.go(self.base + 5, spots[2], spots[2], self.core)
        links.got(self.base + 2, spots[3])
        links.go(self.base + 6, spots[3], spots[3], self.core)

    def end(self):
        for index, land in enumerate(self.lands):
            self.links.got(self.base + 3 + index, land)


class Halves:
    def __init__(self, parts):
        self.parts = parts

    def one(self):
        for part in self.parts:
            part.one()

    def two(self, *given):
        for index, part in enumerate(self.parts):
            part.two(*[one[index] for one in given])

    def three(self):
        for part in self.parts:
            part.three()

    def end(self):
        for part in self.parts:
            part.end()


def half_of(ref, half):
    rows = ref.shape[-2] // 2
    lead = (slice(None),) * (len(ref.shape) - 2)
    return ref.at[(*lead, pl.ds(half * rows, rows), slice(None))]


def halved_spread(links, own, spot):
    return Halves(
        [
            Spread(
                links,
                half_of(own, half),
                lambda piece, half=half: half_of(spot(piece), half),
                ((2, 4), (4, 2))[half],
            )
            for half in range(2)
        ]
    )


class Relay:
    def __init__(self, links, own, put):
        self.links, self.own, self.put = links, own, put
        self.base = links.number(2 * (PLANES - 1))
        self.waited = links.waited

    def send(self, hop, only=None):
        links, depth = self.links, self.links.depth
        for way in range(2):
            to = depth + (1 if way else -1)
            when = (
                (depth >= hop - 1) & (depth < PLANES - 1)
                if way
                else (depth <= PLANES - hop) & (depth > 0)
            )
            if only is not None:
                when = when & (depth == only[way])
            source = self.own if hop == 1 else self.put(depth, way, hop - 1)
            links.go(
                self.base + 2 * (hop - 1) + way,
                source,
                self.put(to, way, hop),
                (links.place, jnp.clip(to, 0, PLANES - 1)),
                when,
            )

    def take(self, hop, only=None):
        links, depth = self.links, self.links.depth
        for way in range(2):
            when = depth >= hop if way else depth + hop < PLANES
            if only is not None:
                when = when & (depth == only[way])
            links.got(self.base + 2 * (hop - 1) + way, self.put(depth, way, hop), when)

    def left(self, hop, only):
        links, depth = self.links, self.links.depth
        for way in range(2):
            source = self.own if hop == 1 else self.put(depth, way, hop - 1)
            to = (links.place, jnp.clip(depth + (1 if way else -1), 0, PLANES - 1))
            copy = links.copy(self.base + 2 * (hop - 1) + way, source, source, to)
            pl.when(depth == only[way])(copy.wait_send)
            self.waited.append((self.base + 2 * (hop - 1) + way, only[way]))


def position_tables(length):
    rates = 10000.0 ** (-2.0 * np.arange(HD // 2) / HD)
    angles = np.arange(length)[:, None] * rates[None, :]
    cosine, sine = np.cos(angles), np.sin(angles)
    return (
        jnp.asarray(np.concatenate([cosine] * 4, axis=1), jnp.float32),
        jnp.asarray(np.concatenate([-sine, sine, -sine, sine], axis=1), jnp.float32),
    )


def rope_tables_from(seg_ref, cos_at, sin_at, cos_ref, sin_ref, begin_ref, marks):
    length = cos_at.shape[0]
    segs = seg_ref[0:1, :].astype(jnp.float32)
    spots = lax.broadcasted_iota(jnp.int32, (1, length), 1).astype(jnp.float32)
    begins = jnp.zeros((1, length), jnp.float32)
    marks[...] = jnp.zeros_like(marks)
    for number in range(7):
        start = jnp.sum(jnp.where(segs < number, 1.0, 0.0), axis=1, keepdims=True)
        begins = jnp.where(segs == number, start, begins)
        marks[number : number + 1, :] = jnp.where(spots == start, 1.0, 0.0)
    begin_ref[...] = jnp.broadcast_to(begins.astype(jnp.int32), begin_ref.shape)
    pick = lambda table: lax.dot_general(
        marks[...],
        table[...],
        (((1,), (0,)), ((), ())),
        precision=lax.Precision.HIGHEST,
        preferred_element_type=jnp.float32,
    )
    first_cos, first_sin = pick(cos_at), pick(sin_at)
    rows = length // PLANES
    for block in range(PLANES):
        span = pl.ds(block * rows, rows)
        documents = jnp.transpose(
            jnp.broadcast_to(segs[:, block * rows : block * rows + rows], (128, rows))
        )
        cosine = jnp.zeros((rows, 128), jnp.float32)
        sine = jnp.zeros((rows, 128), jnp.float32)
        for number in range(7):
            here = documents == number
            cosine = jnp.where(here, first_cos[number : number + 1], cosine)
            sine = jnp.where(here, first_sin[number : number + 1], sine)
        cos_ref[span, :] = cos_at[span, :] * cosine + sin_at[span, :] * sine
        sin_ref[span, :] = sin_at[span, :] * cosine - cos_at[span, :] * sine


def open_kernel(*refs):
    hidden, attn_piece, out_piece, feed_piece, cos_at, sin_at, first_ref, seg_ref = refs[:8]
    q_out, k_out, v_out, o_out, n_out, weight_out, out_weight_out, feed_all, cos_out, sin_out = refs[8:18]
    gain_ref, square_ref, log_ref, middle_ref, normed_ref, attended_ref, begin_ref = refs[18:25]
    held, q_ref, k_ref, v_ref, o_ref, n_ref, weight_ref, out_ref, cos_ref, sin_ref, turned_v, marks = refs[25:37]
    send, recv, local = refs[37:]
    links = Links(send, recv)
    place, depth = links.place, links.depth
    shard = hidden.shape[0]
    stores = []

    def store(source, target):
        copy = pltpu.make_async_copy(source, target, local.at[len(stores)])
        copy.start()
        stores.append(copy)
        return copy

    block_at = lambda plane, way, hop: jnp.clip(plane + (-hop if way else hop), 0, PLANES - 1)
    wide = Relay(links, hidden, lambda plane, way, hop: held.at[block_at(plane, way, hop)])
    out_rows = lambda block: out_ref.at[
        pl.ds(pl.multiple_of(block * 256, 256), 256), columns_of(place)
    ]
    thin = Relay(links, out_piece, lambda plane, way, hop: out_rows(block_at(plane, way, hop)))
    feeds = Relay(
        links,
        feed_piece,
        lambda plane, way, hop: feed_all.at[slot_at(plane, way, hop), place],
    )
    attn = Spread(links, attn_piece, lambda piece: weight_ref.at[:, columns_of(piece)], (2, 4))
    outs = Spread(
        links, out_ref.at[:, columns_of(place)], lambda piece: out_ref.at[:, columns_of(piece)], (2, 4)
    )
    slots = [
        halved_spread(
            links,
            feed_piece if slot == 0 else feed_all.at[slot, place],
            lambda piece, slot=slot: feed_all.at[slot, piece],
        )
        for slot in range(PLANES - 1)
    ]
    across = links.number(PLANES)

    links.greet()
    thin.send(1)
    wide.send(1)
    attn.one()
    own_hidden = store(hidden, held.at[depth])
    own_attn = store(attn_piece, weight_ref.at[:, columns_of(place)])
    own_out = store(out_piece, out_rows(depth))
    own_feed = store(feed_piece, feed_all.at[0, place])
    square_ref[...] = jnp.zeros_like(square_ref)
    attn.two()
    attn.three()
    slots[0].one()
    rope_tables_from(seg_ref, cos_at, sin_at, cos_ref, sin_ref, begin_ref, marks)
    attn.end()
    for copy in (own_hidden, own_attn, own_out, own_feed):
        copy.wait()
    store(weight_ref, weight_out)
    store(cos_ref, cos_out)
    store(sin_ref, sin_out)
    gain_ref[...] = weight_ref[pl.ds(768, 16), :].astype(jnp.float32)

    def project(block):
        rows = pl.ds(pl.multiple_of(block * shard, shard), shard)
        values = held[block].astype(jnp.float32)
        factor = lax.rsqrt(jnp.mean(values * values, axis=-1, keepdims=True) + 1e-06)
        normed = (values * factor * gain_ref[0:1, :]).astype(jnp.bfloat16)
        n_ref[rows, :] = normed
        cosine, sine_part = cos_ref[rows, :], sin_ref[rows, :]
        query = tokens_dot(normed, weight_ref[pl.ds(0, 256), :], 1, 1)
        key = tokens_dot(normed, weight_ref[pl.ds(256, 256), :], 1, 1)
        value = tokens_dot(normed, weight_ref[pl.ds(512, 256), :], 1, 1)
        for half in range(2):
            lanes = slice(half * 128, half * 128 + 128)
            turned = turn(query[:, lanes], cosine, sine_part, True)
            q_ref[rows, lanes] = (turned * (HD**-0.5 * LOG2E)).astype(jnp.bfloat16)
            k_ref[rows, lanes] = turn(key[:, lanes], cosine, sine_part, True).astype(jnp.bfloat16)
        first = first_ref[rows, :].astype(jnp.float32)
        blended = 0.5 * value + 0.5 * first
        v_ref[rows, :] = blended.astype(jnp.bfloat16)
        for half in range(2):
            turned_v[half, :, rows] = jnp.transpose(
                blended[:, half * 128 : half * 128 + 128]
            ).astype(jnp.bfloat16)
        square_ref[0:1, :] += jnp.sum(first * first, axis=0, keepdims=True)
        square_ref[1:2, :] += jnp.sum(blended * blended, axis=0, keepdims=True)

    def project_hop(hop):
        def one(side, carried):
            block = depth + hop * (2 * side - 1)
            pl.when((block >= 0) & (block < PLANES))(lambda: project(block))
            return carried

        lax.fori_loop(0, 2, one, 0)

    ends, inner = (PLANES - 1, 0), (PLANES - 2, 1)
    project(depth)
    wide.take(1)
    wide.send(2)
    feeds.send(1, ends)
    thin.take(1)
    thin.send(2)
    slots[0].two()
    project_hop(1)
    wide.take(2)
    wide.send(3)
    feeds.take(1, inner)
    feeds.send(1, inner)
    feeds.send(2, inner)
    thin.take(2)
    thin.send(3)
    project_hop(2)
    slots[0].three()
    wide.take(3)
    wide.left(3, (1, PLANES - 2))
    feeds.take(1, (1, PLANES - 2))
    feeds.take(2, (1, PLANES - 2))
    feeds.send(1, (1, PLANES - 2))
    feeds.send(2, (1, PLANES - 2))
    thin.take(3)
    outs.one()
    project_hop(3)
    store(n_ref, n_out)
    store(q_ref, q_out)
    store(k_ref, k_out)
    store(v_ref, v_out)

    lane = lax.broadcasted_iota(jnp.int32, (shard, 128), 1)
    down = lax.broadcasted_iota(jnp.int32, (shard, shard), 0)
    along = lax.broadcasted_iota(jnp.int32, (1, shard), 1)

    def flash_block(block):
        rows = pl.ds(pl.multiple_of(block * shard, shard), shard)
        begin = begin_ref[0:1, rows]
        pairs = [q_ref[rows, pl.ds(pair * 128, 128)] for pair in range(2)]
        parts = [
            jnp.where((lane < HD) == (head % 2 == 0), pairs[head // 2], jnp.zeros_like(pairs[0]))
            for head in range(4)
        ]

        def tile(index, carried, visible):
            span = pl.ds(pl.multiple_of(index * shard, shard), shard)
            raw = [
                tokens_dot(k_ref[span, pl.ds(head // 2 * 128, 128)], parts[head], 1, 1)
                for head in range(4)
            ]
            after = []
            for head in range(4):
                top, total, summed = carried[3 * head : 3 * head + 3]
                scores = jnp.where(visible, raw[head], -1e30)
                raised_top = jnp.maximum(top, jnp.max(scores, axis=0, keepdims=True))
                shrink = jnp.exp2(top - raised_top)
                shares = jnp.exp2(scores - raised_top)
                total = total * shrink + jnp.sum(shares, axis=0, keepdims=True)
                values = turned_v[head // 2, pl.ds(head % 2 * HD, HD), span]
                summed = summed * shrink + tokens_dot(values, shares.astype(jnp.bfloat16), 1, 0)
                after += [raised_top, total, summed]
            return tuple(after)

        fresh = (
            jnp.full((1, shard), -1e30, jnp.float32),
            jnp.zeros((1, shard), jnp.float32),
            jnp.zeros((HD, shard), jnp.float32),
        )
        carried = tile(block, fresh * 4, (down >= begin - block * shard) & (down <= along))
        carried = lax.fori_loop(
            0, block, lambda j, held: tile(j, held, down >= begin - j * shard), carried
        )
        for pair in range(2):
            ends = [carried[3 * (2 * pair + head) : 3 * (2 * pair + head) + 3] for head in range(2)]
            both = jnp.concatenate([summed / total for _, total, summed in ends], axis=0)
            o_ref[rows, pl.ds(pair * 128, 128)] = jnp.transpose(both).astype(jnp.bfloat16)
            for head, (top, total, _) in enumerate(ends):
                log_ref[pair, head : head + 1, rows] = top + jnp.log2(total)

    own_columns = attended_ref.at[:, columns_of(depth, 256)]

    def hand(step):
        block = lax.rem(depth + step, PLANES)
        rows = pl.ds(pl.multiple_of(block * shard, shard), shard)
        return links.copy(across + step, o_ref.at[rows, :], own_columns, (place, block))

    near = (0, PLANES - 1)

    def pump_a():
        feeds.take(1, near)
        slots[1].one()
        outs.two()

    def pump_b():
        slots[1].two()
        slots[0].end()

    def pump_c():
        feeds.take(2, near)
        slots[2].one()
        outs.three()

    pumps = ((0, pump_a), (1, pump_b), (2, pump_c))

    def flash(index, carried):
        step = PLANES - 1 - index
        flash_block(lax.rem(depth + step, PLANES))
        pl.when(step > 0)(lambda: hand(step).start())
        for when, pump in pumps:
            pl.when(index == when)(pump)
        return carried

    lax.fori_loop(0, PLANES, flash, 0)
    feeds.send(3, (1, PLANES - 2))
    own_rows = pl.ds(pl.multiple_of(depth * shard, shard), shard)
    attended_ref[:, columns_of(depth, 256)] = o_ref[own_rows, :]
    store(o_ref, o_out)
    outs.end()
    store(out_ref, out_weight_out)
    slots[1].three()
    slots[2].two()
    for step in range(1, PLANES):
        source = lax.rem(depth - step + PLANES, PLANES)
        links.got(across + step, attended_ref.at[:, columns_of(source, 256)])
    half = shard // 2
    for part in range(2):
        rows = pl.ds(part * half, half)
        middle = held[depth, rows, :].astype(jnp.float32) + tokens_dot(
            attended_ref[rows, :], out_ref[...], 1, 0
        )
        middle_ref[rows, :] = middle
        factor = lax.rsqrt(jnp.mean(middle * middle, axis=-1, keepdims=True) + 1e-06)
        normed_ref[rows, :] = (middle * factor * gain_ref[1:2, :]).astype(jnp.bfloat16)
    slots[2].three()
    slots[1].end()
    feeds.take(3)
    slots[2].end()
    for step in range(1, PLANES):
        hand(step).wait_send()
    links.drain()
    for copy in stores[4:]:
        copy.wait()


def opening(hidden, attn_piece, out_piece, feed_piece, first_values, seg_row):
    length, width = first_values.shape
    rows = hidden.shape[0]
    count = feed_piece.shape[0]
    low, full = jnp.bfloat16, jnp.float32
    any_spec, vmem = pl.BlockSpec(memory_space=pl.ANY), pl.BlockSpec(memory_space=pltpu.VMEM)
    shape = jax.ShapeDtypeStruct
    cos_at, sin_at = position_tables(length)
    return pl.pallas_call(
        open_kernel,
        in_specs=[any_spec] * 4 + [vmem] * 4,
        out_specs=[any_spec] * 10 + [vmem] * 7,
        out_shape=[
            shape((length, width), low),
            shape((length, width), low),
            shape((length, width), low),
            shape((length, width), low),
            shape((length, D), low),
            shape((ATTN_ROWS, D), low),
            shape((D, D), low),
            shape((PLANES, 8, count, PIECE), low),
            shape((length, 128), full),
            shape((length, 128), full),
            shape((16, D), full),
            shape((8, width), full),
            shape((width // 128, 8, length), full),
            shape((rows, D), full),
            shape((rows, D), low),
            shape((rows, D), low),
            shape((8, length), jnp.int32),
        ],
        scratch_shapes=[
            pltpu.VMEM((PLANES, rows, D), low),
            pltpu.VMEM((length, width), low),
            pltpu.VMEM((length, width), low),
            pltpu.VMEM((length, width), low),
            pltpu.VMEM((length, width), low),
            pltpu.VMEM((length, D), low),
            pltpu.VMEM((ATTN_ROWS, D), low),
            pltpu.VMEM((D, D), low),
            pltpu.VMEM((length, 128), full),
            pltpu.VMEM((length, 128), full),
            pltpu.VMEM((width // 128, 128, length), low),
            pltpu.VMEM((8, length), full),
            pltpu.SemaphoreType.DMA((OPEN_COPIES,)),
            pltpu.SemaphoreType.DMA((OPEN_COPIES,)),
            pltpu.SemaphoreType.DMA((14,)),
        ],
        compiler_params=pltpu.CompilerParams(
            vmem_limit_bytes=VMEM_LIMIT, collective_id=1, has_side_effects=True
        ),
        name="opening",
    )(hidden, attn_piece, out_piece, feed_piece, cos_at, sin_at, first_values, seg_row)


def feed_kernel(*refs):
    normed_ref, grad_ref, middle_ref, pieces = refs[:4]
    back_ref, out_ref, made_out = refs[4:7]
    fed, weight, mine, theirs, made, halves, other_halves, send, recv, sem, out_sem, last_sem = refs[7:]
    links = Links(send, recv)
    place = links.place
    core = (flip(links.place, 1), links.depth)
    mine_first, theirs_first = lax.rem(links.place, 2), 1 - lax.rem(links.place, 2)
    count = weight.shape[1] // 3
    rows = normed_ref.shape[0]

    def load(which, buffer):
        return [
            pltpu.make_async_copy(
                pieces.at[which, piece],
                weight.at[buffer, :, pl.ds(piece * PIECE, PIECE)],
                sem.at[buffer, piece],
            )
            for piece in range(8)
        ]

    def flush(which, buffer):
        return [
            pltpu.make_async_copy(
                made.at[buffer, :, pl.ds(piece * PIECE, PIECE)],
                made_out.at[which, piece],
                out_sem.at[buffer, piece],
            )
            for piece in range(4)
        ]

    for copy in load(0, 0):
        copy.start()
    far = pieces.at[PLANES - 1, place]
    last = halved_spread(links, far, lambda piece: weight.at[2, :, columns_of(piece)])
    last_own = pltpu.make_async_copy(far, weight.at[2, :, columns_of(place)], last_sem)
    last_own.start()
    links.greet(planes=False)
    last.one()
    base = links.number(8)
    for index, ref in enumerate((normed_ref, grad_ref)):
        for piece in range(4):
            links.go(
                base + 4 * index + piece,
                ref.at[:, columns_of(2 * piece + theirs_first)],
                other_halves.at[index, :, pl.ds(piece * PIECE, PIECE)],
                core,
            )
            halves[index, :, pl.ds(piece * PIECE, PIECE)] = ref[:, columns_of(2 * piece + mine_first)]
    fed[...] = jnp.zeros_like(fed)
    back_ref[...] = jnp.zeros_like(back_ref)
    for index in range(2):
        for piece in range(4):
            links.got(
                base + 4 * index + piece, other_halves.at[index, :, pl.ds(piece * PIECE, PIECE)]
            )
    given = links.number(PLANES)
    hand = lambda slot: links.copy(given + slot, mine.at[lax.rem(slot, 2)], theirs.at[slot], core)
    spans = [pl.ds(index * count, count) for index in range(3)]
    half = rows // 2

    def forward(slot):
        now = lax.rem(slot, 2)
        held = jnp.where(slot == PLANES - 1, 2, now)

        @pl.when(slot < PLANES - 1)
        def _():
            for copy in load(slot, now):
                copy.wait()

        @pl.when(slot + 2 < PLANES)
        def _():
            for copy in load(slot + 1, 1 - now):
                copy.start()

        @pl.when(slot == PLANES - 1)
        def _():
            last_own.wait()
            last.end()

        @pl.when(slot >= 2)
        def _():
            hand(slot - 2).wait_send()

        for tile in range(2):
            at = pl.ds(tile * half, half)
            normed, grad = normed_ref[at, :], grad_ref[at, :]
            gates = tokens_dot(weight[held, spans[0], :], normed, 1, 1)
            ups = tokens_dot(weight[held, spans[1], :], normed, 1, 1)
            backs = tokens_dot(weight[held, spans[2], :], grad, 1, 1)
            sig = jax.nn.sigmoid(gates)
            active = gates * sig
            mine[now, 2, :, at] = (active * ups).astype(jnp.bfloat16)
            mine[now, 0, :, at] = (backs * ups * sig * (1.0 + gates * (1.0 - sig))).astype(jnp.bfloat16)
            mine[now, 1, :, at] = (backs * active).astype(jnp.bfloat16)
        hand(slot).start()

        fed[...] += tokens_dot(mine[now, 2], weight[held, spans[2], :], 0, 0)
        back_ref[...] += tokens_dot(mine[now, 0], weight[held, spans[0], :], 0, 0) + tokens_dot(
            mine[now, 1], weight[held, spans[1], :], 0, 0
        )

    def backward(slot):
        now = lax.rem(slot, 2)
        hand(slot).wait_recv()

        @pl.when(slot >= 2)
        def _():
            for copy in flush(slot - 2, now):
                copy.wait()

        def columns(tile, carried):
            lanes = columns_of(tile, 256)
            for index in range(3):
                which = index // 2
                made[now, spans[index], lanes] = (
                    tokens_dot(mine[now, index], halves[which, :, lanes], 1, 0)
                    + tokens_dot(theirs[slot, index], other_halves[which, :, lanes], 1, 0)
                ).astype(jnp.bfloat16)
            return carried

        lax.fori_loop(0, 2, columns, 0)
        for copy in flush(slot, now):
            copy.start()

    def one(step, carried):
        pl.when(step < PLANES)(lambda: forward(step))
        pl.when(step == 0)(last.two)
        pl.when(step == 2)(last.three)
        pl.when(step >= 1)(lambda: backward(step - 1))
        return carried

    lax.fori_loop(0, PLANES + 1, one, 0)
    out_ref[...] = (middle_ref[...] + fed[...]).astype(jnp.bfloat16)
    for slot in (PLANES - 2, PLANES - 1):
        hand(slot).wait_send()
        for copy in flush(slot, slot % 2):
            copy.wait()
    links.drain()


def feed(normed, grad, middle, pieces):
    rows = normed.shape[0]
    count = pieces.shape[2]
    any_spec, vmem = pl.BlockSpec(memory_space=pl.ANY), pl.BlockSpec(memory_space=pltpu.VMEM)
    low = jnp.bfloat16
    return pl.pallas_call(
        feed_kernel,
        in_specs=[vmem, vmem, vmem, any_spec],
        out_specs=[vmem, vmem, any_spec],
        out_shape=[
            jax.ShapeDtypeStruct((rows, D), jnp.float32),
            jax.ShapeDtypeStruct((rows, D), low),
            jax.ShapeDtypeStruct((PLANES, 4, count, PIECE), low),
        ],
        scratch_shapes=[
            pltpu.VMEM((rows, D), jnp.float32),
            pltpu.VMEM((3, count, D), low),
            pltpu.VMEM((2, 3, count // 3, rows), low),
            pltpu.VMEM((PLANES, 3, count // 3, rows), low),
            pltpu.VMEM((2, count, 4 * PIECE), low),
            pltpu.VMEM((2, rows, 4 * PIECE), low),
            pltpu.VMEM((2, rows, 4 * PIECE), low),
            pltpu.SemaphoreType.DMA((26,)),
            pltpu.SemaphoreType.DMA((26,)),
            pltpu.SemaphoreType.DMA((2, 8)),
            pltpu.SemaphoreType.DMA((2, 4)),
            pltpu.SemaphoreType.DMA,
        ],
        compiler_params=pltpu.CompilerParams(
            vmem_limit_bytes=VMEM_LIMIT, collective_id=2, has_side_effects=True
        ),
        name="feed",
    )(normed, grad, middle, pieces)


def add_into(target, source):
    rows = target.shape[0]
    chunk = next(c for c in (352, 256, rows) if rows % c == 0 and c <= rows)

    def one(index, carried):
        span = pl.ds(pl.multiple_of(index * chunk, chunk), chunk)
        target[span, :] = (
            target[span, :].astype(jnp.float32) + source[span, :].astype(jnp.float32)
        ).astype(jnp.bfloat16)
        return carried

    lax.fori_loop(0, rows // chunk, one, 0)


class Fold:
    def __init__(self, links, whole, first, final, bits):
        self.links, self.first, self.final = links, [first.at[m] for m in range(2)], final
        self.base = links.number(3)
        chip = lax.div(links.place, 2)
        ones = lambda bit: lax.rem(lax.div(chip, bit), 2)
        near, far = ones(bits[0]), ones(bits[1])
        self.away = [whole((1 - near) * bits[0] + m * bits[1]) for m in range(2)]
        self.stay = [whole(near * bits[0] + m * bits[1]) for m in range(2)]
        self.near_to = (flip(links.place, 2 * bits[0]), links.depth)
        self.far_to = (flip(links.place, 2 * bits[1]), links.depth)
        self.passed, self.own = first.at[1 - far], first.at[far]

    def one(self):
        for m in range(2):
            self.links.go(self.base + m, self.away[m], self.first[m], self.near_to)

    def two(self, stay=None):
        for m in range(2):
            self.links.got(self.base + m, self.first[m])
            add_into(self.first[m], self.stay[m] if stay is None else stay[m])
        self.links.go(self.base + 2, self.passed, self.final, self.far_to)

    def end(self):
        self.links.got(self.base + 2, self.final)
        add_into(self.final, self.own)


class LineFold:
    def __init__(self, links, block, held):
        self.links = links
        self.held = [[held.at[way, step] for step in range(PLANES - 1)] for way in range(2)]
        self.base = links.number(2 * (PLANES - 1))
        depth = links.depth
        self.blocks, self.sends, self.sums, self.takes, self.to = [], [], [], [], []
        for step in range(1, PLANES):
            right = jnp.minimum(depth + PLANES - step, PLANES - 1)
            left = jnp.maximum(depth - PLANES + step, 0)
            self.blocks.append((block(left), block(right)))
            self.sends.append((depth >= PLANES - step, depth < step))
            self.takes.append(((depth >= PLANES - 1 - step) & (depth < PLANES - 1), (depth <= step) & (depth > 0)))
        self.ends = (depth == PLANES - 1, depth == 0)
        self.to = (
            (links.place, jnp.maximum(depth - 1, 0)),
            (links.place, jnp.minimum(depth + 1, PLANES - 1)),
        )
        self.inner = [
            [self.sends[step][way] & jnp.logical_not(self.ends[way]) for way in range(2)]
            for step in range(PLANES - 1)
        ]
        self.outer = [
            [self.sends[step][way] & self.ends[way] for way in range(2)] for step in range(PLANES - 1)
        ]

    def launch(self, step):
        for way in range(2):
            self.links.go(
                self.base + 2 * (step - 1) + way,
                self.blocks[step - 1][way],
                self.held[way][step - 1],
                self.to[way],
                self.outer[step - 1][way],
            )

    def take(self, step):
        for way in range(2):
            self.links.got(
                self.base + 2 * (step - 1) + way, self.held[way][step - 1], self.takes[step - 1][way]
            )

    def forward(self, step):
        for way in range(2):
            before = self.held[way][step - 2]
            block = self.blocks[step - 1][way]

            @pl.when(self.inner[step - 1][way])
            def _():
                add_into(before, block)

            self.links.go(
                self.base + 2 * (step - 1) + way,
                before,
                self.held[way][step - 1],
                self.to[way],
                self.inner[step - 1][way],
            )

    def total(self, own, out):
        depth = self.links.depth
        rows = out.shape[0]
        chunk = next(c for c in (352, 256, rows) if rows % c == 0)

        def one(index, carried):
            span = pl.ds(pl.multiple_of(index * chunk, chunk), chunk)
            value = own[span, :].astype(jnp.float32)
            sides = [self.held[way][PLANES - 2][span, :].astype(jnp.float32) for way in range(2)]
            value = value + jnp.where(depth < PLANES - 1, sides[0], 0.0)
            out[span, :] = value + jnp.where(depth > 0, sides[1], 0.0)
            return carried

        lax.fori_loop(0, rows // chunk, one, 0)


def close_kernel(*refs):
    (made, low_in, attended_in, q_in, k_in, v_in, o_in, n_in, weight_in, cos_in, sin_in) = refs[:11]
    incoming = refs[11:15]
    log_ref, begin_ref, gain_ref, small_in = refs[15:19]
    first_ref, back_ref, feed_total, out_total, attn_total, small_ref = refs[19:25]
    (
        q_ref, k_ref, v_ref, o_ref, weight_ref, cos_ref, sin_ref, grad, inner, total, made_ref,
        stay, feed_first, feed_final, feed_held, out_made, out_core, out_first, out_final, out_held,
        attn_core, attn_first, attn_final, partial, partial_held, small_got,
        send, recv, local,
    ) = refs[25:]
    links = Links(send, recv)
    place, depth = links.place, links.depth
    length = q_ref.shape[0]
    shard = length // PLANES
    parity, chip = lax.rem(place, 2), lax.div(place, 2)
    core = (flip(place, 1), depth)
    loads = []

    def load(source, target):
        copy = pltpu.make_async_copy(source, target, local.at[len(loads)])
        copy.start()
        loads.append(copy)
        return copy

    order = (3, 2, 1, 0)

    def halved_fold(whole, first, final):
        return Halves(
            [
                Fold(
                    links,
                    lambda i, half=half: half_of(whole(i), half),
                    half_of(first, half),
                    half_of(final, half),
                    ((1, 2), (2, 1))[half],
                )
                for half in range(2)
            ]
        )

    folds = {
        slot: halved_fold(
            lambda i, slot=slot: made.at[slot, i], feed_first.at[slot], feed_final.at[slot]
        )
        for slot in order
    }
    out_fold = halved_fold(lambda i: out_core.at[i], out_first, out_final)
    attn_fold = halved_fold(lambda i: attn_core.at[i], attn_first, attn_final)

    def slot_holding(block):
        found = 0
        for plane in range(PLANES):
            for slot, (_, _, held) in enumerate(SLOTS[plane]):
                found = found + jnp.where((depth == plane) & (block == held), slot, 0)
        return found

    feed_line = LineFold(links, lambda j: feed_final.at[slot_holding(j)], feed_held)
    out_line = LineFold(
        links, lambda j: out_final.at[pl.ds(pl.multiple_of(j * 256, 256), 256), :], out_held
    )
    line = LineFold(links, lambda j: partial.at[j], partial_held)
    out_swap, attn_swap = links.number(4), links.number(4)
    sides = [columns_of(2 * i + parity) for i in range(4)]
    others = [columns_of(2 * i + 1 - parity) for i in range(4)]
    across = links.number(2 * PLANES)
    tiny = links.number(6)
    stays = [
        [[half_of(stay.at[index, m], half) for m in range(2)] for half in range(2)] for index in range(2)
    ]
    stay_sems = [[[16 + 4 * index + 2 * half + m for m in range(2)] for half in range(2)] for index in range(2)]

    def restay(slot):
        return [
            pltpu.make_async_copy(
                folds[slot].parts[half].stay[m],
                stays[slot % 2][half][m],
                local.at[stay_sems[slot % 2][half][m]],
            )
            for half in range(2)
            for m in range(2)
        ]

    tiny_to = [core, (flip(place, 2), depth), (flip(place, 4), depth)]
    plane_to = [(place, lax.rem(depth + step, PLANES)) for step in range(1, PLANES)]
    plane_rows = [lax.rem(depth - step + PLANES, PLANES) for step in range(PLANES)]

    attended_ref, low_ref = partial.at[0], partial.at[1]
    first_loads = [load(attended_in, attended_ref), load(low_in, low_ref)]
    for slot in order[:2]:
        for copy in restay(slot):
            copy.start()
    q_loads = [load(source, target) for source, target in ((q_in, q_ref), (k_in, k_ref), (v_in, v_ref), (o_in, o_ref), (cos_in, cos_ref), (sin_in, sin_ref))]
    own_rows = pl.ds(pl.multiple_of(depth * shard, shard), shard)
    q_loads.append(load(incoming[0], grad.at[own_rows, :]))
    weight_load = load(weight_in, weight_ref)

    links.greet()
    for pair in range(2):
        lanes = pl.ds(pair * 128, 128)
        for step in range(1, PLANES):
            links.go(
                across + 4 * pair + step,
                incoming[step].at[:, lanes],
                grad.at[own_rows, lanes],
                plane_to[step - 1],
            )
    folds[3].one()

    for copy in first_loads:
        copy.wait()
    for index in range(4):
        rows = pl.ds(index * 256, 256)
        out_made[rows, :] = tokens_dot(attended_ref[:, rows], low_ref[...], 0, 0).astype(jnp.bfloat16)
    out_swaps = [links.copy(out_swap + i, out_made.at[:, others[i]], out_core.at[i], core) for i in range(4)]
    for copy in out_swaps:
        copy.start()
    for i in range(4):
        links.got(out_swap + i, out_core.at[i])
        add_into(out_core.at[i], out_made.at[:, sides[i]])
    for copy in q_loads:
        copy.wait()

    def fold_two(slot):
        for copy in restay(slot):
            copy.wait()
        folds[slot].two(stays[slot % 2])

    fold_two(3)
    folds[2].one()
    grad_rows = [
        [
            grad.at[pl.ds(pl.multiple_of(plane_rows[step] * shard, shard), shard), pl.ds(pair * 128, 128)]
            for step in range(PLANES)
        ]
        for pair in range(2)
    ]

    def take_grads(pair):
        for step in range(1, PLANES):
            links.got(across + 4 * pair + step, grad_rows[pair][step])

    take_grads(0)

    lane = lax.broadcasted_iota(jnp.int32, (shard, 128), 1)
    keeps = [lane < HD, lane >= HD]
    down = lax.broadcasted_iota(jnp.int32, (shard, shard), 0)
    along = lax.broadcasted_iota(jnp.int32, (1, shard), 1)

    def masked(values, head):
        return jnp.where(keeps[head], values, jnp.zeros_like(values))

    def after_a():
        folds[3].end()
        feed_line.launch(1)
        out_fold.one()

    def after_b():
        fold_two(2)
        folds[1].one()
        for copy in restay(1):
            copy.start()

    def after_c():
        folds[2].end()
        feed_line.launch(2)
        feed_line.take(1)
        feed_line.forward(2)
        out_fold.two()
        take_grads(1)

    def after_d():
        fold_two(1)
        folds[0].one()
        for copy in restay(0):
            copy.start()
        out_fold.end()

    def after_e():
        folds[1].end()
        feed_line.launch(3)
        feed_line.take(2)
        feed_line.forward(3)
        for step in range(1, PLANES):
            out_line.launch(step)

    def back_step(step, carried):
        pair, block = lax.div(step, PLANES), lax.rem(step, PLANES)
        lanes = columns_of(pair)
        start = pl.multiple_of(block * shard, shard)
        own = pl.ds(start, shard)

        @pl.when(block == 0)
        def _():
            total[...] = jnp.zeros_like(total)
            for index in range(PLANES):
                span = pl.ds(index * shard, shard)
                turned = jnp.transpose(
                    grad[span, lanes].astype(jnp.float32) * o_ref[span, lanes].astype(jnp.float32)
                )
                for head in range(2):
                    inner[head : head + 1, span] = jnp.sum(
                        turned[head * HD : head * HD + HD], axis=0, keepdims=True
                    )

        keys, values = k_ref[own, lanes], v_ref[own, lanes]
        own_keys = [masked(keys, head) for head in range(2)]

        def tile(index, sums, visible):
            key_sum, value_sum = sums
            span = pl.ds(pl.multiple_of(index * shard, shard), shard)
            query_block, grad_block = q_ref[span, lanes], grad[span, lanes]
            queries = [masked(query_block, head) for head in range(2)]
            out_grads = [masked(grad_block, head) for head in range(2)]
            scores = [tokens_dot(keys, queries[head], 1, 1) for head in range(2)]
            share_grads = [tokens_dot(values, out_grads[head], 1, 1) for head in range(2)]
            score_grads = []
            for head in range(2):
                shares = jnp.where(
                    visible, jnp.exp2(scores[head] - log_ref[pair, head : head + 1, span]), 0.0
                )
                score_grads.append(
                    (shares * (share_grads[head] - inner[head : head + 1, span])).astype(jnp.bfloat16)
                )
                value_sum = value_sum + tokens_dot(shares.astype(jnp.bfloat16), out_grads[head], 1, 0)
            for head in range(2):
                key_sum = key_sum + tokens_dot(score_grads[head], queries[head], 1, 0)
            total[span, :] += tokens_dot(score_grads[0], own_keys[0], 0, 0) + tokens_dot(
                score_grads[1], own_keys[1], 0, 0
            )
            return (key_sum, value_sum)

        empty = jnp.zeros((shard, 128), jnp.float32)
        sums = tile(
            block, (empty, empty), (down >= begin_ref[0:1, own] - start) & (down <= along)
        )
        key_sum, value_sum = lax.fori_loop(
            block + 1,
            PLANES,
            lambda i, held: tile(
                i,
                held,
                down >= begin_ref[0:1, pl.ds(pl.multiple_of(i * shard, shard), shard)] - start,
            ),
            sums,
        )
        cosine, sine_part = cos_ref[own, :], sin_ref[own, :]
        made_ref[own, columns_of(pair)] = turn(
            total[own, :] * HD**-0.5, cosine, sine_part, False
        ).astype(jnp.bfloat16)
        made_ref[own, columns_of(2 + pair)] = turn(
            key_sum * (1 / LOG2E), cosine, sine_part, False
        ).astype(jnp.bfloat16)
        half_sum = 0.5 * value_sum
        made_ref[own, columns_of(4 + pair)] = half_sum.astype(jnp.bfloat16)
        first_ref[own, lanes] = half_sum
        for when, pump in ((0, after_a), (1, after_b), (3, after_c), (5, after_d), (7, after_e)):
            pl.when(step == when)(pump)
        return carried

    lax.fori_loop(0, 2 * PLANES, back_step, 0)
    quarters = [q_ref, k_ref, v_ref, o_ref]
    quarter_loads = [
        load(n_in.at[:, pl.ds(index * 256, 256)], quarter) for index, quarter in enumerate(quarters)
    ]
    weight_load.wait()
    small_ref[...] = small_in[...]

    def input_back(index, carried):
        block = jnp.where(depth < PLANES // 2, PLANES - 1 - index, index)
        rows = pl.ds(pl.multiple_of(block * shard, shard), shard)
        partial[block] = tokens_dot(made_ref[rows, :], weight_ref[pl.ds(0, 768), :], 1, 0).astype(
            jnp.bfloat16
        )
        return carried

    input_back(0, 0)
    line.launch(1)
    lax.fori_loop(1, PLANES, input_back, 0)
    line.launch(2)
    line.launch(3)
    for copy in quarter_loads:
        copy.wait()

    def gain_back(block, carried):
        rows = pl.ds(pl.multiple_of(block * shard, shard), shard)
        for index, quarter in enumerate(quarters):
            value = partial[block, :, pl.ds(index * 256, 256)].astype(jnp.float32)
            lanes = pl.ds(index * 256, 256)
            gain = (
                jnp.sum(value * quarter[rows, :].astype(jnp.float32), axis=0, keepdims=True)
                / gain_ref[0:1, lanes]
            )
            for half in range(2):
                piece = 2 * index + half
                small_ref[0, piece : piece + 1, :] += gain[:, half * PIECE : half * PIECE + PIECE]
        return carried

    lax.fori_loop(0, PLANES, gain_back, 0)
    fold_two(0)
    out_line.take(1)
    out_line.forward(2)

    links.go(tiny, small_ref.at[0], small_got.at[0], tiny_to[0])
    for copy in out_swaps:
        copy.wait_send()
    attn_made = out_made.at[pl.ds(0, 768), :]
    for index in range(3):
        rows = pl.ds(index * 256, 256)
        for quarter in range(4):
            attn_made[rows, pl.ds(quarter * 256, 256)] = tokens_dot(
                made_ref[:, rows], quarters[quarter][...], 0, 0
            ).astype(jnp.bfloat16)
    for i in range(4):
        links.go(attn_swap + i, attn_made.at[:, others[i]], attn_core.at[i], core)
    links.got(tiny, small_got.at[0])
    small_ref[1] = small_ref[0] + small_got[0]
    links.go(tiny + 1, small_ref.at[1], small_got.at[1], tiny_to[1])
    for i in range(4):
        links.got(attn_swap + i, attn_core.at[i])
        add_into(attn_core.at[i], attn_made.at[:, sides[i]])
    attn_fold.one()
    line.take(1)
    line.forward(2)
    links.got(tiny + 1, small_got.at[1])
    small_ref[2] = small_ref[1] + small_got[1]
    links.go(tiny + 2, small_ref.at[2], small_got.at[2], tiny_to[2])
    folds[0].end()
    feed_line.take(3)
    feed_line.total(feed_final.at[0], feed_total)
    out_line.take(2)
    out_line.forward(3)
    attn_fold.two()
    links.got(tiny + 2, small_got.at[2])
    small_ref[3] = small_ref[2] + small_got[2]
    small_place = small_got.at[3 + depth]
    for step in range(1, PLANES):
        links.go(tiny + 2 + step, small_ref.at[3], small_place, plane_to[step - 1])
    small_got[3 + depth] = small_ref[3]
    out_line.take(3)
    out_line.total(out_final.at[pl.ds(pl.multiple_of(depth * 256, 256), 256), :], out_total)
    line.take(2)
    line.forward(3)
    attn_fold.end()
    attn_total[...] = attn_final[...].astype(jnp.float32)
    for step in range(1, PLANES):
        links.got(tiny + 2 + step, small_got.at[3 + plane_rows[step]])
    small_ref[4] = small_got[3] + small_got[4] + small_got[5] + small_got[6]
    line.take(3)
    line.total(partial.at[depth], back_ref)
    links.drain()


def closing(made, low_ref, attended_own, heads, normed, weight, tables, incoming, logs, begin_row, gains, small):
    length, width = heads[0].shape
    rows = low_ref.shape[0]
    count = made.shape[2]
    low, full = jnp.bfloat16, jnp.float32
    any_spec, vmem = pl.BlockSpec(memory_space=pl.ANY), pl.BlockSpec(memory_space=pltpu.VMEM)
    shape = jax.ShapeDtypeStruct
    return pl.pallas_call(
        close_kernel,
        in_specs=[any_spec] * 15 + [vmem] * 4,
        out_specs=[vmem] * 6,
        out_shape=[
            shape((length, width), full),
            shape((rows, D), full),
            shape((count, PIECE), full),
            shape((256, PIECE), full),
            shape((768, PIECE), full),
            shape((5, 24, PIECE), full),
        ],
        scratch_shapes=[pltpu.VMEM((length, width), low)] * 4
        + [
            pltpu.VMEM((ATTN_ROWS, D), low),
            pltpu.VMEM((length, 128), full),
            pltpu.VMEM((length, 128), full),
            pltpu.VMEM((length, width), low),
            pltpu.VMEM((8, length), full),
            pltpu.VMEM((length, 128), full),
            pltpu.VMEM((length, 768), low),
            pltpu.VMEM((2, 2, count, PIECE), low),
            pltpu.VMEM((PLANES, 2, count, PIECE), low),
            pltpu.VMEM((PLANES, count, PIECE), low),
            pltpu.VMEM((2, PLANES - 1, count, PIECE), low),
            pltpu.VMEM((D, D), low),
            pltpu.VMEM((4, D, PIECE), low),
            pltpu.VMEM((2, D, PIECE), low),
            pltpu.VMEM((D, PIECE), low),
            pltpu.VMEM((2, PLANES - 1, 256, PIECE), low),
            pltpu.VMEM((4, 768, PIECE), low),
            pltpu.VMEM((2, 768, PIECE), low),
            pltpu.VMEM((768, PIECE), low),
            pltpu.VMEM((PLANES, rows, D), low),
            pltpu.VMEM((2, PLANES - 1, rows, D), low),
            pltpu.VMEM((7, 24, PIECE), full),
            pltpu.SemaphoreType.DMA((CLOSE_COPIES,)),
            pltpu.SemaphoreType.DMA((CLOSE_COPIES,)),
            pltpu.SemaphoreType.DMA((24,)),
        ],
        compiler_params=pltpu.CompilerParams(
            vmem_limit_bytes=CLOSE_VMEM, collective_id=3, has_side_effects=True
        ),
        name="closing",
    )(made, low_ref, attended_own, *heads, normed, weight, *tables, *incoming, logs, begin_row, gains, small)


def middle_back_kernel(*refs):
    middle_ref, grad_ref, back_ref, weight_ref, gain_ref = refs[:5]
    low_ref, dm_ref, gain_grad_ref = refs[5:8]
    outs = refs[8:12]
    depth = lax.axis_index("mp")
    half = middle_ref.shape[0] // 2
    gain = gain_ref[1:2, :]
    gain_grad_ref[...] = jnp.zeros_like(gain_grad_ref)
    for tile in range(2):
        rows = pl.ds(tile * half, half)
        middle, incoming = middle_ref[rows, :], back_ref[rows, :]
        factor = lax.rsqrt(jnp.mean(middle * middle, axis=-1, keepdims=True) + 1e-06)
        scaled = incoming * gain
        mean = jnp.mean(scaled * middle, axis=-1, keepdims=True)
        total = grad_ref[rows, :].astype(jnp.float32) + factor * scaled - middle * (factor**3 * mean)
        gain_grad_ref[0:1, :] += jnp.sum(incoming * middle * factor, axis=0, keepdims=True)
        dm_ref[rows, :] = total
        low_ref[rows, :] = total.astype(jnp.bfloat16)
    for index, out in enumerate(outs):
        owner = lax.rem(depth + index, PLANES)
        rows = pl.ds(pl.multiple_of(owner * 256, 256), 256)
        out[...] = tokens_dot(low_ref[...], weight_ref[rows, :], 1, 1).astype(jnp.bfloat16)


def middle_back(middle, grad, back, weight, gains):
    rows = middle.shape[0]
    return pl.pallas_call(
        middle_back_kernel,
        out_shape=[
            jax.ShapeDtypeStruct((rows, D), jnp.bfloat16),
            jax.ShapeDtypeStruct((rows, D), jnp.float32),
            jax.ShapeDtypeStruct((8, D), jnp.float32),
        ]
        + [jax.ShapeDtypeStruct((rows, 256), jnp.bfloat16)] * PLANES,
        compiler_params=pltpu.CompilerParams(vmem_limit_bytes=VMEM_LIMIT),
        cost_estimate=cost(2 * rows * D * D, 12 << 20),
        name="middle_back",
    )(middle, grad, back, weight, gains)


def stepped(master, gradient, moment, square, step_rate, decay, outs, at):
    new = adamw(master[at], gradient, moment[at], square[at], step_rate, decay)
    for out, value in zip(outs, new):
        out[at] = value


def update_kernel(*refs):
    hidden_ref, dm_ref, back_ref, gain_ref, attn_ref, out_ref, feed_ref, small_ref = refs[:8]
    masters, moments, squares = refs[8:13], refs[13:18], refs[18:23]
    grad_ref, norm_ref = refs[23:25]
    outs = [refs[25 + index : 40 : 5] for index in range(5)]
    place = lax.axis_index("dp")
    hidden = hidden_ref[...].astype(jnp.float32)
    factor = rms_factor(hidden)
    grad_ref[...] = dm_ref[...] + norm_back(hidden, factor, gain_ref[0:1, :], back_ref[...])[0]
    tokens = 8.0 * hidden_ref.shape[0] * PLANES
    norm_ref[...] = jnp.sqrt(small_ref[16:24, :] / (tokens * D))
    every = slice(None)
    rates = (D**-0.5, max(1, 8 * HEADS * HD // LEN) ** -0.5, D**-0.5, (FF // 3) ** -0.5)

    def weight(index, gradient, at):
        stepped(
            masters[index], gradient, moments[index], squares[index], rates[index], 0.1, outs[index], at
        )

    for which in range(3):
        weight(0, jnp.transpose(attn_ref[pl.ds(which * 256, 256), :]), which)
    weight(1, out_ref[...], (every, every))
    count = masters[3].shape[0]
    for which in range(2):
        weight(2, feed_ref[pl.ds(which * count, count), :], which)
    weight(3, feed_ref[pl.ds(2 * count, count), :], (every, every))
    for which in range(2):
        at = pl.ds(which, 1)
        stepped(
            masters[4],
            small_ref[pl.ds(8 * which + place, 1), :],
            moments[4],
            squares[4],
            0.2,
            0.0,
            outs[4],
            (at, every),
        )


def update(hidden, dm, back, gains, totals, small, masters, moments, squares):
    full = jnp.float32
    shape = jax.ShapeDtypeStruct
    return pl.pallas_call(
        update_kernel,
        out_shape=[shape(dm.shape, full), shape((8, PIECE), full)]
        + [shape(one.shape, full) for one in masters] * 3,
        compiler_params=pltpu.CompilerParams(vmem_limit_bytes=VMEM_LIMIT),
        cost_estimate=cost(0, 16 << 20),
        name="update",
    )(hidden, dm, back, gains, *totals, small, *masters, *moments, *squares)


def fast_shards(
    hidden_in,
    segment_ids,
    first_values,
    grad_out,
    input_proj,
    output_proj,
    expand_proj,
    reduce_proj,
    norm_gains,
    old_moment_input,
    old_moment_output,
    old_moment_expand,
    old_moment_reduce,
    old_moment_gains,
    old_square_input,
    old_square_output,
    old_square_expand,
    old_square_reduce,
    old_square_gains,
):
    place, depth = lax.axis_index("dp"), lax.axis_index("mp")
    low = jnp.bfloat16
    hidden, out_cotangent = hidden_in[0], grad_out[0]
    ffs = reduce_proj.shape[0]

    attn_piece = jnp.concatenate(
        [
            input_proj.astype(low).transpose(0, 2, 1).reshape(768, PIECE),
            norm_gains.astype(low),
            jnp.zeros((14, PIECE), low),
        ]
    )
    feed_piece = jnp.concatenate(
        [
            expand_proj.astype(low).transpose(0, 2, 1).reshape(2 * ffs, PIECE),
            reduce_proj.astype(low),
        ]
    )

    (
        queries,
        keys,
        values,
        attended,
        normed,
        attn_weight,
        out_weight,
        feed_all,
        cosine,
        sine_part,
        gains,
        squares,
        logs,
        middle,
        normed_two,
        attended_own,
        begin_row,
    ) = opening(hidden, attn_piece, output_proj.astype(low), feed_piece, first_values[0], segment_ids)
    normed_two_grad, layer_output, made = feed(normed_two, out_cotangent, middle, feed_all)
    layer_output = layer_output[None]
    branch_low, middle_grad, gain_two, *out_grads = middle_back(
        middle, out_cotangent, normed_two_grad, out_weight, gains
    )
    small = jnp.concatenate(
        [
            jnp.zeros((8, PIECE), jnp.float32),
            gain_two[0].reshape(8, PIECE),
            jnp.broadcast_to(jnp.sum(squares[:2], axis=1)[:, None], (2, PIECE)),
            jnp.zeros((6, PIECE), jnp.float32),
        ]
    )
    values_grad, normed_grad, feed_total, out_total, attn_total, small = closing(
        made,
        branch_low,
        attended_own,
        (queries, keys, values, attended),
        normed,
        attn_weight,
        (cosine, sine_part),
        out_grads,
        logs,
        begin_row,
        gains,
        jnp.broadcast_to(small[None], (5, 24, PIECE)),
    )
    small = small[4]
    masters = [input_proj, output_proj, expand_proj, reduce_proj, norm_gains]
    moments = [
        old_moment_input,
        old_moment_output,
        old_moment_expand,
        old_moment_reduce,
        old_moment_gains,
    ]
    squares = [
        old_square_input,
        old_square_output,
        old_square_expand,
        old_square_reduce,
        old_square_gains,
    ]
    for group in (masters, moments, squares):
        group[2] = group[2].transpose(0, 2, 1)
    input_grad, norms, *updated = update(
        hidden,
        middle_grad,
        normed_grad,
        gains,
        (attn_total, out_total, feed_total),
        small,
        masters,
        moments,
        squares,
    )
    for index in (2, 7, 12):
        updated[index] = updated[index].transpose(0, 2, 1)
    return (layer_output, input_grad[None], values_grad[None], norms[:2, 0], *updated)


def solution(mesh):
    quick = mesh.shape["dp"] == 8 and mesh.shape["mp"] == PLANES
    return jax.shard_map(
        fast_shards if quick else shards,
        mesh=mesh,
        in_specs=(
            P("dp", "mp", None),
            P("dp", None),
            P("dp", None, "mp"),
            P("dp", "mp", None),
            P(None, "dp", "mp"),
            P("mp", "dp"),
            P(None, "dp", "mp"),
            P("mp", "dp"),
            P(None, "dp"),
            P(None, "dp", "mp"),
            P("mp", "dp"),
            P(None, "dp", "mp"),
            P("mp", "dp"),
            P(None, "dp"),
            P(None, "dp", "mp"),
            P("mp", "dp"),
            P(None, "dp", "mp"),
            P("mp", "dp"),
            P(None, "dp"),
        ),
        out_specs=(
            P("dp", "mp", None),
            P("dp", "mp", None),
            P("dp", None, "mp"),
            P(),
            P(None, "dp", "mp"),
            P("mp", "dp"),
            P(None, "dp", "mp"),
            P("mp", "dp"),
            P(None, "dp"),
            P(None, "dp", "mp"),
            P("mp", "dp"),
            P(None, "dp", "mp"),
            P("mp", "dp"),
            P(None, "dp"),
            P(None, "dp", "mp"),
            P("mp", "dp"),
            P(None, "dp", "mp"),
            P("mp", "dp"),
            P(None, "dp"),
        ),
        check_vma=False,
    )
```

```python
import functools
import math

import jax
import jax.numpy as jnp
import numpy as np
from jax import lax
from jax.experimental import pallas as pl
from jax.experimental.pallas import tpu as pltpu
from jax.sharding import PartitionSpec as P

D = 1024
HEADS = 16
HD = 64
FF = 2816
LEN = 2048
STEP = 5
PLANES = 4
PIECE = 128
BLOCKS = 4
ATTN_ROWS = 784
VMEM_LIMIT = 56 << 20
OPEN_COPIES = 80
CLOSE_COPIES = 80
CLOSE_VMEM = 60 << 20


def arrivals(plane):
    order = [(0, 0, plane)]
    for hop in range(1, PLANES):
        if plane + hop < PLANES:
            order.append((0, hop, plane + hop))
        if plane - hop >= 0:
            order.append((1, hop, plane - hop))
    return order


SLOTS = [arrivals(plane) for plane in range(PLANES)]


def cost(flops, moved):
    return pl.CostEstimate(flops=flops, bytes_accessed=moved, transcendentals=0)


def rope_tables(seg_row, head_size):
    length = seg_row.shape[0]
    places = jnp.arange(length, dtype=jnp.int32)
    begins = jnp.sum((seg_row[None, :] < seg_row[:, None]).astype(jnp.int32), axis=1)
    offset = (places - begins).astype(jnp.float32)
    inverse_rates = 10000.0 ** (-2.0 * jnp.arange(head_size // 2, dtype=jnp.float32) / head_size)
    angles = offset[:, None] * inverse_rates[None, :]
    return (jnp.cos(angles)[:, None, :], jnp.sin(angles)[:, None, :])


def rotate(values, cosine, sine_part, forward):
    half_size = values.shape[-1] // 2
    first_half = values[..., :half_size]
    second_half = values[..., half_size:]
    if forward:
        return jnp.concatenate(
            [
                first_half * cosine - second_half * sine_part,
                second_half * cosine + first_half * sine_part,
            ],
            axis=-1,
        )
    return jnp.concatenate(
        [
            first_half * cosine + second_half * sine_part,
            second_half * cosine - first_half * sine_part,
        ],
        axis=-1,
    )


def rms_factor(values):
    return lax.rsqrt(jnp.mean(values * values, axis=-1, keepdims=True) + 1e-06)


def norm_back(values, factor, gain_row, incoming):
    scaled = incoming * gain_row
    value_grad = factor * scaled - values * factor**3 * jnp.mean(
        scaled * values, axis=-1, keepdims=True
    )
    gain_grad = jnp.sum(incoming * values * factor, axis=0)
    return (value_grad, gain_grad)


def visible_block(seg_row, first_row, block_rows):
    length = seg_row.shape[0]
    query_seg = lax.dynamic_slice_in_dim(seg_row, first_row, block_rows, 0)
    query_places = first_row + jnp.arange(block_rows, dtype=jnp.int32)
    key_places = jnp.arange(length, dtype=jnp.int32)
    return (query_seg[:, None] == seg_row[None, :]) & (query_places[:, None] >= key_places[None, :])


def block_scores(queries, keys_rot, seg_row, first_row, block_rows, score_scale):
    query_block = lax.dynamic_slice_in_dim(queries, first_row, block_rows, 0)
    visible = visible_block(seg_row, first_row, block_rows)
    scores = (
        jnp.einsum("qhd,khd->hqk", query_block, keys_rot, preferred_element_type=jnp.float32)
        * score_scale
    )
    return (query_block, jnp.where(visible[None], scores, -1e30))


def attend(queries, keys_rot, mixed_values, seg_row, score_scale):
    length = queries.shape[0]
    block_rows = min(512, length)

    def one_block(block_index):
        first_row = block_index * block_rows
        query_block, scores = block_scores(
            queries, keys_rot, seg_row, first_row, block_rows, score_scale
        )
        top_score = jnp.max(scores, axis=-1, keepdims=True)
        raised = jnp.exp(scores - top_score)
        totals = jnp.sum(raised, axis=-1, keepdims=True)
        shares = (raised / totals).astype(jnp.bfloat16)
        combined = jnp.einsum(
            "hqk,khd->qhd", shares, mixed_values, preferred_element_type=jnp.float32
        )
        return (combined, (top_score + jnp.log(totals))[..., 0])

    combined, log_totals = lax.map(one_block, jnp.arange(length // block_rows, dtype=jnp.int32))
    return (combined.reshape(length, -1), log_totals)


def attend_back(queries, keys_rot, mixed_values, out_grad, log_totals, seg_row, score_scale):
    length = queries.shape[0]
    block_rows = min(512, length)

    def one_block(running, operands):
        key_sum, value_sum = running
        block_index, block_totals = operands
        first_row = block_index * block_rows
        query_block, scores = block_scores(
            queries, keys_rot, seg_row, first_row, block_rows, score_scale
        )
        grad_block = lax.dynamic_slice_in_dim(out_grad, first_row, block_rows, 0)
        shares = jnp.exp(scores - block_totals[..., None])
        share_grad = jnp.einsum(
            "qhd,khd->hqk", grad_block, mixed_values, preferred_element_type=jnp.float32
        )
        inner = jnp.sum(shares * share_grad, axis=-1, keepdims=True)
        score_grad = (shares * (share_grad - inner)).astype(jnp.bfloat16)
        query_grad = (
            jnp.einsum("hqk,khd->qhd", score_grad, keys_rot, preferred_element_type=jnp.float32)
            * score_scale
        )
        key_sum = (
            key_sum
            + jnp.einsum(
                "hqk,qhd->khd", score_grad, query_block, preferred_element_type=jnp.float32
            )
            * score_scale
        )
        value_sum = value_sum + jnp.einsum(
            "hqk,qhd->khd",
            shares.astype(jnp.bfloat16),
            grad_block,
            preferred_element_type=jnp.float32,
        )
        return ((key_sum, value_sum), query_grad)

    empty_sum = jnp.zeros(keys_rot.shape, jnp.float32)
    (key_grad, value_grad), query_grad = lax.scan(
        one_block,
        (empty_sum, empty_sum),
        (jnp.arange(length // block_rows, dtype=jnp.int32), log_totals),
    )
    return (query_grad.reshape(keys_rot.shape), key_grad, value_grad)


def adamw(master, gradient, moment, square, step_rate, decay):
    new_moment = 0.5 * moment + 0.5 * gradient
    new_square = 0.5 * square + 0.5 * gradient * gradient
    correct = 1.0 - 0.5**STEP
    update = new_moment / correct / (jnp.sqrt(new_square / correct) + 1e-08)
    return (master - step_rate * (update + decay * master), new_moment, new_square)


def shards(
    hidden_in,
    segment_ids,
    first_values,
    grad_out,
    input_proj,
    output_proj,
    expand_proj,
    reduce_proj,
    norm_gains,
    old_moment_input,
    old_moment_output,
    old_moment_expand,
    old_moment_reduce,
    old_moment_gains,
    old_square_input,
    old_square_output,
    old_square_expand,
    old_square_reduce,
    old_square_gains,
):
    attn_weight, out_weight, expand_weight, reduce_weight, gains_low = (
        lax.all_gather(input_proj.astype(jnp.bfloat16), "dp", axis=1, tiled=True),
        lax.all_gather(output_proj.astype(jnp.bfloat16), "dp", axis=1, tiled=True),
        lax.all_gather(expand_proj.astype(jnp.bfloat16), "dp", axis=1, tiled=True),
        lax.all_gather(reduce_proj.astype(jnp.bfloat16), "dp", axis=1, tiled=True),
        lax.all_gather(norm_gains.astype(jnp.bfloat16), "dp", axis=1, tiled=True),
    )
    gains = gains_low.astype(jnp.float32)
    hidden = hidden_in[0].astype(jnp.float32)
    seg_row = segment_ids[0]
    length = seg_row.shape[0]
    first_in = first_values[0].astype(jnp.float32)
    local_heads = attn_weight.shape[2] // HD
    score_scale = 1.0 / math.sqrt(HD)
    factor_one = rms_factor(hidden)
    normed_one = (hidden * factor_one * gains[0]).astype(jnp.bfloat16)
    all_normed, all_grad_out = (
        lax.all_gather(normed_one, "mp", axis=0, tiled=True),
        lax.all_gather(grad_out[0], "mp", axis=0, tiled=True),
    )
    projected = jnp.einsum(
        "td,cde->cte", all_normed, attn_weight, preferred_element_type=jnp.float32
    )
    cosine, sine_part = rope_tables(seg_row, HD)
    queries = rotate(projected[0].reshape(length, local_heads, HD), cosine, sine_part, True).astype(
        jnp.bfloat16
    )
    keys_rot = rotate(
        projected[1].reshape(length, local_heads, HD), cosine, sine_part, True
    ).astype(jnp.bfloat16)
    blended = 0.5 * projected[2] + 0.5 * first_in
    mixed_values = blended.astype(jnp.bfloat16).reshape(length, local_heads, HD)
    square_terms = jnp.stack([jnp.sum(first_in * first_in), jnp.sum(blended * blended)])
    attended, log_totals = attend(queries, keys_rot, mixed_values, seg_row, score_scale)
    attended_low = attended.astype(jnp.bfloat16)
    rows_part = attended_low
    branch = lax.psum_scatter(
        jnp.dot(rows_part, out_weight, preferred_element_type=jnp.float32),
        "mp",
        scatter_dimension=0,
        tiled=True,
    )
    middle = hidden + branch
    factor_two = rms_factor(middle)
    normed_two = (middle * factor_two * gains[1]).astype(jnp.bfloat16)
    all_normed_two = lax.all_gather(normed_two, "mp", axis=0, tiled=True)
    gate_up = jnp.einsum(
        "td,cdf->ctf", all_normed_two, expand_weight, preferred_element_type=jnp.float32
    )
    gate_sig = jax.nn.sigmoid(gate_up[0])
    gate_act = gate_up[0] * gate_sig
    activated = (gate_act * gate_up[1]).astype(jnp.bfloat16)
    rows_part = activated
    feed_out = lax.psum_scatter(
        jnp.dot(rows_part, reduce_weight, preferred_element_type=jnp.float32).astype(jnp.bfloat16),
        "mp",
        scatter_dimension=0,
        tiled=True,
    ).astype(jnp.float32)
    layer_output = (middle + feed_out).astype(jnp.bfloat16)[None]
    hidden_grad = jnp.einsum(
        "td,fd->tf", all_grad_out, reduce_weight, preferred_element_type=jnp.float32
    )
    reduce_grad = jnp.einsum(
        "tf,td->fd", activated, all_grad_out, preferred_element_type=jnp.float32
    )
    gate_grad = hidden_grad * gate_up[1] * gate_sig * (1.0 + gate_up[0] * (1.0 - gate_sig))
    up_grad = hidden_grad * gate_act
    pair_grad = jnp.stack([gate_grad, up_grad]).astype(jnp.bfloat16)
    expand_grad = jnp.einsum(
        "ctf,td->cdf", pair_grad, all_normed_two, preferred_element_type=jnp.float32
    )
    rows_part = pair_grad
    normed_two_grad = lax.psum_scatter(
        jnp.einsum(
            "ctf,cdf->td", rows_part, expand_weight, preferred_element_type=jnp.float32
        ).astype(jnp.bfloat16),
        "mp",
        scatter_dimension=0,
        tiled=True,
    ).astype(jnp.float32)
    middle_part, gain_two_grad = norm_back(middle, factor_two, gains[1], normed_two_grad)
    middle_grad = grad_out[0].astype(jnp.float32) + middle_part
    branch_low = middle_grad.astype(jnp.bfloat16)
    all_branch = lax.all_gather(branch_low, "mp", axis=0, tiled=True)
    out_grad = jnp.einsum("te,td->ed", attended_low, all_branch, preferred_element_type=jnp.float32)
    attended_grad = jnp.einsum(
        "td,ed->te", all_branch, out_weight, preferred_element_type=jnp.float32
    ).astype(jnp.bfloat16)
    query_grad, key_grad, mix_grad = attend_back(
        queries,
        keys_rot,
        mixed_values,
        attended_grad.reshape(length, local_heads, HD),
        log_totals,
        seg_row,
        score_scale,
    )
    query_grad = rotate(query_grad, cosine, sine_part, False).reshape(length, -1)
    key_grad = rotate(key_grad, cosine, sine_part, False).reshape(length, -1)
    mix_grad = mix_grad.reshape(length, -1)
    values_grad = (0.5 * mix_grad)[None]
    proj_grad = jnp.stack([query_grad, key_grad, 0.5 * mix_grad]).astype(jnp.bfloat16)
    attn_grad = jnp.einsum("cte,td->cde", proj_grad, all_normed, preferred_element_type=jnp.float32)
    rows_part = proj_grad
    normed_one_grad = lax.psum_scatter(
        jnp.einsum(
            "cte,cde->td", rows_part, attn_weight, preferred_element_type=jnp.float32
        ).astype(jnp.bfloat16),
        "mp",
        scatter_dimension=0,
        tiled=True,
    ).astype(jnp.float32)
    input_part, gain_one_grad = norm_back(hidden, factor_one, gains[0], normed_one_grad)
    input_grad = (middle_grad + input_part)[None]
    attn_total, out_total, expand_total, reduce_total = (
        lax.psum_scatter(
            attn_grad.astype(jnp.bfloat16), "dp", scatter_dimension=1, tiled=True
        ).astype(jnp.float32),
        lax.psum_scatter(
            out_grad.astype(jnp.bfloat16), "dp", scatter_dimension=1, tiled=True
        ).astype(jnp.float32),
        lax.psum_scatter(
            expand_grad.astype(jnp.bfloat16), "dp", scatter_dimension=1, tiled=True
        ).astype(jnp.float32),
        lax.psum_scatter(
            reduce_grad.astype(jnp.bfloat16), "dp", scatter_dimension=1, tiled=True
        ).astype(jnp.float32),
    )
    gain_totals, square_sums = lax.psum(
        (jnp.stack([gain_one_grad, gain_two_grad]), square_terms), ("dp", "mp")
    )
    gain_width = norm_gains.shape[1]
    gain_total = lax.dynamic_slice_in_dim(
        gain_totals, lax.axis_index("dp") * gain_width, gain_width, 1
    )
    value_norms = jnp.sqrt(square_sums / (lax.axis_size("dp") * length * D))
    new_input = adamw(input_proj, attn_total, old_moment_input, old_square_input, D ** (-0.5), 0.1)
    new_output = adamw(
        output_proj,
        out_total,
        old_moment_output,
        old_square_output,
        max(1, 8 * HEADS * HD // LEN) ** (-0.5),
        0.1,
    )
    new_expand = adamw(
        expand_proj, expand_total, old_moment_expand, old_square_expand, D ** (-0.5), 0.1
    )
    new_reduce = adamw(
        reduce_proj, reduce_total, old_moment_reduce, old_square_reduce, (FF // 3) ** (-0.5), 0.1
    )
    new_gains = adamw(norm_gains, gain_total, old_moment_gains, old_square_gains, 0.2, 0.0)
    return (
        layer_output,
        input_grad,
        values_grad,
        value_norms,
        new_input[0],
        new_output[0],
        new_expand[0],
        new_reduce[0],
        new_gains[0],
        new_input[1],
        new_output[1],
        new_expand[1],
        new_reduce[1],
        new_gains[1],
        new_input[2],
        new_output[2],
        new_expand[2],
        new_reduce[2],
        new_gains[2],
    )


def tokens_dot(a, b, left, right):
    return lax.dot_general(a, b, (((left,), (right,)), ((), ())), preferred_element_type=jnp.float32)


def piece_columns(place, step):
    start = jnp.bitwise_xor(place, step) * PIECE
    return pl.ds(pl.multiple_of(start, PIECE), PIECE)


def turn(values, cosine, sine_part, forward):
    lane = lax.broadcasted_iota(jnp.int32, values.shape, 1)
    swapped = jnp.where(
        lax.rem(lane, HD) < HD // 2, pltpu.roll(values, 96, 1), pltpu.roll(values, 32, 1)
    )
    if forward:
        return values * cosine + swapped * sine_part
    return values * cosine - swapped * sine_part


MESH = pl.DeviceIdType.MESH
LOG2E = 1.4426950408889634


def flip(place, bit):
    return place + bit - 2 * bit * lax.rem(lax.div(place, bit), 2)


def at_plane(depth, values):
    found = 0
    for plane, value in enumerate(values):
        found = found + jnp.where(depth == plane, value, 0)
    return found


def slot_at(depth, way, hop):
    return at_plane(
        depth,
        [
            next((k for k, s in enumerate(SLOTS[plane]) if s[:2] == (way, hop)), 0)
            for plane in range(PLANES)
        ],
    )


def columns_of(piece, width=PIECE):
    return pl.ds(pl.multiple_of(piece * width, width), width)


class Links:
    def __init__(self, send, recv):
        self.send, self.recv, self.count, self.started, self.waited = send, recv, 0, [], []
        self.place, self.depth = lax.axis_index("dp"), lax.axis_index("mp")

    def number(self, count=1):
        self.count += count
        return self.count - count

    def copy(self, number, source, target, to):
        return pltpu.make_async_remote_copy(
            src_ref=source,
            dst_ref=target,
            send_sem=self.send.at[number],
            recv_sem=self.recv.at[number],
            device_id=to,
            device_id_type=MESH,
        )

    def go(self, number, source, target, to, when=None):
        copy = self.copy(number, source, target, to)
        self.started.append((number, source, target, to, when))
        if when is None:
            copy.start()
        else:
            pl.when(when)(copy.start)

    def got(self, number, landed, when=None):
        copy = self.copy(number, landed, landed, (flip(self.place, 1), self.depth))
        if when is None:
            copy.wait_recv()
        else:
            pl.when(when)(copy.wait_recv)

    def drain(self):
        for *parts, when in self.started:
            copy = self.copy(*parts)
            for plane in [plane for number, plane in self.waited if number == parts[0]]:
                when = when & (self.depth != plane)
            if when is None:
                copy.wait_send()
            else:
                pl.when(when)(copy.wait_send)

    def greet(self, planes=True):
        barrier = pltpu.get_barrier_semaphore()
        others = [(flip(self.place, bit), self.depth) for bit in (1, 2, 4)]
        if planes:
            others += [(self.place, lax.rem(self.depth + step, PLANES)) for step in range(1, PLANES)]
        for other in others:
            pl.semaphore_signal(barrier, inc=1, device_id=other, device_id_type=MESH)
        pl.semaphore_wait(barrier, len(others))


class Spread:
    def __init__(self, links, own, spot, bits):
        self.links, self.own = links, own
        self.base = links.number(7)
        place = links.place
        first, second = flip(place, bits[0]), flip(place, bits[1])
        self.spots = [spot(piece) for piece in (place, first, second, flip(first, bits[1]))]
        self.lands = [
            spot(flip(piece, 1)) for piece in (place, first, second, flip(first, bits[1]))
        ]
        self.near, self.far, self.core = [
            (flip(place, bit), links.depth) for bit in (bits[0], bits[1], 1)
        ]

    def one(self):
        self.links.go(self.base, self.own, self.spots[0], self.near)

    def two(self):
        links, spots = self.links, self.spots
        links.go(self.base + 1, self.own, spots[0], self.far)
        links.got(self.base, spots[1])
        links.go(self.base + 2, spots[1], spots[1], self.far)

    def landed(self):
        self.links.got(self.base + 1, self.spots[2])
        self.links.got(self.base + 2, self.spots[3])

    def three(self):
        links, spots = self.links, self.spots
        links.go(self.base + 3, self.own, spots[0], self.core)
        links.go(self.base + 4, spots[1], spots[1], self.core)
        links.got(self.base + 1, spots[2])
        links.go(self.base + 5, spots[2], spots[2], self.core)
        links.got(self.base + 2, spots[3])
        links.go(self.base + 6, spots[3], spots[3], self.core)

    def end(self):
        for index, land in enumerate(self.lands):
            self.links.got(self.base + 3 + index, land)


class Halves:
    def __init__(self, parts):
        self.parts = parts

    def one(self):
        for part in self.parts:
            part.one()

    def two(self, *given):
        for index, part in enumerate(self.parts):
            part.two(*[one[index] for one in given])

    def landed(self):
        for part in self.parts:
            part.landed()

    def three(self):
        for part in self.parts:
            part.three()

    def end(self):
        for part in self.parts:
            part.end()


def half_of(ref, half):
    rows = ref.shape[-2] // 2
    lead = (slice(None),) * (len(ref.shape) - 2)
    return ref.at[(*lead, pl.ds(half * rows, rows), slice(None))]


def halved_spread(links, own, spot):
    return Halves(
        [
            Spread(
                links,
                half_of(own, half),
                lambda piece, half=half: half_of(spot(piece), half),
                ((2, 4), (4, 2))[half],
            )
            for half in range(2)
        ]
    )


class Relay:
    def __init__(self, links, own, put):
        self.links, self.own, self.put = links, own, put
        self.base = links.number(2 * (PLANES - 1))
        self.waited = links.waited

    def plan(self, hop, only=None):
        links, depth = self.links, self.links.depth
        planned = []
        for way in range(2):
            to = depth + (1 if way else -1)
            when = (
                (depth >= hop - 1) & (depth < PLANES - 1)
                if way
                else (depth <= PLANES - hop) & (depth > 0)
            )
            if only is not None:
                when = when & (depth == only[way])
            source = self.own if hop == 1 else self.put(depth, way, hop - 1)
            planned.append(
                (
                    self.base + 2 * (hop - 1) + way,
                    source,
                    self.put(to, way, hop),
                    (links.place, jnp.clip(to, 0, PLANES - 1)),
                    when,
                )
            )
        return planned

    def send(self, hop, only=None):
        for parts in self.plan(hop, only):
            self.links.go(*parts)

    def take(self, hop, only=None):
        links, depth = self.links, self.links.depth
        for way in range(2):
            when = depth >= hop if way else depth + hop < PLANES
            if only is not None:
                when = when & (depth == only[way])
            links.got(self.base + 2 * (hop - 1) + way, self.put(depth, way, hop), when)

    def left(self, hop, only):
        links, depth = self.links, self.links.depth
        for way in range(2):
            source = self.own if hop == 1 else self.put(depth, way, hop - 1)
            to = (links.place, jnp.clip(depth + (1 if way else -1), 0, PLANES - 1))
            copy = links.copy(self.base + 2 * (hop - 1) + way, source, source, to)
            pl.when(depth == only[way])(copy.wait_send)
            self.waited.append((self.base + 2 * (hop - 1) + way, only[way]))


def position_tables(length):
    rates = 10000.0 ** (-2.0 * np.arange(HD // 2) / HD)
    angles = np.arange(length)[:, None] * rates[None, :]
    cosine, sine = np.cos(angles), np.sin(angles)
    return (
        jnp.asarray(np.concatenate([cosine] * 4, axis=1), jnp.float32),
        jnp.asarray(np.concatenate([-sine, sine, -sine, sine], axis=1), jnp.float32),
    )


def rope_tables_from(seg_ref, cos_at, sin_at, cos_ref, sin_ref, begin_ref, marks):
    length = cos_at.shape[0]
    segs = seg_ref[0:1, :].astype(jnp.float32)
    spots = lax.broadcasted_iota(jnp.int32, (1, length), 1).astype(jnp.float32)
    begins = jnp.zeros((1, length), jnp.float32)
    marks[...] = jnp.zeros_like(marks)
    for number in range(7):
        start = jnp.sum(jnp.where(segs < number, 1.0, 0.0), axis=1, keepdims=True)
        begins = jnp.where(segs == number, start, begins)
        marks[number : number + 1, :] = jnp.where(spots == start, 1.0, 0.0)
    begin_ref[...] = jnp.broadcast_to(begins.astype(jnp.int32), begin_ref.shape)
    pick = lambda table: lax.dot_general(
        marks[...],
        table[...],
        (((1,), (0,)), ((), ())),
        precision=lax.Precision.HIGHEST,
        preferred_element_type=jnp.float32,
    )
    first_cos, first_sin = pick(cos_at), pick(sin_at)
    rows = length // PLANES
    for block in range(PLANES):
        span = pl.ds(block * rows, rows)
        documents = jnp.transpose(
            jnp.broadcast_to(segs[:, block * rows : block * rows + rows], (128, rows))
        )
        cosine = jnp.zeros((rows, 128), jnp.float32)
        sine = jnp.zeros((rows, 128), jnp.float32)
        for number in range(7):
            here = documents == number
            cosine = jnp.where(here, first_cos[number : number + 1], cosine)
            sine = jnp.where(here, first_sin[number : number + 1], sine)
        cos_ref[span, :] = cos_at[span, :] * cosine + sin_at[span, :] * sine
        sin_ref[span, :] = sin_at[span, :] * cosine - cos_at[span, :] * sine


def open_kernel(*refs):
    hidden, attn_piece, out_piece, feed_piece, cos_at, sin_at, first_ref, seg_ref = refs[:8]
    q_out, k_out, v_out, o_out, n_out, weight_out, out_weight_out, feed_all, cos_out, sin_out = refs[8:18]
    gain_ref, square_ref, log_ref, middle_ref, normed_ref, attended_ref, begin_ref = refs[18:25]
    held, q_ref, k_ref, v_ref, o_ref, n_ref, weight_ref, out_ref, cos_ref, sin_ref, turned_v, marks = refs[25:37]
    send, recv, local = refs[37:]
    links = Links(send, recv)
    place, depth = links.place, links.depth
    shard = hidden.shape[0]
    stores = []

    def store(source, target):
        copy = pltpu.make_async_copy(source, target, local.at[len(stores)])
        copy.start()
        stores.append(copy)
        return copy

    block_at = lambda plane, way, hop: jnp.clip(plane + (-hop if way else hop), 0, PLANES - 1)
    wide = Relay(links, hidden, lambda plane, way, hop: held.at[block_at(plane, way, hop)])
    out_rows = lambda block: out_ref.at[
        pl.ds(pl.multiple_of(block * 256, 256), 256), columns_of(place)
    ]
    thin = Relay(links, out_piece, lambda plane, way, hop: out_rows(block_at(plane, way, hop)))
    feeds = Relay(
        links,
        feed_piece,
        lambda plane, way, hop: feed_all.at[slot_at(plane, way, hop), place],
    )
    attn = Spread(links, attn_piece, lambda piece: weight_ref.at[:, columns_of(piece)], (2, 4))
    outs = Spread(
        links, out_ref.at[:, columns_of(place)], lambda piece: out_ref.at[:, columns_of(piece)], (2, 4)
    )
    slots = [
        halved_spread(
            links,
            feed_piece if slot == 0 else feed_all.at[slot, place],
            lambda piece, slot=slot: feed_all.at[slot, piece],
        )
        for slot in range(PLANES - 1)
    ]
    across = links.number(PLANES)

    links.greet()
    thin.send(1)
    wide.send(1)
    attn.one()
    own_hidden = store(hidden, held.at[depth])
    own_attn = store(attn_piece, weight_ref.at[:, columns_of(place)])
    own_out = store(out_piece, out_rows(depth))
    own_feed = store(feed_piece, feed_all.at[0, place])
    square_ref[...] = jnp.zeros_like(square_ref)
    attn.two()
    attn.three()
    slots[0].one()
    rope_tables_from(seg_ref, cos_at, sin_at, cos_ref, sin_ref, begin_ref, marks)
    attn.end()
    for copy in (own_hidden, own_attn, own_out, own_feed):
        copy.wait()
    store(weight_ref, weight_out)
    store(cos_ref, cos_out)
    store(sin_ref, sin_out)
    gain_ref[...] = weight_ref[pl.ds(768, 16), :].astype(jnp.float32)

    def project(block):
        rows = pl.ds(pl.multiple_of(block * shard, shard), shard)
        values = held[block].astype(jnp.float32)
        factor = lax.rsqrt(jnp.mean(values * values, axis=-1, keepdims=True) + 1e-06)
        normed = (values * factor * gain_ref[0:1, :]).astype(jnp.bfloat16)
        n_ref[rows, :] = normed
        cosine, sine_part = cos_ref[rows, :], sin_ref[rows, :]
        query = tokens_dot(normed, weight_ref[pl.ds(0, 256), :], 1, 1)
        key = tokens_dot(normed, weight_ref[pl.ds(256, 256), :], 1, 1)
        value = tokens_dot(normed, weight_ref[pl.ds(512, 256), :], 1, 1)
        for half in range(2):
            lanes = slice(half * 128, half * 128 + 128)
            turned = turn(query[:, lanes], cosine, sine_part, True)
            q_ref[rows, lanes] = (turned * (HD**-0.5 * LOG2E)).astype(jnp.bfloat16)
            k_ref[rows, lanes] = turn(key[:, lanes], cosine, sine_part, True).astype(jnp.bfloat16)
        first = first_ref[rows, :].astype(jnp.float32)
        blended = 0.5 * value + 0.5 * first
        v_ref[rows, :] = blended.astype(jnp.bfloat16)
        for half in range(2):
            turned_v[half, :, rows] = jnp.transpose(
                blended[:, half * 128 : half * 128 + 128]
            ).astype(jnp.bfloat16)
        square_ref[0:1, :] += jnp.sum(first * first, axis=0, keepdims=True)
        square_ref[1:2, :] += jnp.sum(blended * blended, axis=0, keepdims=True)

    def project_hop(hop):
        def one(side, carried):
            block = depth + hop * (2 * side - 1)
            pl.when((block >= 0) & (block < PLANES))(lambda: project(block))
            return carried

        lax.fori_loop(0, 2, one, 0)

    ends, inner = (PLANES - 1, 0), (PLANES - 2, 1)
    project(depth)
    wide.take(1)
    wide.send(2)
    feeds.send(1, ends)
    thin.take(1)
    thin.send(2)
    slots[0].two()
    project_hop(1)
    wide.take(2)
    wide.send(3)
    feeds.take(1, inner)
    feeds.send(1, inner)
    feeds.send(2, inner)
    thin.take(2)
    thin.send(3)
    project_hop(2)
    slots[0].three()
    wide.take(3)
    wide.left(3, (1, PLANES - 2))
    feeds.take(1, (1, PLANES - 2))
    feeds.take(2, (1, PLANES - 2))
    feeds.send(1, (1, PLANES - 2))
    second = feeds.plan(2, (1, PLANES - 2))
    thin.take(3)
    outs.one()
    project_hop(3)
    store(n_ref, n_out)
    store(q_ref, q_out)
    store(k_ref, k_out)
    store(v_ref, v_out)

    lane = lax.broadcasted_iota(jnp.int32, (shard, 128), 1)
    down = lax.broadcasted_iota(jnp.int32, (shard, shard), 0)
    along = lax.broadcasted_iota(jnp.int32, (1, shard), 1)

    def flash_block(block):
        rows = pl.ds(pl.multiple_of(block * shard, shard), shard)
        begin = begin_ref[0:1, rows]
        pairs = [q_ref[rows, pl.ds(pair * 128, 128)] for pair in range(2)]
        parts = [
            jnp.where((lane < HD) == (head % 2 == 0), pairs[head // 2], jnp.zeros_like(pairs[0]))
            for head in range(4)
        ]

        def tile(index, carried, visible):
            span = pl.ds(pl.multiple_of(index * shard, shard), shard)
            raw = [
                tokens_dot(k_ref[span, pl.ds(head // 2 * 128, 128)], parts[head], 1, 1)
                for head in range(4)
            ]
            after = []
            for head in range(4):
                top, total, summed = carried[3 * head : 3 * head + 3]
                scores = jnp.where(visible, raw[head], -1e30)
                raised_top = jnp.maximum(top, jnp.max(scores, axis=0, keepdims=True))
                shrink = jnp.exp2(top - raised_top)
                shares = jnp.exp2(scores - raised_top)
                total = total * shrink + jnp.sum(shares, axis=0, keepdims=True)
                values = turned_v[head // 2, pl.ds(head % 2 * HD, HD), span]
                summed = summed * shrink + tokens_dot(values, shares.astype(jnp.bfloat16), 1, 0)
                after += [raised_top, total, summed]
            return tuple(after)

        fresh = (
            jnp.full((1, shard), -1e30, jnp.float32),
            jnp.zeros((1, shard), jnp.float32),
            jnp.zeros((HD, shard), jnp.float32),
        )
        carried = tile(block, fresh * 4, (down >= begin - block * shard) & (down <= along))
        carried = lax.fori_loop(
            0, block, lambda j, held: tile(j, held, down >= begin - j * shard), carried
        )
        for pair in range(2):
            ends = [carried[3 * (2 * pair + head) : 3 * (2 * pair + head) + 3] for head in range(2)]
            both = jnp.concatenate([summed / total for _, total, summed in ends], axis=0)
            o_ref[rows, pl.ds(pair * 128, 128)] = jnp.transpose(both).astype(jnp.bfloat16)
            for head, (top, total, _) in enumerate(ends):
                log_ref[pair, head : head + 1, rows] = top + jnp.log2(total)

    own_columns = attended_ref.at[:, columns_of(depth, 256)]

    def hand(step):
        block = lax.rem(depth + step, PLANES)
        rows = pl.ds(pl.multiple_of(block * shard, shard), shard)
        return links.copy(across + step, o_ref.at[rows, :], own_columns, (place, block))

    near = (0, PLANES - 1)

    def pump_a():
        feeds.take(1, near)
        slots[1].one()
        outs.two()

    def pump_b():
        slots[1].two()
        slots[0].end()
        feeds.left(1, (1, PLANES - 2))
        for parts in second:
            links.go(*parts)

    def pump_c():
        feeds.take(2, near)
        slots[2].one()
        outs.three()

    pumps = ((0, pump_a), (1, pump_b), (2, pump_c))

    def flash(index, carried):
        step = PLANES - 1 - index
        flash_block(lax.rem(depth + step, PLANES))
        pl.when(step > 0)(lambda: hand(step).start())
        for when, pump in pumps:
            pl.when(index == when)(pump)
        return carried

    lax.fori_loop(0, PLANES, flash, 0)
    feeds.send(3, (1, PLANES - 2))
    own_rows = pl.ds(pl.multiple_of(depth * shard, shard), shard)
    attended_ref[:, columns_of(depth, 256)] = o_ref[own_rows, :]
    store(o_ref, o_out)
    outs.end()
    store(out_ref, out_weight_out)
    slots[2].two()
    for step in range(1, PLANES):
        source = lax.rem(depth - step + PLANES, PLANES)
        links.got(across + step, attended_ref.at[:, columns_of(source, 256)])
    half = shard // 2
    for part in range(2):
        rows = pl.ds(part * half, half)
        middle = held[depth, rows, :].astype(jnp.float32) + tokens_dot(
            attended_ref[rows, :], out_ref[...], 1, 0
        )
        middle_ref[rows, :] = middle
        factor = lax.rsqrt(jnp.mean(middle * middle, axis=-1, keepdims=True) + 1e-06)
        normed_ref[rows, :] = (middle * factor * gain_ref[1:2, :]).astype(jnp.bfloat16)
    slots[1].landed()
    slots[2].landed()
    feeds.take(3)
    for step in range(1, PLANES):
        hand(step).wait_send()
    links.drain()
    for copy in stores[4:]:
        copy.wait()


def opening(hidden, attn_piece, out_piece, feed_piece, first_values, seg_row):
    length, width = first_values.shape
    rows = hidden.shape[0]
    count = feed_piece.shape[0]
    low, full = jnp.bfloat16, jnp.float32
    any_spec, vmem = pl.BlockSpec(memory_space=pl.ANY), pl.BlockSpec(memory_space=pltpu.VMEM)
    shape = jax.ShapeDtypeStruct
    cos_at, sin_at = position_tables(length)
    return pl.pallas_call(
        open_kernel,
        in_specs=[any_spec] * 4 + [vmem] * 4,
        out_specs=[any_spec] * 10 + [vmem] * 7,
        out_shape=[
            shape((length, width), low),
            shape((length, width), low),
            shape((length, width), low),
            shape((length, width), low),
            shape((length, D), low),
            shape((ATTN_ROWS, D), low),
            shape((D, D), low),
            shape((PLANES, 8, count, PIECE), low),
            shape((length, 128), full),
            shape((length, 128), full),
            shape((16, D), full),
            shape((8, width), full),
            shape((width // 128, 8, length), full),
            shape((rows, D), full),
            shape((rows, D), low),
            shape((rows, D), low),
            shape((8, length), jnp.int32),
        ],
        scratch_shapes=[
            pltpu.VMEM((PLANES, rows, D), low),
            pltpu.VMEM((length, width), low),
            pltpu.VMEM((length, width), low),
            pltpu.VMEM((length, width), low),
            pltpu.VMEM((length, width), low),
            pltpu.VMEM((length, D), low),
            pltpu.VMEM((ATTN_ROWS, D), low),
            pltpu.VMEM((D, D), low),
            pltpu.VMEM((length, 128), full),
            pltpu.VMEM((length, 128), full),
            pltpu.VMEM((width // 128, 128, length), low),
            pltpu.VMEM((8, length), full),
            pltpu.SemaphoreType.DMA((OPEN_COPIES,)),
            pltpu.SemaphoreType.DMA((OPEN_COPIES,)),
            pltpu.SemaphoreType.DMA((14,)),
        ],
        compiler_params=pltpu.CompilerParams(
            vmem_limit_bytes=VMEM_LIMIT, collective_id=1, has_side_effects=True
        ),
        name="opening",
    )(hidden, attn_piece, out_piece, feed_piece, cos_at, sin_at, first_values, seg_row)


def feed_kernel(*refs):
    normed_ref, grad_ref, middle_ref, pieces = refs[:4]
    back_ref, out_ref, made_out = refs[4:7]
    fed, weight, mine, theirs, made, halves, other_halves, send, recv, sem, out_sem, last_sem = refs[7:]
    links = Links(send, recv)
    place = links.place
    core = (flip(links.place, 1), links.depth)
    mine_first, theirs_first = lax.rem(links.place, 2), 1 - lax.rem(links.place, 2)
    count = weight.shape[1] // 3
    rows = normed_ref.shape[0]

    def load(slot):
        own = range(8) if slot == 0 else [2 * piece + mine_first for piece in range(4)]
        return [
            pltpu.make_async_copy(
                pieces.at[slot, piece], weight.at[slot, :, columns_of(piece)], sem.at[slot, index]
            )
            for index, piece in enumerate(own)
        ]

    def flush(which, buffer):
        return [
            pltpu.make_async_copy(
                made.at[buffer, :, pl.ds(piece * PIECE, PIECE)],
                made_out.at[which, piece],
                out_sem.at[buffer, piece],
            )
            for piece in range(4)
        ]

    loads = [load(slot) for slot in range(PLANES - 1)]
    for copies in loads:
        for copy in copies:
            copy.start()
    far = pieces.at[PLANES - 1, place]
    last = halved_spread(links, far, lambda piece: weight.at[PLANES - 1, :, columns_of(piece)])
    last_own = pltpu.make_async_copy(far, weight.at[PLANES - 1, :, columns_of(place)], last_sem)
    crossed = {slot: links.number(4) for slot in range(1, PLANES - 1)}
    landings = {
        slot: [
            weight.at[slot, :, columns_of(2 * piece + theirs_first)] for piece in range(4)
        ]
        for slot in crossed
    }
    last_own.start()
    links.greet(planes=False)
    last.one()
    base = links.number(8)
    for index, ref in enumerate((normed_ref, grad_ref)):
        for piece in range(4):
            links.go(
                base + 4 * index + piece,
                ref.at[:, columns_of(2 * piece + theirs_first)],
                other_halves.at[index, :, pl.ds(piece * PIECE, PIECE)],
                core,
            )
            halves[index, :, pl.ds(piece * PIECE, PIECE)] = ref[:, columns_of(2 * piece + mine_first)]
    for slot, number in crossed.items():
        for piece in range(4):
            own = 2 * piece + mine_first
            links.go(
                number + piece, pieces.at[slot, own], weight.at[slot, :, columns_of(own)], core
            )
    fed[...] = jnp.zeros_like(fed)
    back_ref[...] = jnp.zeros_like(back_ref)
    for index in range(2):
        for piece in range(4):
            links.got(
                base + 4 * index + piece, other_halves.at[index, :, pl.ds(piece * PIECE, PIECE)]
            )
    given = links.number(PLANES)
    hand = lambda slot: links.copy(given + slot, mine.at[lax.rem(slot, 2)], theirs.at[slot], core)
    spans = [pl.ds(index * count, count) for index in range(3)]
    half = rows // 2

    def forward(slot):
        now = lax.rem(slot, 2)
        held = slot

        def ready(which):
            for copy in loads[which]:
                copy.wait()
            if which:
                for piece in range(4):
                    links.got(crossed[which] + piece, landings[which][piece])

        for which in range(PLANES - 1):
            pl.when(slot == which)(functools.partial(ready, which))

        @pl.when(slot == PLANES - 1)
        def _():
            last_own.wait()
            last.end()

        @pl.when(slot >= 2)
        def _():
            hand(slot - 2).wait_send()

        for tile in range(2):
            at = pl.ds(tile * half, half)
            normed, grad = normed_ref[at, :], grad_ref[at, :]
            gates = tokens_dot(weight[held, spans[0], :], normed, 1, 1)
            ups = tokens_dot(weight[held, spans[1], :], normed, 1, 1)
            backs = tokens_dot(weight[held, spans[2], :], grad, 1, 1)
            sig = jax.nn.sigmoid(gates)
            active = gates * sig
            mine[now, 2, :, at] = (active * ups).astype(jnp.bfloat16)
            mine[now, 0, :, at] = (backs * ups * sig * (1.0 + gates * (1.0 - sig))).astype(jnp.bfloat16)
            mine[now, 1, :, at] = (backs * active).astype(jnp.bfloat16)
        hand(slot).start()

        fed[...] += tokens_dot(mine[now, 2], weight[held, spans[2], :], 0, 0)
        back_ref[...] += tokens_dot(mine[now, 0], weight[held, spans[0], :], 0, 0) + tokens_dot(
            mine[now, 1], weight[held, spans[1], :], 0, 0
        )

    def backward(slot):
        now = lax.rem(slot, 2)
        hand(slot).wait_recv()

        @pl.when(slot >= 2)
        def _():
            for copy in flush(slot - 2, now):
                copy.wait()

        def columns(tile, carried):
            lanes = columns_of(tile, 256)
            for index in range(3):
                which = index // 2
                made[now, spans[index], lanes] = (
                    tokens_dot(mine[now, index], halves[which, :, lanes], 1, 0)
                    + tokens_dot(theirs[slot, index], other_halves[which, :, lanes], 1, 0)
                ).astype(jnp.bfloat16)
            return carried

        lax.fori_loop(0, 2, columns, 0)
        for copy in flush(slot, now):
            copy.start()

    def one(step, carried):
        pl.when(step < PLANES)(lambda: forward(step))
        pl.when(step == 0)(last.two)
        pl.when(step == 2)(last.three)
        pl.when(step >= 1)(lambda: backward(step - 1))
        return carried

    lax.fori_loop(0, PLANES + 1, one, 0)
    out_ref[...] = (middle_ref[...] + fed[...]).astype(jnp.bfloat16)
    for slot in (PLANES - 2, PLANES - 1):
        hand(slot).wait_send()
        for copy in flush(slot, slot % 2):
            copy.wait()
    links.drain()


def feed(normed, grad, middle, pieces):
    rows = normed.shape[0]
    count = pieces.shape[2]
    any_spec, vmem = pl.BlockSpec(memory_space=pl.ANY), pl.BlockSpec(memory_space=pltpu.VMEM)
    low = jnp.bfloat16
    return pl.pallas_call(
        feed_kernel,
        in_specs=[vmem, vmem, vmem, any_spec],
        out_specs=[vmem, vmem, any_spec],
        out_shape=[
            jax.ShapeDtypeStruct((rows, D), jnp.float32),
            jax.ShapeDtypeStruct((rows, D), low),
            jax.ShapeDtypeStruct((PLANES, 4, count, PIECE), low),
        ],
        scratch_shapes=[
            pltpu.VMEM((rows, D), jnp.float32),
            pltpu.VMEM((PLANES, count, D), low),
            pltpu.VMEM((2, 3, count // 3, rows), low),
            pltpu.VMEM((PLANES, 3, count // 3, rows), low),
            pltpu.VMEM((2, count, 4 * PIECE), low),
            pltpu.VMEM((2, rows, 4 * PIECE), low),
            pltpu.VMEM((2, rows, 4 * PIECE), low),
            pltpu.SemaphoreType.DMA((34,)),
            pltpu.SemaphoreType.DMA((34,)),
            pltpu.SemaphoreType.DMA((3, 8)),
            pltpu.SemaphoreType.DMA((2, 4)),
            pltpu.SemaphoreType.DMA,
        ],
        compiler_params=pltpu.CompilerParams(
            vmem_limit_bytes=CLOSE_VMEM, collective_id=2, has_side_effects=True
        ),
        name="feed",
    )(normed, grad, middle, pieces)


def add_into(target, source):
    rows = target.shape[0]
    chunk = next(c for c in (352, 256, rows) if rows % c == 0 and c <= rows)

    def one(index, carried):
        span = pl.ds(pl.multiple_of(index * chunk, chunk), chunk)
        target[span, :] = (
            target[span, :].astype(jnp.float32) + source[span, :].astype(jnp.float32)
        ).astype(jnp.bfloat16)
        return carried

    lax.fori_loop(0, rows // chunk, one, 0)


class Fold:
    def __init__(self, links, whole, first, final, bits):
        self.links, self.first, self.final = links, [first.at[m] for m in range(2)], final
        self.base = links.number(3)
        chip = lax.div(links.place, 2)
        ones = lambda bit: lax.rem(lax.div(chip, bit), 2)
        near, far = ones(bits[0]), ones(bits[1])
        self.away = [whole((1 - near) * bits[0] + m * bits[1]) for m in range(2)]
        self.stay = [whole(near * bits[0] + m * bits[1]) for m in range(2)]
        self.near_to = (flip(links.place, 2 * bits[0]), links.depth)
        self.far_to = (flip(links.place, 2 * bits[1]), links.depth)
        self.passed, self.own = first.at[1 - far], first.at[far]

    def one(self):
        for m in range(2):
            self.links.go(self.base + m, self.away[m], self.first[m], self.near_to)

    def two(self, stay=None):
        for m in range(2):
            self.links.got(self.base + m, self.first[m])
            add_into(self.first[m], self.stay[m] if stay is None else stay[m])
        self.links.go(self.base + 2, self.passed, self.final, self.far_to)

    def end(self):
        self.links.got(self.base + 2, self.final)
        add_into(self.final, self.own)


class LineFold:
    def __init__(self, links, block, held):
        self.links = links
        self.held = [[held.at[way, step] for step in range(PLANES - 1)] for way in range(2)]
        self.base = links.number(2 * (PLANES - 1))
        depth = links.depth
        self.blocks, self.sends, self.sums, self.takes, self.to = [], [], [], [], []
        for step in range(1, PLANES):
            right = jnp.minimum(depth + PLANES - step, PLANES - 1)
            left = jnp.maximum(depth - PLANES + step, 0)
            self.blocks.append((block(left), block(right)))
            self.sends.append((depth >= PLANES - step, depth < step))
            self.takes.append(((depth >= PLANES - 1 - step) & (depth < PLANES - 1), (depth <= step) & (depth > 0)))
        self.ends = (depth == PLANES - 1, depth == 0)
        self.to = (
            (links.place, jnp.maximum(depth - 1, 0)),
            (links.place, jnp.minimum(depth + 1, PLANES - 1)),
        )
        self.inner = [
            [self.sends[step][way] & jnp.logical_not(self.ends[way]) for way in range(2)]
            for step in range(PLANES - 1)
        ]
        self.outer = [
            [self.sends[step][way] & self.ends[way] for way in range(2)] for step in range(PLANES - 1)
        ]

    def launch(self, step):
        for way in range(2):
            self.links.go(
                self.base + 2 * (step - 1) + way,
                self.blocks[step - 1][way],
                self.held[way][step - 1],
                self.to[way],
                self.outer[step - 1][way],
            )

    def left(self, step):
        for way in range(2):
            number = self.base + 2 * (step - 1) + way
            block = self.blocks[step - 1][way]
            copy = self.links.copy(number, block, block, self.to[way])
            pl.when(self.outer[step - 1][way])(copy.wait_send)
            self.links.waited.append((number, 0 if way else PLANES - 1))

    def take(self, step):
        for way in range(2):
            self.links.got(
                self.base + 2 * (step - 1) + way, self.held[way][step - 1], self.takes[step - 1][way]
            )

    def forward(self, step):
        for way in range(2):
            before = self.held[way][step - 2]
            block = self.blocks[step - 1][way]

            @pl.when(self.inner[step - 1][way])
            def _():
                add_into(before, block)

            self.links.go(
                self.base + 2 * (step - 1) + way,
                before,
                self.held[way][step - 1],
                self.to[way],
                self.inner[step - 1][way],
            )

    def total(self, own, out):
        depth = self.links.depth
        rows = out.shape[0]
        chunk = next(c for c in (352, 256, rows) if rows % c == 0)

        def one(index, carried):
            span = pl.ds(pl.multiple_of(index * chunk, chunk), chunk)
            value = own[span, :].astype(jnp.float32)
            sides = [self.held[way][PLANES - 2][span, :].astype(jnp.float32) for way in range(2)]
            value = value + jnp.where(depth < PLANES - 1, sides[0], 0.0)
            out[span, :] = value + jnp.where(depth > 0, sides[1], 0.0)
            return carried

        lax.fori_loop(0, rows // chunk, one, 0)


def close_kernel(*refs):
    (made, low_in, attended_in, q_in, k_in, v_in, o_in, n_in, weight_in, cos_in, sin_in) = refs[:11]
    incoming = refs[11:15]
    log_ref, begin_ref, gain_ref, small_in = refs[15:19]
    first_ref, back_ref, feed_total, out_total, attn_total, small_ref = refs[19:25]
    (
        q_ref, k_ref, v_ref, o_ref, weight_ref, cos_ref, sin_ref, grad, inner, total, made_ref,
        stay, feed_first, feed_final, feed_held, out_made, out_core, out_first, out_final, out_held,
        attn_core, attn_first, attn_final, partial, partial_held, small_got,
        send, recv, local,
    ) = refs[25:]
    links = Links(send, recv)
    place, depth = links.place, links.depth
    length = q_ref.shape[0]
    shard = length // PLANES
    parity, chip = lax.rem(place, 2), lax.div(place, 2)
    core = (flip(place, 1), depth)
    loads = []

    def load(source, target):
        copy = pltpu.make_async_copy(source, target, local.at[len(loads)])
        copy.start()
        loads.append(copy)
        return copy

    order = (3, 2, 1, 0)

    def halved_fold(whole, first, final):
        return Halves(
            [
                Fold(
                    links,
                    lambda i, half=half: half_of(whole(i), half),
                    half_of(first, half),
                    half_of(final, half),
                    ((1, 2), (2, 1))[half],
                )
                for half in range(2)
            ]
        )

    folds = {
        slot: halved_fold(
            lambda i, slot=slot: made.at[slot, i], feed_first.at[slot], feed_final.at[slot]
        )
        for slot in order
    }
    out_fold = halved_fold(lambda i: out_core.at[i], out_first, out_final)
    attn_fold = halved_fold(lambda i: attn_core.at[i], attn_first, attn_final)

    def slot_holding(block):
        found = 0
        for plane in range(PLANES):
            for slot, (_, _, held) in enumerate(SLOTS[plane]):
                found = found + jnp.where((depth == plane) & (block == held), slot, 0)
        return found

    feed_line = LineFold(links, lambda j: feed_final.at[slot_holding(j)], feed_held)
    out_line = LineFold(
        links, lambda j: out_final.at[pl.ds(pl.multiple_of(j * 256, 256), 256), :], out_held
    )
    line = LineFold(links, lambda j: partial.at[j], partial_held)
    out_swap, attn_swap = links.number(4), links.number(4)
    sides = [columns_of(2 * i + parity) for i in range(4)]
    others = [columns_of(2 * i + 1 - parity) for i in range(4)]
    across = links.number(2 * PLANES)
    tiny = links.number(6)
    stays = [
        [[half_of(stay.at[index, m], half) for m in range(2)] for half in range(2)] for index in range(2)
    ]
    stay_sems = [[[16 + 4 * index + 2 * half + m for m in range(2)] for half in range(2)] for index in range(2)]

    def restay(slot):
        return [
            pltpu.make_async_copy(
                folds[slot].parts[half].stay[m],
                stays[slot % 2][half][m],
                local.at[stay_sems[slot % 2][half][m]],
            )
            for half in range(2)
            for m in range(2)
        ]

    tiny_to = [core, (flip(place, 2), depth), (flip(place, 4), depth)]
    plane_to = [(place, lax.rem(depth + step, PLANES)) for step in range(1, PLANES)]
    plane_rows = [lax.rem(depth - step + PLANES, PLANES) for step in range(PLANES)]

    attended_ref, low_ref = partial.at[0], partial.at[1]
    first_loads = [load(attended_in, attended_ref), load(low_in, low_ref)]
    for slot in order[:2]:
        for copy in restay(slot):
            copy.start()
    q_loads = [load(source, target) for source, target in ((q_in, q_ref), (k_in, k_ref), (v_in, v_ref), (o_in, o_ref), (cos_in, cos_ref), (sin_in, sin_ref))]
    own_rows = pl.ds(pl.multiple_of(depth * shard, shard), shard)
    q_loads.append(load(incoming[0], grad.at[own_rows, :]))
    weight_load = load(weight_in, weight_ref)

    links.greet()
    for pair in range(2):
        lanes = pl.ds(pair * 128, 128)
        for step in range(1, PLANES):
            links.go(
                across + 4 * pair + step,
                incoming[step].at[:, lanes],
                grad.at[own_rows, lanes],
                plane_to[step - 1],
            )
    folds[3].one()

    for copy in first_loads:
        copy.wait()
    for index in range(4):
        rows = pl.ds(index * 256, 256)
        out_made[rows, :] = tokens_dot(attended_ref[:, rows], low_ref[...], 0, 0).astype(jnp.bfloat16)
    out_swaps = [links.copy(out_swap + i, out_made.at[:, others[i]], out_core.at[i], core) for i in range(4)]
    for copy in out_swaps:
        copy.start()
    for i in range(4):
        links.got(out_swap + i, out_core.at[i])
        add_into(out_core.at[i], out_made.at[:, sides[i]])
    for copy in q_loads:
        copy.wait()

    def fold_two(slot):
        for copy in restay(slot):
            copy.wait()
        folds[slot].two(stays[slot % 2])

    fold_two(3)
    folds[2].one()
    grad_rows = [
        [
            grad.at[pl.ds(pl.multiple_of(plane_rows[step] * shard, shard), shard), pl.ds(pair * 128, 128)]
            for step in range(PLANES)
        ]
        for pair in range(2)
    ]

    def take_grads(pair):
        for step in range(1, PLANES):
            links.got(across + 4 * pair + step, grad_rows[pair][step])

    take_grads(0)

    lane = lax.broadcasted_iota(jnp.int32, (shard, 128), 1)
    keeps = [lane < HD, lane >= HD]
    down = lax.broadcasted_iota(jnp.int32, (shard, shard), 0)
    along = lax.broadcasted_iota(jnp.int32, (1, shard), 1)

    def masked(values, head):
        return jnp.where(keeps[head], values, jnp.zeros_like(values))

    def after_a():
        folds[3].end()
        feed_line.launch(1)
        out_fold.one()

    def after_b():
        fold_two(2)
        folds[1].one()
        for copy in restay(1):
            copy.start()

    def after_c():
        folds[2].end()
        feed_line.launch(2)
        feed_line.take(1)
        feed_line.forward(2)
        out_fold.two()
        take_grads(1)

    def after_d():
        fold_two(1)
        folds[0].one()
        for copy in restay(0):
            copy.start()
        out_fold.end()

    def after_e():
        folds[1].end()
        feed_line.launch(3)
        feed_line.take(2)
        feed_line.forward(3)
        for step in range(1, PLANES):
            out_line.launch(step)

    def back_step(step, carried):
        pair, block = lax.div(step, PLANES), lax.rem(step, PLANES)
        lanes = columns_of(pair)
        start = pl.multiple_of(block * shard, shard)
        own = pl.ds(start, shard)

        @pl.when(block == 0)
        def _():
            total[...] = jnp.zeros_like(total)
            for index in range(PLANES):
                span = pl.ds(index * shard, shard)
                turned = jnp.transpose(
                    grad[span, lanes].astype(jnp.float32) * o_ref[span, lanes].astype(jnp.float32)
                )
                for head in range(2):
                    inner[head : head + 1, span] = jnp.sum(
                        turned[head * HD : head * HD + HD], axis=0, keepdims=True
                    )

        keys, values = k_ref[own, lanes], v_ref[own, lanes]
        own_keys = [masked(keys, head) for head in range(2)]

        def tile(index, sums, visible):
            key_sum, value_sum = sums
            span = pl.ds(pl.multiple_of(index * shard, shard), shard)
            query_block, grad_block = q_ref[span, lanes], grad[span, lanes]
            queries = [masked(query_block, head) for head in range(2)]
            out_grads = [masked(grad_block, head) for head in range(2)]
            scores = [tokens_dot(keys, queries[head], 1, 1) for head in range(2)]
            share_grads = [tokens_dot(values, out_grads[head], 1, 1) for head in range(2)]
            score_grads = []
            for head in range(2):
                shares = jnp.where(
                    visible, jnp.exp2(scores[head] - log_ref[pair, head : head + 1, span]), 0.0
                )
                score_grads.append(
                    (shares * (share_grads[head] - inner[head : head + 1, span])).astype(jnp.bfloat16)
                )
                value_sum = value_sum + tokens_dot(shares.astype(jnp.bfloat16), out_grads[head], 1, 0)
            for head in range(2):
                key_sum = key_sum + tokens_dot(score_grads[head], queries[head], 1, 0)
            total[span, :] += tokens_dot(score_grads[0], own_keys[0], 0, 0) + tokens_dot(
                score_grads[1], own_keys[1], 0, 0
            )
            return (key_sum, value_sum)

        empty = jnp.zeros((shard, 128), jnp.float32)
        sums = tile(
            block, (empty, empty), (down >= begin_ref[0:1, own] - start) & (down <= along)
        )
        key_sum, value_sum = lax.fori_loop(
            block + 1,
            PLANES,
            lambda i, held: tile(
                i,
                held,
                down >= begin_ref[0:1, pl.ds(pl.multiple_of(i * shard, shard), shard)] - start,
            ),
            sums,
        )
        cosine, sine_part = cos_ref[own, :], sin_ref[own, :]
        made_ref[own, columns_of(pair)] = turn(
            total[own, :] * HD**-0.5, cosine, sine_part, False
        ).astype(jnp.bfloat16)
        made_ref[own, columns_of(2 + pair)] = turn(
            key_sum * (1 / LOG2E), cosine, sine_part, False
        ).astype(jnp.bfloat16)
        half_sum = 0.5 * value_sum
        made_ref[own, columns_of(4 + pair)] = half_sum.astype(jnp.bfloat16)
        first_ref[own, lanes] = half_sum
        for when, pump in ((0, after_a), (1, after_b), (3, after_c), (5, after_d), (7, after_e)):
            pl.when(step == when)(pump)
        return carried

    lax.fori_loop(0, 2 * PLANES, back_step, 0)
    quarters = [q_ref, k_ref, v_ref, o_ref]
    quarter_loads = [
        load(n_in.at[:, pl.ds(index * 256, 256)], quarter) for index, quarter in enumerate(quarters)
    ]
    weight_load.wait()
    small_ref[...] = small_in[...]

    def input_back(index, carried):
        block = jnp.where(depth < PLANES // 2, PLANES - 1 - index, index)
        rows = pl.ds(pl.multiple_of(block * shard, shard), shard)
        partial[block] = tokens_dot(made_ref[rows, :], weight_ref[pl.ds(0, 768), :], 1, 0).astype(
            jnp.bfloat16
        )
        return carried

    input_back(0, 0)
    line.launch(1)
    lax.fori_loop(1, PLANES, input_back, 0)
    for copy in quarter_loads:
        copy.wait()

    def gain_back(block, carried):
        rows = pl.ds(pl.multiple_of(block * shard, shard), shard)
        for index, quarter in enumerate(quarters):
            value = partial[block, :, pl.ds(index * 256, 256)].astype(jnp.float32)
            lanes = pl.ds(index * 256, 256)
            gain = (
                jnp.sum(value * quarter[rows, :].astype(jnp.float32), axis=0, keepdims=True)
                / gain_ref[0:1, lanes]
            )
            for half in range(2):
                piece = 2 * index + half
                small_ref[0, piece : piece + 1, :] += gain[:, half * PIECE : half * PIECE + PIECE]
        return carried

    lax.fori_loop(0, PLANES, gain_back, 0)
    fold_two(0)
    out_line.take(1)
    out_line.forward(2)

    links.go(tiny, small_ref.at[0], small_got.at[0], tiny_to[0])
    for copy in out_swaps:
        copy.wait_send()
    attn_made = out_made.at[pl.ds(0, 768), :]
    for index in range(3):
        rows = pl.ds(index * 256, 256)
        for quarter in range(4):
            attn_made[rows, pl.ds(quarter * 256, 256)] = tokens_dot(
                made_ref[:, rows], quarters[quarter][...], 0, 0
            ).astype(jnp.bfloat16)
    for i in range(4):
        links.go(attn_swap + i, attn_made.at[:, others[i]], attn_core.at[i], core)
    links.got(tiny, small_got.at[0])
    small_ref[1] = small_ref[0] + small_got[0]
    links.go(tiny + 1, small_ref.at[1], small_got.at[1], tiny_to[1])
    for i in range(4):
        links.got(attn_swap + i, attn_core.at[i])
        add_into(attn_core.at[i], attn_made.at[:, sides[i]])
    attn_fold.one()
    line.left(1)
    line.launch(2)
    line.take(1)
    line.forward(2)
    links.got(tiny + 1, small_got.at[1])
    small_ref[2] = small_ref[1] + small_got[1]
    links.go(tiny + 2, small_ref.at[2], small_got.at[2], tiny_to[2])
    folds[0].end()
    feed_line.take(3)
    feed_line.total(feed_final.at[0], feed_total)
    out_line.take(2)
    out_line.forward(3)
    attn_fold.two()
    links.got(tiny + 2, small_got.at[2])
    small_ref[3] = small_ref[2] + small_got[2]
    small_place = small_got.at[3 + depth]
    for step in range(1, PLANES):
        links.go(tiny + 2 + step, small_ref.at[3], small_place, plane_to[step - 1])
    small_got[3 + depth] = small_ref[3]
    out_line.take(3)
    out_line.total(out_final.at[pl.ds(pl.multiple_of(depth * 256, 256), 256), :], out_total)
    line.left(2)
    line.launch(3)
    line.take(2)
    line.forward(3)
    attn_fold.end()
    attn_total[...] = attn_final[...].astype(jnp.float32)
    for step in range(1, PLANES):
        links.got(tiny + 2 + step, small_got.at[3 + plane_rows[step]])
    small_ref[4] = small_got[3] + small_got[4] + small_got[5] + small_got[6]
    line.take(3)
    line.total(partial.at[depth], back_ref)
    links.drain()


def closing(made, low_ref, attended_own, heads, normed, weight, tables, incoming, logs, begin_row, gains, small):
    length, width = heads[0].shape
    rows = low_ref.shape[0]
    count = made.shape[2]
    low, full = jnp.bfloat16, jnp.float32
    any_spec, vmem = pl.BlockSpec(memory_space=pl.ANY), pl.BlockSpec(memory_space=pltpu.VMEM)
    shape = jax.ShapeDtypeStruct
    return pl.pallas_call(
        close_kernel,
        in_specs=[any_spec] * 15 + [vmem] * 4,
        out_specs=[vmem] * 6,
        out_shape=[
            shape((length, width), full),
            shape((rows, D), full),
            shape((count, PIECE), full),
            shape((256, PIECE), full),
            shape((768, PIECE), full),
            shape((5, 24, PIECE), full),
        ],
        scratch_shapes=[pltpu.VMEM((length, width), low)] * 4
        + [
            pltpu.VMEM((ATTN_ROWS, D), low),
            pltpu.VMEM((length, 128), full),
            pltpu.VMEM((length, 128), full),
            pltpu.VMEM((length, width), low),
            pltpu.VMEM((8, length), full),
            pltpu.VMEM((length, 128), full),
            pltpu.VMEM((length, 768), low),
            pltpu.VMEM((2, 2, count, PIECE), low),
            pltpu.VMEM((PLANES, 2, count, PIECE), low),
            pltpu.VMEM((PLANES, count, PIECE), low),
            pltpu.VMEM((2, PLANES - 1, count, PIECE), low),
            pltpu.VMEM((D, D), low),
            pltpu.VMEM((4, D, PIECE), low),
            pltpu.VMEM((2, D, PIECE), low),
            pltpu.VMEM((D, PIECE), low),
            pltpu.VMEM((2, PLANES - 1, 256, PIECE), low),
            pltpu.VMEM((4, 768, PIECE), low),
            pltpu.VMEM((2, 768, PIECE), low),
            pltpu.VMEM((768, PIECE), low),
            pltpu.VMEM((PLANES, rows, D), low),
            pltpu.VMEM((2, PLANES - 1, rows, D), low),
            pltpu.VMEM((7, 24, PIECE), full),
            pltpu.SemaphoreType.DMA((CLOSE_COPIES,)),
            pltpu.SemaphoreType.DMA((CLOSE_COPIES,)),
            pltpu.SemaphoreType.DMA((24,)),
        ],
        compiler_params=pltpu.CompilerParams(
            vmem_limit_bytes=CLOSE_VMEM, collective_id=3, has_side_effects=True
        ),
        name="closing",
    )(made, low_ref, attended_own, *heads, normed, weight, *tables, *incoming, logs, begin_row, gains, small)


def middle_back_kernel(*refs):
    middle_ref, grad_ref, back_ref, weight_ref, gain_ref = refs[:5]
    low_ref, dm_ref, gain_grad_ref = refs[5:8]
    outs = refs[8:12]
    depth = lax.axis_index("mp")
    half = middle_ref.shape[0] // 2
    gain = gain_ref[1:2, :]
    gain_grad_ref[...] = jnp.zeros_like(gain_grad_ref)
    for tile in range(2):
        rows = pl.ds(tile * half, half)
        middle, incoming = middle_ref[rows, :], back_ref[rows, :]
        factor = lax.rsqrt(jnp.mean(middle * middle, axis=-1, keepdims=True) + 1e-06)
        scaled = incoming * gain
        mean = jnp.mean(scaled * middle, axis=-1, keepdims=True)
        total = grad_ref[rows, :].astype(jnp.float32) + factor * scaled - middle * (factor**3 * mean)
        gain_grad_ref[0:1, :] += jnp.sum(incoming * middle * factor, axis=0, keepdims=True)
        dm_ref[rows, :] = total
        low_ref[rows, :] = total.astype(jnp.bfloat16)
    for index, out in enumerate(outs):
        owner = lax.rem(depth + index, PLANES)
        rows = pl.ds(pl.multiple_of(owner * 256, 256), 256)
        out[...] = tokens_dot(low_ref[...], weight_ref[rows, :], 1, 1).astype(jnp.bfloat16)


def middle_back(middle, grad, back, weight, gains):
    rows = middle.shape[0]
    return pl.pallas_call(
        middle_back_kernel,
        out_shape=[
            jax.ShapeDtypeStruct((rows, D), jnp.bfloat16),
            jax.ShapeDtypeStruct((rows, D), jnp.float32),
            jax.ShapeDtypeStruct((8, D), jnp.float32),
        ]
        + [jax.ShapeDtypeStruct((rows, 256), jnp.bfloat16)] * PLANES,
        compiler_params=pltpu.CompilerParams(vmem_limit_bytes=VMEM_LIMIT),
        cost_estimate=cost(2 * rows * D * D, 12 << 20),
        name="middle_back",
    )(middle, grad, back, weight, gains)


def stepped(master, gradient, moment, square, step_rate, decay, outs, at):
    new = adamw(master[at], gradient, moment[at], square[at], step_rate, decay)
    for out, value in zip(outs, new):
        out[at] = value


def update_kernel(*refs):
    hidden_ref, dm_ref, back_ref, gain_ref, attn_ref, out_ref, feed_ref, small_ref = refs[:8]
    masters, moments, squares = refs[8:13], refs[13:18], refs[18:23]
    grad_ref, norm_ref = refs[23:25]
    outs = [refs[25 + index : 40 : 5] for index in range(5)]
    place = lax.axis_index("dp")
    hidden = hidden_ref[...].astype(jnp.float32)
    factor = rms_factor(hidden)
    grad_ref[...] = dm_ref[...] + norm_back(hidden, factor, gain_ref[0:1, :], back_ref[...])[0]
    tokens = 8.0 * hidden_ref.shape[0] * PLANES
    norm_ref[...] = jnp.sqrt(small_ref[16:24, :] / (tokens * D))
    every = slice(None)
    rates = (D**-0.5, max(1, 8 * HEADS * HD // LEN) ** -0.5, D**-0.5, (FF // 3) ** -0.5)

    def weight(index, gradient, at):
        stepped(
            masters[index], gradient, moments[index], squares[index], rates[index], 0.1, outs[index], at
        )

    for which in range(3):
        weight(0, jnp.transpose(attn_ref[pl.ds(which * 256, 256), :]), which)
    weight(1, out_ref[...], (every, every))
    count = masters[3].shape[0]
    for which in range(2):
        weight(2, feed_ref[pl.ds(which * count, count), :], which)
    weight(3, feed_ref[pl.ds(2 * count, count), :], (every, every))
    for which in range(2):
        at = pl.ds(which, 1)
        stepped(
            masters[4],
            small_ref[pl.ds(8 * which + place, 1), :],
            moments[4],
            squares[4],
            0.2,
            0.0,
            outs[4],
            (at, every),
        )


def update(hidden, dm, back, gains, totals, small, masters, moments, squares):
    full = jnp.float32
    shape = jax.ShapeDtypeStruct
    return pl.pallas_call(
        update_kernel,
        out_shape=[shape(dm.shape, full), shape((8, PIECE), full)]
        + [shape(one.shape, full) for one in masters] * 3,
        compiler_params=pltpu.CompilerParams(vmem_limit_bytes=VMEM_LIMIT),
        cost_estimate=cost(0, 16 << 20),
        name="update",
    )(hidden, dm, back, gains, *totals, small, *masters, *moments, *squares)


def fast_shards(
    hidden_in,
    segment_ids,
    first_values,
    grad_out,
    input_proj,
    output_proj,
    expand_proj,
    reduce_proj,
    norm_gains,
    old_moment_input,
    old_moment_output,
    old_moment_expand,
    old_moment_reduce,
    old_moment_gains,
    old_square_input,
    old_square_output,
    old_square_expand,
    old_square_reduce,
    old_square_gains,
):
    place, depth = lax.axis_index("dp"), lax.axis_index("mp")
    low = jnp.bfloat16
    hidden, out_cotangent = hidden_in[0], grad_out[0]
    ffs = reduce_proj.shape[0]

    attn_piece = jnp.concatenate(
        [
            input_proj.astype(low).transpose(0, 2, 1).reshape(768, PIECE),
            norm_gains.astype(low),
            jnp.zeros((14, PIECE), low),
        ]
    )
    feed_piece = jnp.concatenate(
        [
            expand_proj.astype(low).transpose(0, 2, 1).reshape(2 * ffs, PIECE),
            reduce_proj.astype(low),
        ]
    )

    (
        queries,
        keys,
        values,
        attended,
        normed,
        attn_weight,
        out_weight,
        feed_all,
        cosine,
        sine_part,
        gains,
        squares,
        logs,
        middle,
        normed_two,
        attended_own,
        begin_row,
    ) = opening(hidden, attn_piece, output_proj.astype(low), feed_piece, first_values[0], segment_ids)
    normed_two_grad, layer_output, made = feed(normed_two, out_cotangent, middle, feed_all)
    layer_output = layer_output[None]
    branch_low, middle_grad, gain_two, *out_grads = middle_back(
        middle, out_cotangent, normed_two_grad, out_weight, gains
    )
    small = jnp.concatenate(
        [
            jnp.zeros((8, PIECE), jnp.float32),
            gain_two[0].reshape(8, PIECE),
            jnp.broadcast_to(jnp.sum(squares[:2], axis=1)[:, None], (2, PIECE)),
            jnp.zeros((6, PIECE), jnp.float32),
        ]
    )
    values_grad, normed_grad, feed_total, out_total, attn_total, small = closing(
        made,
        branch_low,
        attended_own,
        (queries, keys, values, attended),
        normed,
        attn_weight,
        (cosine, sine_part),
        out_grads,
        logs,
        begin_row,
        gains,
        jnp.broadcast_to(small[None], (5, 24, PIECE)),
    )
    small = small[4]
    masters = [input_proj, output_proj, expand_proj, reduce_proj, norm_gains]
    moments = [
        old_moment_input,
        old_moment_output,
        old_moment_expand,
        old_moment_reduce,
        old_moment_gains,
    ]
    squares = [
        old_square_input,
        old_square_output,
        old_square_expand,
        old_square_reduce,
        old_square_gains,
    ]
    for group in (masters, moments, squares):
        group[2] = group[2].transpose(0, 2, 1)
    input_grad, norms, *updated = update(
        hidden,
        middle_grad,
        normed_grad,
        gains,
        (attn_total, out_total, feed_total),
        small,
        masters,
        moments,
        squares,
    )
    for index in (2, 7, 12):
        updated[index] = updated[index].transpose(0, 2, 1)
    return (layer_output, input_grad[None], values_grad[None], norms[:2, 0], *updated)


def solution(mesh):
    quick = mesh.shape["dp"] == 8 and mesh.shape["mp"] == PLANES
    return jax.shard_map(
        fast_shards if quick else shards,
        mesh=mesh,
        in_specs=(
            P("dp", "mp", None),
            P("dp", None),
            P("dp", None, "mp"),
            P("dp", "mp", None),
            P(None, "dp", "mp"),
            P("mp", "dp"),
            P(None, "dp", "mp"),
            P("mp", "dp"),
            P(None, "dp"),
            P(None, "dp", "mp"),
            P("mp", "dp"),
            P(None, "dp", "mp"),
            P("mp", "dp"),
            P(None, "dp"),
            P(None, "dp", "mp"),
            P("mp", "dp"),
            P(None, "dp", "mp"),
            P("mp", "dp"),
            P(None, "dp"),
        ),
        out_specs=(
            P("dp", "mp", None),
            P("dp", "mp", None),
            P("dp", None, "mp"),
            P(),
            P(None, "dp", "mp"),
            P("mp", "dp"),
            P(None, "dp", "mp"),
            P("mp", "dp"),
            P(None, "dp"),
            P(None, "dp", "mp"),
            P("mp", "dp"),
            P(None, "dp", "mp"),
            P("mp", "dp"),
            P(None, "dp"),
            P(None, "dp", "mp"),
            P("mp", "dp"),
            P(None, "dp", "mp"),
            P("mp", "dp"),
            P(None, "dp"),
        ),
        check_vma=False,
    )
```

```python
import functools
import math

import jax
import jax.numpy as jnp
import numpy as np
from jax import lax
from jax.experimental import pallas as pl
from jax.experimental.pallas import tpu as pltpu
from jax.sharding import PartitionSpec as P

D = 1024
HEADS = 16
HD = 64
FF = 2816
LEN = 2048
STEP = 5
PLANES = 4
PIECE = 128
BLOCKS = 4
ATTN_ROWS = 784
VMEM_LIMIT = 56 << 20
OPEN_COPIES = 80
CLOSE_COPIES = 80
CLOSE_VMEM = 60 << 20


def arrivals(plane):
    order = [(0, 0, plane)]
    for hop in range(1, PLANES):
        if plane + hop < PLANES:
            order.append((0, hop, plane + hop))
        if plane - hop >= 0:
            order.append((1, hop, plane - hop))
    return order


SLOTS = [arrivals(plane) for plane in range(PLANES)]


def cost(flops, moved):
    return pl.CostEstimate(flops=flops, bytes_accessed=moved, transcendentals=0)


def rope_tables(seg_row, head_size):
    length = seg_row.shape[0]
    places = jnp.arange(length, dtype=jnp.int32)
    begins = jnp.sum((seg_row[None, :] < seg_row[:, None]).astype(jnp.int32), axis=1)
    offset = (places - begins).astype(jnp.float32)
    inverse_rates = 10000.0 ** (-2.0 * jnp.arange(head_size // 2, dtype=jnp.float32) / head_size)
    angles = offset[:, None] * inverse_rates[None, :]
    return (jnp.cos(angles)[:, None, :], jnp.sin(angles)[:, None, :])


def rotate(values, cosine, sine_part, forward):
    half_size = values.shape[-1] // 2
    first_half = values[..., :half_size]
    second_half = values[..., half_size:]
    if forward:
        return jnp.concatenate(
            [
                first_half * cosine - second_half * sine_part,
                second_half * cosine + first_half * sine_part,
            ],
            axis=-1,
        )
    return jnp.concatenate(
        [
            first_half * cosine + second_half * sine_part,
            second_half * cosine - first_half * sine_part,
        ],
        axis=-1,
    )


def rms_factor(values):
    return lax.rsqrt(jnp.mean(values * values, axis=-1, keepdims=True) + 1e-06)


def norm_back(values, factor, gain_row, incoming):
    scaled = incoming * gain_row
    value_grad = factor * scaled - values * factor**3 * jnp.mean(
        scaled * values, axis=-1, keepdims=True
    )
    gain_grad = jnp.sum(incoming * values * factor, axis=0)
    return (value_grad, gain_grad)


def visible_block(seg_row, first_row, block_rows):
    length = seg_row.shape[0]
    query_seg = lax.dynamic_slice_in_dim(seg_row, first_row, block_rows, 0)
    query_places = first_row + jnp.arange(block_rows, dtype=jnp.int32)
    key_places = jnp.arange(length, dtype=jnp.int32)
    return (query_seg[:, None] == seg_row[None, :]) & (query_places[:, None] >= key_places[None, :])


def block_scores(queries, keys_rot, seg_row, first_row, block_rows, score_scale):
    query_block = lax.dynamic_slice_in_dim(queries, first_row, block_rows, 0)
    visible = visible_block(seg_row, first_row, block_rows)
    scores = (
        jnp.einsum("qhd,khd->hqk", query_block, keys_rot, preferred_element_type=jnp.float32)
        * score_scale
    )
    return (query_block, jnp.where(visible[None], scores, -1e30))


def attend(queries, keys_rot, mixed_values, seg_row, score_scale):
    length = queries.shape[0]
    block_rows = min(512, length)

    def one_block(block_index):
        first_row = block_index * block_rows
        query_block, scores = block_scores(
            queries, keys_rot, seg_row, first_row, block_rows, score_scale
        )
        top_score = jnp.max(scores, axis=-1, keepdims=True)
        raised = jnp.exp(scores - top_score)
        totals = jnp.sum(raised, axis=-1, keepdims=True)
        shares = (raised / totals).astype(jnp.bfloat16)
        combined = jnp.einsum(
            "hqk,khd->qhd", shares, mixed_values, preferred_element_type=jnp.float32
        )
        return (combined, (top_score + jnp.log(totals))[..., 0])

    combined, log_totals = lax.map(one_block, jnp.arange(length // block_rows, dtype=jnp.int32))
    return (combined.reshape(length, -1), log_totals)


def attend_back(queries, keys_rot, mixed_values, out_grad, log_totals, seg_row, score_scale):
    length = queries.shape[0]
    block_rows = min(512, length)

    def one_block(running, operands):
        key_sum, value_sum = running
        block_index, block_totals = operands
        first_row = block_index * block_rows
        query_block, scores = block_scores(
            queries, keys_rot, seg_row, first_row, block_rows, score_scale
        )
        grad_block = lax.dynamic_slice_in_dim(out_grad, first_row, block_rows, 0)
        shares = jnp.exp(scores - block_totals[..., None])
        share_grad = jnp.einsum(
            "qhd,khd->hqk", grad_block, mixed_values, preferred_element_type=jnp.float32
        )
        inner = jnp.sum(shares * share_grad, axis=-1, keepdims=True)
        score_grad = (shares * (share_grad - inner)).astype(jnp.bfloat16)
        query_grad = (
            jnp.einsum("hqk,khd->qhd", score_grad, keys_rot, preferred_element_type=jnp.float32)
            * score_scale
        )
        key_sum = (
            key_sum
            + jnp.einsum(
                "hqk,qhd->khd", score_grad, query_block, preferred_element_type=jnp.float32
            )
            * score_scale
        )
        value_sum = value_sum + jnp.einsum(
            "hqk,qhd->khd",
            shares.astype(jnp.bfloat16),
            grad_block,
            preferred_element_type=jnp.float32,
        )
        return ((key_sum, value_sum), query_grad)

    empty_sum = jnp.zeros(keys_rot.shape, jnp.float32)
    (key_grad, value_grad), query_grad = lax.scan(
        one_block,
        (empty_sum, empty_sum),
        (jnp.arange(length // block_rows, dtype=jnp.int32), log_totals),
    )
    return (query_grad.reshape(keys_rot.shape), key_grad, value_grad)


def adamw(master, gradient, moment, square, step_rate, decay):
    new_moment = 0.5 * moment + 0.5 * gradient
    new_square = 0.5 * square + 0.5 * gradient * gradient
    correct = 1.0 - 0.5**STEP
    update = new_moment / correct / (jnp.sqrt(new_square / correct) + 1e-08)
    return (master - step_rate * (update + decay * master), new_moment, new_square)


def shards(
    hidden_in,
    segment_ids,
    first_values,
    grad_out,
    input_proj,
    output_proj,
    expand_proj,
    reduce_proj,
    norm_gains,
    old_moment_input,
    old_moment_output,
    old_moment_expand,
    old_moment_reduce,
    old_moment_gains,
    old_square_input,
    old_square_output,
    old_square_expand,
    old_square_reduce,
    old_square_gains,
):
    attn_weight, out_weight, expand_weight, reduce_weight, gains_low = (
        lax.all_gather(input_proj.astype(jnp.bfloat16), "dp", axis=1, tiled=True),
        lax.all_gather(output_proj.astype(jnp.bfloat16), "dp", axis=1, tiled=True),
        lax.all_gather(expand_proj.astype(jnp.bfloat16), "dp", axis=1, tiled=True),
        lax.all_gather(reduce_proj.astype(jnp.bfloat16), "dp", axis=1, tiled=True),
        lax.all_gather(norm_gains.astype(jnp.bfloat16), "dp", axis=1, tiled=True),
    )
    gains = gains_low.astype(jnp.float32)
    hidden = hidden_in[0].astype(jnp.float32)
    seg_row = segment_ids[0]
    length = seg_row.shape[0]
    first_in = first_values[0].astype(jnp.float32)
    local_heads = attn_weight.shape[2] // HD
    score_scale = 1.0 / math.sqrt(HD)
    factor_one = rms_factor(hidden)
    normed_one = (hidden * factor_one * gains[0]).astype(jnp.bfloat16)
    all_normed, all_grad_out = (
        lax.all_gather(normed_one, "mp", axis=0, tiled=True),
        lax.all_gather(grad_out[0], "mp", axis=0, tiled=True),
    )
    projected = jnp.einsum(
        "td,cde->cte", all_normed, attn_weight, preferred_element_type=jnp.float32
    )
    cosine, sine_part = rope_tables(seg_row, HD)
    queries = rotate(projected[0].reshape(length, local_heads, HD), cosine, sine_part, True).astype(
        jnp.bfloat16
    )
    keys_rot = rotate(
        projected[1].reshape(length, local_heads, HD), cosine, sine_part, True
    ).astype(jnp.bfloat16)
    blended = 0.5 * projected[2] + 0.5 * first_in
    mixed_values = blended.astype(jnp.bfloat16).reshape(length, local_heads, HD)
    square_terms = jnp.stack([jnp.sum(first_in * first_in), jnp.sum(blended * blended)])
    attended, log_totals = attend(queries, keys_rot, mixed_values, seg_row, score_scale)
    attended_low = attended.astype(jnp.bfloat16)
    rows_part = attended_low
    branch = lax.psum_scatter(
        jnp.dot(rows_part, out_weight, preferred_element_type=jnp.float32),
        "mp",
        scatter_dimension=0,
        tiled=True,
    )
    middle = hidden + branch
    factor_two = rms_factor(middle)
    normed_two = (middle * factor_two * gains[1]).astype(jnp.bfloat16)
    all_normed_two = lax.all_gather(normed_two, "mp", axis=0, tiled=True)
    gate_up = jnp.einsum(
        "td,cdf->ctf", all_normed_two, expand_weight, preferred_element_type=jnp.float32
    )
    gate_sig = jax.nn.sigmoid(gate_up[0])
    gate_act = gate_up[0] * gate_sig
    activated = (gate_act * gate_up[1]).astype(jnp.bfloat16)
    rows_part = activated
    feed_out = lax.psum_scatter(
        jnp.dot(rows_part, reduce_weight, preferred_element_type=jnp.float32).astype(jnp.bfloat16),
        "mp",
        scatter_dimension=0,
        tiled=True,
    ).astype(jnp.float32)
    layer_output = (middle + feed_out).astype(jnp.bfloat16)[None]
    hidden_grad = jnp.einsum(
        "td,fd->tf", all_grad_out, reduce_weight, preferred_element_type=jnp.float32
    )
    reduce_grad = jnp.einsum(
        "tf,td->fd", activated, all_grad_out, preferred_element_type=jnp.float32
    )
    gate_grad = hidden_grad * gate_up[1] * gate_sig * (1.0 + gate_up[0] * (1.0 - gate_sig))
    up_grad = hidden_grad * gate_act
    pair_grad = jnp.stack([gate_grad, up_grad]).astype(jnp.bfloat16)
    expand_grad = jnp.einsum(
        "ctf,td->cdf", pair_grad, all_normed_two, preferred_element_type=jnp.float32
    )
    rows_part = pair_grad
    normed_two_grad = lax.psum_scatter(
        jnp.einsum(
            "ctf,cdf->td", rows_part, expand_weight, preferred_element_type=jnp.float32
        ).astype(jnp.bfloat16),
        "mp",
        scatter_dimension=0,
        tiled=True,
    ).astype(jnp.float32)
    middle_part, gain_two_grad = norm_back(middle, factor_two, gains[1], normed_two_grad)
    middle_grad = grad_out[0].astype(jnp.float32) + middle_part
    branch_low = middle_grad.astype(jnp.bfloat16)
    all_branch = lax.all_gather(branch_low, "mp", axis=0, tiled=True)
    out_grad = jnp.einsum("te,td->ed", attended_low, all_branch, preferred_element_type=jnp.float32)
    attended_grad = jnp.einsum(
        "td,ed->te", all_branch, out_weight, preferred_element_type=jnp.float32
    ).astype(jnp.bfloat16)
    query_grad, key_grad, mix_grad = attend_back(
        queries,
        keys_rot,
        mixed_values,
        attended_grad.reshape(length, local_heads, HD),
        log_totals,
        seg_row,
        score_scale,
    )
    query_grad = rotate(query_grad, cosine, sine_part, False).reshape(length, -1)
    key_grad = rotate(key_grad, cosine, sine_part, False).reshape(length, -1)
    mix_grad = mix_grad.reshape(length, -1)
    values_grad = (0.5 * mix_grad)[None]
    proj_grad = jnp.stack([query_grad, key_grad, 0.5 * mix_grad]).astype(jnp.bfloat16)
    attn_grad = jnp.einsum("cte,td->cde", proj_grad, all_normed, preferred_element_type=jnp.float32)
    rows_part = proj_grad
    normed_one_grad = lax.psum_scatter(
        jnp.einsum(
            "cte,cde->td", rows_part, attn_weight, preferred_element_type=jnp.float32
        ).astype(jnp.bfloat16),
        "mp",
        scatter_dimension=0,
        tiled=True,
    ).astype(jnp.float32)
    input_part, gain_one_grad = norm_back(hidden, factor_one, gains[0], normed_one_grad)
    input_grad = (middle_grad + input_part)[None]
    attn_total, out_total, expand_total, reduce_total = (
        lax.psum_scatter(
            attn_grad.astype(jnp.bfloat16), "dp", scatter_dimension=1, tiled=True
        ).astype(jnp.float32),
        lax.psum_scatter(
            out_grad.astype(jnp.bfloat16), "dp", scatter_dimension=1, tiled=True
        ).astype(jnp.float32),
        lax.psum_scatter(
            expand_grad.astype(jnp.bfloat16), "dp", scatter_dimension=1, tiled=True
        ).astype(jnp.float32),
        lax.psum_scatter(
            reduce_grad.astype(jnp.bfloat16), "dp", scatter_dimension=1, tiled=True
        ).astype(jnp.float32),
    )
    gain_totals, square_sums = lax.psum(
        (jnp.stack([gain_one_grad, gain_two_grad]), square_terms), ("dp", "mp")
    )
    gain_width = norm_gains.shape[1]
    gain_total = lax.dynamic_slice_in_dim(
        gain_totals, lax.axis_index("dp") * gain_width, gain_width, 1
    )
    value_norms = jnp.sqrt(square_sums / (lax.axis_size("dp") * length * D))
    new_input = adamw(input_proj, attn_total, old_moment_input, old_square_input, D ** (-0.5), 0.1)
    new_output = adamw(
        output_proj,
        out_total,
        old_moment_output,
        old_square_output,
        max(1, 8 * HEADS * HD // LEN) ** (-0.5),
        0.1,
    )
    new_expand = adamw(
        expand_proj, expand_total, old_moment_expand, old_square_expand, D ** (-0.5), 0.1
    )
    new_reduce = adamw(
        reduce_proj, reduce_total, old_moment_reduce, old_square_reduce, (FF // 3) ** (-0.5), 0.1
    )
    new_gains = adamw(norm_gains, gain_total, old_moment_gains, old_square_gains, 0.2, 0.0)
    return (
        layer_output,
        input_grad,
        values_grad,
        value_norms,
        new_input[0],
        new_output[0],
        new_expand[0],
        new_reduce[0],
        new_gains[0],
        new_input[1],
        new_output[1],
        new_expand[1],
        new_reduce[1],
        new_gains[1],
        new_input[2],
        new_output[2],
        new_expand[2],
        new_reduce[2],
        new_gains[2],
    )


def tokens_dot(a, b, left, right):
    return lax.dot_general(a, b, (((left,), (right,)), ((), ())), preferred_element_type=jnp.float32)


def piece_columns(place, step):
    start = jnp.bitwise_xor(place, step) * PIECE
    return pl.ds(pl.multiple_of(start, PIECE), PIECE)


def turn(values, cosine, sine_part, forward):
    lane = lax.broadcasted_iota(jnp.int32, values.shape, 1)
    swapped = jnp.where(
        lax.rem(lane, HD) < HD // 2, pltpu.roll(values, 96, 1), pltpu.roll(values, 32, 1)
    )
    if forward:
        return values * cosine + swapped * sine_part
    return values * cosine - swapped * sine_part


MESH = pl.DeviceIdType.MESH
LOG2E = 1.4426950408889634


def flip(place, bit):
    return place + bit - 2 * bit * lax.rem(lax.div(place, bit), 2)


def at_plane(depth, values):
    found = 0
    for plane, value in enumerate(values):
        found = found + jnp.where(depth == plane, value, 0)
    return found


def slot_at(depth, way, hop):
    return at_plane(
        depth,
        [
            next((k for k, s in enumerate(SLOTS[plane]) if s[:2] == (way, hop)), 0)
            for plane in range(PLANES)
        ],
    )


def columns_of(piece, width=PIECE):
    return pl.ds(pl.multiple_of(piece * width, width), width)


class Links:
    def __init__(self, send, recv):
        self.send, self.recv, self.count, self.started, self.waited = send, recv, 0, [], []
        self.place, self.depth = lax.axis_index("dp"), lax.axis_index("mp")

    def number(self, count=1):
        self.count += count
        return self.count - count

    def copy(self, number, source, target, to):
        return pltpu.make_async_remote_copy(
            src_ref=source,
            dst_ref=target,
            send_sem=self.send.at[number],
            recv_sem=self.recv.at[number],
            device_id=to,
            device_id_type=MESH,
        )

    def go(self, number, source, target, to, when=None):
        copy = self.copy(number, source, target, to)
        self.started.append((number, source, target, to, when))
        if when is None:
            copy.start()
        else:
            pl.when(when)(copy.start)

    def got(self, number, landed, when=None):
        copy = self.copy(number, landed, landed, (flip(self.place, 1), self.depth))
        if when is None:
            copy.wait_recv()
        else:
            pl.when(when)(copy.wait_recv)

    def drain(self):
        for *parts, when in self.started:
            copy = self.copy(*parts)
            for plane in [plane for number, plane in self.waited if number == parts[0]]:
                when = when & (self.depth != plane)
            if when is None:
                copy.wait_send()
            else:
                pl.when(when)(copy.wait_send)

    def greet(self, planes=True):
        barrier = pltpu.get_barrier_semaphore()
        others = [(flip(self.place, bit), self.depth) for bit in (1, 2, 4)]
        if planes:
            others += [(self.place, lax.rem(self.depth + step, PLANES)) for step in range(1, PLANES)]
        for other in others:
            pl.semaphore_signal(barrier, inc=1, device_id=other, device_id_type=MESH)
        pl.semaphore_wait(barrier, len(others))


class Spread:
    def __init__(self, links, own, spot, bits):
        self.links, self.own = links, own
        self.base = links.number(7)
        place = links.place
        first, second = flip(place, bits[0]), flip(place, bits[1])
        self.spots = [spot(piece) for piece in (place, first, second, flip(first, bits[1]))]
        self.lands = [
            spot(flip(piece, 1)) for piece in (place, first, second, flip(first, bits[1]))
        ]
        self.near, self.far, self.core = [
            (flip(place, bit), links.depth) for bit in (bits[0], bits[1], 1)
        ]

    def one(self):
        self.links.go(self.base, self.own, self.spots[0], self.near)

    def two(self):
        links, spots = self.links, self.spots
        links.go(self.base + 1, self.own, spots[0], self.far)
        links.got(self.base, spots[1])
        links.go(self.base + 2, spots[1], spots[1], self.far)

    def landed(self):
        self.links.got(self.base + 1, self.spots[2])
        self.links.got(self.base + 2, self.spots[3])

    def three(self):
        links, spots = self.links, self.spots
        links.go(self.base + 3, self.own, spots[0], self.core)
        links.go(self.base + 4, spots[1], spots[1], self.core)
        links.got(self.base + 1, spots[2])
        links.go(self.base + 5, spots[2], spots[2], self.core)
        links.got(self.base + 2, spots[3])
        links.go(self.base + 6, spots[3], spots[3], self.core)

    def end(self):
        for index, land in enumerate(self.lands):
            self.links.got(self.base + 3 + index, land)


class Halves:
    def __init__(self, parts):
        self.parts = parts

    def one(self):
        for part in self.parts:
            part.one()

    def two(self, *given):
        for index, part in enumerate(self.parts):
            part.two(*[one[index] for one in given])

    def landed(self):
        for part in self.parts:
            part.landed()

    def three(self):
        for part in self.parts:
            part.three()

    def end(self):
        for part in self.parts:
            part.end()


def half_of(ref, half):
    rows = ref.shape[-2] // 2
    lead = (slice(None),) * (len(ref.shape) - 2)
    return ref.at[(*lead, pl.ds(half * rows, rows), slice(None))]


def halved_spread(links, own, spot):
    return Halves(
        [
            Spread(
                links,
                half_of(own, half),
                lambda piece, half=half: half_of(spot(piece), half),
                ((2, 4), (4, 2))[half],
            )
            for half in range(2)
        ]
    )


class Relay:
    def __init__(self, links, own, put):
        self.links, self.own, self.put = links, own, put
        self.base = links.number(2 * (PLANES - 1))
        self.waited = links.waited

    def plan(self, hop, only=None):
        links, depth = self.links, self.links.depth
        planned = []
        for way in range(2):
            to = depth + (1 if way else -1)
            when = (
                (depth >= hop - 1) & (depth < PLANES - 1)
                if way
                else (depth <= PLANES - hop) & (depth > 0)
            )
            if only is not None:
                when = when & (depth == only[way])
            source = self.own if hop == 1 else self.put(depth, way, hop - 1)
            planned.append(
                (
                    self.base + 2 * (hop - 1) + way,
                    source,
                    self.put(to, way, hop),
                    (links.place, jnp.clip(to, 0, PLANES - 1)),
                    when,
                )
            )
        return planned

    def send(self, hop, only=None):
        for parts in self.plan(hop, only):
            self.links.go(*parts)

    def take(self, hop, only=None):
        links, depth = self.links, self.links.depth
        for way in range(2):
            when = depth >= hop if way else depth + hop < PLANES
            if only is not None:
                when = when & (depth == only[way])
            links.got(self.base + 2 * (hop - 1) + way, self.put(depth, way, hop), when)

    def left(self, hop, only):
        links, depth = self.links, self.links.depth
        for way in range(2):
            source = self.own if hop == 1 else self.put(depth, way, hop - 1)
            to = (links.place, jnp.clip(depth + (1 if way else -1), 0, PLANES - 1))
            copy = links.copy(self.base + 2 * (hop - 1) + way, source, source, to)
            pl.when(depth == only[way])(copy.wait_send)
            self.waited.append((self.base + 2 * (hop - 1) + way, only[way]))


def position_tables(length):
    rates = 10000.0 ** (-2.0 * np.arange(HD // 2) / HD)
    angles = np.arange(length)[:, None] * rates[None, :]
    cosine, sine = np.cos(angles), np.sin(angles)
    return (
        jnp.asarray(np.concatenate([cosine] * 4, axis=1), jnp.float32),
        jnp.asarray(np.concatenate([-sine, sine, -sine, sine], axis=1), jnp.float32),
    )


def rope_tables_from(seg_ref, cos_at, sin_at, cos_ref, sin_ref, begin_ref, marks):
    length = cos_at.shape[0]
    segs = seg_ref[0:1, :].astype(jnp.float32)
    spots = lax.broadcasted_iota(jnp.int32, (1, length), 1).astype(jnp.float32)
    begins = jnp.zeros((1, length), jnp.float32)
    marks[...] = jnp.zeros_like(marks)
    for number in range(7):
        start = jnp.sum(jnp.where(segs < number, 1.0, 0.0), axis=1, keepdims=True)
        begins = jnp.where(segs == number, start, begins)
        marks[number : number + 1, :] = jnp.where(spots == start, 1.0, 0.0)
    begin_ref[...] = jnp.broadcast_to(begins.astype(jnp.int32), begin_ref.shape)
    pick = lambda table: lax.dot_general(
        marks[...],
        table[...],
        (((1,), (0,)), ((), ())),
        precision=lax.Precision.HIGHEST,
        preferred_element_type=jnp.float32,
    )
    first_cos, first_sin = pick(cos_at), pick(sin_at)
    rows = length // PLANES
    for block in range(PLANES):
        span = pl.ds(block * rows, rows)
        documents = jnp.transpose(
            jnp.broadcast_to(segs[:, block * rows : block * rows + rows], (128, rows))
        )
        cosine = jnp.zeros((rows, 128), jnp.float32)
        sine = jnp.zeros((rows, 128), jnp.float32)
        for number in range(7):
            here = documents == number
            cosine = jnp.where(here, first_cos[number : number + 1], cosine)
            sine = jnp.where(here, first_sin[number : number + 1], sine)
        cos_ref[span, :] = cos_at[span, :] * cosine + sin_at[span, :] * sine
        sin_ref[span, :] = sin_at[span, :] * cosine - cos_at[span, :] * sine


def open_kernel(*refs):
    hidden, attn_piece, out_piece, feed_piece, cos_at, sin_at, first_ref, seg_ref = refs[:8]
    q_out, k_out, v_out, o_out, n_out, weight_out, out_weight_out, feed_all, cos_out, sin_out = refs[8:18]
    gain_ref, square_ref, log_ref, middle_ref, normed_ref, attended_ref, begin_ref = refs[18:25]
    held, q_ref, k_ref, v_ref, o_ref, n_ref, weight_ref, out_ref, cos_ref, sin_ref, turned_v, marks = refs[25:37]
    send, recv, local = refs[37:]
    links = Links(send, recv)
    place, depth = links.place, links.depth
    shard = hidden.shape[0]
    stores = []

    def store(source, target):
        copy = pltpu.make_async_copy(source, target, local.at[len(stores)])
        copy.start()
        stores.append(copy)
        return copy

    block_at = lambda plane, way, hop: jnp.clip(plane + (-hop if way else hop), 0, PLANES - 1)
    wide = Relay(links, hidden, lambda plane, way, hop: held.at[block_at(plane, way, hop)])
    out_rows = lambda block: out_ref.at[
        pl.ds(pl.multiple_of(block * 256, 256), 256), columns_of(place)
    ]
    thin = Relay(links, out_piece, lambda plane, way, hop: out_rows(block_at(plane, way, hop)))
    feeds = Relay(
        links,
        feed_piece,
        lambda plane, way, hop: feed_all.at[slot_at(plane, way, hop), place],
    )
    attn = Spread(links, attn_piece, lambda piece: weight_ref.at[:, columns_of(piece)], (2, 4))
    outs = Spread(
        links, out_ref.at[:, columns_of(place)], lambda piece: out_ref.at[:, columns_of(piece)], (2, 4)
    )
    slots = [
        halved_spread(
            links,
            feed_piece if slot == 0 else feed_all.at[slot, place],
            lambda piece, slot=slot: feed_all.at[slot, piece],
        )
        for slot in range(PLANES - 1)
    ]
    across = links.number(PLANES)

    links.greet()
    thin.send(1)
    wide.send(1)
    attn.one()
    own_hidden = store(hidden, held.at[depth])
    own_attn = store(attn_piece, weight_ref.at[:, columns_of(place)])
    own_out = store(out_piece, out_rows(depth))
    own_feed = store(feed_piece, feed_all.at[0, place])
    square_ref[...] = jnp.zeros_like(square_ref)
    attn.two()
    attn.three()
    slots[0].one()
    rope_tables_from(seg_ref, cos_at, sin_at, cos_ref, sin_ref, begin_ref, marks)
    attn.end()
    for copy in (own_hidden, own_attn, own_out, own_feed):
        copy.wait()
    store(weight_ref, weight_out)
    store(cos_ref, cos_out)
    store(sin_ref, sin_out)
    gain_ref[...] = weight_ref[pl.ds(768, 16), :].astype(jnp.float32)

    def project(block):
        rows = pl.ds(pl.multiple_of(block * shard, shard), shard)
        values = held[block].astype(jnp.float32)
        factor = lax.rsqrt(jnp.mean(values * values, axis=-1, keepdims=True) + 1e-06)
        normed = (values * factor * gain_ref[0:1, :]).astype(jnp.bfloat16)
        n_ref[rows, :] = normed
        cosine, sine_part = cos_ref[rows, :], sin_ref[rows, :]
        query = tokens_dot(normed, weight_ref[pl.ds(0, 256), :], 1, 1)
        key = tokens_dot(normed, weight_ref[pl.ds(256, 256), :], 1, 1)
        value = tokens_dot(normed, weight_ref[pl.ds(512, 256), :], 1, 1)
        for half in range(2):
            lanes = slice(half * 128, half * 128 + 128)
            turned = turn(query[:, lanes], cosine, sine_part, True)
            q_ref[rows, lanes] = (turned * (HD**-0.5 * LOG2E)).astype(jnp.bfloat16)
            k_ref[rows, lanes] = turn(key[:, lanes], cosine, sine_part, True).astype(jnp.bfloat16)
        first = first_ref[rows, :].astype(jnp.float32)
        blended = 0.5 * value + 0.5 * first
        v_ref[rows, :] = blended.astype(jnp.bfloat16)
        for half in range(2):
            turned_v[half, :, rows] = jnp.transpose(
                blended[:, half * 128 : half * 128 + 128]
            ).astype(jnp.bfloat16)
        square_ref[0:1, :] += jnp.sum(first * first, axis=0, keepdims=True)
        square_ref[1:2, :] += jnp.sum(blended * blended, axis=0, keepdims=True)

    def project_hop(hop):
        def one(side, carried):
            block = depth + hop * (2 * side - 1)
            pl.when((block >= 0) & (block < PLANES))(lambda: project(block))
            return carried

        lax.fori_loop(0, 2, one, 0)

    ends, inner = (PLANES - 1, 0), (PLANES - 2, 1)
    project(depth)
    wide.take(1)
    wide.send(2)
    feeds.send(1, ends)
    thin.take(1)
    thin.send(2)
    slots[0].two()
    project_hop(1)
    wide.take(2)
    wide.send(3)
    feeds.take(1, inner)
    feeds.send(1, inner)
    feeds.send(2, inner)
    thin.take(2)
    thin.send(3)
    project_hop(2)
    slots[0].three()
    wide.take(3)
    wide.left(3, (1, PLANES - 2))
    feeds.take(1, (1, PLANES - 2))
    feeds.take(2, (1, PLANES - 2))
    feeds.send(1, (1, PLANES - 2))
    second = feeds.plan(2, (1, PLANES - 2))
    thin.take(3)
    outs.one()
    project_hop(3)
    store(n_ref, n_out)
    store(q_ref, q_out)
    store(k_ref, k_out)
    store(v_ref, v_out)

    lane = lax.broadcasted_iota(jnp.int32, (shard, 128), 1)
    down = lax.broadcasted_iota(jnp.int32, (shard, shard), 0)
    along = lax.broadcasted_iota(jnp.int32, (1, shard), 1)

    def flash_block(block):
        rows = pl.ds(pl.multiple_of(block * shard, shard), shard)
        begin = begin_ref[0:1, rows]
        pairs = [q_ref[rows, pl.ds(pair * 128, 128)] for pair in range(2)]
        parts = [
            jnp.where((lane < HD) == (head % 2 == 0), pairs[head // 2], jnp.zeros_like(pairs[0]))
            for head in range(4)
        ]

        def tile(index, carried, visible):
            span = pl.ds(pl.multiple_of(index * shard, shard), shard)
            raw = [
                tokens_dot(k_ref[span, pl.ds(head // 2 * 128, 128)], parts[head], 1, 1)
                for head in range(4)
            ]
            after = []
            for head in range(4):
                top, total, summed = carried[3 * head : 3 * head + 3]
                scores = jnp.where(visible, raw[head], -1e30)
                raised_top = jnp.maximum(top, jnp.max(scores, axis=0, keepdims=True))
                shrink = jnp.exp2(top - raised_top)
                shares = jnp.exp2(scores - raised_top)
                total = total * shrink + jnp.sum(shares, axis=0, keepdims=True)
                values = turned_v[head // 2, pl.ds(head % 2 * HD, HD), span]
                summed = summed * shrink + tokens_dot(values, shares.astype(jnp.bfloat16), 1, 0)
                after += [raised_top, total, summed]
            return tuple(after)

        fresh = (
            jnp.full((1, shard), -1e30, jnp.float32),
            jnp.zeros((1, shard), jnp.float32),
            jnp.zeros((HD, shard), jnp.float32),
        )
        carried = tile(block, fresh * 4, (down >= begin - block * shard) & (down <= along))
        carried = lax.fori_loop(
            0, block, lambda j, held: tile(j, held, down >= begin - j * shard), carried
        )
        for pair in range(2):
            ends = [carried[3 * (2 * pair + head) : 3 * (2 * pair + head) + 3] for head in range(2)]
            both = jnp.concatenate([summed / total for _, total, summed in ends], axis=0)
            o_ref[rows, pl.ds(pair * 128, 128)] = jnp.transpose(both).astype(jnp.bfloat16)
            for head, (top, total, _) in enumerate(ends):
                log_ref[pair, head : head + 1, rows] = top + jnp.log2(total)

    own_columns = attended_ref.at[:, columns_of(depth, 256)]

    def hand(step):
        block = lax.rem(depth + step, PLANES)
        rows = pl.ds(pl.multiple_of(block * shard, shard), shard)
        return links.copy(across + step, o_ref.at[rows, :], own_columns, (place, block))

    near = (0, PLANES - 1)

    def pump_a():
        feeds.take(1, near)
        slots[1].one()
        outs.two()

    def pump_b():
        slots[1].two()
        slots[0].end()
        feeds.left(1, (1, PLANES - 2))
        for parts in second:
            links.go(*parts)

    def pump_c():
        feeds.take(2, near)
        slots[2].one()
        outs.three()

    pumps = ((0, pump_a), (1, pump_b), (2, pump_c))

    def flash(index, carried):
        step = PLANES - 1 - index
        flash_block(lax.rem(depth + step, PLANES))
        pl.when(step > 0)(lambda: hand(step).start())
        for when, pump in pumps:
            pl.when(index == when)(pump)
        return carried

    lax.fori_loop(0, PLANES, flash, 0)
    feeds.send(3, (1, PLANES - 2))
    own_rows = pl.ds(pl.multiple_of(depth * shard, shard), shard)
    attended_ref[:, columns_of(depth, 256)] = o_ref[own_rows, :]
    store(o_ref, o_out)
    outs.end()
    store(out_ref, out_weight_out)
    slots[2].two()
    for step in range(1, PLANES):
        source = lax.rem(depth - step + PLANES, PLANES)
        links.got(across + step, attended_ref.at[:, columns_of(source, 256)])
    half = shard // 2
    for part in range(2):
        rows = pl.ds(part * half, half)
        middle = held[depth, rows, :].astype(jnp.float32) + tokens_dot(
            attended_ref[rows, :], out_ref[...], 1, 0
        )
        middle_ref[rows, :] = middle
        factor = lax.rsqrt(jnp.mean(middle * middle, axis=-1, keepdims=True) + 1e-06)
        normed_ref[rows, :] = (middle * factor * gain_ref[1:2, :]).astype(jnp.bfloat16)
    slots[1].landed()
    slots[2].landed()
    feeds.take(3)
    for step in range(1, PLANES):
        hand(step).wait_send()
    links.drain()
    for copy in stores[4:]:
        copy.wait()


def opening(hidden, attn_piece, out_piece, feed_piece, first_values, seg_row):
    length, width = first_values.shape
    rows = hidden.shape[0]
    count = feed_piece.shape[0]
    low, full = jnp.bfloat16, jnp.float32
    any_spec, vmem = pl.BlockSpec(memory_space=pl.ANY), pl.BlockSpec(memory_space=pltpu.VMEM)
    shape = jax.ShapeDtypeStruct
    cos_at, sin_at = position_tables(length)
    return pl.pallas_call(
        open_kernel,
        in_specs=[any_spec] * 4 + [vmem] * 4,
        out_specs=[any_spec] * 10 + [vmem] * 7,
        out_shape=[
            shape((length, width), low),
            shape((length, width), low),
            shape((length, width), low),
            shape((length, width), low),
            shape((length, D), low),
            shape((ATTN_ROWS, D), low),
            shape((D, D), low),
            shape((PLANES, 8, count, PIECE), low),
            shape((length, 128), full),
            shape((length, 128), full),
            shape((16, D), full),
            shape((8, width), full),
            shape((width // 128, 8, length), full),
            shape((rows, D), full),
            shape((rows, D), low),
            shape((rows, D), low),
            shape((8, length), jnp.int32),
        ],
        scratch_shapes=[
            pltpu.VMEM((PLANES, rows, D), low),
            pltpu.VMEM((length, width), low),
            pltpu.VMEM((length, width), low),
            pltpu.VMEM((length, width), low),
            pltpu.VMEM((length, width), low),
            pltpu.VMEM((length, D), low),
            pltpu.VMEM((ATTN_ROWS, D), low),
            pltpu.VMEM((D, D), low),
            pltpu.VMEM((length, 128), full),
            pltpu.VMEM((length, 128), full),
            pltpu.VMEM((width // 128, 128, length), low),
            pltpu.VMEM((8, length), full),
            pltpu.SemaphoreType.DMA((OPEN_COPIES,)),
            pltpu.SemaphoreType.DMA((OPEN_COPIES,)),
            pltpu.SemaphoreType.DMA((14,)),
        ],
        compiler_params=pltpu.CompilerParams(
            vmem_limit_bytes=VMEM_LIMIT, collective_id=1, has_side_effects=True
        ),
        name="opening",
    )(hidden, attn_piece, out_piece, feed_piece, cos_at, sin_at, first_values, seg_row)


def feed_kernel(*refs):
    normed_ref, grad_ref, middle_ref, pieces = refs[:4]
    back_ref, out_ref, made_out = refs[4:7]
    fed, weight, mine, theirs, made, halves, other_halves, send, recv, sem, out_sem, last_sem = refs[7:]
    links = Links(send, recv)
    place = links.place
    core = (flip(links.place, 1), links.depth)
    mine_first, theirs_first = lax.rem(links.place, 2), 1 - lax.rem(links.place, 2)
    count = weight.shape[1] // 3
    rows = normed_ref.shape[0]

    def load(slot):
        own = range(8) if slot == 0 else [2 * piece + mine_first for piece in range(4)]
        return [
            pltpu.make_async_copy(
                pieces.at[slot, piece], weight.at[slot, :, columns_of(piece)], sem.at[slot, index]
            )
            for index, piece in enumerate(own)
        ]

    def flush(which, buffer):
        return [
            pltpu.make_async_copy(
                made.at[buffer, :, pl.ds(piece * PIECE, PIECE)],
                made_out.at[which, piece],
                out_sem.at[buffer, piece],
            )
            for piece in range(4)
        ]

    loads = [load(slot) for slot in range(PLANES - 1)]
    for copies in loads:
        for copy in copies:
            copy.start()
    far = pieces.at[PLANES - 1, place]
    last = halved_spread(links, far, lambda piece: weight.at[PLANES - 1, :, columns_of(piece)])
    last_own = pltpu.make_async_copy(far, weight.at[PLANES - 1, :, columns_of(place)], last_sem)
    crossed = {slot: links.number(4) for slot in range(1, PLANES - 1)}
    landings = {
        slot: [
            weight.at[slot, :, columns_of(2 * piece + theirs_first)] for piece in range(4)
        ]
        for slot in crossed
    }
    last_own.start()
    links.greet(planes=False)
    last.one()
    base = links.number(8)
    for index, ref in enumerate((normed_ref, grad_ref)):
        for piece in range(4):
            links.go(
                base + 4 * index + piece,
                ref.at[:, columns_of(2 * piece + theirs_first)],
                other_halves.at[index, :, pl.ds(piece * PIECE, PIECE)],
                core,
            )
            halves[index, :, pl.ds(piece * PIECE, PIECE)] = ref[:, columns_of(2 * piece + mine_first)]
    for slot, number in crossed.items():
        for piece in range(4):
            own = 2 * piece + mine_first
            links.go(
                number + piece, pieces.at[slot, own], weight.at[slot, :, columns_of(own)], core
            )
    fed[...] = jnp.zeros_like(fed)
    back_ref[...] = jnp.zeros_like(back_ref)
    for index in range(2):
        for piece in range(4):
            links.got(
                base + 4 * index + piece, other_halves.at[index, :, pl.ds(piece * PIECE, PIECE)]
            )
    given = links.number(PLANES)
    hand = lambda slot: links.copy(given + slot, mine.at[lax.rem(slot, 2)], theirs.at[slot], core)
    spans = [pl.ds(index * count, count) for index in range(3)]
    half = rows // 2

    def forward(slot):
        now = lax.rem(slot, 2)
        held = slot

        def ready(which):
            for copy in loads[which]:
                copy.wait()
            if which:
                for piece in range(4):
                    links.got(crossed[which] + piece, landings[which][piece])

        for which in range(PLANES - 1):
            pl.when(slot == which)(functools.partial(ready, which))

        @pl.when(slot == PLANES - 1)
        def _():
            last_own.wait()
            last.end()

        @pl.when(slot >= 2)
        def _():
            hand(slot - 2).wait_send()

        for tile in range(2):
            at = pl.ds(tile * half, half)
            normed, grad = normed_ref[at, :], grad_ref[at, :]
            gates = tokens_dot(weight[held, spans[0], :], normed, 1, 1)
            ups = tokens_dot(weight[held, spans[1], :], normed, 1, 1)
            backs = tokens_dot(weight[held, spans[2], :], grad, 1, 1)
            sig = jax.nn.sigmoid(gates)
            active = gates * sig
            mine[now, 2, :, at] = (active * ups).astype(jnp.bfloat16)
            mine[now, 0, :, at] = (backs * ups * sig * (1.0 + gates * (1.0 - sig))).astype(jnp.bfloat16)
            mine[now, 1, :, at] = (backs * active).astype(jnp.bfloat16)
        hand(slot).start()

        fed[...] += tokens_dot(mine[now, 2], weight[held, spans[2], :], 0, 0)
        back_ref[...] += tokens_dot(mine[now, 0], weight[held, spans[0], :], 0, 0) + tokens_dot(
            mine[now, 1], weight[held, spans[1], :], 0, 0
        )

    def backward(slot):
        now = lax.rem(slot, 2)
        hand(slot).wait_recv()

        @pl.when(slot >= 2)
        def _():
            for copy in flush(slot - 2, now):
                copy.wait()

        def columns(tile, carried):
            lanes = columns_of(tile, 256)
            for index in range(3):
                which = index // 2
                made[now, spans[index], lanes] = (
                    tokens_dot(mine[now, index], halves[which, :, lanes], 1, 0)
                    + tokens_dot(theirs[slot, index], other_halves[which, :, lanes], 1, 0)
                ).astype(jnp.bfloat16)
            return carried

        lax.fori_loop(0, 2, columns, 0)
        for copy in flush(slot, now):
            copy.start()

    def one(step, carried):
        pl.when(step < PLANES)(lambda: forward(step))
        pl.when(step == 0)(last.two)
        pl.when(step == 2)(last.three)
        pl.when(step >= 1)(lambda: backward(step - 1))
        return carried

    lax.fori_loop(0, PLANES + 1, one, 0)
    out_ref[...] = (middle_ref[...] + fed[...]).astype(jnp.bfloat16)
    for slot in (PLANES - 2, PLANES - 1):
        hand(slot).wait_send()
        for copy in flush(slot, slot % 2):
            copy.wait()
    links.drain()


def feed(normed, grad, middle, pieces):
    rows = normed.shape[0]
    count = pieces.shape[2]
    any_spec, vmem = pl.BlockSpec(memory_space=pl.ANY), pl.BlockSpec(memory_space=pltpu.VMEM)
    low = jnp.bfloat16
    return pl.pallas_call(
        feed_kernel,
        in_specs=[vmem, vmem, vmem, any_spec],
        out_specs=[vmem, vmem, any_spec],
        out_shape=[
            jax.ShapeDtypeStruct((rows, D), jnp.float32),
            jax.ShapeDtypeStruct((rows, D), low),
            jax.ShapeDtypeStruct((PLANES, 4, count, PIECE), low),
        ],
        scratch_shapes=[
            pltpu.VMEM((rows, D), jnp.float32),
            pltpu.VMEM((PLANES, count, D), low),
            pltpu.VMEM((2, 3, count // 3, rows), low),
            pltpu.VMEM((PLANES, 3, count // 3, rows), low),
            pltpu.VMEM((2, count, 4 * PIECE), low),
            pltpu.VMEM((2, rows, 4 * PIECE), low),
            pltpu.VMEM((2, rows, 4 * PIECE), low),
            pltpu.SemaphoreType.DMA((34,)),
            pltpu.SemaphoreType.DMA((34,)),
            pltpu.SemaphoreType.DMA((3, 8)),
            pltpu.SemaphoreType.DMA((2, 4)),
            pltpu.SemaphoreType.DMA,
        ],
        compiler_params=pltpu.CompilerParams(
            vmem_limit_bytes=CLOSE_VMEM, collective_id=2, has_side_effects=True
        ),
        name="feed",
    )(normed, grad, middle, pieces)


def add_into(target, source):
    rows = target.shape[0]
    chunk = next(c for c in (352, 256, rows) if rows % c == 0 and c <= rows)

    def one(index, carried):
        span = pl.ds(pl.multiple_of(index * chunk, chunk), chunk)
        target[span, :] = (
            target[span, :].astype(jnp.float32) + source[span, :].astype(jnp.float32)
        ).astype(jnp.bfloat16)
        return carried

    lax.fori_loop(0, rows // chunk, one, 0)


class Fold:
    def __init__(self, links, whole, first, final, bits):
        self.links, self.first, self.final = links, [first.at[m] for m in range(2)], final
        self.base = links.number(3)
        chip = lax.div(links.place, 2)
        ones = lambda bit: lax.rem(lax.div(chip, bit), 2)
        near, far = ones(bits[0]), ones(bits[1])
        self.away = [whole((1 - near) * bits[0] + m * bits[1]) for m in range(2)]
        self.stay = [whole(near * bits[0] + m * bits[1]) for m in range(2)]
        self.near_to = (flip(links.place, 2 * bits[0]), links.depth)
        self.far_to = (flip(links.place, 2 * bits[1]), links.depth)
        self.passed, self.own = first.at[1 - far], first.at[far]

    def one(self):
        for m in range(2):
            self.links.go(self.base + m, self.away[m], self.first[m], self.near_to)

    def two(self, stay=None):
        for m in range(2):
            self.links.got(self.base + m, self.first[m])
            add_into(self.first[m], self.stay[m] if stay is None else stay[m])
        self.links.go(self.base + 2, self.passed, self.final, self.far_to)

    def end(self):
        self.links.got(self.base + 2, self.final)
        add_into(self.final, self.own)


class LineFold:
    def __init__(self, links, block, held):
        self.links = links
        self.held = [[held.at[way, step] for step in range(PLANES - 1)] for way in range(2)]
        self.base = links.number(2 * (PLANES - 1))
        depth = links.depth
        self.blocks, self.sends, self.sums, self.takes, self.to = [], [], [], [], []
        for step in range(1, PLANES):
            right = jnp.minimum(depth + PLANES - step, PLANES - 1)
            left = jnp.maximum(depth - PLANES + step, 0)
            self.blocks.append((block(left), block(right)))
            self.sends.append((depth >= PLANES - step, depth < step))
            self.takes.append(((depth >= PLANES - 1 - step) & (depth < PLANES - 1), (depth <= step) & (depth > 0)))
        self.ends = (depth == PLANES - 1, depth == 0)
        self.to = (
            (links.place, jnp.maximum(depth - 1, 0)),
            (links.place, jnp.minimum(depth + 1, PLANES - 1)),
        )
        self.inner = [
            [self.sends[step][way] & jnp.logical_not(self.ends[way]) for way in range(2)]
            for step in range(PLANES - 1)
        ]
        self.outer = [
            [self.sends[step][way] & self.ends[way] for way in range(2)] for step in range(PLANES - 1)
        ]

    def launch(self, step):
        for way in range(2):
            self.links.go(
                self.base + 2 * (step - 1) + way,
                self.blocks[step - 1][way],
                self.held[way][step - 1],
                self.to[way],
                self.outer[step - 1][way],
            )

    def outer_plan(self, step):
        return [
            (
                self.base + 2 * (step - 1) + way,
                self.blocks[step - 1][way],
                self.held[way][step - 1],
                self.to[way],
                self.outer[step - 1][way],
            )
            for way in range(2)
        ]

    def go_all(self, planned):
        for parts in planned:
            self.links.go(*parts)

    def take(self, step):
        for way in range(2):
            self.links.got(
                self.base + 2 * (step - 1) + way, self.held[way][step - 1], self.takes[step - 1][way]
            )

    def forward(self, step):
        for way in range(2):
            before = self.held[way][step - 2]
            block = self.blocks[step - 1][way]

            @pl.when(self.inner[step - 1][way])
            def _():
                add_into(before, block)

            self.links.go(
                self.base + 2 * (step - 1) + way,
                before,
                self.held[way][step - 1],
                self.to[way],
                self.inner[step - 1][way],
            )

    def total(self, own, out):
        depth = self.links.depth
        rows = out.shape[0]
        chunk = next(c for c in (352, 256, rows) if rows % c == 0)

        def one(index, carried):
            span = pl.ds(pl.multiple_of(index * chunk, chunk), chunk)
            value = own[span, :].astype(jnp.float32)
            sides = [self.held[way][PLANES - 2][span, :].astype(jnp.float32) for way in range(2)]
            value = value + jnp.where(depth < PLANES - 1, sides[0], 0.0)
            out[span, :] = value + jnp.where(depth > 0, sides[1], 0.0)
            return carried

        lax.fori_loop(0, rows // chunk, one, 0)


def close_kernel(*refs):
    (made, low_in, attended_in, q_in, k_in, v_in, o_in, n_in, weight_in, cos_in, sin_in) = refs[:11]
    incoming = refs[11:15]
    log_ref, begin_ref, gain_ref, small_in = refs[15:19]
    first_ref, back_ref, feed_total, out_total, attn_total, small_ref = refs[19:25]
    (
        q_ref, k_ref, v_ref, o_ref, weight_ref, cos_ref, sin_ref, grad, inner, query_acc, key_acc, made_ref,
        stay, feed_first, feed_final, feed_held, out_made, out_core, out_first, out_final, out_held,
        attn_core, attn_first, attn_final, partial, partial_held, small_got,
        send, recv, local,
    ) = refs[25:]
    links = Links(send, recv)
    place, depth = links.place, links.depth
    length = q_ref.shape[0]
    shard = length // PLANES
    parity, chip = lax.rem(place, 2), lax.div(place, 2)
    core = (flip(place, 1), depth)
    loads = []

    def load(source, target):
        copy = pltpu.make_async_copy(source, target, local.at[len(loads)])
        copy.start()
        loads.append(copy)
        return copy

    order = (3, 2, 1, 0)

    def halved_fold(whole, first, final):
        return Halves(
            [
                Fold(
                    links,
                    lambda i, half=half: half_of(whole(i), half),
                    half_of(first, half),
                    half_of(final, half),
                    ((1, 2), (2, 1))[half],
                )
                for half in range(2)
            ]
        )

    folds = {
        slot: halved_fold(
            lambda i, slot=slot: made.at[slot, i], feed_first.at[slot], feed_final.at[slot]
        )
        for slot in order
    }
    out_fold = halved_fold(lambda i: out_core.at[i], out_first, out_final)
    attn_fold = halved_fold(lambda i: attn_core.at[i], attn_first, attn_final)

    def slot_holding(block):
        found = 0
        for plane in range(PLANES):
            for slot, (_, _, held) in enumerate(SLOTS[plane]):
                found = found + jnp.where((depth == plane) & (block == held), slot, 0)
        return found

    feed_line = LineFold(links, lambda j: feed_final.at[slot_holding(j)], feed_held)
    out_line = LineFold(
        links, lambda j: out_final.at[pl.ds(pl.multiple_of(j * 256, 256), 256), :], out_held
    )
    line = LineFold(links, lambda j: partial.at[j], partial_held)
    out_swap, attn_swap = links.number(4), links.number(4)
    sides = [columns_of(2 * i + parity) for i in range(4)]
    others = [columns_of(2 * i + 1 - parity) for i in range(4)]
    across = links.number(2 * PLANES)
    tiny = links.number(6)
    stays = [
        [[half_of(stay.at[index, m], half) for m in range(2)] for half in range(2)] for index in range(2)
    ]
    stay_sems = [[[16 + 4 * index + 2 * half + m for m in range(2)] for half in range(2)] for index in range(2)]

    def restay(slot):
        return [
            pltpu.make_async_copy(
                folds[slot].parts[half].stay[m],
                stays[slot % 2][half][m],
                local.at[stay_sems[slot % 2][half][m]],
            )
            for half in range(2)
            for m in range(2)
        ]

    tiny_to = [core, (flip(place, 2), depth), (flip(place, 4), depth)]
    plane_to = [(place, lax.rem(depth + step, PLANES)) for step in range(1, PLANES)]
    plane_rows = [lax.rem(depth - step + PLANES, PLANES) for step in range(PLANES)]

    attended_ref, low_ref = partial.at[0], partial.at[1]
    first_loads = [load(attended_in, attended_ref), load(low_in, low_ref)]
    for slot in order[:2]:
        for copy in restay(slot):
            copy.start()
    q_loads = [load(source, target) for source, target in ((q_in, q_ref), (k_in, k_ref), (v_in, v_ref), (o_in, o_ref), (cos_in, cos_ref), (sin_in, sin_ref))]
    own_rows = pl.ds(pl.multiple_of(depth * shard, shard), shard)
    q_loads.append(load(incoming[0], grad.at[own_rows, :]))
    weight_load = load(weight_in, weight_ref)

    links.greet()
    for pair in range(2):
        lanes = pl.ds(pair * 128, 128)
        for step in range(1, PLANES):
            links.go(
                across + 4 * pair + step,
                incoming[step].at[:, lanes],
                grad.at[own_rows, lanes],
                plane_to[step - 1],
            )
    folds[3].one()

    for copy in first_loads:
        copy.wait()
    for index in range(4):
        rows = pl.ds(index * 256, 256)
        out_made[rows, :] = tokens_dot(attended_ref[:, rows], low_ref[...], 0, 0).astype(jnp.bfloat16)
    out_swaps = [links.copy(out_swap + i, out_made.at[:, others[i]], out_core.at[i], core) for i in range(4)]
    for copy in out_swaps:
        copy.start()
    for i in range(4):
        links.got(out_swap + i, out_core.at[i])
        add_into(out_core.at[i], out_made.at[:, sides[i]])
    for copy in q_loads:
        copy.wait()

    def fold_two(slot):
        for copy in restay(slot):
            copy.wait()
        folds[slot].two(stays[slot % 2])

    fold_two(3)
    folds[2].one()
    grad_rows = [
        [
            grad.at[pl.ds(pl.multiple_of(plane_rows[step] * shard, shard), shard), pl.ds(pair * 128, 128)]
            for step in range(PLANES)
        ]
        for pair in range(2)
    ]

    def take_grads(pair):
        for step in range(1, PLANES):
            links.got(across + 4 * pair + step, grad_rows[pair][step])

    take_grads(0)

    lane = lax.broadcasted_iota(jnp.int32, (shard, 128), 1)
    keeps = [lane < HD, lane >= HD]
    down = lax.broadcasted_iota(jnp.int32, (shard, shard), 0)
    along = lax.broadcasted_iota(jnp.int32, (1, shard), 1)

    def masked(values, head):
        return jnp.where(keeps[head], values, jnp.zeros_like(values))

    def after_a():
        folds[3].end()
        feed_line.launch(1)
        out_fold.one()

    def after_b():
        fold_two(2)
        folds[1].one()
        for copy in restay(1):
            copy.start()

    def after_c():
        folds[2].end()
        feed_line.launch(2)
        feed_line.take(1)
        feed_line.forward(2)
        out_fold.two()

    def after_d():
        fold_two(1)
        folds[0].one()
        for copy in restay(0):
            copy.start()
        out_fold.end()
        for step in range(1, PLANES):
            out_line.launch(step)

    def after_e():
        folds[1].end()
        feed_line.launch(3)

    weight_load.wait()
    lower = depth < PLANES // 2
    query_acc[...] = jnp.zeros_like(query_acc)
    key_acc[...] = jnp.zeros_like(key_acc)
    first_ref[...] = jnp.zeros_like(first_ref)
    launches = [line.outer_plan(step) for step in range(1, PLANES)]

    def rows_of(block):
        return pl.ds(pl.multiple_of(block * shard, shard), shard)

    def back_step(index, carried):
        stage, pair = lax.div(index, 2), lax.rem(index, 2)
        block = jnp.where(lower, PLANES - 1 - stage, stage)
        lanes = columns_of(pair)
        own = rows_of(block)

        @pl.when(stage == 0)
        def _():
            for other in range(PLANES):
                span = pl.ds(other * shard, shard)
                turned = jnp.transpose(
                    grad[span, lanes].astype(jnp.float32) * o_ref[span, lanes].astype(jnp.float32)
                )
                for head in range(2):
                    inner[pair, head : head + 1, span] = jnp.sum(
                        turned[head * HD : head * HD + HD], axis=0, keepdims=True
                    )

        def tile(query_rows, key_rows, visible):
            keys, values = k_ref[key_rows, lanes], v_ref[key_rows, lanes]
            query_block, grad_block = q_ref[query_rows, lanes], grad[query_rows, lanes]
            queries = [masked(query_block, head) for head in range(2)]
            out_grads = [masked(grad_block, head) for head in range(2)]
            scores = [tokens_dot(keys, queries[head], 1, 1) for head in range(2)]
            share_grads = [tokens_dot(values, out_grads[head], 1, 1) for head in range(2)]
            score_grads, value_sum, key_sum = [], 0.0, 0.0
            for head in range(2):
                shares = jnp.where(
                    visible,
                    jnp.exp2(scores[head] - log_ref[pair, head : head + 1, query_rows]),
                    0.0,
                )
                score_grads.append(
                    (shares * (share_grads[head] - inner[pair, head : head + 1, query_rows])).astype(
                        jnp.bfloat16
                    )
                )
                value_sum = value_sum + tokens_dot(shares.astype(jnp.bfloat16), out_grads[head], 1, 0)
            for head in range(2):
                key_sum = key_sum + tokens_dot(score_grads[head], queries[head], 1, 0)
            first_ref[key_rows, lanes] += value_sum
            key_acc[key_rows, lanes] += key_sum
            query_acc[query_rows, lanes] += tokens_dot(
                score_grads[0], masked(keys, 0), 0, 0
            ) + tokens_dot(score_grads[1], masked(keys, 1), 0, 0)

        def off(other, held):
            query = rows_of(jnp.where(lower, block, block + 1 + other))
            key_block = jnp.where(lower, other, block)
            tile(query, rows_of(key_block), down >= begin_ref[0:1, query] - key_block * shard)
            return held

        tile(own, own, (down >= begin_ref[0:1, own] - block * shard) & (down <= along))
        lax.fori_loop(0, PLANES - 1 - stage, off, 0)
        cosine, sine_part = cos_ref[own, :], sin_ref[own, :]
        made_ref[own, columns_of(pair)] = turn(
            query_acc[own, lanes] * HD**-0.5, cosine, sine_part, False
        ).astype(jnp.bfloat16)
        made_ref[own, columns_of(2 + pair)] = turn(
            key_acc[own, lanes] * (1 / LOG2E), cosine, sine_part, False
        ).astype(jnp.bfloat16)
        half_sum = 0.5 * first_ref[own, lanes]
        made_ref[own, columns_of(4 + pair)] = half_sum.astype(jnp.bfloat16)
        first_ref[own, lanes] = half_sum

        @pl.when(pair == 1)
        def _():
            partial[block] = tokens_dot(
                made_ref[own, :], weight_ref[pl.ds(0, 768), :], 1, 0
            ).astype(jnp.bfloat16)
            for number, parts in enumerate(launches):
                pl.when(stage == number)(functools.partial(line.go_all, parts))

        pl.when(index == 0)(lambda: take_grads(1))
        for when, pump in ((0, after_a), (1, after_b), (2, after_c), (4, after_d), (7, after_e)):
            pl.when(index == when)(pump)
        return carried

    lax.fori_loop(0, 2 * PLANES, back_step, 0)
    quarters = [q_ref, k_ref, v_ref, o_ref]
    quarter_loads = [
        load(n_in.at[:, pl.ds(index * 256, 256)], quarter) for index, quarter in enumerate(quarters)
    ]
    small_ref[...] = small_in[...]
    line.take(1)
    line.forward(2)
    for copy in quarter_loads:
        copy.wait()

    def gain_back(block, carried):
        rows = pl.ds(pl.multiple_of(block * shard, shard), shard)
        for index, quarter in enumerate(quarters):
            value = partial[block, :, pl.ds(index * 256, 256)].astype(jnp.float32)
            lanes = pl.ds(index * 256, 256)
            gain = (
                jnp.sum(value * quarter[rows, :].astype(jnp.float32), axis=0, keepdims=True)
                / gain_ref[0:1, lanes]
            )
            for half in range(2):
                piece = 2 * index + half
                small_ref[0, piece : piece + 1, :] += gain[:, half * PIECE : half * PIECE + PIECE]
        return carried

    lax.fori_loop(0, PLANES, gain_back, 0)
    fold_two(0)
    links.go(tiny, small_ref.at[0], small_got.at[0], tiny_to[0])
    feed_line.take(2)
    feed_line.forward(3)
    for copy in out_swaps:
        copy.wait_send()
    attn_made = out_made.at[pl.ds(0, 768), :]
    for index in range(3):
        rows = pl.ds(index * 256, 256)
        for quarter in range(4):
            attn_made[rows, pl.ds(quarter * 256, 256)] = tokens_dot(
                made_ref[:, rows], quarters[quarter][...], 0, 0
            ).astype(jnp.bfloat16)
    for i in range(4):
        links.go(attn_swap + i, attn_made.at[:, others[i]], attn_core.at[i], core)
    links.got(tiny, small_got.at[0])
    small_ref[1] = small_ref[0] + small_got[0]
    links.go(tiny + 1, small_ref.at[1], small_got.at[1], tiny_to[1])
    for i in range(4):
        links.got(attn_swap + i, attn_core.at[i])
        add_into(attn_core.at[i], attn_made.at[:, sides[i]])
    attn_fold.one()
    links.got(tiny + 1, small_got.at[1])
    small_ref[2] = small_ref[1] + small_got[1]
    links.go(tiny + 2, small_ref.at[2], small_got.at[2], tiny_to[2])
    line.take(2)
    line.forward(3)
    links.got(tiny + 2, small_got.at[2])
    small_ref[3] = small_ref[2] + small_got[2]
    small_place = small_got.at[3 + depth]
    for step in range(1, PLANES):
        links.go(tiny + 2 + step, small_ref.at[3], small_place, plane_to[step - 1])
    small_got[3 + depth] = small_ref[3]
    out_line.take(1)
    out_line.forward(2)
    attn_fold.two()
    folds[0].end()
    out_line.take(2)
    out_line.forward(3)
    attn_fold.end()
    attn_total[...] = attn_final[...].astype(jnp.float32)
    line.take(3)
    line.total(partial.at[depth], back_ref)
    feed_line.take(3)
    feed_line.total(feed_final.at[0], feed_total)
    out_line.take(3)
    out_line.total(out_final.at[pl.ds(pl.multiple_of(depth * 256, 256), 256), :], out_total)
    for step in range(1, PLANES):
        links.got(tiny + 2 + step, small_got.at[3 + plane_rows[step]])
    small_ref[4] = small_got[3] + small_got[4] + small_got[5] + small_got[6]
    links.drain()


def closing(made, low_ref, attended_own, heads, normed, weight, tables, incoming, logs, begin_row, gains, small):
    length, width = heads[0].shape
    rows = low_ref.shape[0]
    count = made.shape[2]
    low, full = jnp.bfloat16, jnp.float32
    any_spec, vmem = pl.BlockSpec(memory_space=pl.ANY), pl.BlockSpec(memory_space=pltpu.VMEM)
    shape = jax.ShapeDtypeStruct
    return pl.pallas_call(
        close_kernel,
        in_specs=[any_spec] * 15 + [vmem] * 4,
        out_specs=[vmem] * 6,
        out_shape=[
            shape((length, width), full),
            shape((rows, D), full),
            shape((count, PIECE), full),
            shape((256, PIECE), full),
            shape((768, PIECE), full),
            shape((5, 24, PIECE), full),
        ],
        scratch_shapes=[pltpu.VMEM((length, width), low)] * 4
        + [
            pltpu.VMEM((ATTN_ROWS, D), low),
            pltpu.VMEM((length, 128), full),
            pltpu.VMEM((length, 128), full),
            pltpu.VMEM((length, width), low),
            pltpu.VMEM((2, 8, length), full),
            pltpu.VMEM((length, width), full),
            pltpu.VMEM((length, width), full),
            pltpu.VMEM((length, 768), low),
            pltpu.VMEM((2, 2, count, PIECE), low),
            pltpu.VMEM((PLANES, 2, count, PIECE), low),
            pltpu.VMEM((PLANES, count, PIECE), low),
            pltpu.VMEM((2, PLANES - 1, count, PIECE), low),
            pltpu.VMEM((D, D), low),
            pltpu.VMEM((4, D, PIECE), low),
            pltpu.VMEM((2, D, PIECE), low),
            pltpu.VMEM((D, PIECE), low),
            pltpu.VMEM((2, PLANES - 1, 256, PIECE), low),
            pltpu.VMEM((4, 768, PIECE), low),
            pltpu.VMEM((2, 768, PIECE), low),
            pltpu.VMEM((768, PIECE), low),
            pltpu.VMEM((PLANES, rows, D), low),
            pltpu.VMEM((2, PLANES - 1, rows, D), low),
            pltpu.VMEM((7, 24, PIECE), full),
            pltpu.SemaphoreType.DMA((CLOSE_COPIES,)),
            pltpu.SemaphoreType.DMA((CLOSE_COPIES,)),
            pltpu.SemaphoreType.DMA((24,)),
        ],
        compiler_params=pltpu.CompilerParams(
            vmem_limit_bytes=CLOSE_VMEM, collective_id=3, has_side_effects=True
        ),
        name="closing",
    )(made, low_ref, attended_own, *heads, normed, weight, *tables, *incoming, logs, begin_row, gains, small)


def middle_back_kernel(*refs):
    middle_ref, grad_ref, back_ref, weight_ref, gain_ref = refs[:5]
    low_ref, dm_ref, gain_grad_ref = refs[5:8]
    outs = refs[8:12]
    depth = lax.axis_index("mp")
    half = middle_ref.shape[0] // 2
    gain = gain_ref[1:2, :]
    gain_grad_ref[...] = jnp.zeros_like(gain_grad_ref)
    for tile in range(2):
        rows = pl.ds(tile * half, half)
        middle, incoming = middle_ref[rows, :], back_ref[rows, :]
        factor = lax.rsqrt(jnp.mean(middle * middle, axis=-1, keepdims=True) + 1e-06)
        scaled = incoming * gain
        mean = jnp.mean(scaled * middle, axis=-1, keepdims=True)
        total = grad_ref[rows, :].astype(jnp.float32) + factor * scaled - middle * (factor**3 * mean)
        gain_grad_ref[0:1, :] += jnp.sum(incoming * middle * factor, axis=0, keepdims=True)
        dm_ref[rows, :] = total
        low_ref[rows, :] = total.astype(jnp.bfloat16)
    for index, out in enumerate(outs):
        owner = lax.rem(depth + index, PLANES)
        rows = pl.ds(pl.multiple_of(owner * 256, 256), 256)
        out[...] = tokens_dot(low_ref[...], weight_ref[rows, :], 1, 1).astype(jnp.bfloat16)


def middle_back(middle, grad, back, weight, gains):
    rows = middle.shape[0]
    return pl.pallas_call(
        middle_back_kernel,
        out_shape=[
            jax.ShapeDtypeStruct((rows, D), jnp.bfloat16),
            jax.ShapeDtypeStruct((rows, D), jnp.float32),
            jax.ShapeDtypeStruct((8, D), jnp.float32),
        ]
        + [jax.ShapeDtypeStruct((rows, 256), jnp.bfloat16)] * PLANES,
        compiler_params=pltpu.CompilerParams(vmem_limit_bytes=VMEM_LIMIT),
        cost_estimate=cost(2 * rows * D * D, 12 << 20),
        name="middle_back",
    )(middle, grad, back, weight, gains)


def stepped(master, gradient, moment, square, step_rate, decay, outs, at):
    new = adamw(master[at], gradient, moment[at], square[at], step_rate, decay)
    for out, value in zip(outs, new):
        out[at] = value


def update_kernel(*refs):
    hidden_ref, dm_ref, back_ref, gain_ref, attn_ref, out_ref, feed_ref, small_ref = refs[:8]
    masters, moments, squares = refs[8:13], refs[13:18], refs[18:23]
    grad_ref, norm_ref = refs[23:25]
    outs = [refs[25 + index : 40 : 5] for index in range(5)]
    place = lax.axis_index("dp")
    hidden = hidden_ref[...].astype(jnp.float32)
    factor = rms_factor(hidden)
    grad_ref[...] = dm_ref[...] + norm_back(hidden, factor, gain_ref[0:1, :], back_ref[...])[0]
    tokens = 8.0 * hidden_ref.shape[0] * PLANES
    norm_ref[...] = jnp.sqrt(small_ref[16:24, :] / (tokens * D))
    every = slice(None)
    rates = (D**-0.5, max(1, 8 * HEADS * HD // LEN) ** -0.5, D**-0.5, (FF // 3) ** -0.5)

    def weight(index, gradient, at):
        stepped(
            masters[index], gradient, moments[index], squares[index], rates[index], 0.1, outs[index], at
        )

    for which in range(3):
        weight(0, jnp.transpose(attn_ref[pl.ds(which * 256, 256), :]), which)
    weight(1, out_ref[...], (every, every))
    count = masters[3].shape[0]
    for which in range(2):
        weight(2, feed_ref[pl.ds(which * count, count), :], which)
    weight(3, feed_ref[pl.ds(2 * count, count), :], (every, every))
    for which in range(2):
        at = pl.ds(which, 1)
        stepped(
            masters[4],
            small_ref[pl.ds(8 * which + place, 1), :],
            moments[4],
            squares[4],
            0.2,
            0.0,
            outs[4],
            (at, every),
        )


def update(hidden, dm, back, gains, totals, small, masters, moments, squares):
    full = jnp.float32
    shape = jax.ShapeDtypeStruct
    return pl.pallas_call(
        update_kernel,
        out_shape=[shape(dm.shape, full), shape((8, PIECE), full)]
        + [shape(one.shape, full) for one in masters] * 3,
        compiler_params=pltpu.CompilerParams(vmem_limit_bytes=VMEM_LIMIT),
        cost_estimate=cost(0, 16 << 20),
        name="update",
    )(hidden, dm, back, gains, *totals, small, *masters, *moments, *squares)


def fast_shards(
    hidden_in,
    segment_ids,
    first_values,
    grad_out,
    input_proj,
    output_proj,
    expand_proj,
    reduce_proj,
    norm_gains,
    old_moment_input,
    old_moment_output,
    old_moment_expand,
    old_moment_reduce,
    old_moment_gains,
    old_square_input,
    old_square_output,
    old_square_expand,
    old_square_reduce,
    old_square_gains,
):
    place, depth = lax.axis_index("dp"), lax.axis_index("mp")
    low = jnp.bfloat16
    hidden, out_cotangent = hidden_in[0], grad_out[0]
    ffs = reduce_proj.shape[0]

    attn_piece = jnp.concatenate(
        [
            input_proj.astype(low).transpose(0, 2, 1).reshape(768, PIECE),
            norm_gains.astype(low),
            jnp.zeros((14, PIECE), low),
        ]
    )
    feed_piece = jnp.concatenate(
        [
            expand_proj.astype(low).transpose(0, 2, 1).reshape(2 * ffs, PIECE),
            reduce_proj.astype(low),
        ]
    )

    (
        queries,
        keys,
        values,
        attended,
        normed,
        attn_weight,
        out_weight,
        feed_all,
        cosine,
        sine_part,
        gains,
        squares,
        logs,
        middle,
        normed_two,
        attended_own,
        begin_row,
    ) = opening(hidden, attn_piece, output_proj.astype(low), feed_piece, first_values[0], segment_ids)
    normed_two_grad, layer_output, made = feed(normed_two, out_cotangent, middle, feed_all)
    layer_output = layer_output[None]
    branch_low, middle_grad, gain_two, *out_grads = middle_back(
        middle, out_cotangent, normed_two_grad, out_weight, gains
    )
    small = jnp.concatenate(
        [
            jnp.zeros((8, PIECE), jnp.float32),
            gain_two[0].reshape(8, PIECE),
            jnp.broadcast_to(jnp.sum(squares[:2], axis=1)[:, None], (2, PIECE)),
            jnp.zeros((6, PIECE), jnp.float32),
        ]
    )
    values_grad, normed_grad, feed_total, out_total, attn_total, small = closing(
        made,
        branch_low,
        attended_own,
        (queries, keys, values, attended),
        normed,
        attn_weight,
        (cosine, sine_part),
        out_grads,
        logs,
        begin_row,
        gains,
        jnp.broadcast_to(small[None], (5, 24, PIECE)),
    )
    small = small[4]
    masters = [input_proj, output_proj, expand_proj, reduce_proj, norm_gains]
    moments = [
        old_moment_input,
        old_moment_output,
        old_moment_expand,
        old_moment_reduce,
        old_moment_gains,
    ]
    squares = [
        old_square_input,
        old_square_output,
        old_square_expand,
        old_square_reduce,
        old_square_gains,
    ]
    for group in (masters, moments, squares):
        group[2] = group[2].transpose(0, 2, 1)
    input_grad, norms, *updated = update(
        hidden,
        middle_grad,
        normed_grad,
        gains,
        (attn_total, out_total, feed_total),
        small,
        masters,
        moments,
        squares,
    )
    for index in (2, 7, 12):
        updated[index] = updated[index].transpose(0, 2, 1)
    return (layer_output, input_grad[None], values_grad[None], norms[:2, 0], *updated)


def solution(mesh):
    quick = mesh.shape["dp"] == 8 and mesh.shape["mp"] == PLANES
    return jax.shard_map(
        fast_shards if quick else shards,
        mesh=mesh,
        in_specs=(
            P("dp", "mp", None),
            P("dp", None),
            P("dp", None, "mp"),
            P("dp", "mp", None),
            P(None, "dp", "mp"),
            P("mp", "dp"),
            P(None, "dp", "mp"),
            P("mp", "dp"),
            P(None, "dp"),
            P(None, "dp", "mp"),
            P("mp", "dp"),
            P(None, "dp", "mp"),
            P("mp", "dp"),
            P(None, "dp"),
            P(None, "dp", "mp"),
            P("mp", "dp"),
            P(None, "dp", "mp"),
            P("mp", "dp"),
            P(None, "dp"),
        ),
        out_specs=(
            P("dp", "mp", None),
            P("dp", "mp", None),
            P("dp", None, "mp"),
            P(),
            P(None, "dp", "mp"),
            P("mp", "dp"),
            P(None, "dp", "mp"),
            P("mp", "dp"),
            P(None, "dp"),
            P(None, "dp", "mp"),
            P("mp", "dp"),
            P(None, "dp", "mp"),
            P("mp", "dp"),
            P(None, "dp"),
            P(None, "dp", "mp"),
            P("mp", "dp"),
            P(None, "dp", "mp"),
            P("mp", "dp"),
            P(None, "dp"),
        ),
        check_vma=False,
    )
```

```python
import functools
import math

import jax
import jax.numpy as jnp
import numpy as np
from jax import lax
from jax.experimental import pallas as pl
from jax.experimental.pallas import tpu as pltpu
from jax.sharding import PartitionSpec as P

D = 1024
HEADS = 16
HD = 64
FF = 2816
LEN = 2048
STEP = 5
PLANES = 4
PIECE = 128
BLOCKS = 4
ATTN_ROWS = 784
VMEM_LIMIT = 56 << 20
OPEN_COPIES = 100
CLOSE_COPIES = 80
CLOSE_VMEM = 60 << 20


def arrivals(plane):
    order = [(0, 0, plane)]
    for hop in range(1, PLANES):
        if plane + hop < PLANES:
            order.append((0, hop, plane + hop))
        if plane - hop >= 0:
            order.append((1, hop, plane - hop))
    return order


SLOTS = [arrivals(plane) for plane in range(PLANES)]


def cost(flops, moved):
    return pl.CostEstimate(flops=flops, bytes_accessed=moved, transcendentals=0)


def rope_tables(seg_row, head_size):
    length = seg_row.shape[0]
    places = jnp.arange(length, dtype=jnp.int32)
    begins = jnp.sum((seg_row[None, :] < seg_row[:, None]).astype(jnp.int32), axis=1)
    offset = (places - begins).astype(jnp.float32)
    inverse_rates = 10000.0 ** (-2.0 * jnp.arange(head_size // 2, dtype=jnp.float32) / head_size)
    angles = offset[:, None] * inverse_rates[None, :]
    return (jnp.cos(angles)[:, None, :], jnp.sin(angles)[:, None, :])


def rotate(values, cosine, sine_part, forward):
    half_size = values.shape[-1] // 2
    first_half = values[..., :half_size]
    second_half = values[..., half_size:]
    if forward:
        return jnp.concatenate(
            [
                first_half * cosine - second_half * sine_part,
                second_half * cosine + first_half * sine_part,
            ],
            axis=-1,
        )
    return jnp.concatenate(
        [
            first_half * cosine + second_half * sine_part,
            second_half * cosine - first_half * sine_part,
        ],
        axis=-1,
    )


def rms_factor(values):
    return lax.rsqrt(jnp.mean(values * values, axis=-1, keepdims=True) + 1e-06)


def norm_back(values, factor, gain_row, incoming):
    scaled = incoming * gain_row
    value_grad = factor * scaled - values * factor**3 * jnp.mean(
        scaled * values, axis=-1, keepdims=True
    )
    gain_grad = jnp.sum(incoming * values * factor, axis=0)
    return (value_grad, gain_grad)


def visible_block(seg_row, first_row, block_rows):
    length = seg_row.shape[0]
    query_seg = lax.dynamic_slice_in_dim(seg_row, first_row, block_rows, 0)
    query_places = first_row + jnp.arange(block_rows, dtype=jnp.int32)
    key_places = jnp.arange(length, dtype=jnp.int32)
    return (query_seg[:, None] == seg_row[None, :]) & (query_places[:, None] >= key_places[None, :])


def block_scores(queries, keys_rot, seg_row, first_row, block_rows, score_scale):
    query_block = lax.dynamic_slice_in_dim(queries, first_row, block_rows, 0)
    visible = visible_block(seg_row, first_row, block_rows)
    scores = (
        jnp.einsum("qhd,khd->hqk", query_block, keys_rot, preferred_element_type=jnp.float32)
        * score_scale
    )
    return (query_block, jnp.where(visible[None], scores, -1e30))


def attend(queries, keys_rot, mixed_values, seg_row, score_scale):
    length = queries.shape[0]
    block_rows = min(512, length)

    def one_block(block_index):
        first_row = block_index * block_rows
        query_block, scores = block_scores(
            queries, keys_rot, seg_row, first_row, block_rows, score_scale
        )
        top_score = jnp.max(scores, axis=-1, keepdims=True)
        raised = jnp.exp(scores - top_score)
        totals = jnp.sum(raised, axis=-1, keepdims=True)
        shares = (raised / totals).astype(jnp.bfloat16)
        combined = jnp.einsum(
            "hqk,khd->qhd", shares, mixed_values, preferred_element_type=jnp.float32
        )
        return (combined, (top_score + jnp.log(totals))[..., 0])

    combined, log_totals = lax.map(one_block, jnp.arange(length // block_rows, dtype=jnp.int32))
    return (combined.reshape(length, -1), log_totals)


def attend_back(queries, keys_rot, mixed_values, out_grad, log_totals, seg_row, score_scale):
    length = queries.shape[0]
    block_rows = min(512, length)

    def one_block(running, operands):
        key_sum, value_sum = running
        block_index, block_totals = operands
        first_row = block_index * block_rows
        query_block, scores = block_scores(
            queries, keys_rot, seg_row, first_row, block_rows, score_scale
        )
        grad_block = lax.dynamic_slice_in_dim(out_grad, first_row, block_rows, 0)
        shares = jnp.exp(scores - block_totals[..., None])
        share_grad = jnp.einsum(
            "qhd,khd->hqk", grad_block, mixed_values, preferred_element_type=jnp.float32
        )
        inner = jnp.sum(shares * share_grad, axis=-1, keepdims=True)
        score_grad = (shares * (share_grad - inner)).astype(jnp.bfloat16)
        query_grad = (
            jnp.einsum("hqk,khd->qhd", score_grad, keys_rot, preferred_element_type=jnp.float32)
            * score_scale
        )
        key_sum = (
            key_sum
            + jnp.einsum(
                "hqk,qhd->khd", score_grad, query_block, preferred_element_type=jnp.float32
            )
            * score_scale
        )
        value_sum = value_sum + jnp.einsum(
            "hqk,qhd->khd",
            shares.astype(jnp.bfloat16),
            grad_block,
            preferred_element_type=jnp.float32,
        )
        return ((key_sum, value_sum), query_grad)

    empty_sum = jnp.zeros(keys_rot.shape, jnp.float32)
    (key_grad, value_grad), query_grad = lax.scan(
        one_block,
        (empty_sum, empty_sum),
        (jnp.arange(length // block_rows, dtype=jnp.int32), log_totals),
    )
    return (query_grad.reshape(keys_rot.shape), key_grad, value_grad)


def adamw(master, gradient, moment, square, step_rate, decay):
    new_moment = 0.5 * moment + 0.5 * gradient
    new_square = 0.5 * square + 0.5 * gradient * gradient
    correct = 1.0 - 0.5**STEP
    update = new_moment / correct / (jnp.sqrt(new_square / correct) + 1e-08)
    return (master - step_rate * (update + decay * master), new_moment, new_square)


def shards(
    hidden_in,
    segment_ids,
    first_values,
    grad_out,
    input_proj,
    output_proj,
    expand_proj,
    reduce_proj,
    norm_gains,
    old_moment_input,
    old_moment_output,
    old_moment_expand,
    old_moment_reduce,
    old_moment_gains,
    old_square_input,
    old_square_output,
    old_square_expand,
    old_square_reduce,
    old_square_gains,
):
    attn_weight, out_weight, expand_weight, reduce_weight, gains_low = (
        lax.all_gather(input_proj.astype(jnp.bfloat16), "dp", axis=1, tiled=True),
        lax.all_gather(output_proj.astype(jnp.bfloat16), "dp", axis=1, tiled=True),
        lax.all_gather(expand_proj.astype(jnp.bfloat16), "dp", axis=1, tiled=True),
        lax.all_gather(reduce_proj.astype(jnp.bfloat16), "dp", axis=1, tiled=True),
        lax.all_gather(norm_gains.astype(jnp.bfloat16), "dp", axis=1, tiled=True),
    )
    gains = gains_low.astype(jnp.float32)
    hidden = hidden_in[0].astype(jnp.float32)
    seg_row = segment_ids[0]
    length = seg_row.shape[0]
    first_in = first_values[0].astype(jnp.float32)
    local_heads = attn_weight.shape[2] // HD
    score_scale = 1.0 / math.sqrt(HD)
    factor_one = rms_factor(hidden)
    normed_one = (hidden * factor_one * gains[0]).astype(jnp.bfloat16)
    all_normed, all_grad_out = (
        lax.all_gather(normed_one, "mp", axis=0, tiled=True),
        lax.all_gather(grad_out[0], "mp", axis=0, tiled=True),
    )
    projected = jnp.einsum(
        "td,cde->cte", all_normed, attn_weight, preferred_element_type=jnp.float32
    )
    cosine, sine_part = rope_tables(seg_row, HD)
    queries = rotate(projected[0].reshape(length, local_heads, HD), cosine, sine_part, True).astype(
        jnp.bfloat16
    )
    keys_rot = rotate(
        projected[1].reshape(length, local_heads, HD), cosine, sine_part, True
    ).astype(jnp.bfloat16)
    blended = 0.5 * projected[2] + 0.5 * first_in
    mixed_values = blended.astype(jnp.bfloat16).reshape(length, local_heads, HD)
    square_terms = jnp.stack([jnp.sum(first_in * first_in), jnp.sum(blended * blended)])
    attended, log_totals = attend(queries, keys_rot, mixed_values, seg_row, score_scale)
    attended_low = attended.astype(jnp.bfloat16)
    rows_part = attended_low
    branch = lax.psum_scatter(
        jnp.dot(rows_part, out_weight, preferred_element_type=jnp.float32),
        "mp",
        scatter_dimension=0,
        tiled=True,
    )
    middle = hidden + branch
    factor_two = rms_factor(middle)
    normed_two = (middle * factor_two * gains[1]).astype(jnp.bfloat16)
    all_normed_two = lax.all_gather(normed_two, "mp", axis=0, tiled=True)
    gate_up = jnp.einsum(
        "td,cdf->ctf", all_normed_two, expand_weight, preferred_element_type=jnp.float32
    )
    gate_sig = jax.nn.sigmoid(gate_up[0])
    gate_act = gate_up[0] * gate_sig
    activated = (gate_act * gate_up[1]).astype(jnp.bfloat16)
    rows_part = activated
    feed_out = lax.psum_scatter(
        jnp.dot(rows_part, reduce_weight, preferred_element_type=jnp.float32).astype(jnp.bfloat16),
        "mp",
        scatter_dimension=0,
        tiled=True,
    ).astype(jnp.float32)
    layer_output = (middle + feed_out).astype(jnp.bfloat16)[None]
    hidden_grad = jnp.einsum(
        "td,fd->tf", all_grad_out, reduce_weight, preferred_element_type=jnp.float32
    )
    reduce_grad = jnp.einsum(
        "tf,td->fd", activated, all_grad_out, preferred_element_type=jnp.float32
    )
    gate_grad = hidden_grad * gate_up[1] * gate_sig * (1.0 + gate_up[0] * (1.0 - gate_sig))
    up_grad = hidden_grad * gate_act
    pair_grad = jnp.stack([gate_grad, up_grad]).astype(jnp.bfloat16)
    expand_grad = jnp.einsum(
        "ctf,td->cdf", pair_grad, all_normed_two, preferred_element_type=jnp.float32
    )
    rows_part = pair_grad
    normed_two_grad = lax.psum_scatter(
        jnp.einsum(
            "ctf,cdf->td", rows_part, expand_weight, preferred_element_type=jnp.float32
        ).astype(jnp.bfloat16),
        "mp",
        scatter_dimension=0,
        tiled=True,
    ).astype(jnp.float32)
    middle_part, gain_two_grad = norm_back(middle, factor_two, gains[1], normed_two_grad)
    middle_grad = grad_out[0].astype(jnp.float32) + middle_part
    branch_low = middle_grad.astype(jnp.bfloat16)
    all_branch = lax.all_gather(branch_low, "mp", axis=0, tiled=True)
    out_grad = jnp.einsum("te,td->ed", attended_low, all_branch, preferred_element_type=jnp.float32)
    attended_grad = jnp.einsum(
        "td,ed->te", all_branch, out_weight, preferred_element_type=jnp.float32
    ).astype(jnp.bfloat16)
    query_grad, key_grad, mix_grad = attend_back(
        queries,
        keys_rot,
        mixed_values,
        attended_grad.reshape(length, local_heads, HD),
        log_totals,
        seg_row,
        score_scale,
    )
    query_grad = rotate(query_grad, cosine, sine_part, False).reshape(length, -1)
    key_grad = rotate(key_grad, cosine, sine_part, False).reshape(length, -1)
    mix_grad = mix_grad.reshape(length, -1)
    values_grad = (0.5 * mix_grad)[None]
    proj_grad = jnp.stack([query_grad, key_grad, 0.5 * mix_grad]).astype(jnp.bfloat16)
    attn_grad = jnp.einsum("cte,td->cde", proj_grad, all_normed, preferred_element_type=jnp.float32)
    rows_part = proj_grad
    normed_one_grad = lax.psum_scatter(
        jnp.einsum(
            "cte,cde->td", rows_part, attn_weight, preferred_element_type=jnp.float32
        ).astype(jnp.bfloat16),
        "mp",
        scatter_dimension=0,
        tiled=True,
    ).astype(jnp.float32)
    input_part, gain_one_grad = norm_back(hidden, factor_one, gains[0], normed_one_grad)
    input_grad = (middle_grad + input_part)[None]
    attn_total, out_total, expand_total, reduce_total = (
        lax.psum_scatter(
            attn_grad.astype(jnp.bfloat16), "dp", scatter_dimension=1, tiled=True
        ).astype(jnp.float32),
        lax.psum_scatter(
            out_grad.astype(jnp.bfloat16), "dp", scatter_dimension=1, tiled=True
        ).astype(jnp.float32),
        lax.psum_scatter(
            expand_grad.astype(jnp.bfloat16), "dp", scatter_dimension=1, tiled=True
        ).astype(jnp.float32),
        lax.psum_scatter(
            reduce_grad.astype(jnp.bfloat16), "dp", scatter_dimension=1, tiled=True
        ).astype(jnp.float32),
    )
    gain_totals, square_sums = lax.psum(
        (jnp.stack([gain_one_grad, gain_two_grad]), square_terms), ("dp", "mp")
    )
    gain_width = norm_gains.shape[1]
    gain_total = lax.dynamic_slice_in_dim(
        gain_totals, lax.axis_index("dp") * gain_width, gain_width, 1
    )
    value_norms = jnp.sqrt(square_sums / (lax.axis_size("dp") * length * D))
    new_input = adamw(input_proj, attn_total, old_moment_input, old_square_input, D ** (-0.5), 0.1)
    new_output = adamw(
        output_proj,
        out_total,
        old_moment_output,
        old_square_output,
        max(1, 8 * HEADS * HD // LEN) ** (-0.5),
        0.1,
    )
    new_expand = adamw(
        expand_proj, expand_total, old_moment_expand, old_square_expand, D ** (-0.5), 0.1
    )
    new_reduce = adamw(
        reduce_proj, reduce_total, old_moment_reduce, old_square_reduce, (FF // 3) ** (-0.5), 0.1
    )
    new_gains = adamw(norm_gains, gain_total, old_moment_gains, old_square_gains, 0.2, 0.0)
    return (
        layer_output,
        input_grad,
        values_grad,
        value_norms,
        new_input[0],
        new_output[0],
        new_expand[0],
        new_reduce[0],
        new_gains[0],
        new_input[1],
        new_output[1],
        new_expand[1],
        new_reduce[1],
        new_gains[1],
        new_input[2],
        new_output[2],
        new_expand[2],
        new_reduce[2],
        new_gains[2],
    )


def tokens_dot(a, b, left, right):
    return lax.dot_general(a, b, (((left,), (right,)), ((), ())), preferred_element_type=jnp.float32)


def piece_columns(place, step):
    start = jnp.bitwise_xor(place, step) * PIECE
    return pl.ds(pl.multiple_of(start, PIECE), PIECE)


def turn(values, cosine, sine_part, forward):
    lane = lax.broadcasted_iota(jnp.int32, values.shape, 1)
    swapped = jnp.where(
        lax.rem(lane, HD) < HD // 2, pltpu.roll(values, 96, 1), pltpu.roll(values, 32, 1)
    )
    if forward:
        return values * cosine + swapped * sine_part
    return values * cosine - swapped * sine_part


MESH = pl.DeviceIdType.MESH
LOG2E = 1.4426950408889634


def flip(place, bit):
    return place + bit - 2 * bit * lax.rem(lax.div(place, bit), 2)


def at_plane(depth, values):
    found = 0
    for plane, value in enumerate(values):
        found = found + jnp.where(depth == plane, value, 0)
    return found


def slot_at(depth, way, hop):
    return at_plane(
        depth,
        [
            next((k for k, s in enumerate(SLOTS[plane]) if s[:2] == (way, hop)), 0)
            for plane in range(PLANES)
        ],
    )


def columns_of(piece, width=PIECE):
    return pl.ds(pl.multiple_of(piece * width, width), width)


class Links:
    def __init__(self, send, recv):
        self.send, self.recv, self.count, self.started, self.waited = send, recv, 0, [], []
        self.place, self.depth = lax.axis_index("dp"), lax.axis_index("mp")

    def number(self, count=1):
        self.count += count
        return self.count - count

    def copy(self, number, source, target, to):
        return pltpu.make_async_remote_copy(
            src_ref=source,
            dst_ref=target,
            send_sem=self.send.at[number],
            recv_sem=self.recv.at[number],
            device_id=to,
            device_id_type=MESH,
        )

    def go(self, number, source, target, to, when=None):
        copy = self.copy(number, source, target, to)
        self.started.append((number, source, target, to, when))
        if when is None:
            copy.start()
        else:
            pl.when(when)(copy.start)

    def got(self, number, landed, when=None):
        copy = self.copy(number, landed, landed, (flip(self.place, 1), self.depth))
        if when is None:
            copy.wait_recv()
        else:
            pl.when(when)(copy.wait_recv)

    def drain(self):
        for *parts, when in self.started:
            copy = self.copy(*parts)
            for plane in [plane for number, plane in self.waited if number == parts[0]]:
                when = when & (self.depth != plane)
            if when is None:
                copy.wait_send()
            else:
                pl.when(when)(copy.wait_send)

    def greet(self, planes=True):
        barrier = pltpu.get_barrier_semaphore()
        others = [(flip(self.place, bit), self.depth) for bit in (1, 2, 4)]
        if planes:
            others += [(self.place, lax.rem(self.depth + step, PLANES)) for step in range(1, PLANES)]
        for other in others:
            pl.semaphore_signal(barrier, inc=1, device_id=other, device_id_type=MESH)
        pl.semaphore_wait(barrier, len(others))


class Spread:
    def __init__(self, links, own, spot, bits):
        self.links, self.own = links, own
        self.base = links.number(7)
        place = links.place
        first, second = flip(place, bits[0]), flip(place, bits[1])
        self.spots = [spot(piece) for piece in (place, first, second, flip(first, bits[1]))]
        self.lands = [
            spot(flip(piece, 1)) for piece in (place, first, second, flip(first, bits[1]))
        ]
        self.near, self.far, self.core = [
            (flip(place, bit), links.depth) for bit in (bits[0], bits[1], 1)
        ]

    def one(self):
        self.links.go(self.base, self.own, self.spots[0], self.near)

    def two(self):
        links, spots = self.links, self.spots
        links.go(self.base + 1, self.own, spots[0], self.far)
        links.got(self.base, spots[1])
        links.go(self.base + 2, spots[1], spots[1], self.far)

    def landed(self):
        self.links.got(self.base + 1, self.spots[2])
        self.links.got(self.base + 2, self.spots[3])

    def three(self):
        links, spots = self.links, self.spots
        links.go(self.base + 3, self.own, spots[0], self.core)
        links.go(self.base + 4, spots[1], spots[1], self.core)
        links.got(self.base + 1, spots[2])
        links.go(self.base + 5, spots[2], spots[2], self.core)
        links.got(self.base + 2, spots[3])
        links.go(self.base + 6, spots[3], spots[3], self.core)

    def end(self):
        for index, land in enumerate(self.lands):
            self.links.got(self.base + 3 + index, land)


class Halves:
    def __init__(self, parts):
        self.parts = parts

    def one(self):
        for part in self.parts:
            part.one()

    def two(self, *given):
        for index, part in enumerate(self.parts):
            part.two(*[one[index] for one in given])

    def landed(self):
        for part in self.parts:
            part.landed()

    def three(self):
        for part in self.parts:
            part.three()

    def end(self):
        for part in self.parts:
            part.end()


def half_of(ref, half):
    rows = ref.shape[-2] // 2
    lead = (slice(None),) * (len(ref.shape) - 2)
    return ref.at[(*lead, pl.ds(half * rows, rows), slice(None))]


def halved_spread(links, own, spot):
    return Halves(
        [
            Spread(
                links,
                half_of(own, half),
                lambda piece, half=half: half_of(spot(piece), half),
                ((2, 4), (4, 2))[half],
            )
            for half in range(2)
        ]
    )


class Relay:
    def __init__(self, links, own, put):
        self.links, self.own, self.put = links, own, put
        self.base = links.number(2 * (PLANES - 1))
        self.waited = links.waited

    def plan(self, hop, only=None):
        links, depth = self.links, self.links.depth
        planned = []
        for way in range(2):
            to = depth + (1 if way else -1)
            when = (
                (depth >= hop - 1) & (depth < PLANES - 1)
                if way
                else (depth <= PLANES - hop) & (depth > 0)
            )
            if only is not None:
                when = when & (depth == only[way])
            source = self.own if hop == 1 else self.put(depth, way, hop - 1)
            planned.append(
                (
                    self.base + 2 * (hop - 1) + way,
                    source,
                    self.put(to, way, hop),
                    (links.place, jnp.clip(to, 0, PLANES - 1)),
                    when,
                )
            )
        return planned

    def send(self, hop, only=None):
        for parts in self.plan(hop, only):
            self.links.go(*parts)

    def take(self, hop, only=None):
        links, depth = self.links, self.links.depth
        for way in range(2):
            when = depth >= hop if way else depth + hop < PLANES
            if only is not None:
                when = when & (depth == only[way])
            links.got(self.base + 2 * (hop - 1) + way, self.put(depth, way, hop), when)

    def left(self, hop, only):
        links, depth = self.links, self.links.depth
        for way in range(2):
            source = self.own if hop == 1 else self.put(depth, way, hop - 1)
            to = (links.place, jnp.clip(depth + (1 if way else -1), 0, PLANES - 1))
            copy = links.copy(self.base + 2 * (hop - 1) + way, source, source, to)
            pl.when(depth == only[way])(copy.wait_send)
            self.waited.append((self.base + 2 * (hop - 1) + way, only[way]))


def position_tables(length):
    rates = 10000.0 ** (-2.0 * np.arange(HD // 2) / HD)
    angles = np.arange(length)[:, None] * rates[None, :]
    cosine, sine = np.cos(angles), np.sin(angles)
    return (
        jnp.asarray(np.concatenate([cosine] * 4, axis=1), jnp.float32),
        jnp.asarray(np.concatenate([-sine, sine, -sine, sine], axis=1), jnp.float32),
    )


def rope_tables_from(seg_ref, cos_at, sin_at, cos_ref, sin_ref, begin_ref, marks):
    length = cos_at.shape[0]
    segs = seg_ref[0:1, :].astype(jnp.float32)
    spots = lax.broadcasted_iota(jnp.int32, (1, length), 1).astype(jnp.float32)
    begins = jnp.zeros((1, length), jnp.float32)
    marks[...] = jnp.zeros_like(marks)
    for number in range(7):
        start = jnp.sum(jnp.where(segs < number, 1.0, 0.0), axis=1, keepdims=True)
        begins = jnp.where(segs == number, start, begins)
        marks[number : number + 1, :] = jnp.where(spots == start, 1.0, 0.0)
    begin_ref[...] = jnp.broadcast_to(begins.astype(jnp.int32), begin_ref.shape)
    pick = lambda table: lax.dot_general(
        marks[...],
        table[...],
        (((1,), (0,)), ((), ())),
        precision=lax.Precision.HIGHEST,
        preferred_element_type=jnp.float32,
    )
    first_cos, first_sin = pick(cos_at), pick(sin_at)
    rows = length // PLANES
    for block in range(PLANES):
        span = pl.ds(block * rows, rows)
        documents = jnp.transpose(
            jnp.broadcast_to(segs[:, block * rows : block * rows + rows], (128, rows))
        )
        cosine = jnp.zeros((rows, 128), jnp.float32)
        sine = jnp.zeros((rows, 128), jnp.float32)
        for number in range(7):
            here = documents == number
            cosine = jnp.where(here, first_cos[number : number + 1], cosine)
            sine = jnp.where(here, first_sin[number : number + 1], sine)
        cos_ref[span, :] = cos_at[span, :] * cosine + sin_at[span, :] * sine
        sin_ref[span, :] = sin_at[span, :] * cosine - cos_at[span, :] * sine


def open_kernel(*refs):
    hidden, attn_piece, out_piece, feed_piece, cos_at, sin_at, first_ref, seg_ref = refs[:8]
    q_out, k_out, v_out, o_out, n_out, weight_out, out_weight_out, feed_all, cos_out, sin_out = refs[8:18]
    gain_ref, square_ref, log_ref, middle_ref, normed_ref, attended_ref, begin_ref = refs[18:25]
    held, q_ref, k_ref, v_ref, o_ref, n_ref, weight_ref, out_ref, cos_ref, sin_ref, turned_v, marks = refs[25:37]
    send, recv, local = refs[37:]
    links = Links(send, recv)
    place, depth = links.place, links.depth
    shard = hidden.shape[0]
    stores = []

    def store(source, target):
        copy = pltpu.make_async_copy(source, target, local.at[len(stores)])
        copy.start()
        stores.append(copy)
        return copy

    block_at = lambda plane, way, hop: jnp.clip(plane + (-hop if way else hop), 0, PLANES - 1)
    wide = Relay(links, hidden, lambda plane, way, hop: held.at[block_at(plane, way, hop)])
    out_rows = lambda block: out_ref.at[
        pl.ds(pl.multiple_of(block * 256, 256), 256), columns_of(place)
    ]
    thin = Relay(links, out_piece, lambda plane, way, hop: out_rows(block_at(plane, way, hop)))
    feeds = Relay(
        links,
        feed_piece,
        lambda plane, way, hop: feed_all.at[slot_at(plane, way, hop), place],
    )
    attn = Spread(links, attn_piece, lambda piece: weight_ref.at[:, columns_of(piece)], (2, 4))
    outs = []
    for slot in range(PLANES):
        block = at_plane(depth, [SLOTS[plane][slot][2] for plane in range(PLANES)])
        rows = pl.ds(pl.multiple_of(block * 256, 256), 256)
        outs.append(
            Spread(
                links,
                out_piece if slot == 0 else out_ref.at[rows, columns_of(place)],
                lambda piece, rows=rows: out_ref.at[rows, columns_of(piece)],
                (2, 4) if slot % 2 else (4, 2),
            )
        )
    slots = [
        halved_spread(
            links,
            feed_piece if slot == 0 else feed_all.at[slot, place],
            lambda piece, slot=slot: feed_all.at[slot, piece],
        )
        for slot in range(PLANES - 1)
    ]
    across = links.number(PLANES)

    links.greet()
    thin.send(1)
    wide.send(1)
    attn.one()
    own_hidden = store(hidden, held.at[depth])
    own_attn = store(attn_piece, weight_ref.at[:, columns_of(place)])
    own_out = store(out_piece, out_rows(depth))
    own_feed = store(feed_piece, feed_all.at[0, place])
    square_ref[...] = jnp.zeros_like(square_ref)
    attn.two()
    attn.three()
    outs[0].one()
    slots[0].one()
    rope_tables_from(seg_ref, cos_at, sin_at, cos_ref, sin_ref, begin_ref, marks)
    attn.end()
    outs[0].two()
    for copy in (own_hidden, own_attn, own_out, own_feed):
        copy.wait()
    store(weight_ref, weight_out)
    store(cos_ref, cos_out)
    store(sin_ref, sin_out)
    gain_ref[...] = weight_ref[pl.ds(768, 16), :].astype(jnp.float32)

    def project(block):
        rows = pl.ds(pl.multiple_of(block * shard, shard), shard)
        values = held[block].astype(jnp.float32)
        factor = lax.rsqrt(jnp.mean(values * values, axis=-1, keepdims=True) + 1e-06)
        normed = (values * factor * gain_ref[0:1, :]).astype(jnp.bfloat16)
        n_ref[rows, :] = normed
        cosine, sine_part = cos_ref[rows, :], sin_ref[rows, :]
        query = tokens_dot(normed, weight_ref[pl.ds(0, 256), :], 1, 1)
        key = tokens_dot(normed, weight_ref[pl.ds(256, 256), :], 1, 1)
        value = tokens_dot(normed, weight_ref[pl.ds(512, 256), :], 1, 1)
        for half in range(2):
            lanes = slice(half * 128, half * 128 + 128)
            turned = turn(query[:, lanes], cosine, sine_part, True)
            q_ref[rows, lanes] = (turned * (HD**-0.5 * LOG2E)).astype(jnp.bfloat16)
            k_ref[rows, lanes] = turn(key[:, lanes], cosine, sine_part, True).astype(jnp.bfloat16)
        first = first_ref[rows, :].astype(jnp.float32)
        blended = 0.5 * value + 0.5 * first
        v_ref[rows, :] = blended.astype(jnp.bfloat16)
        for half in range(2):
            turned_v[half, :, rows] = jnp.transpose(
                blended[:, half * 128 : half * 128 + 128]
            ).astype(jnp.bfloat16)
        square_ref[0:1, :] += jnp.sum(first * first, axis=0, keepdims=True)
        square_ref[1:2, :] += jnp.sum(blended * blended, axis=0, keepdims=True)

    def project_hop(hop):
        def one(side, carried):
            block = depth + hop * (2 * side - 1)
            pl.when((block >= 0) & (block < PLANES))(lambda: project(block))
            return carried

        lax.fori_loop(0, 2, one, 0)

    ends, inner = (PLANES - 1, 0), (PLANES - 2, 1)
    project(depth)
    wide.take(1)
    wide.send(2)
    feeds.send(1, ends)
    thin.take(1)
    thin.send(2)
    outs[1].one()
    outs[0].three()
    slots[0].two()
    project_hop(1)
    outs[1].two()
    wide.take(2)
    wide.send(3)
    feeds.take(1, inner)
    feeds.send(1, inner)
    feeds.send(2, inner)
    thin.take(2)
    thin.send(3)
    outs[2].one()
    outs[1].three()
    project_hop(2)
    outs[2].two()
    slots[0].three()
    wide.take(3)
    wide.left(3, (1, PLANES - 2))
    feeds.take(1, (1, PLANES - 2))
    feeds.take(2, (1, PLANES - 2))
    feeds.send(1, (1, PLANES - 2))
    second = feeds.plan(2, (1, PLANES - 2))
    thin.take(3)
    outs[3].one()
    outs[2].three()
    project_hop(3)
    outs[3].two()
    store(n_ref, n_out)
    store(q_ref, q_out)
    store(k_ref, k_out)
    store(v_ref, v_out)

    lane = lax.broadcasted_iota(jnp.int32, (shard, 128), 1)
    down = lax.broadcasted_iota(jnp.int32, (shard, shard), 0)
    along = lax.broadcasted_iota(jnp.int32, (1, shard), 1)

    def flash_block(block):
        rows = pl.ds(pl.multiple_of(block * shard, shard), shard)
        begin = begin_ref[0:1, rows]
        pairs = [q_ref[rows, pl.ds(pair * 128, 128)] for pair in range(2)]
        parts = [
            jnp.where((lane < HD) == (head % 2 == 0), pairs[head // 2], jnp.zeros_like(pairs[0]))
            for head in range(4)
        ]

        def tile(index, carried, visible):
            span = pl.ds(pl.multiple_of(index * shard, shard), shard)
            raw = [
                tokens_dot(k_ref[span, pl.ds(head // 2 * 128, 128)], parts[head], 1, 1)
                for head in range(4)
            ]
            after = []
            for head in range(4):
                top, total, summed = carried[3 * head : 3 * head + 3]
                scores = jnp.where(visible, raw[head], -1e30)
                raised_top = jnp.maximum(top, jnp.max(scores, axis=0, keepdims=True))
                shrink = jnp.exp2(top - raised_top)
                shares = jnp.exp2(scores - raised_top)
                total = total * shrink + jnp.sum(shares, axis=0, keepdims=True)
                values = turned_v[head // 2, pl.ds(head % 2 * HD, HD), span]
                summed = summed * shrink + tokens_dot(values, shares.astype(jnp.bfloat16), 1, 0)
                after += [raised_top, total, summed]
            return tuple(after)

        fresh = (
            jnp.full((1, shard), -1e30, jnp.float32),
            jnp.zeros((1, shard), jnp.float32),
            jnp.zeros((HD, shard), jnp.float32),
        )
        carried = tile(block, fresh * 4, (down >= begin - block * shard) & (down <= along))
        carried = lax.fori_loop(
            0, block, lambda j, held: tile(j, held, down >= begin - j * shard), carried
        )
        for pair in range(2):
            ends = [carried[3 * (2 * pair + head) : 3 * (2 * pair + head) + 3] for head in range(2)]
            both = jnp.concatenate([summed / total for _, total, summed in ends], axis=0)
            o_ref[rows, pl.ds(pair * 128, 128)] = jnp.transpose(both).astype(jnp.bfloat16)
            for head, (top, total, _) in enumerate(ends):
                log_ref[pair, head : head + 1, rows] = top + jnp.log2(total)

    own_columns = attended_ref.at[:, columns_of(depth, 256)]

    def hand(step):
        block = lax.rem(depth + step, PLANES)
        rows = pl.ds(pl.multiple_of(block * shard, shard), shard)
        return links.copy(across + step, o_ref.at[rows, :], own_columns, (place, block))

    near = (0, PLANES - 1)

    def pump_a():
        feeds.take(1, near)
        slots[1].one()
        outs[3].three()

    def pump_b():
        slots[1].two()
        slots[0].end()
        feeds.left(1, (1, PLANES - 2))
        for parts in second:
            links.go(*parts)

    def pump_c():
        feeds.take(2, near)
        slots[2].one()

    pumps = ((0, pump_a), (1, pump_b), (2, pump_c))

    def flash(index, carried):
        step = PLANES - 1 - index
        flash_block(lax.rem(depth + step, PLANES))
        pl.when((step > 0) & (step < PLANES - 1))(lambda: hand(step).start())
        for when, pump in pumps:
            pl.when(index == when)(pump)
        pl.when(index == 1)(lambda: hand(PLANES - 1).start())
        return carried

    lax.fori_loop(0, PLANES, flash, 0)
    feeds.send(3, (1, PLANES - 2))
    own_rows = pl.ds(pl.multiple_of(depth * shard, shard), shard)
    attended_ref[:, columns_of(depth, 256)] = o_ref[own_rows, :]
    store(o_ref, o_out)
    for part in outs:
        part.end()
    store(out_ref, out_weight_out)
    slots[2].two()
    for step in range(1, PLANES):
        source = lax.rem(depth - step + PLANES, PLANES)
        links.got(across + step, attended_ref.at[:, columns_of(source, 256)])
    half = shard // 2
    for part in range(2):
        rows = pl.ds(part * half, half)
        middle = held[depth, rows, :].astype(jnp.float32) + tokens_dot(
            attended_ref[rows, :], out_ref[...], 1, 0
        )
        middle_ref[rows, :] = middle
        factor = lax.rsqrt(jnp.mean(middle * middle, axis=-1, keepdims=True) + 1e-06)
        normed_ref[rows, :] = (middle * factor * gain_ref[1:2, :]).astype(jnp.bfloat16)
    slots[1].landed()
    slots[2].landed()
    feeds.take(3)
    for step in range(1, PLANES):
        hand(step).wait_send()
    links.drain()
    for copy in stores[4:]:
        copy.wait()


def opening(hidden, attn_piece, out_piece, feed_piece, first_values, seg_row):
    length, width = first_values.shape
    rows = hidden.shape[0]
    count = feed_piece.shape[0]
    low, full = jnp.bfloat16, jnp.float32
    any_spec, vmem = pl.BlockSpec(memory_space=pl.ANY), pl.BlockSpec(memory_space=pltpu.VMEM)
    shape = jax.ShapeDtypeStruct
    cos_at, sin_at = position_tables(length)
    return pl.pallas_call(
        open_kernel,
        in_specs=[any_spec] * 4 + [vmem] * 4,
        out_specs=[any_spec] * 10 + [vmem] * 7,
        out_shape=[
            shape((length, width), low),
            shape((length, width), low),
            shape((length, width), low),
            shape((length, width), low),
            shape((length, D), low),
            shape((ATTN_ROWS, D), low),
            shape((D, D), low),
            shape((PLANES, 8, count, PIECE), low),
            shape((length, 128), full),
            shape((length, 128), full),
            shape((16, D), full),
            shape((8, width), full),
            shape((width // 128, 8, length), full),
            shape((rows, D), full),
            shape((rows, D), low),
            shape((rows, D), low),
            shape((8, length), jnp.int32),
        ],
        scratch_shapes=[
            pltpu.VMEM((PLANES, rows, D), low),
            pltpu.VMEM((length, width), low),
            pltpu.VMEM((length, width), low),
            pltpu.VMEM((length, width), low),
            pltpu.VMEM((length, width), low),
            pltpu.VMEM((length, D), low),
            pltpu.VMEM((ATTN_ROWS, D), low),
            pltpu.VMEM((D, D), low),
            pltpu.VMEM((length, 128), full),
            pltpu.VMEM((length, 128), full),
            pltpu.VMEM((width // 128, 128, length), low),
            pltpu.VMEM((8, length), full),
            pltpu.SemaphoreType.DMA((OPEN_COPIES,)),
            pltpu.SemaphoreType.DMA((OPEN_COPIES,)),
            pltpu.SemaphoreType.DMA((14,)),
        ],
        compiler_params=pltpu.CompilerParams(
            vmem_limit_bytes=VMEM_LIMIT, collective_id=1, has_side_effects=True
        ),
        name="opening",
    )(hidden, attn_piece, out_piece, feed_piece, cos_at, sin_at, first_values, seg_row)


def feed_kernel(*refs):
    normed_ref, grad_ref, middle_ref, pieces = refs[:4]
    back_ref, out_ref, made_out = refs[4:7]
    fed, weight, mine, theirs, made, halves, other_halves, send, recv, sem, out_sem, last_sem = refs[7:]
    links = Links(send, recv)
    place = links.place
    core = (flip(links.place, 1), links.depth)
    mine_first, theirs_first = lax.rem(links.place, 2), 1 - lax.rem(links.place, 2)
    count = weight.shape[1] // 3
    rows = normed_ref.shape[0]

    def load(slot):
        own = range(8) if slot == 0 else [2 * piece + mine_first for piece in range(4)]
        return [
            pltpu.make_async_copy(
                pieces.at[slot, piece], weight.at[slot, :, columns_of(piece)], sem.at[slot, index]
            )
            for index, piece in enumerate(own)
        ]

    def flush(which, buffer):
        return [
            pltpu.make_async_copy(
                made.at[buffer, :, pl.ds(piece * PIECE, PIECE)],
                made_out.at[which, piece],
                out_sem.at[buffer, piece],
            )
            for piece in range(4)
        ]

    loads = [load(slot) for slot in range(PLANES - 1)]
    for copies in loads:
        for copy in copies:
            copy.start()
    far = pieces.at[PLANES - 1, place]
    last = halved_spread(links, far, lambda piece: weight.at[PLANES - 1, :, columns_of(piece)])
    last_own = pltpu.make_async_copy(far, weight.at[PLANES - 1, :, columns_of(place)], last_sem)
    crossed = {slot: links.number(4) for slot in range(1, PLANES - 1)}
    landings = {
        slot: [
            weight.at[slot, :, columns_of(2 * piece + theirs_first)] for piece in range(4)
        ]
        for slot in crossed
    }
    last_own.start()
    links.greet(planes=False)
    last.one()
    base = links.number(8)
    for index, ref in enumerate((normed_ref, grad_ref)):
        for piece in range(4):
            links.go(
                base + 4 * index + piece,
                ref.at[:, columns_of(2 * piece + theirs_first)],
                other_halves.at[index, :, pl.ds(piece * PIECE, PIECE)],
                core,
            )
            halves[index, :, pl.ds(piece * PIECE, PIECE)] = ref[:, columns_of(2 * piece + mine_first)]
    for slot, number in crossed.items():
        for piece in range(4):
            own = 2 * piece + mine_first
            links.go(
                number + piece, pieces.at[slot, own], weight.at[slot, :, columns_of(own)], core
            )
    fed[...] = jnp.zeros_like(fed)
    back_ref[...] = jnp.zeros_like(back_ref)
    for index in range(2):
        for piece in range(4):
            links.got(
                base + 4 * index + piece, other_halves.at[index, :, pl.ds(piece * PIECE, PIECE)]
            )
    given = links.number(PLANES)
    hand = lambda slot: links.copy(given + slot, mine.at[lax.rem(slot, 2)], theirs.at[slot], core)
    spans = [pl.ds(index * count, count) for index in range(3)]
    half = rows // 2

    def forward(slot):
        now = lax.rem(slot, 2)
        held = slot

        def ready(which):
            for copy in loads[which]:
                copy.wait()
            if which:
                for piece in range(4):
                    links.got(crossed[which] + piece, landings[which][piece])

        for which in range(PLANES - 1):
            pl.when(slot == which)(functools.partial(ready, which))

        @pl.when(slot == PLANES - 1)
        def _():
            last_own.wait()
            last.end()

        @pl.when(slot >= 2)
        def _():
            hand(slot - 2).wait_send()

        for tile in range(2):
            at = pl.ds(tile * half, half)
            normed, grad = normed_ref[at, :], grad_ref[at, :]
            gates = tokens_dot(weight[held, spans[0], :], normed, 1, 1)
            ups = tokens_dot(weight[held, spans[1], :], normed, 1, 1)
            backs = tokens_dot(weight[held, spans[2], :], grad, 1, 1)
            sig = jax.nn.sigmoid(gates)
            active = gates * sig
            mine[now, 2, :, at] = (active * ups).astype(jnp.bfloat16)
            mine[now, 0, :, at] = (backs * ups * sig * (1.0 + gates * (1.0 - sig))).astype(jnp.bfloat16)
            mine[now, 1, :, at] = (backs * active).astype(jnp.bfloat16)
        hand(slot).start()

        fed[...] += tokens_dot(mine[now, 2], weight[held, spans[2], :], 0, 0)
        back_ref[...] += tokens_dot(mine[now, 0], weight[held, spans[0], :], 0, 0) + tokens_dot(
            mine[now, 1], weight[held, spans[1], :], 0, 0
        )

    def backward(slot):
        now = lax.rem(slot, 2)
        hand(slot).wait_recv()

        @pl.when(slot >= 2)
        def _():
            for copy in flush(slot - 2, now):
                copy.wait()

        def columns(tile, carried):
            lanes = columns_of(tile, 256)
            for index in range(3):
                which = index // 2
                made[now, spans[index], lanes] = (
                    tokens_dot(mine[now, index], halves[which, :, lanes], 1, 0)
                    + tokens_dot(theirs[slot, index], other_halves[which, :, lanes], 1, 0)
                ).astype(jnp.bfloat16)
            return carried

        lax.fori_loop(0, 2, columns, 0)
        for copy in flush(slot, now):
            copy.start()

    def one(step, carried):
        pl.when(step < PLANES)(lambda: forward(step))
        pl.when(step == 0)(last.two)
        pl.when(step == 2)(last.three)
        pl.when(step >= 1)(lambda: backward(step - 1))
        return carried

    lax.fori_loop(0, PLANES + 1, one, 0)
    out_ref[...] = (middle_ref[...] + fed[...]).astype(jnp.bfloat16)
    for slot in (PLANES - 2, PLANES - 1):
        hand(slot).wait_send()
        for copy in flush(slot, slot % 2):
            copy.wait()
    links.drain()


def feed(normed, grad, middle, pieces):
    rows = normed.shape[0]
    count = pieces.shape[2]
    any_spec, vmem = pl.BlockSpec(memory_space=pl.ANY), pl.BlockSpec(memory_space=pltpu.VMEM)
    low = jnp.bfloat16
    return pl.pallas_call(
        feed_kernel,
        in_specs=[vmem, vmem, vmem, any_spec],
        out_specs=[vmem, vmem, any_spec],
        out_shape=[
            jax.ShapeDtypeStruct((rows, D), jnp.float32),
            jax.ShapeDtypeStruct((rows, D), low),
            jax.ShapeDtypeStruct((PLANES, 4, count, PIECE), low),
        ],
        scratch_shapes=[
            pltpu.VMEM((rows, D), jnp.float32),
            pltpu.VMEM((PLANES, count, D), low),
            pltpu.VMEM((2, 3, count // 3, rows), low),
            pltpu.VMEM((PLANES, 3, count // 3, rows), low),
            pltpu.VMEM((2, count, 4 * PIECE), low),
            pltpu.VMEM((2, rows, 4 * PIECE), low),
            pltpu.VMEM((2, rows, 4 * PIECE), low),
            pltpu.SemaphoreType.DMA((34,)),
            pltpu.SemaphoreType.DMA((34,)),
            pltpu.SemaphoreType.DMA((3, 8)),
            pltpu.SemaphoreType.DMA((2, 4)),
            pltpu.SemaphoreType.DMA,
        ],
        compiler_params=pltpu.CompilerParams(
            vmem_limit_bytes=CLOSE_VMEM, collective_id=2, has_side_effects=True
        ),
        name="feed",
    )(normed, grad, middle, pieces)


def add_into(target, source):
    rows = target.shape[0]
    chunk = next(c for c in (352, 256, rows) if rows % c == 0 and c <= rows)

    def one(index, carried):
        span = pl.ds(pl.multiple_of(index * chunk, chunk), chunk)
        target[span, :] = (
            target[span, :].astype(jnp.float32) + source[span, :].astype(jnp.float32)
        ).astype(jnp.bfloat16)
        return carried

    lax.fori_loop(0, rows // chunk, one, 0)


class Fold:
    def __init__(self, links, whole, first, final, bits):
        self.links, self.first, self.final = links, [first.at[m] for m in range(2)], final
        self.base = links.number(3)
        chip = lax.div(links.place, 2)
        ones = lambda bit: lax.rem(lax.div(chip, bit), 2)
        near, far = ones(bits[0]), ones(bits[1])
        self.away = [whole((1 - near) * bits[0] + m * bits[1]) for m in range(2)]
        self.stay = [whole(near * bits[0] + m * bits[1]) for m in range(2)]
        self.near_to = (flip(links.place, 2 * bits[0]), links.depth)
        self.far_to = (flip(links.place, 2 * bits[1]), links.depth)
        self.passed, self.own = first.at[1 - far], first.at[far]

    def one(self):
        for m in range(2):
            self.links.go(self.base + m, self.away[m], self.first[m], self.near_to)

    def two(self, stay=None):
        for m in range(2):
            self.links.got(self.base + m, self.first[m])
            add_into(self.first[m], self.stay[m] if stay is None else stay[m])
        self.links.go(self.base + 2, self.passed, self.final, self.far_to)

    def end(self):
        self.links.got(self.base + 2, self.final)
        add_into(self.final, self.own)


class LineFold:
    def __init__(self, links, block, held):
        self.links = links
        self.held = [[held.at[way, step] for step in range(PLANES - 1)] for way in range(2)]
        self.base = links.number(2 * (PLANES - 1))
        depth = links.depth
        self.blocks, self.sends, self.sums, self.takes, self.to = [], [], [], [], []
        for step in range(1, PLANES):
            right = jnp.minimum(depth + PLANES - step, PLANES - 1)
            left = jnp.maximum(depth - PLANES + step, 0)
            self.blocks.append((block(left), block(right)))
            self.sends.append((depth >= PLANES - step, depth < step))
            self.takes.append(((depth >= PLANES - 1 - step) & (depth < PLANES - 1), (depth <= step) & (depth > 0)))
        self.ends = (depth == PLANES - 1, depth == 0)
        self.to = (
            (links.place, jnp.maximum(depth - 1, 0)),
            (links.place, jnp.minimum(depth + 1, PLANES - 1)),
        )
        self.inner = [
            [self.sends[step][way] & jnp.logical_not(self.ends[way]) for way in range(2)]
            for step in range(PLANES - 1)
        ]
        self.outer = [
            [self.sends[step][way] & self.ends[way] for way in range(2)] for step in range(PLANES - 1)
        ]

    def launch(self, step):
        for way in range(2):
            self.links.go(
                self.base + 2 * (step - 1) + way,
                self.blocks[step - 1][way],
                self.held[way][step - 1],
                self.to[way],
                self.outer[step - 1][way],
            )

    def outer_plan(self, step):
        return [
            (
                self.base + 2 * (step - 1) + way,
                self.blocks[step - 1][way],
                self.held[way][step - 1],
                self.to[way],
                self.outer[step - 1][way],
            )
            for way in range(2)
        ]

    def go_all(self, planned):
        for parts in planned:
            self.links.go(*parts)

    def take(self, step):
        for way in range(2):
            self.links.got(
                self.base + 2 * (step - 1) + way, self.held[way][step - 1], self.takes[step - 1][way]
            )

    def forward(self, step):
        for way in range(2):
            before = self.held[way][step - 2]
            block = self.blocks[step - 1][way]

            @pl.when(self.inner[step - 1][way])
            def _():
                add_into(before, block)

            self.links.go(
                self.base + 2 * (step - 1) + way,
                before,
                self.held[way][step - 1],
                self.to[way],
                self.inner[step - 1][way],
            )

    def total(self, own, out):
        depth = self.links.depth
        rows = out.shape[0]
        chunk = next(c for c in (352, 256, rows) if rows % c == 0)

        def one(index, carried):
            span = pl.ds(pl.multiple_of(index * chunk, chunk), chunk)
            value = own[span, :].astype(jnp.float32)
            sides = [self.held[way][PLANES - 2][span, :].astype(jnp.float32) for way in range(2)]
            value = value + jnp.where(depth < PLANES - 1, sides[0], 0.0)
            out[span, :] = value + jnp.where(depth > 0, sides[1], 0.0)
            return carried

        lax.fori_loop(0, rows // chunk, one, 0)


def close_kernel(*refs):
    (made, low_in, attended_in, q_in, k_in, v_in, o_in, n_in, weight_in, cos_in, sin_in) = refs[:11]
    incoming = refs[11:15]
    log_ref, begin_ref, gain_ref, small_in = refs[15:19]
    first_ref, back_ref, feed_total, out_total, attn_total, small_ref = refs[19:25]
    (
        q_ref, k_ref, v_ref, o_ref, weight_ref, cos_ref, sin_ref, grad, inner, query_acc, key_acc, made_ref,
        stay, feed_first, feed_final, feed_held, out_made, out_core, out_first, out_final, out_held,
        attn_core, attn_first, attn_final, partial, partial_held, small_got,
        send, recv, local,
    ) = refs[25:]
    links = Links(send, recv)
    place, depth = links.place, links.depth
    length = q_ref.shape[0]
    shard = length // PLANES
    parity, chip = lax.rem(place, 2), lax.div(place, 2)
    core = (flip(place, 1), depth)
    loads = []

    def load(source, target):
        copy = pltpu.make_async_copy(source, target, local.at[len(loads)])
        copy.start()
        loads.append(copy)
        return copy

    order = (3, 2, 1, 0)

    def halved_fold(whole, first, final):
        return Halves(
            [
                Fold(
                    links,
                    lambda i, half=half: half_of(whole(i), half),
                    half_of(first, half),
                    half_of(final, half),
                    ((1, 2), (2, 1))[half],
                )
                for half in range(2)
            ]
        )

    folds = {
        slot: halved_fold(
            lambda i, slot=slot: made.at[slot, i], feed_first.at[slot], feed_final.at[slot]
        )
        for slot in order
    }
    out_fold = halved_fold(lambda i: out_core.at[i], out_first, out_final)
    attn_fold = halved_fold(lambda i: attn_core.at[i], attn_first, attn_final)

    def slot_holding(block):
        found = 0
        for plane in range(PLANES):
            for slot, (_, _, held) in enumerate(SLOTS[plane]):
                found = found + jnp.where((depth == plane) & (block == held), slot, 0)
        return found

    feed_line = LineFold(links, lambda j: feed_final.at[slot_holding(j)], feed_held)
    out_line = LineFold(
        links, lambda j: out_final.at[pl.ds(pl.multiple_of(j * 256, 256), 256), :], out_held
    )
    line = LineFold(links, lambda j: partial.at[j], partial_held)
    out_swap, attn_swap = links.number(4), links.number(4)
    sides = [columns_of(2 * i + parity) for i in range(4)]
    others = [columns_of(2 * i + 1 - parity) for i in range(4)]
    across = links.number(2 * PLANES)
    tiny = links.number(6)
    stays = [
        [[half_of(stay.at[index, m], half) for m in range(2)] for half in range(2)] for index in range(2)
    ]
    stay_sems = [[[16 + 4 * index + 2 * half + m for m in range(2)] for half in range(2)] for index in range(2)]

    def restay(slot):
        return [
            pltpu.make_async_copy(
                folds[slot].parts[half].stay[m],
                stays[slot % 2][half][m],
                local.at[stay_sems[slot % 2][half][m]],
            )
            for half in range(2)
            for m in range(2)
        ]

    tiny_to = [core, (flip(place, 2), depth), (flip(place, 4), depth)]
    plane_to = [(place, lax.rem(depth + step, PLANES)) for step in range(1, PLANES)]
    plane_rows = [lax.rem(depth - step + PLANES, PLANES) for step in range(PLANES)]

    attended_ref, low_ref = partial.at[0], partial.at[1]
    first_loads = [load(attended_in, attended_ref), load(low_in, low_ref)]
    for slot in order[:2]:
        for copy in restay(slot):
            copy.start()
    q_loads = [load(source, target) for source, target in ((q_in, q_ref), (k_in, k_ref), (v_in, v_ref), (o_in, o_ref), (cos_in, cos_ref), (sin_in, sin_ref))]
    own_rows = pl.ds(pl.multiple_of(depth * shard, shard), shard)
    q_loads.append(load(incoming[0], grad.at[own_rows, :]))
    weight_load = load(weight_in, weight_ref)

    links.greet()
    for pair in range(2):
        lanes = pl.ds(pair * 128, 128)
        for step in range(1, PLANES):
            links.go(
                across + 4 * pair + step,
                incoming[step].at[:, lanes],
                grad.at[own_rows, lanes],
                plane_to[step - 1],
            )
    folds[3].one()

    for copy in first_loads:
        copy.wait()
    for index in range(4):
        rows = pl.ds(index * 256, 256)
        out_made[rows, :] = tokens_dot(attended_ref[:, rows], low_ref[...], 0, 0).astype(jnp.bfloat16)
    out_swaps = [links.copy(out_swap + i, out_made.at[:, others[i]], out_core.at[i], core) for i in range(4)]
    for copy in out_swaps:
        copy.start()
    for i in range(4):
        links.got(out_swap + i, out_core.at[i])
        add_into(out_core.at[i], out_made.at[:, sides[i]])
    for copy in q_loads:
        copy.wait()

    def fold_two(slot):
        for copy in restay(slot):
            copy.wait()
        folds[slot].two(stays[slot % 2])

    fold_two(3)
    folds[2].one()
    grad_rows = [
        [
            grad.at[pl.ds(pl.multiple_of(plane_rows[step] * shard, shard), shard), pl.ds(pair * 128, 128)]
            for step in range(PLANES)
        ]
        for pair in range(2)
    ]

    def take_grads(pair):
        for step in range(1, PLANES):
            links.got(across + 4 * pair + step, grad_rows[pair][step])

    take_grads(0)

    lane = lax.broadcasted_iota(jnp.int32, (shard, 128), 1)
    keeps = [lane < HD, lane >= HD]
    down = lax.broadcasted_iota(jnp.int32, (shard, shard), 0)
    along = lax.broadcasted_iota(jnp.int32, (1, shard), 1)

    def masked(values, head):
        return jnp.where(keeps[head], values, jnp.zeros_like(values))

    def after_a():
        folds[3].end()
        feed_line.launch(1)
        out_fold.one()

    def after_b():
        fold_two(2)
        folds[1].one()
        for copy in restay(1):
            copy.start()

    def after_c():
        folds[2].end()
        feed_line.launch(2)
        feed_line.take(1)
        feed_line.forward(2)
        out_fold.two()

    def after_d():
        fold_two(1)
        folds[0].one()
        for copy in restay(0):
            copy.start()
        out_fold.end()
        for step in range(1, PLANES):
            out_line.launch(step)

    def after_e():
        folds[1].end()
        feed_line.launch(3)

    weight_load.wait()
    lower = depth < PLANES // 2
    query_acc[...] = jnp.zeros_like(query_acc)
    key_acc[...] = jnp.zeros_like(key_acc)
    first_ref[...] = jnp.zeros_like(first_ref)
    launches = [line.outer_plan(step) for step in range(1, PLANES)]

    def rows_of(block):
        return pl.ds(pl.multiple_of(block * shard, shard), shard)

    def back_step(index, carried):
        stage, pair = lax.div(index, 2), lax.rem(index, 2)
        block = jnp.where(lower, PLANES - 1 - stage, stage)
        lanes = columns_of(pair)
        own = rows_of(block)

        @pl.when(stage == 0)
        def _():
            for other in range(PLANES):
                span = pl.ds(other * shard, shard)
                turned = jnp.transpose(
                    grad[span, lanes].astype(jnp.float32) * o_ref[span, lanes].astype(jnp.float32)
                )
                for head in range(2):
                    inner[pair, head : head + 1, span] = jnp.sum(
                        turned[head * HD : head * HD + HD], axis=0, keepdims=True
                    )

        def tile(query_rows, key_rows, visible):
            keys, values = k_ref[key_rows, lanes], v_ref[key_rows, lanes]
            query_block, grad_block = q_ref[query_rows, lanes], grad[query_rows, lanes]
            queries = [masked(query_block, head) for head in range(2)]
            out_grads = [masked(grad_block, head) for head in range(2)]
            scores = [tokens_dot(keys, queries[head], 1, 1) for head in range(2)]
            share_grads = [tokens_dot(values, out_grads[head], 1, 1) for head in range(2)]
            score_grads, value_sum, key_sum = [], 0.0, 0.0
            for head in range(2):
                shares = jnp.where(
                    visible,
                    jnp.exp2(scores[head] - log_ref[pair, head : head + 1, query_rows]),
                    0.0,
                )
                score_grads.append(
                    (shares * (share_grads[head] - inner[pair, head : head + 1, query_rows])).astype(
                        jnp.bfloat16
                    )
                )
                value_sum = value_sum + tokens_dot(shares.astype(jnp.bfloat16), out_grads[head], 1, 0)
            for head in range(2):
                key_sum = key_sum + tokens_dot(score_grads[head], queries[head], 1, 0)
            first_ref[key_rows, lanes] += value_sum
            key_acc[key_rows, lanes] += key_sum
            query_acc[query_rows, lanes] += tokens_dot(
                score_grads[0], masked(keys, 0), 0, 0
            ) + tokens_dot(score_grads[1], masked(keys, 1), 0, 0)

        def off(other, held):
            query = rows_of(jnp.where(lower, block, block + 1 + other))
            key_block = jnp.where(lower, other, block)
            tile(query, rows_of(key_block), down >= begin_ref[0:1, query] - key_block * shard)
            return held

        tile(own, own, (down >= begin_ref[0:1, own] - block * shard) & (down <= along))
        lax.fori_loop(0, PLANES - 1 - stage, off, 0)
        cosine, sine_part = cos_ref[own, :], sin_ref[own, :]
        made_ref[own, columns_of(pair)] = turn(
            query_acc[own, lanes] * HD**-0.5, cosine, sine_part, False
        ).astype(jnp.bfloat16)
        made_ref[own, columns_of(2 + pair)] = turn(
            key_acc[own, lanes] * (1 / LOG2E), cosine, sine_part, False
        ).astype(jnp.bfloat16)
        half_sum = 0.5 * first_ref[own, lanes]
        made_ref[own, columns_of(4 + pair)] = half_sum.astype(jnp.bfloat16)
        first_ref[own, lanes] = half_sum

        @pl.when(pair == 1)
        def _():
            partial[block] = tokens_dot(
                made_ref[own, :], weight_ref[pl.ds(0, 768), :], 1, 0
            ).astype(jnp.bfloat16)
            for number, parts in enumerate(launches):
                pl.when(stage == number)(functools.partial(line.go_all, parts))

        pl.when(index == 0)(lambda: take_grads(1))
        for when, pump in ((0, after_a), (1, after_b), (2, after_c), (4, after_d), (7, after_e)):
            pl.when(index == when)(pump)
        return carried

    lax.fori_loop(0, 2 * PLANES, back_step, 0)
    quarters = [q_ref, k_ref, v_ref, o_ref]
    quarter_loads = [
        load(n_in.at[:, pl.ds(index * 256, 256)], quarter) for index, quarter in enumerate(quarters)
    ]
    small_ref[...] = small_in[...]
    line.take(1)
    line.forward(2)
    for copy in quarter_loads:
        copy.wait()

    def gain_back(block, carried):
        rows = pl.ds(pl.multiple_of(block * shard, shard), shard)
        for index, quarter in enumerate(quarters):
            value = partial[block, :, pl.ds(index * 256, 256)].astype(jnp.float32)
            lanes = pl.ds(index * 256, 256)
            gain = (
                jnp.sum(value * quarter[rows, :].astype(jnp.float32), axis=0, keepdims=True)
                / gain_ref[0:1, lanes]
            )
            for half in range(2):
                piece = 2 * index + half
                small_ref[0, piece : piece + 1, :] += gain[:, half * PIECE : half * PIECE + PIECE]
        return carried

    lax.fori_loop(0, PLANES, gain_back, 0)
    fold_two(0)
    links.go(tiny, small_ref.at[0], small_got.at[0], tiny_to[0])
    feed_line.take(2)
    feed_line.forward(3)
    for copy in out_swaps:
        copy.wait_send()
    attn_made = out_made.at[pl.ds(0, 768), :]
    for index in range(3):
        rows = pl.ds(index * 256, 256)
        for quarter in range(4):
            attn_made[rows, pl.ds(quarter * 256, 256)] = tokens_dot(
                made_ref[:, rows], quarters[quarter][...], 0, 0
            ).astype(jnp.bfloat16)
    for i in range(4):
        links.go(attn_swap + i, attn_made.at[:, others[i]], attn_core.at[i], core)
    links.got(tiny, small_got.at[0])
    small_ref[1] = small_ref[0] + small_got[0]
    links.go(tiny + 1, small_ref.at[1], small_got.at[1], tiny_to[1])
    for i in range(4):
        links.got(attn_swap + i, attn_core.at[i])
        add_into(attn_core.at[i], attn_made.at[:, sides[i]])
    attn_fold.one()
    links.got(tiny + 1, small_got.at[1])
    small_ref[2] = small_ref[1] + small_got[1]
    links.go(tiny + 2, small_ref.at[2], small_got.at[2], tiny_to[2])
    line.take(2)
    line.forward(3)
    links.got(tiny + 2, small_got.at[2])
    small_ref[3] = small_ref[2] + small_got[2]
    small_place = small_got.at[3 + depth]
    for step in range(1, PLANES):
        links.go(tiny + 2 + step, small_ref.at[3], small_place, plane_to[step - 1])
    small_got[3 + depth] = small_ref[3]
    out_line.take(1)
    out_line.forward(2)
    attn_fold.two()
    folds[0].end()
    out_line.take(2)
    out_line.forward(3)
    attn_fold.end()
    attn_total[...] = attn_final[...].astype(jnp.float32)
    line.take(3)
    line.total(partial.at[depth], back_ref)
    feed_line.take(3)
    feed_line.total(feed_final.at[0], feed_total)
    out_line.take(3)
    out_line.total(out_final.at[pl.ds(pl.multiple_of(depth * 256, 256), 256), :], out_total)
    for step in range(1, PLANES):
        links.got(tiny + 2 + step, small_got.at[3 + plane_rows[step]])
    small_ref[4] = small_got[3] + small_got[4] + small_got[5] + small_got[6]
    links.drain()


def closing(made, low_ref, attended_own, heads, normed, weight, tables, incoming, logs, begin_row, gains, small):
    length, width = heads[0].shape
    rows = low_ref.shape[0]
    count = made.shape[2]
    low, full = jnp.bfloat16, jnp.float32
    any_spec, vmem = pl.BlockSpec(memory_space=pl.ANY), pl.BlockSpec(memory_space=pltpu.VMEM)
    shape = jax.ShapeDtypeStruct
    return pl.pallas_call(
        close_kernel,
        in_specs=[any_spec] * 15 + [vmem] * 4,
        out_specs=[vmem] * 6,
        out_shape=[
            shape((length, width), full),
            shape((rows, D), full),
            shape((count, PIECE), full),
            shape((256, PIECE), full),
            shape((768, PIECE), full),
            shape((5, 24, PIECE), full),
        ],
        scratch_shapes=[pltpu.VMEM((length, width), low)] * 4
        + [
            pltpu.VMEM((ATTN_ROWS, D), low),
            pltpu.VMEM((length, 128), full),
            pltpu.VMEM((length, 128), full),
            pltpu.VMEM((length, width), low),
            pltpu.VMEM((2, 8, length), full),
            pltpu.VMEM((length, width), full),
            pltpu.VMEM((length, width), full),
            pltpu.VMEM((length, 768), low),
            pltpu.VMEM((2, 2, count, PIECE), low),
            pltpu.VMEM((PLANES, 2, count, PIECE), low),
            pltpu.VMEM((PLANES, count, PIECE), low),
            pltpu.VMEM((2, PLANES - 1, count, PIECE), low),
            pltpu.VMEM((D, D), low),
            pltpu.VMEM((4, D, PIECE), low),
            pltpu.VMEM((2, D, PIECE), low),
            pltpu.VMEM((D, PIECE), low),
            pltpu.VMEM((2, PLANES - 1, 256, PIECE), low),
            pltpu.VMEM((4, 768, PIECE), low),
            pltpu.VMEM((2, 768, PIECE), low),
            pltpu.VMEM((768, PIECE), low),
            pltpu.VMEM((PLANES, rows, D), low),
            pltpu.VMEM((2, PLANES - 1, rows, D), low),
            pltpu.VMEM((7, 24, PIECE), full),
            pltpu.SemaphoreType.DMA((CLOSE_COPIES,)),
            pltpu.SemaphoreType.DMA((CLOSE_COPIES,)),
            pltpu.SemaphoreType.DMA((24,)),
        ],
        compiler_params=pltpu.CompilerParams(
            vmem_limit_bytes=CLOSE_VMEM, collective_id=3, has_side_effects=True
        ),
        name="closing",
    )(made, low_ref, attended_own, *heads, normed, weight, *tables, *incoming, logs, begin_row, gains, small)


def middle_back_kernel(*refs):
    middle_ref, grad_ref, back_ref, weight_ref, gain_ref = refs[:5]
    low_ref, dm_ref, gain_grad_ref = refs[5:8]
    outs = refs[8:12]
    depth = lax.axis_index("mp")
    half = middle_ref.shape[0] // 2
    gain = gain_ref[1:2, :]
    gain_grad_ref[...] = jnp.zeros_like(gain_grad_ref)
    for tile in range(2):
        rows = pl.ds(tile * half, half)
        middle, incoming = middle_ref[rows, :], back_ref[rows, :]
        factor = lax.rsqrt(jnp.mean(middle * middle, axis=-1, keepdims=True) + 1e-06)
        scaled = incoming * gain
        mean = jnp.mean(scaled * middle, axis=-1, keepdims=True)
        total = grad_ref[rows, :].astype(jnp.float32) + factor * scaled - middle * (factor**3 * mean)
        gain_grad_ref[0:1, :] += jnp.sum(incoming * middle * factor, axis=0, keepdims=True)
        dm_ref[rows, :] = total
        low_ref[rows, :] = total.astype(jnp.bfloat16)
    for index, out in enumerate(outs):
        owner = lax.rem(depth + index, PLANES)
        rows = pl.ds(pl.multiple_of(owner * 256, 256), 256)
        out[...] = tokens_dot(low_ref[...], weight_ref[rows, :], 1, 1).astype(jnp.bfloat16)


def middle_back(middle, grad, back, weight, gains):
    rows = middle.shape[0]
    return pl.pallas_call(
        middle_back_kernel,
        out_shape=[
            jax.ShapeDtypeStruct((rows, D), jnp.bfloat16),
            jax.ShapeDtypeStruct((rows, D), jnp.float32),
            jax.ShapeDtypeStruct((8, D), jnp.float32),
        ]
        + [jax.ShapeDtypeStruct((rows, 256), jnp.bfloat16)] * PLANES,
        compiler_params=pltpu.CompilerParams(vmem_limit_bytes=VMEM_LIMIT),
        cost_estimate=cost(2 * rows * D * D, 12 << 20),
        name="middle_back",
    )(middle, grad, back, weight, gains)


def stepped(master, gradient, moment, square, step_rate, decay, outs, at):
    new = adamw(master[at], gradient, moment[at], square[at], step_rate, decay)
    for out, value in zip(outs, new):
        out[at] = value


def update_kernel(*refs):
    hidden_ref, dm_ref, back_ref, gain_ref, attn_ref, out_ref, feed_ref, small_ref = refs[:8]
    masters, moments, squares = refs[8:13], refs[13:18], refs[18:23]
    grad_ref, norm_ref = refs[23:25]
    outs = [refs[25 + index : 40 : 5] for index in range(5)]
    place = lax.axis_index("dp")
    hidden = hidden_ref[...].astype(jnp.float32)
    factor = rms_factor(hidden)
    grad_ref[...] = dm_ref[...] + norm_back(hidden, factor, gain_ref[0:1, :], back_ref[...])[0]
    tokens = 8.0 * hidden_ref.shape[0] * PLANES
    norm_ref[...] = jnp.sqrt(small_ref[16:24, :] / (tokens * D))
    every = slice(None)
    rates = (D**-0.5, max(1, 8 * HEADS * HD // LEN) ** -0.5, D**-0.5, (FF // 3) ** -0.5)

    def weight(index, gradient, at):
        stepped(
            masters[index], gradient, moments[index], squares[index], rates[index], 0.1, outs[index], at
        )

    for which in range(3):
        weight(0, jnp.transpose(attn_ref[pl.ds(which * 256, 256), :]), which)
    weight(1, out_ref[...], (every, every))
    count = masters[3].shape[0]
    for which in range(2):
        weight(2, feed_ref[pl.ds(which * count, count), :], which)
    weight(3, feed_ref[pl.ds(2 * count, count), :], (every, every))
    for which in range(2):
        at = pl.ds(which, 1)
        stepped(
            masters[4],
            small_ref[pl.ds(8 * which + place, 1), :],
            moments[4],
            squares[4],
            0.2,
            0.0,
            outs[4],
            (at, every),
        )


def update(hidden, dm, back, gains, totals, small, masters, moments, squares):
    full = jnp.float32
    shape = jax.ShapeDtypeStruct
    return pl.pallas_call(
        update_kernel,
        out_shape=[shape(dm.shape, full), shape((8, PIECE), full)]
        + [shape(one.shape, full) for one in masters] * 3,
        compiler_params=pltpu.CompilerParams(vmem_limit_bytes=VMEM_LIMIT),
        cost_estimate=cost(0, 16 << 20),
        name="update",
    )(hidden, dm, back, gains, *totals, small, *masters, *moments, *squares)


def fast_shards(
    hidden_in,
    segment_ids,
    first_values,
    grad_out,
    input_proj,
    output_proj,
    expand_proj,
    reduce_proj,
    norm_gains,
    old_moment_input,
    old_moment_output,
    old_moment_expand,
    old_moment_reduce,
    old_moment_gains,
    old_square_input,
    old_square_output,
    old_square_expand,
    old_square_reduce,
    old_square_gains,
):
    place, depth = lax.axis_index("dp"), lax.axis_index("mp")
    low = jnp.bfloat16
    hidden, out_cotangent = hidden_in[0], grad_out[0]
    ffs = reduce_proj.shape[0]

    attn_piece = jnp.concatenate(
        [
            input_proj.astype(low).transpose(0, 2, 1).reshape(768, PIECE),
            norm_gains.astype(low),
            jnp.zeros((14, PIECE), low),
        ]
    )
    feed_piece = jnp.concatenate(
        [
            expand_proj.astype(low).transpose(0, 2, 1).reshape(2 * ffs, PIECE),
            reduce_proj.astype(low),
        ]
    )

    (
        queries,
        keys,
        values,
        attended,
        normed,
        attn_weight,
        out_weight,
        feed_all,
        cosine,
        sine_part,
        gains,
        squares,
        logs,
        middle,
        normed_two,
        attended_own,
        begin_row,
    ) = opening(hidden, attn_piece, output_proj.astype(low), feed_piece, first_values[0], segment_ids)
    normed_two_grad, layer_output, made = feed(normed_two, out_cotangent, middle, feed_all)
    layer_output = layer_output[None]
    branch_low, middle_grad, gain_two, *out_grads = middle_back(
        middle, out_cotangent, normed_two_grad, out_weight, gains
    )
    small = jnp.concatenate(
        [
            jnp.zeros((8, PIECE), jnp.float32),
            gain_two[0].reshape(8, PIECE),
            jnp.broadcast_to(jnp.sum(squares[:2], axis=1)[:, None], (2, PIECE)),
            jnp.zeros((6, PIECE), jnp.float32),
        ]
    )
    values_grad, normed_grad, feed_total, out_total, attn_total, small = closing(
        made,
        branch_low,
        attended_own,
        (queries, keys, values, attended),
        normed,
        attn_weight,
        (cosine, sine_part),
        out_grads,
        logs,
        begin_row,
        gains,
        jnp.broadcast_to(small[None], (5, 24, PIECE)),
    )
    small = small[4]
    masters = [input_proj, output_proj, expand_proj, reduce_proj, norm_gains]
    moments = [
        old_moment_input,
        old_moment_output,
        old_moment_expand,
        old_moment_reduce,
        old_moment_gains,
    ]
    squares = [
        old_square_input,
        old_square_output,
        old_square_expand,
        old_square_reduce,
        old_square_gains,
    ]
    for group in (masters, moments, squares):
        group[2] = group[2].transpose(0, 2, 1)
    input_grad, norms, *updated = update(
        hidden,
        middle_grad,
        normed_grad,
        gains,
        (attn_total, out_total, feed_total),
        small,
        masters,
        moments,
        squares,
    )
    for index in (2, 7, 12):
        updated[index] = updated[index].transpose(0, 2, 1)
    return (layer_output, input_grad[None], values_grad[None], norms[:2, 0], *updated)


def solution(mesh):
    quick = mesh.shape["dp"] == 8 and mesh.shape["mp"] == PLANES
    return jax.shard_map(
        fast_shards if quick else shards,
        mesh=mesh,
        in_specs=(
            P("dp", "mp", None),
            P("dp", None),
            P("dp", None, "mp"),
            P("dp", "mp", None),
            P(None, "dp", "mp"),
            P("mp", "dp"),
            P(None, "dp", "mp"),
            P("mp", "dp"),
            P(None, "dp"),
            P(None, "dp", "mp"),
            P("mp", "dp"),
            P(None, "dp", "mp"),
            P("mp", "dp"),
            P(None, "dp"),
            P(None, "dp", "mp"),
            P("mp", "dp"),
            P(None, "dp", "mp"),
            P("mp", "dp"),
            P(None, "dp"),
        ),
        out_specs=(
            P("dp", "mp", None),
            P("dp", "mp", None),
            P("dp", None, "mp"),
            P(),
            P(None, "dp", "mp"),
            P("mp", "dp"),
            P(None, "dp", "mp"),
            P("mp", "dp"),
            P(None, "dp"),
            P(None, "dp", "mp"),
            P("mp", "dp"),
            P(None, "dp", "mp"),
            P("mp", "dp"),
            P(None, "dp"),
            P(None, "dp", "mp"),
            P("mp", "dp"),
            P(None, "dp", "mp"),
            P("mp", "dp"),
            P(None, "dp"),
        ),
        check_vma=False,
    )
```

```python
import functools
import math

import jax
import jax.numpy as jnp
import numpy as np
from jax import lax
from jax.experimental import pallas as pl
from jax.experimental.pallas import tpu as pltpu
from jax.sharding import PartitionSpec as P

D = 1024
HEADS = 16
HD = 64
FF = 2816
LEN = 2048
STEP = 5
PLANES = 4
PIECE = 128
BLOCKS = 4
ATTN_ROWS = 784
VMEM_LIMIT = 56 << 20
OPEN_COPIES = 100
CLOSE_COPIES = 80
CLOSE_VMEM = 60 << 20


def arrivals(plane):
    order = [(0, 0, plane)]
    for hop in range(1, PLANES):
        if plane + hop < PLANES:
            order.append((0, hop, plane + hop))
        if plane - hop >= 0:
            order.append((1, hop, plane - hop))
    return order


SLOTS = [arrivals(plane) for plane in range(PLANES)]


def cost(flops, moved):
    return pl.CostEstimate(flops=flops, bytes_accessed=moved, transcendentals=0)


def rope_tables(seg_row, head_size):
    length = seg_row.shape[0]
    places = jnp.arange(length, dtype=jnp.int32)
    begins = jnp.sum((seg_row[None, :] < seg_row[:, None]).astype(jnp.int32), axis=1)
    offset = (places - begins).astype(jnp.float32)
    inverse_rates = 10000.0 ** (-2.0 * jnp.arange(head_size // 2, dtype=jnp.float32) / head_size)
    angles = offset[:, None] * inverse_rates[None, :]
    return (jnp.cos(angles)[:, None, :], jnp.sin(angles)[:, None, :])


def rotate(values, cosine, sine_part, forward):
    half_size = values.shape[-1] // 2
    first_half = values[..., :half_size]
    second_half = values[..., half_size:]
    if forward:
        return jnp.concatenate(
            [
                first_half * cosine - second_half * sine_part,
                second_half * cosine + first_half * sine_part,
            ],
            axis=-1,
        )
    return jnp.concatenate(
        [
            first_half * cosine + second_half * sine_part,
            second_half * cosine - first_half * sine_part,
        ],
        axis=-1,
    )


def rms_factor(values):
    return lax.rsqrt(jnp.mean(values * values, axis=-1, keepdims=True) + 1e-06)


def norm_back(values, factor, gain_row, incoming):
    scaled = incoming * gain_row
    value_grad = factor * scaled - values * factor**3 * jnp.mean(
        scaled * values, axis=-1, keepdims=True
    )
    gain_grad = jnp.sum(incoming * values * factor, axis=0)
    return (value_grad, gain_grad)


def visible_block(seg_row, first_row, block_rows):
    length = seg_row.shape[0]
    query_seg = lax.dynamic_slice_in_dim(seg_row, first_row, block_rows, 0)
    query_places = first_row + jnp.arange(block_rows, dtype=jnp.int32)
    key_places = jnp.arange(length, dtype=jnp.int32)
    return (query_seg[:, None] == seg_row[None, :]) & (query_places[:, None] >= key_places[None, :])


def block_scores(queries, keys_rot, seg_row, first_row, block_rows, score_scale):
    query_block = lax.dynamic_slice_in_dim(queries, first_row, block_rows, 0)
    visible = visible_block(seg_row, first_row, block_rows)
    scores = (
        jnp.einsum("qhd,khd->hqk", query_block, keys_rot, preferred_element_type=jnp.float32)
        * score_scale
    )
    return (query_block, jnp.where(visible[None], scores, -1e30))


def attend(queries, keys_rot, mixed_values, seg_row, score_scale):
    length = queries.shape[0]
    block_rows = min(512, length)

    def one_block(block_index):
        first_row = block_index * block_rows
        query_block, scores = block_scores(
            queries, keys_rot, seg_row, first_row, block_rows, score_scale
        )
        top_score = jnp.max(scores, axis=-1, keepdims=True)
        raised = jnp.exp(scores - top_score)
        totals = jnp.sum(raised, axis=-1, keepdims=True)
        shares = (raised / totals).astype(jnp.bfloat16)
        combined = jnp.einsum(
            "hqk,khd->qhd", shares, mixed_values, preferred_element_type=jnp.float32
        )
        return (combined, (top_score + jnp.log(totals))[..., 0])

    combined, log_totals = lax.map(one_block, jnp.arange(length // block_rows, dtype=jnp.int32))
    return (combined.reshape(length, -1), log_totals)


def attend_back(queries, keys_rot, mixed_values, out_grad, log_totals, seg_row, score_scale):
    length = queries.shape[0]
    block_rows = min(512, length)

    def one_block(running, operands):
        key_sum, value_sum = running
        block_index, block_totals = operands
        first_row = block_index * block_rows
        query_block, scores = block_scores(
            queries, keys_rot, seg_row, first_row, block_rows, score_scale
        )
        grad_block = lax.dynamic_slice_in_dim(out_grad, first_row, block_rows, 0)
        shares = jnp.exp(scores - block_totals[..., None])
        share_grad = jnp.einsum(
            "qhd,khd->hqk", grad_block, mixed_values, preferred_element_type=jnp.float32
        )
        inner = jnp.sum(shares * share_grad, axis=-1, keepdims=True)
        score_grad = (shares * (share_grad - inner)).astype(jnp.bfloat16)
        query_grad = (
            jnp.einsum("hqk,khd->qhd", score_grad, keys_rot, preferred_element_type=jnp.float32)
            * score_scale
        )
        key_sum = (
            key_sum
            + jnp.einsum(
                "hqk,qhd->khd", score_grad, query_block, preferred_element_type=jnp.float32
            )
            * score_scale
        )
        value_sum = value_sum + jnp.einsum(
            "hqk,qhd->khd",
            shares.astype(jnp.bfloat16),
            grad_block,
            preferred_element_type=jnp.float32,
        )
        return ((key_sum, value_sum), query_grad)

    empty_sum = jnp.zeros(keys_rot.shape, jnp.float32)
    (key_grad, value_grad), query_grad = lax.scan(
        one_block,
        (empty_sum, empty_sum),
        (jnp.arange(length // block_rows, dtype=jnp.int32), log_totals),
    )
    return (query_grad.reshape(keys_rot.shape), key_grad, value_grad)


def adamw(master, gradient, moment, square, step_rate, decay):
    new_moment = 0.5 * moment + 0.5 * gradient
    new_square = 0.5 * square + 0.5 * gradient * gradient
    correct = 1.0 - 0.5**STEP
    update = new_moment / correct / (jnp.sqrt(new_square / correct) + 1e-08)
    return (master - step_rate * (update + decay * master), new_moment, new_square)


def shards(
    hidden_in,
    segment_ids,
    first_values,
    grad_out,
    input_proj,
    output_proj,
    expand_proj,
    reduce_proj,
    norm_gains,
    old_moment_input,
    old_moment_output,
    old_moment_expand,
    old_moment_reduce,
    old_moment_gains,
    old_square_input,
    old_square_output,
    old_square_expand,
    old_square_reduce,
    old_square_gains,
):
    attn_weight, out_weight, expand_weight, reduce_weight, gains_low = (
        lax.all_gather(input_proj.astype(jnp.bfloat16), "dp", axis=1, tiled=True),
        lax.all_gather(output_proj.astype(jnp.bfloat16), "dp", axis=1, tiled=True),
        lax.all_gather(expand_proj.astype(jnp.bfloat16), "dp", axis=1, tiled=True),
        lax.all_gather(reduce_proj.astype(jnp.bfloat16), "dp", axis=1, tiled=True),
        lax.all_gather(norm_gains.astype(jnp.bfloat16), "dp", axis=1, tiled=True),
    )
    gains = gains_low.astype(jnp.float32)
    hidden = hidden_in[0].astype(jnp.float32)
    seg_row = segment_ids[0]
    length = seg_row.shape[0]
    first_in = first_values[0].astype(jnp.float32)
    local_heads = attn_weight.shape[2] // HD
    score_scale = 1.0 / math.sqrt(HD)
    factor_one = rms_factor(hidden)
    normed_one = (hidden * factor_one * gains[0]).astype(jnp.bfloat16)
    all_normed, all_grad_out = (
        lax.all_gather(normed_one, "mp", axis=0, tiled=True),
        lax.all_gather(grad_out[0], "mp", axis=0, tiled=True),
    )
    projected = jnp.einsum(
        "td,cde->cte", all_normed, attn_weight, preferred_element_type=jnp.float32
    )
    cosine, sine_part = rope_tables(seg_row, HD)
    queries = rotate(projected[0].reshape(length, local_heads, HD), cosine, sine_part, True).astype(
        jnp.bfloat16
    )
    keys_rot = rotate(
        projected[1].reshape(length, local_heads, HD), cosine, sine_part, True
    ).astype(jnp.bfloat16)
    blended = 0.5 * projected[2] + 0.5 * first_in
    mixed_values = blended.astype(jnp.bfloat16).reshape(length, local_heads, HD)
    square_terms = jnp.stack([jnp.sum(first_in * first_in), jnp.sum(blended * blended)])
    attended, log_totals = attend(queries, keys_rot, mixed_values, seg_row, score_scale)
    attended_low = attended.astype(jnp.bfloat16)
    rows_part = attended_low
    branch = lax.psum_scatter(
        jnp.dot(rows_part, out_weight, preferred_element_type=jnp.float32),
        "mp",
        scatter_dimension=0,
        tiled=True,
    )
    middle = hidden + branch
    factor_two = rms_factor(middle)
    normed_two = (middle * factor_two * gains[1]).astype(jnp.bfloat16)
    all_normed_two = lax.all_gather(normed_two, "mp", axis=0, tiled=True)
    gate_up = jnp.einsum(
        "td,cdf->ctf", all_normed_two, expand_weight, preferred_element_type=jnp.float32
    )
    gate_sig = jax.nn.sigmoid(gate_up[0])
    gate_act = gate_up[0] * gate_sig
    activated = (gate_act * gate_up[1]).astype(jnp.bfloat16)
    rows_part = activated
    feed_out = lax.psum_scatter(
        jnp.dot(rows_part, reduce_weight, preferred_element_type=jnp.float32).astype(jnp.bfloat16),
        "mp",
        scatter_dimension=0,
        tiled=True,
    ).astype(jnp.float32)
    layer_output = (middle + feed_out).astype(jnp.bfloat16)[None]
    hidden_grad = jnp.einsum(
        "td,fd->tf", all_grad_out, reduce_weight, preferred_element_type=jnp.float32
    )
    reduce_grad = jnp.einsum(
        "tf,td->fd", activated, all_grad_out, preferred_element_type=jnp.float32
    )
    gate_grad = hidden_grad * gate_up[1] * gate_sig * (1.0 + gate_up[0] * (1.0 - gate_sig))
    up_grad = hidden_grad * gate_act
    pair_grad = jnp.stack([gate_grad, up_grad]).astype(jnp.bfloat16)
    expand_grad = jnp.einsum(
        "ctf,td->cdf", pair_grad, all_normed_two, preferred_element_type=jnp.float32
    )
    rows_part = pair_grad
    normed_two_grad = lax.psum_scatter(
        jnp.einsum(
            "ctf,cdf->td", rows_part, expand_weight, preferred_element_type=jnp.float32
        ).astype(jnp.bfloat16),
        "mp",
        scatter_dimension=0,
        tiled=True,
    ).astype(jnp.float32)
    middle_part, gain_two_grad = norm_back(middle, factor_two, gains[1], normed_two_grad)
    middle_grad = grad_out[0].astype(jnp.float32) + middle_part
    branch_low = middle_grad.astype(jnp.bfloat16)
    all_branch = lax.all_gather(branch_low, "mp", axis=0, tiled=True)
    out_grad = jnp.einsum("te,td->ed", attended_low, all_branch, preferred_element_type=jnp.float32)
    attended_grad = jnp.einsum(
        "td,ed->te", all_branch, out_weight, preferred_element_type=jnp.float32
    ).astype(jnp.bfloat16)
    query_grad, key_grad, mix_grad = attend_back(
        queries,
        keys_rot,
        mixed_values,
        attended_grad.reshape(length, local_heads, HD),
        log_totals,
        seg_row,
        score_scale,
    )
    query_grad = rotate(query_grad, cosine, sine_part, False).reshape(length, -1)
    key_grad = rotate(key_grad, cosine, sine_part, False).reshape(length, -1)
    mix_grad = mix_grad.reshape(length, -1)
    values_grad = (0.5 * mix_grad)[None]
    proj_grad = jnp.stack([query_grad, key_grad, 0.5 * mix_grad]).astype(jnp.bfloat16)
    attn_grad = jnp.einsum("cte,td->cde", proj_grad, all_normed, preferred_element_type=jnp.float32)
    rows_part = proj_grad
    normed_one_grad = lax.psum_scatter(
        jnp.einsum(
            "cte,cde->td", rows_part, attn_weight, preferred_element_type=jnp.float32
        ).astype(jnp.bfloat16),
        "mp",
        scatter_dimension=0,
        tiled=True,
    ).astype(jnp.float32)
    input_part, gain_one_grad = norm_back(hidden, factor_one, gains[0], normed_one_grad)
    input_grad = (middle_grad + input_part)[None]
    attn_total, out_total, expand_total, reduce_total = (
        lax.psum_scatter(
            attn_grad.astype(jnp.bfloat16), "dp", scatter_dimension=1, tiled=True
        ).astype(jnp.float32),
        lax.psum_scatter(
            out_grad.astype(jnp.bfloat16), "dp", scatter_dimension=1, tiled=True
        ).astype(jnp.float32),
        lax.psum_scatter(
            expand_grad.astype(jnp.bfloat16), "dp", scatter_dimension=1, tiled=True
        ).astype(jnp.float32),
        lax.psum_scatter(
            reduce_grad.astype(jnp.bfloat16), "dp", scatter_dimension=1, tiled=True
        ).astype(jnp.float32),
    )
    gain_totals, square_sums = lax.psum(
        (jnp.stack([gain_one_grad, gain_two_grad]), square_terms), ("dp", "mp")
    )
    gain_width = norm_gains.shape[1]
    gain_total = lax.dynamic_slice_in_dim(
        gain_totals, lax.axis_index("dp") * gain_width, gain_width, 1
    )
    value_norms = jnp.sqrt(square_sums / (lax.axis_size("dp") * length * D))
    new_input = adamw(input_proj, attn_total, old_moment_input, old_square_input, D ** (-0.5), 0.1)
    new_output = adamw(
        output_proj,
        out_total,
        old_moment_output,
        old_square_output,
        max(1, 8 * HEADS * HD // LEN) ** (-0.5),
        0.1,
    )
    new_expand = adamw(
        expand_proj, expand_total, old_moment_expand, old_square_expand, D ** (-0.5), 0.1
    )
    new_reduce = adamw(
        reduce_proj, reduce_total, old_moment_reduce, old_square_reduce, (FF // 3) ** (-0.5), 0.1
    )
    new_gains = adamw(norm_gains, gain_total, old_moment_gains, old_square_gains, 0.2, 0.0)
    return (
        layer_output,
        input_grad,
        values_grad,
        value_norms,
        new_input[0],
        new_output[0],
        new_expand[0],
        new_reduce[0],
        new_gains[0],
        new_input[1],
        new_output[1],
        new_expand[1],
        new_reduce[1],
        new_gains[1],
        new_input[2],
        new_output[2],
        new_expand[2],
        new_reduce[2],
        new_gains[2],
    )


def tokens_dot(a, b, left, right):
    return lax.dot_general(a, b, (((left,), (right,)), ((), ())), preferred_element_type=jnp.float32)


def piece_columns(place, step):
    start = jnp.bitwise_xor(place, step) * PIECE
    return pl.ds(pl.multiple_of(start, PIECE), PIECE)


def turn(values, cosine, sine_part, forward):
    lane = lax.broadcasted_iota(jnp.int32, values.shape, 1)
    swapped = jnp.where(
        lax.rem(lane, HD) < HD // 2, pltpu.roll(values, 96, 1), pltpu.roll(values, 32, 1)
    )
    if forward:
        return values * cosine + swapped * sine_part
    return values * cosine - swapped * sine_part


MESH = pl.DeviceIdType.MESH
LOG2E = 1.4426950408889634


def flip(place, bit):
    return place + bit - 2 * bit * lax.rem(lax.div(place, bit), 2)


def at_plane(depth, values):
    found = 0
    for plane, value in enumerate(values):
        found = found + jnp.where(depth == plane, value, 0)
    return found


def slot_at(depth, way, hop):
    return at_plane(
        depth,
        [
            next((k for k, s in enumerate(SLOTS[plane]) if s[:2] == (way, hop)), 0)
            for plane in range(PLANES)
        ],
    )


def columns_of(piece, width=PIECE):
    return pl.ds(pl.multiple_of(piece * width, width), width)


class Links:
    def __init__(self, send, recv):
        self.send, self.recv, self.count, self.started, self.waited = send, recv, 0, [], []
        self.place, self.depth = lax.axis_index("dp"), lax.axis_index("mp")

    def number(self, count=1):
        self.count += count
        return self.count - count

    def copy(self, number, source, target, to):
        return pltpu.make_async_remote_copy(
            src_ref=source,
            dst_ref=target,
            send_sem=self.send.at[number],
            recv_sem=self.recv.at[number],
            device_id=to,
            device_id_type=MESH,
        )

    def go(self, number, source, target, to, when=None):
        copy = self.copy(number, source, target, to)
        self.started.append((number, source, target, to, when))
        if when is None:
            copy.start()
        else:
            pl.when(when)(copy.start)

    def got(self, number, landed, when=None):
        copy = self.copy(number, landed, landed, (flip(self.place, 1), self.depth))
        if when is None:
            copy.wait_recv()
        else:
            pl.when(when)(copy.wait_recv)

    def drain(self):
        for *parts, when in self.started:
            copy = self.copy(*parts)
            for plane in [plane for number, plane in self.waited if number == parts[0]]:
                when = when & (self.depth != plane)
            if when is None:
                copy.wait_send()
            else:
                pl.when(when)(copy.wait_send)

    def greet(self, planes=True):
        barrier = pltpu.get_barrier_semaphore()
        others = [(flip(self.place, bit), self.depth) for bit in (1, 2, 4)]
        if planes:
            others += [(self.place, lax.rem(self.depth + step, PLANES)) for step in range(1, PLANES)]
        for other in others:
            pl.semaphore_signal(barrier, inc=1, device_id=other, device_id_type=MESH)
        pl.semaphore_wait(barrier, len(others))


class Spread:
    def __init__(self, links, own, spot, bits):
        self.links, self.own = links, own
        self.base = links.number(7)
        place = links.place
        first, second = flip(place, bits[0]), flip(place, bits[1])
        self.spots = [spot(piece) for piece in (place, first, second, flip(first, bits[1]))]
        self.lands = [
            spot(flip(piece, 1)) for piece in (place, first, second, flip(first, bits[1]))
        ]
        self.near, self.far, self.core = [
            (flip(place, bit), links.depth) for bit in (bits[0], bits[1], 1)
        ]

    def one(self):
        self.links.go(self.base, self.own, self.spots[0], self.near)

    def two(self):
        links, spots = self.links, self.spots
        links.go(self.base + 1, self.own, spots[0], self.far)
        links.got(self.base, spots[1])
        links.go(self.base + 2, spots[1], spots[1], self.far)

    def landed(self):
        self.links.got(self.base + 1, self.spots[2])
        self.links.got(self.base + 2, self.spots[3])

    def three(self):
        links, spots = self.links, self.spots
        links.go(self.base + 3, self.own, spots[0], self.core)
        links.go(self.base + 4, spots[1], spots[1], self.core)
        links.got(self.base + 1, spots[2])
        links.go(self.base + 5, spots[2], spots[2], self.core)
        links.got(self.base + 2, spots[3])
        links.go(self.base + 6, spots[3], spots[3], self.core)

    def end(self):
        for index, land in enumerate(self.lands):
            self.links.got(self.base + 3 + index, land)


class Halves:
    def __init__(self, parts):
        self.parts = parts

    def one(self):
        for part in self.parts:
            part.one()

    def two(self, *given):
        for index, part in enumerate(self.parts):
            part.two(*[one[index] for one in given])

    def landed(self):
        for part in self.parts:
            part.landed()

    def three(self):
        for part in self.parts:
            part.three()

    def end(self):
        for part in self.parts:
            part.end()


def half_of(ref, half):
    rows = ref.shape[-2] // 2
    lead = (slice(None),) * (len(ref.shape) - 2)
    return ref.at[(*lead, pl.ds(half * rows, rows), slice(None))]


def halved_spread(links, own, spot):
    return Halves(
        [
            Spread(
                links,
                half_of(own, half),
                lambda piece, half=half: half_of(spot(piece), half),
                ((2, 4), (4, 2))[half],
            )
            for half in range(2)
        ]
    )


class Relay:
    def __init__(self, links, own, put):
        self.links, self.own, self.put = links, own, put
        self.base = links.number(2 * (PLANES - 1))
        self.waited = links.waited

    def plan(self, hop, only=None):
        links, depth = self.links, self.links.depth
        planned = []
        for way in range(2):
            to = depth + (1 if way else -1)
            when = (
                (depth >= hop - 1) & (depth < PLANES - 1)
                if way
                else (depth <= PLANES - hop) & (depth > 0)
            )
            if only is not None:
                when = when & (depth == only[way])
            source = self.own if hop == 1 else self.put(depth, way, hop - 1)
            planned.append(
                (
                    self.base + 2 * (hop - 1) + way,
                    source,
                    self.put(to, way, hop),
                    (links.place, jnp.clip(to, 0, PLANES - 1)),
                    when,
                )
            )
        return planned

    def send(self, hop, only=None):
        for parts in self.plan(hop, only):
            self.links.go(*parts)

    def take(self, hop, only=None):
        links, depth = self.links, self.links.depth
        for way in range(2):
            when = depth >= hop if way else depth + hop < PLANES
            if only is not None:
                when = when & (depth == only[way])
            links.got(self.base + 2 * (hop - 1) + way, self.put(depth, way, hop), when)

    def left(self, hop, only):
        links, depth = self.links, self.links.depth
        for way in range(2):
            source = self.own if hop == 1 else self.put(depth, way, hop - 1)
            to = (links.place, jnp.clip(depth + (1 if way else -1), 0, PLANES - 1))
            copy = links.copy(self.base + 2 * (hop - 1) + way, source, source, to)
            pl.when(depth == only[way])(copy.wait_send)
            self.waited.append((self.base + 2 * (hop - 1) + way, only[way]))


def position_tables(length):
    rates = 10000.0 ** (-2.0 * np.arange(HD // 2) / HD)
    angles = np.arange(length)[:, None] * rates[None, :]
    cosine, sine = np.cos(angles), np.sin(angles)
    return (
        jnp.asarray(np.concatenate([cosine] * 4, axis=1), jnp.float32),
        jnp.asarray(np.concatenate([-sine, sine, -sine, sine], axis=1), jnp.float32),
    )


def rope_tables_from(seg_ref, cos_at, sin_at, cos_ref, sin_ref, begin_ref, marks):
    length = cos_at.shape[0]
    segs = seg_ref[0:1, :].astype(jnp.float32)
    spots = lax.broadcasted_iota(jnp.int32, (1, length), 1).astype(jnp.float32)
    begins = jnp.zeros((1, length), jnp.float32)
    marks[...] = jnp.zeros_like(marks)
    for number in range(7):
        start = jnp.sum(jnp.where(segs < number, 1.0, 0.0), axis=1, keepdims=True)
        begins = jnp.where(segs == number, start, begins)
        marks[number : number + 1, :] = jnp.where(spots == start, 1.0, 0.0)
    begin_ref[...] = jnp.broadcast_to(begins.astype(jnp.int32), begin_ref.shape)
    pick = lambda table: lax.dot_general(
        marks[...],
        table[...],
        (((1,), (0,)), ((), ())),
        precision=lax.Precision.HIGHEST,
        preferred_element_type=jnp.float32,
    )
    first_cos, first_sin = pick(cos_at), pick(sin_at)
    rows = length // PLANES
    for block in range(PLANES):
        span = pl.ds(block * rows, rows)
        documents = jnp.transpose(
            jnp.broadcast_to(segs[:, block * rows : block * rows + rows], (128, rows))
        )
        cosine = jnp.zeros((rows, 128), jnp.float32)
        sine = jnp.zeros((rows, 128), jnp.float32)
        for number in range(7):
            here = documents == number
            cosine = jnp.where(here, first_cos[number : number + 1], cosine)
            sine = jnp.where(here, first_sin[number : number + 1], sine)
        cos_ref[span, :] = cos_at[span, :] * cosine + sin_at[span, :] * sine
        sin_ref[span, :] = sin_at[span, :] * cosine - cos_at[span, :] * sine


def open_kernel(*refs):
    hidden, attn_piece, out_piece, feed_piece, cos_at, sin_at, first_ref, seg_ref = refs[:8]
    q_out, k_out, v_out, o_out, n_out, weight_out, out_weight_out, feed_all, cos_out, sin_out = refs[8:18]
    gain_ref, square_ref, log_ref, middle_ref, normed_ref, attended_ref, begin_ref = refs[18:25]
    held, q_ref, k_ref, v_ref, o_ref, n_ref, weight_ref, out_ref, cos_ref, sin_ref, turned_v, marks = refs[25:37]
    send, recv, local = refs[37:]
    links = Links(send, recv)
    place, depth = links.place, links.depth
    shard = hidden.shape[0]
    stores = []

    def store(source, target):
        copy = pltpu.make_async_copy(source, target, local.at[len(stores)])
        copy.start()
        stores.append(copy)
        return copy

    block_at = lambda plane, way, hop: jnp.clip(plane + (-hop if way else hop), 0, PLANES - 1)
    wide = Relay(links, hidden, lambda plane, way, hop: held.at[block_at(plane, way, hop)])
    out_rows = lambda block: out_ref.at[
        pl.ds(pl.multiple_of(block * 256, 256), 256), columns_of(place)
    ]
    thin = Relay(links, out_piece, lambda plane, way, hop: out_rows(block_at(plane, way, hop)))
    feeds = Relay(
        links,
        feed_piece,
        lambda plane, way, hop: feed_all.at[slot_at(plane, way, hop), place],
    )
    attn = Spread(links, attn_piece, lambda piece: weight_ref.at[:, columns_of(piece)], (2, 4))
    outs = []
    for slot in range(PLANES):
        block = at_plane(depth, [SLOTS[plane][slot][2] for plane in range(PLANES)])
        rows = pl.ds(pl.multiple_of(block * 256, 256), 256)
        outs.append(
            Spread(
                links,
                out_piece if slot == 0 else out_ref.at[rows, columns_of(place)],
                lambda piece, rows=rows: out_ref.at[rows, columns_of(piece)],
                (2, 4) if slot % 2 else (4, 2),
            )
        )
    slots = [
        halved_spread(
            links,
            feed_piece if slot == 0 else feed_all.at[slot, place],
            lambda piece, slot=slot: feed_all.at[slot, piece],
        )
        for slot in range(PLANES - 1)
    ]
    across = links.number(PLANES)

    links.greet()
    thin.send(1)
    wide.send(1)
    attn.one()
    own_hidden = store(hidden, held.at[depth])
    own_attn = store(attn_piece, weight_ref.at[:, columns_of(place)])
    own_out = store(out_piece, out_rows(depth))
    own_feed = store(feed_piece, feed_all.at[0, place])
    square_ref[...] = jnp.zeros_like(square_ref)
    attn.two()
    attn.three()
    outs[0].one()
    slots[0].one()
    rope_tables_from(seg_ref, cos_at, sin_at, cos_ref, sin_ref, begin_ref, marks)
    attn.end()
    outs[0].two()
    for copy in (own_hidden, own_attn, own_out, own_feed):
        copy.wait()
    store(weight_ref, weight_out)
    store(cos_ref, cos_out)
    store(sin_ref, sin_out)
    gain_ref[...] = weight_ref[pl.ds(768, 16), :].astype(jnp.float32)

    def project(block):
        rows = pl.ds(pl.multiple_of(block * shard, shard), shard)
        values = held[block].astype(jnp.float32)
        factor = lax.rsqrt(jnp.mean(values * values, axis=-1, keepdims=True) + 1e-06)
        normed = (values * factor * gain_ref[0:1, :]).astype(jnp.bfloat16)
        n_ref[rows, :] = normed
        cosine, sine_part = cos_ref[rows, :], sin_ref[rows, :]
        query = tokens_dot(normed, weight_ref[pl.ds(0, 256), :], 1, 1)
        key = tokens_dot(normed, weight_ref[pl.ds(256, 256), :], 1, 1)
        value = tokens_dot(normed, weight_ref[pl.ds(512, 256), :], 1, 1)
        for half in range(2):
            lanes = slice(half * 128, half * 128 + 128)
            turned = turn(query[:, lanes], cosine, sine_part, True)
            q_ref[rows, lanes] = (turned * (HD**-0.5 * LOG2E)).astype(jnp.bfloat16)
            k_ref[rows, lanes] = turn(key[:, lanes], cosine, sine_part, True).astype(jnp.bfloat16)
        first = first_ref[rows, :].astype(jnp.float32)
        blended = 0.5 * value + 0.5 * first
        v_ref[rows, :] = blended.astype(jnp.bfloat16)
        for half in range(2):
            turned_v[half, :, rows] = jnp.transpose(
                blended[:, half * 128 : half * 128 + 128]
            ).astype(jnp.bfloat16)
        square_ref[0:1, :] += jnp.sum(first * first, axis=0, keepdims=True)
        square_ref[1:2, :] += jnp.sum(blended * blended, axis=0, keepdims=True)

    def project_hop(hop):
        def one(side, carried):
            block = depth + hop * (2 * side - 1)
            pl.when((block >= 0) & (block < PLANES))(lambda: project(block))
            return carried

        lax.fori_loop(0, 2, one, 0)

    ends, inner = (PLANES - 1, 0), (PLANES - 2, 1)
    project(depth)
    wide.take(1)
    wide.send(2)
    feeds.send(1, ends)
    thin.take(1)
    thin.send(2)
    outs[1].one()
    outs[0].three()
    slots[0].two()
    project_hop(1)
    outs[1].two()
    wide.take(2)
    wide.send(3)
    feeds.take(1, inner)
    feeds.send(1, inner)
    feeds.send(2, inner)
    thin.take(2)
    thin.send(3)
    outs[2].one()
    outs[1].three()
    project_hop(2)
    outs[2].two()
    slots[0].three()
    wide.take(3)
    wide.left(3, (1, PLANES - 2))
    feeds.take(1, (1, PLANES - 2))
    feeds.take(2, (1, PLANES - 2))
    feeds.send(1, (1, PLANES - 2))
    second = feeds.plan(2, (1, PLANES - 2))
    thin.take(3)
    outs[3].one()
    outs[2].three()
    project_hop(3)
    outs[3].two()
    store(n_ref, n_out)
    store(q_ref, q_out)
    store(k_ref, k_out)
    store(v_ref, v_out)

    lane = lax.broadcasted_iota(jnp.int32, (shard, 128), 1)
    down = lax.broadcasted_iota(jnp.int32, (shard, shard), 0)
    along = lax.broadcasted_iota(jnp.int32, (1, shard), 1)

    def flash_block(block):
        rows = pl.ds(pl.multiple_of(block * shard, shard), shard)
        begin = begin_ref[0:1, rows]
        pairs = [q_ref[rows, pl.ds(pair * 128, 128)] for pair in range(2)]
        parts = [
            jnp.where((lane < HD) == (head % 2 == 0), pairs[head // 2], jnp.zeros_like(pairs[0]))
            for head in range(4)
        ]

        def tile(index, carried, visible):
            span = pl.ds(pl.multiple_of(index * shard, shard), shard)
            raw = [
                tokens_dot(k_ref[span, pl.ds(head // 2 * 128, 128)], parts[head], 1, 1)
                for head in range(4)
            ]
            after = []
            for head in range(4):
                top, total, summed = carried[3 * head : 3 * head + 3]
                scores = jnp.where(visible, raw[head], -1e30)
                raised_top = jnp.maximum(top, jnp.max(scores, axis=0, keepdims=True))
                shrink = jnp.exp2(top - raised_top)
                shares = jnp.exp2(scores - raised_top)
                total = total * shrink + jnp.sum(shares, axis=0, keepdims=True)
                values = turned_v[head // 2, pl.ds(head % 2 * HD, HD), span]
                summed = summed * shrink + tokens_dot(values, shares.astype(jnp.bfloat16), 1, 0)
                after += [raised_top, total, summed]
            return tuple(after)

        fresh = (
            jnp.full((1, shard), -1e30, jnp.float32),
            jnp.zeros((1, shard), jnp.float32),
            jnp.zeros((HD, shard), jnp.float32),
        )
        carried = tile(block, fresh * 4, (down >= begin - block * shard) & (down <= along))
        carried = lax.fori_loop(
            0, block, lambda j, held: tile(j, held, down >= begin - j * shard), carried
        )
        for pair in range(2):
            ends = [carried[3 * (2 * pair + head) : 3 * (2 * pair + head) + 3] for head in range(2)]
            both = jnp.concatenate([summed / total for _, total, summed in ends], axis=0)
            o_ref[rows, pl.ds(pair * 128, 128)] = jnp.transpose(both).astype(jnp.bfloat16)
            for head, (top, total, _) in enumerate(ends):
                log_ref[pair, head : head + 1, rows] = top + jnp.log2(total)

    own_columns = attended_ref.at[:, columns_of(depth, 256)]

    def hand(step):
        block = lax.rem(depth + step, PLANES)
        rows = pl.ds(pl.multiple_of(block * shard, shard), shard)
        return links.copy(across + step, o_ref.at[rows, :], own_columns, (place, block))

    near = (0, PLANES - 1)

    def pump_a():
        feeds.take(1, near)
        slots[1].one()
        outs[3].three()

    def pump_b():
        slots[1].two()
        slots[0].end()
        feeds.left(1, (1, PLANES - 2))
        for parts in second:
            links.go(*parts)

    def pump_c():
        feeds.take(2, near)
        slots[2].one()

    pumps = ((0, pump_a), (1, pump_b), (2, pump_c))

    def flash(index, carried):
        step = PLANES - 1 - index
        flash_block(lax.rem(depth + step, PLANES))
        pl.when((step > 0) & (step < PLANES - 1))(lambda: hand(step).start())
        for when, pump in pumps:
            pl.when(index == when)(pump)
        pl.when(index == 1)(lambda: hand(PLANES - 1).start())
        return carried

    lax.fori_loop(0, PLANES, flash, 0)
    feeds.send(3, (1, PLANES - 2))
    own_rows = pl.ds(pl.multiple_of(depth * shard, shard), shard)
    attended_ref[:, columns_of(depth, 256)] = o_ref[own_rows, :]
    store(o_ref, o_out)
    for part in outs:
        part.end()
    store(out_ref, out_weight_out)
    slots[2].two()
    for step in range(1, PLANES):
        source = lax.rem(depth - step + PLANES, PLANES)
        links.got(across + step, attended_ref.at[:, columns_of(source, 256)])
    half = shard // 2
    for part in range(2):
        rows = pl.ds(part * half, half)
        middle = held[depth, rows, :].astype(jnp.float32) + tokens_dot(
            attended_ref[rows, :], out_ref[...], 1, 0
        )
        middle_ref[rows, :] = middle
        factor = lax.rsqrt(jnp.mean(middle * middle, axis=-1, keepdims=True) + 1e-06)
        normed_ref[rows, :] = (middle * factor * gain_ref[1:2, :]).astype(jnp.bfloat16)
    slots[1].landed()
    slots[2].landed()
    feeds.take(3)
    for step in range(1, PLANES):
        hand(step).wait_send()
    links.drain()
    for copy in stores[4:]:
        copy.wait()


def opening(hidden, attn_piece, out_piece, feed_piece, first_values, seg_row):
    length, width = first_values.shape
    rows = hidden.shape[0]
    count = feed_piece.shape[0]
    low, full = jnp.bfloat16, jnp.float32
    any_spec, vmem = pl.BlockSpec(memory_space=pl.ANY), pl.BlockSpec(memory_space=pltpu.VMEM)
    shape = jax.ShapeDtypeStruct
    cos_at, sin_at = position_tables(length)
    return pl.pallas_call(
        open_kernel,
        in_specs=[any_spec] * 4 + [vmem] * 4,
        out_specs=[any_spec] * 10 + [vmem] * 7,
        out_shape=[
            shape((length, width), low),
            shape((length, width), low),
            shape((length, width), low),
            shape((length, width), low),
            shape((length, D), low),
            shape((ATTN_ROWS, D), low),
            shape((D, D), low),
            shape((PLANES, 8, count, PIECE), low),
            shape((length, 128), full),
            shape((length, 128), full),
            shape((16, D), full),
            shape((8, width), full),
            shape((width // 128, 8, length), full),
            shape((rows, D), full),
            shape((rows, D), low),
            shape((rows, D), low),
            shape((8, length), jnp.int32),
        ],
        scratch_shapes=[
            pltpu.VMEM((PLANES, rows, D), low),
            pltpu.VMEM((length, width), low),
            pltpu.VMEM((length, width), low),
            pltpu.VMEM((length, width), low),
            pltpu.VMEM((length, width), low),
            pltpu.VMEM((length, D), low),
            pltpu.VMEM((ATTN_ROWS, D), low),
            pltpu.VMEM((D, D), low),
            pltpu.VMEM((length, 128), full),
            pltpu.VMEM((length, 128), full),
            pltpu.VMEM((width // 128, 128, length), low),
            pltpu.VMEM((8, length), full),
            pltpu.SemaphoreType.DMA((OPEN_COPIES,)),
            pltpu.SemaphoreType.DMA((OPEN_COPIES,)),
            pltpu.SemaphoreType.DMA((14,)),
        ],
        compiler_params=pltpu.CompilerParams(
            vmem_limit_bytes=VMEM_LIMIT, collective_id=1, has_side_effects=True
        ),
        name="opening",
    )(hidden, attn_piece, out_piece, feed_piece, cos_at, sin_at, first_values, seg_row)


def feed_kernel(*refs):
    normed_ref, grad_ref, middle_ref, pieces = refs[:4]
    back_ref, out_ref, made_out = refs[4:7]
    fed, weight, mine, theirs, made, halves, other_halves, send, recv, sem, out_sem, last_sem = refs[7:]
    links = Links(send, recv)
    place = links.place
    core = (flip(links.place, 1), links.depth)
    mine_first, theirs_first = lax.rem(links.place, 2), 1 - lax.rem(links.place, 2)
    count = weight.shape[1] // 3
    rows = normed_ref.shape[0]

    def load(slot):
        own = range(8) if slot == 0 else [2 * piece + mine_first for piece in range(4)]
        return [
            pltpu.make_async_copy(
                pieces.at[slot, piece], weight.at[slot, :, columns_of(piece)], sem.at[slot, index]
            )
            for index, piece in enumerate(own)
        ]

    def flush(which, buffer):
        return [
            pltpu.make_async_copy(
                made.at[buffer, :, pl.ds(piece * PIECE, PIECE)],
                made_out.at[which, piece],
                out_sem.at[buffer, piece],
            )
            for piece in range(4)
        ]

    loads = [load(slot) for slot in range(PLANES - 1)]
    for copies in loads:
        for copy in copies:
            copy.start()
    far = pieces.at[PLANES - 1, place]
    last = halved_spread(links, far, lambda piece: weight.at[PLANES - 1, :, columns_of(piece)])
    last_own = pltpu.make_async_copy(far, weight.at[PLANES - 1, :, columns_of(place)], last_sem)
    crossed = {slot: links.number(4) for slot in range(1, PLANES - 1)}
    landings = {
        slot: [
            weight.at[slot, :, columns_of(2 * piece + theirs_first)] for piece in range(4)
        ]
        for slot in crossed
    }
    last_own.start()
    links.greet(planes=False)
    last.one()
    base = links.number(8)
    for index, ref in enumerate((normed_ref, grad_ref)):
        for piece in range(4):
            links.go(
                base + 4 * index + piece,
                ref.at[:, columns_of(2 * piece + theirs_first)],
                other_halves.at[index, :, pl.ds(piece * PIECE, PIECE)],
                core,
            )
            halves[index, :, pl.ds(piece * PIECE, PIECE)] = ref[:, columns_of(2 * piece + mine_first)]
    for slot, number in crossed.items():
        for piece in range(4):
            own = 2 * piece + mine_first
            links.go(
                number + piece, pieces.at[slot, own], weight.at[slot, :, columns_of(own)], core
            )
    fed[...] = jnp.zeros_like(fed)
    back_ref[...] = jnp.zeros_like(back_ref)
    for index in range(2):
        for piece in range(4):
            links.got(
                base + 4 * index + piece, other_halves.at[index, :, pl.ds(piece * PIECE, PIECE)]
            )
    given = links.number(PLANES)
    hand = lambda slot: links.copy(given + slot, mine.at[lax.rem(slot, 2)], theirs.at[slot], core)
    spans = [pl.ds(index * count, count) for index in range(3)]
    half = rows // 2

    def forward(slot):
        now = lax.rem(slot, 2)
        held = slot

        def ready(which):
            for copy in loads[which]:
                copy.wait()
            if which:
                for piece in range(4):
                    links.got(crossed[which] + piece, landings[which][piece])

        for which in range(PLANES - 1):
            pl.when(slot == which)(functools.partial(ready, which))

        @pl.when(slot == PLANES - 1)
        def _():
            last_own.wait()
            last.end()

        @pl.when(slot >= 2)
        def _():
            hand(slot - 2).wait_send()

        for tile in range(2):
            at = pl.ds(tile * half, half)
            normed, grad = normed_ref[at, :], grad_ref[at, :]
            gates = tokens_dot(weight[held, spans[0], :], normed, 1, 1)
            ups = tokens_dot(weight[held, spans[1], :], normed, 1, 1)
            backs = tokens_dot(weight[held, spans[2], :], grad, 1, 1)
            sig = jax.nn.sigmoid(gates)
            active = gates * sig
            mine[now, 2, :, at] = (active * ups).astype(jnp.bfloat16)
            mine[now, 0, :, at] = (backs * ups * sig * (1.0 + gates * (1.0 - sig))).astype(jnp.bfloat16)
            mine[now, 1, :, at] = (backs * active).astype(jnp.bfloat16)
        hand(slot).start()

        fed[...] += tokens_dot(mine[now, 2], weight[held, spans[2], :], 0, 0)
        back_ref[...] += tokens_dot(mine[now, 0], weight[held, spans[0], :], 0, 0) + tokens_dot(
            mine[now, 1], weight[held, spans[1], :], 0, 0
        )

    def backward(slot):
        now = lax.rem(slot, 2)
        hand(slot).wait_recv()

        @pl.when(slot >= 2)
        def _():
            for copy in flush(slot - 2, now):
                copy.wait()

        def columns(tile, carried):
            lanes = columns_of(tile, 256)
            for index in range(3):
                which = index // 2
                made[now, spans[index], lanes] = (
                    tokens_dot(mine[now, index], halves[which, :, lanes], 1, 0)
                    + tokens_dot(theirs[slot, index], other_halves[which, :, lanes], 1, 0)
                ).astype(jnp.bfloat16)
            return carried

        lax.fori_loop(0, 2, columns, 0)
        for copy in flush(slot, now):
            copy.start()

    def one(step, carried):
        pl.when(step < PLANES)(lambda: forward(step))
        pl.when(step == 0)(last.two)
        pl.when(step == 2)(last.three)
        pl.when(step >= 1)(lambda: backward(step - 1))
        return carried

    lax.fori_loop(0, PLANES + 1, one, 0)
    out_ref[...] = (middle_ref[...] + fed[...]).astype(jnp.bfloat16)
    for slot in (PLANES - 2, PLANES - 1):
        hand(slot).wait_send()
        for copy in flush(slot, slot % 2):
            copy.wait()
    links.drain()


def feed(normed, grad, middle, pieces):
    rows = normed.shape[0]
    count = pieces.shape[2]
    any_spec, vmem = pl.BlockSpec(memory_space=pl.ANY), pl.BlockSpec(memory_space=pltpu.VMEM)
    low = jnp.bfloat16
    return pl.pallas_call(
        feed_kernel,
        in_specs=[vmem, vmem, vmem, any_spec],
        out_specs=[vmem, vmem, any_spec],
        out_shape=[
            jax.ShapeDtypeStruct((rows, D), jnp.float32),
            jax.ShapeDtypeStruct((rows, D), low),
            jax.ShapeDtypeStruct((PLANES, 4, count, PIECE), low),
        ],
        scratch_shapes=[
            pltpu.VMEM((rows, D), jnp.float32),
            pltpu.VMEM((PLANES, count, D), low),
            pltpu.VMEM((2, 3, count // 3, rows), low),
            pltpu.VMEM((PLANES, 3, count // 3, rows), low),
            pltpu.VMEM((2, count, 4 * PIECE), low),
            pltpu.VMEM((2, rows, 4 * PIECE), low),
            pltpu.VMEM((2, rows, 4 * PIECE), low),
            pltpu.SemaphoreType.DMA((34,)),
            pltpu.SemaphoreType.DMA((34,)),
            pltpu.SemaphoreType.DMA((3, 8)),
            pltpu.SemaphoreType.DMA((2, 4)),
            pltpu.SemaphoreType.DMA,
        ],
        compiler_params=pltpu.CompilerParams(
            vmem_limit_bytes=CLOSE_VMEM, collective_id=2, has_side_effects=True
        ),
        name="feed",
    )(normed, grad, middle, pieces)


def add_into(target, source):
    rows = target.shape[0]
    chunk = next(c for c in (352, 256, rows) if rows % c == 0 and c <= rows)

    def one(index, carried):
        span = pl.ds(pl.multiple_of(index * chunk, chunk), chunk)
        target[span, :] = (
            target[span, :].astype(jnp.float32) + source[span, :].astype(jnp.float32)
        ).astype(jnp.bfloat16)
        return carried

    lax.fori_loop(0, rows // chunk, one, 0)


class Fold:
    def __init__(self, links, whole, first, final, bits):
        self.links, self.first, self.final = links, [first.at[m] for m in range(2)], final
        self.base = links.number(3)
        chip = lax.div(links.place, 2)
        ones = lambda bit: lax.rem(lax.div(chip, bit), 2)
        near, far = ones(bits[0]), ones(bits[1])
        self.away = [whole((1 - near) * bits[0] + m * bits[1]) for m in range(2)]
        self.stay = [whole(near * bits[0] + m * bits[1]) for m in range(2)]
        self.near_to = (flip(links.place, 2 * bits[0]), links.depth)
        self.far_to = (flip(links.place, 2 * bits[1]), links.depth)
        self.passed, self.own = first.at[1 - far], first.at[far]

    def one(self):
        for m in range(2):
            self.links.go(self.base + m, self.away[m], self.first[m], self.near_to)

    def two(self, stay=None):
        for m in range(2):
            self.links.got(self.base + m, self.first[m])
            add_into(self.first[m], self.stay[m] if stay is None else stay[m])
        self.links.go(self.base + 2, self.passed, self.final, self.far_to)

    def end(self):
        self.links.got(self.base + 2, self.final)
        add_into(self.final, self.own)


class LineFold:
    def __init__(self, links, block, held):
        self.links = links
        self.held = [[held.at[way, step] for step in range(PLANES - 1)] for way in range(2)]
        self.base = links.number(2 * (PLANES - 1))
        depth = links.depth
        self.blocks, self.sends, self.sums, self.takes, self.to = [], [], [], [], []
        for step in range(1, PLANES):
            right = jnp.minimum(depth + PLANES - step, PLANES - 1)
            left = jnp.maximum(depth - PLANES + step, 0)
            self.blocks.append((block(left), block(right)))
            self.sends.append((depth >= PLANES - step, depth < step))
            self.takes.append(((depth >= PLANES - 1 - step) & (depth < PLANES - 1), (depth <= step) & (depth > 0)))
        self.ends = (depth == PLANES - 1, depth == 0)
        self.to = (
            (links.place, jnp.maximum(depth - 1, 0)),
            (links.place, jnp.minimum(depth + 1, PLANES - 1)),
        )
        self.inner = [
            [self.sends[step][way] & jnp.logical_not(self.ends[way]) for way in range(2)]
            for step in range(PLANES - 1)
        ]
        self.outer = [
            [self.sends[step][way] & self.ends[way] for way in range(2)] for step in range(PLANES - 1)
        ]

    def launch(self, step):
        for way in range(2):
            self.links.go(
                self.base + 2 * (step - 1) + way,
                self.blocks[step - 1][way],
                self.held[way][step - 1],
                self.to[way],
                self.outer[step - 1][way],
            )

    def outer_plan(self, step):
        return [
            (
                self.base + 2 * (step - 1) + way,
                self.blocks[step - 1][way],
                self.held[way][step - 1],
                self.to[way],
                self.outer[step - 1][way],
            )
            for way in range(2)
        ]

    def go_all(self, planned):
        for parts in planned:
            self.links.go(*parts)

    def take(self, step):
        for way in range(2):
            self.links.got(
                self.base + 2 * (step - 1) + way, self.held[way][step - 1], self.takes[step - 1][way]
            )

    def forward(self, step):
        for way in range(2):
            before = self.held[way][step - 2]
            block = self.blocks[step - 1][way]

            @pl.when(self.inner[step - 1][way])
            def _():
                add_into(before, block)

            self.links.go(
                self.base + 2 * (step - 1) + way,
                before,
                self.held[way][step - 1],
                self.to[way],
                self.inner[step - 1][way],
            )

    def total(self, own, out):
        depth = self.links.depth
        rows = out.shape[0]
        chunk = next(c for c in (352, 256, rows) if rows % c == 0)

        def one(index, carried):
            span = pl.ds(pl.multiple_of(index * chunk, chunk), chunk)
            value = own[span, :].astype(jnp.float32)
            sides = [self.held[way][PLANES - 2][span, :].astype(jnp.float32) for way in range(2)]
            value = value + jnp.where(depth < PLANES - 1, sides[0], 0.0)
            out[span, :] = value + jnp.where(depth > 0, sides[1], 0.0)
            return carried

        lax.fori_loop(0, rows // chunk, one, 0)


def close_kernel(*refs):
    (made, low_in, attended_in, q_in, k_in, v_in, o_in, n_in, weight_in, cos_in, sin_in) = refs[:11]
    incoming = refs[11:15]
    log_ref, begin_ref, gain_ref, gain_two_ref, square_ref = refs[15:20]
    first_ref, back_ref, feed_total, out_total, attn_total, small_ref = refs[20:26]
    (
        q_ref, k_ref, v_ref, o_ref, weight_ref, cos_ref, sin_ref, grad, inner, query_acc, key_acc, made_ref,
        stay, feed_first, feed_final, feed_held, out_made, out_core, out_first, out_final, out_held,
        attn_core, attn_first, attn_final, partial, partial_held, small_got,
        send, recv, local,
    ) = refs[26:]
    links = Links(send, recv)
    place, depth = links.place, links.depth
    length = q_ref.shape[0]
    shard = length // PLANES
    parity, chip = lax.rem(place, 2), lax.div(place, 2)
    core = (flip(place, 1), depth)
    loads = []

    def load(source, target):
        copy = pltpu.make_async_copy(source, target, local.at[len(loads)])
        copy.start()
        loads.append(copy)
        return copy

    order = (3, 2, 1, 0)

    def halved_fold(whole, first, final):
        return Halves(
            [
                Fold(
                    links,
                    lambda i, half=half: half_of(whole(i), half),
                    half_of(first, half),
                    half_of(final, half),
                    ((1, 2), (2, 1))[half],
                )
                for half in range(2)
            ]
        )

    folds = {
        slot: halved_fold(
            lambda i, slot=slot: made.at[slot, i], feed_first.at[slot], feed_final.at[slot]
        )
        for slot in order
    }
    out_fold = halved_fold(lambda i: out_core.at[i], out_first, out_final)
    attn_fold = halved_fold(lambda i: attn_core.at[i], attn_first, attn_final)

    def slot_holding(block):
        found = 0
        for plane in range(PLANES):
            for slot, (_, _, held) in enumerate(SLOTS[plane]):
                found = found + jnp.where((depth == plane) & (block == held), slot, 0)
        return found

    feed_line = LineFold(links, lambda j: feed_final.at[slot_holding(j)], feed_held)
    out_line = LineFold(
        links, lambda j: out_final.at[pl.ds(pl.multiple_of(j * 256, 256), 256), :], out_held
    )
    line = LineFold(links, lambda j: partial.at[j], partial_held)
    out_swap, attn_swap = links.number(4), links.number(4)
    sides = [columns_of(2 * i + parity) for i in range(4)]
    others = [columns_of(2 * i + 1 - parity) for i in range(4)]
    across = links.number(2 * PLANES)
    tiny = links.number(6)
    stays = [
        [[half_of(stay.at[index, m], half) for m in range(2)] for half in range(2)] for index in range(2)
    ]
    stay_sems = [[[16 + 4 * index + 2 * half + m for m in range(2)] for half in range(2)] for index in range(2)]

    def restay(slot):
        return [
            pltpu.make_async_copy(
                folds[slot].parts[half].stay[m],
                stays[slot % 2][half][m],
                local.at[stay_sems[slot % 2][half][m]],
            )
            for half in range(2)
            for m in range(2)
        ]

    tiny_to = [core, (flip(place, 2), depth), (flip(place, 4), depth)]
    plane_to = [(place, lax.rem(depth + step, PLANES)) for step in range(1, PLANES)]
    plane_rows = [lax.rem(depth - step + PLANES, PLANES) for step in range(PLANES)]

    attended_ref, low_ref = partial.at[0], partial.at[1]
    first_loads = [load(attended_in, attended_ref), load(low_in, low_ref)]
    for slot in order[:2]:
        for copy in restay(slot):
            copy.start()
    q_loads = [load(source, target) for source, target in ((q_in, q_ref), (k_in, k_ref), (v_in, v_ref), (o_in, o_ref), (cos_in, cos_ref), (sin_in, sin_ref))]
    own_rows = pl.ds(pl.multiple_of(depth * shard, shard), shard)
    q_loads.append(load(incoming[0], grad.at[own_rows, :]))
    weight_load = load(weight_in, weight_ref)

    links.greet()
    for pair in range(2):
        lanes = pl.ds(pair * 128, 128)
        for step in range(1, PLANES):
            links.go(
                across + 4 * pair + step,
                incoming[step].at[:, lanes],
                grad.at[own_rows, lanes],
                plane_to[step - 1],
            )
    folds[3].one()

    for copy in first_loads:
        copy.wait()
    for index in range(4):
        rows = pl.ds(index * 256, 256)
        out_made[rows, :] = tokens_dot(attended_ref[:, rows], low_ref[...], 0, 0).astype(jnp.bfloat16)
    out_swaps = [links.copy(out_swap + i, out_made.at[:, others[i]], out_core.at[i], core) for i in range(4)]
    for copy in out_swaps:
        copy.start()
    for i in range(4):
        links.got(out_swap + i, out_core.at[i])
        add_into(out_core.at[i], out_made.at[:, sides[i]])
    for copy in q_loads:
        copy.wait()

    def fold_two(slot):
        for copy in restay(slot):
            copy.wait()
        folds[slot].two(stays[slot % 2])

    fold_two(3)
    folds[2].one()
    grad_rows = [
        [
            grad.at[pl.ds(pl.multiple_of(plane_rows[step] * shard, shard), shard), pl.ds(pair * 128, 128)]
            for step in range(PLANES)
        ]
        for pair in range(2)
    ]

    def take_grads(pair):
        for step in range(1, PLANES):
            links.got(across + 4 * pair + step, grad_rows[pair][step])

    take_grads(0)

    lane = lax.broadcasted_iota(jnp.int32, (shard, 128), 1)
    keeps = [lane < HD, lane >= HD]
    down = lax.broadcasted_iota(jnp.int32, (shard, shard), 0)
    along = lax.broadcasted_iota(jnp.int32, (1, shard), 1)

    def masked(values, head):
        return jnp.where(keeps[head], values, jnp.zeros_like(values))

    def after_a():
        folds[3].end()
        feed_line.launch(1)
        out_fold.one()

    def after_b():
        fold_two(2)
        folds[1].one()
        for copy in restay(1):
            copy.start()

    def after_c():
        folds[2].end()
        feed_line.launch(2)
        feed_line.take(1)
        feed_line.forward(2)
        out_fold.two()

    def after_d():
        fold_two(1)
        folds[0].one()
        for copy in restay(0):
            copy.start()
        out_fold.end()
        for step in range(1, PLANES):
            out_line.launch(step)

    def after_e():
        folds[1].end()
        feed_line.launch(3)

    weight_load.wait()
    lower = depth < PLANES // 2
    query_acc[...] = jnp.zeros_like(query_acc)
    key_acc[...] = jnp.zeros_like(key_acc)
    first_ref[...] = jnp.zeros_like(first_ref)
    launches = [line.outer_plan(step) for step in range(1, PLANES)]

    def rows_of(block):
        return pl.ds(pl.multiple_of(block * shard, shard), shard)

    def back_step(index, carried):
        stage, pair = lax.div(index, 2), lax.rem(index, 2)
        block = jnp.where(lower, PLANES - 1 - stage, stage)
        lanes = columns_of(pair)
        own = rows_of(block)

        @pl.when(stage == 0)
        def _():
            for other in range(PLANES):
                span = pl.ds(other * shard, shard)
                turned = jnp.transpose(
                    grad[span, lanes].astype(jnp.float32) * o_ref[span, lanes].astype(jnp.float32)
                )
                for head in range(2):
                    inner[pair, head : head + 1, span] = jnp.sum(
                        turned[head * HD : head * HD + HD], axis=0, keepdims=True
                    )

        def tile(query_rows, key_rows, visible):
            keys, values = k_ref[key_rows, lanes], v_ref[key_rows, lanes]
            query_block, grad_block = q_ref[query_rows, lanes], grad[query_rows, lanes]
            queries = [masked(query_block, head) for head in range(2)]
            out_grads = [masked(grad_block, head) for head in range(2)]
            scores = [tokens_dot(keys, queries[head], 1, 1) for head in range(2)]
            share_grads = [tokens_dot(values, out_grads[head], 1, 1) for head in range(2)]
            score_grads, value_sum, key_sum = [], 0.0, 0.0
            for head in range(2):
                shares = jnp.where(
                    visible,
                    jnp.exp2(scores[head] - log_ref[pair, head : head + 1, query_rows]),
                    0.0,
                )
                score_grads.append(
                    (shares * (share_grads[head] - inner[pair, head : head + 1, query_rows])).astype(
                        jnp.bfloat16
                    )
                )
                value_sum = value_sum + tokens_dot(shares.astype(jnp.bfloat16), out_grads[head], 1, 0)
            for head in range(2):
                key_sum = key_sum + tokens_dot(score_grads[head], queries[head], 1, 0)
            first_ref[key_rows, lanes] += value_sum
            key_acc[key_rows, lanes] += key_sum
            query_acc[query_rows, lanes] += tokens_dot(
                score_grads[0], masked(keys, 0), 0, 0
            ) + tokens_dot(score_grads[1], masked(keys, 1), 0, 0)

        def off(other, held):
            query = rows_of(jnp.where(lower, block, block + 1 + other))
            key_block = jnp.where(lower, other, block)
            tile(query, rows_of(key_block), down >= begin_ref[0:1, query] - key_block * shard)
            return held

        tile(own, own, (down >= begin_ref[0:1, own] - block * shard) & (down <= along))
        lax.fori_loop(0, PLANES - 1 - stage, off, 0)
        cosine, sine_part = cos_ref[own, :], sin_ref[own, :]
        made_ref[own, columns_of(pair)] = turn(
            query_acc[own, lanes] * HD**-0.5, cosine, sine_part, False
        ).astype(jnp.bfloat16)
        made_ref[own, columns_of(2 + pair)] = turn(
            key_acc[own, lanes] * (1 / LOG2E), cosine, sine_part, False
        ).astype(jnp.bfloat16)
        half_sum = 0.5 * first_ref[own, lanes]
        made_ref[own, columns_of(4 + pair)] = half_sum.astype(jnp.bfloat16)
        first_ref[own, lanes] = half_sum

        @pl.when(pair == 1)
        def _():
            partial[block] = tokens_dot(
                made_ref[own, :], weight_ref[pl.ds(0, 768), :], 1, 0
            ).astype(jnp.bfloat16)
            for number, parts in enumerate(launches):
                pl.when(stage == number)(functools.partial(line.go_all, parts))

        pl.when(index == 0)(lambda: take_grads(1))
        for when, pump in ((0, after_a), (1, after_b), (2, after_c), (4, after_d), (7, after_e)):
            pl.when(index == when)(pump)
        return carried

    lax.fori_loop(0, 2 * PLANES, back_step, 0)
    quarters = [q_ref, k_ref, v_ref, o_ref]
    quarter_loads = [
        load(n_in.at[:, pl.ds(index * 256, 256)], quarter) for index, quarter in enumerate(quarters)
    ]
    small_ref[...] = jnp.zeros_like(small_ref)
    for piece in range(8):
        small_ref[0, 8 + piece : 9 + piece, :] = gain_two_ref[0:1, piece * PIECE : piece * PIECE + PIECE]
    for which in range(2):
        whole_sum = jnp.sum(square_ref[which : which + 1, :], axis=1, keepdims=True)
        small_ref[0, 16 + which : 17 + which, :] = jnp.broadcast_to(whole_sum, (1, PIECE))
    line.take(1)
    line.forward(2)
    for copy in quarter_loads:
        copy.wait()

    def gain_back(block, carried):
        rows = pl.ds(pl.multiple_of(block * shard, shard), shard)
        for index, quarter in enumerate(quarters):
            value = partial[block, :, pl.ds(index * 256, 256)].astype(jnp.float32)
            lanes = pl.ds(index * 256, 256)
            gain = (
                jnp.sum(value * quarter[rows, :].astype(jnp.float32), axis=0, keepdims=True)
                / gain_ref[0:1, lanes]
            )
            for half in range(2):
                piece = 2 * index + half
                small_ref[0, piece : piece + 1, :] += gain[:, half * PIECE : half * PIECE + PIECE]
        return carried

    lax.fori_loop(0, PLANES, gain_back, 0)
    fold_two(0)
    links.go(tiny, small_ref.at[0], small_got.at[0], tiny_to[0])
    feed_line.take(2)
    feed_line.forward(3)
    for copy in out_swaps:
        copy.wait_send()
    attn_made = out_made.at[pl.ds(0, 768), :]
    for index in range(3):
        rows = pl.ds(index * 256, 256)
        for quarter in range(4):
            attn_made[rows, pl.ds(quarter * 256, 256)] = tokens_dot(
                made_ref[:, rows], quarters[quarter][...], 0, 0
            ).astype(jnp.bfloat16)
    for i in range(4):
        links.go(attn_swap + i, attn_made.at[:, others[i]], attn_core.at[i], core)
    links.got(tiny, small_got.at[0])
    small_ref[1] = small_ref[0] + small_got[0]
    links.go(tiny + 1, small_ref.at[1], small_got.at[1], tiny_to[1])
    for i in range(4):
        links.got(attn_swap + i, attn_core.at[i])
        add_into(attn_core.at[i], attn_made.at[:, sides[i]])
    attn_fold.one()
    links.got(tiny + 1, small_got.at[1])
    small_ref[2] = small_ref[1] + small_got[1]
    links.go(tiny + 2, small_ref.at[2], small_got.at[2], tiny_to[2])
    line.take(2)
    line.forward(3)
    links.got(tiny + 2, small_got.at[2])
    small_ref[3] = small_ref[2] + small_got[2]
    small_place = small_got.at[3 + depth]
    for step in range(1, PLANES):
        links.go(tiny + 2 + step, small_ref.at[3], small_place, plane_to[step - 1])
    small_got[3 + depth] = small_ref[3]
    out_line.take(1)
    out_line.forward(2)
    attn_fold.two()
    folds[0].end()
    out_line.take(2)
    out_line.forward(3)
    attn_fold.end()
    attn_total[...] = attn_final[...].astype(jnp.float32)
    line.take(3)
    line.total(partial.at[depth], back_ref)
    feed_line.take(3)
    feed_line.total(feed_final.at[0], feed_total)
    out_line.take(3)
    out_line.total(out_final.at[pl.ds(pl.multiple_of(depth * 256, 256), 256), :], out_total)
    for step in range(1, PLANES):
        links.got(tiny + 2 + step, small_got.at[3 + plane_rows[step]])
    small_ref[4] = small_got[3] + small_got[4] + small_got[5] + small_got[6]
    links.drain()


def closing(made, low_ref, attended_own, heads, normed, weight, tables, incoming, logs, begin_row, gains, gain_two, squares):
    length, width = heads[0].shape
    rows = low_ref.shape[0]
    count = made.shape[2]
    low, full = jnp.bfloat16, jnp.float32
    any_spec, vmem = pl.BlockSpec(memory_space=pl.ANY), pl.BlockSpec(memory_space=pltpu.VMEM)
    shape = jax.ShapeDtypeStruct
    return pl.pallas_call(
        close_kernel,
        in_specs=[any_spec] * 15 + [vmem] * 5,
        out_specs=[vmem] * 6,
        out_shape=[
            shape((length, width), full),
            shape((rows, D), full),
            shape((count, PIECE), full),
            shape((256, PIECE), full),
            shape((768, PIECE), full),
            shape((5, 24, PIECE), full),
        ],
        scratch_shapes=[pltpu.VMEM((length, width), low)] * 4
        + [
            pltpu.VMEM((ATTN_ROWS, D), low),
            pltpu.VMEM((length, 128), full),
            pltpu.VMEM((length, 128), full),
            pltpu.VMEM((length, width), low),
            pltpu.VMEM((2, 8, length), full),
            pltpu.VMEM((length, width), full),
            pltpu.VMEM((length, width), full),
            pltpu.VMEM((length, 768), low),
            pltpu.VMEM((2, 2, count, PIECE), low),
            pltpu.VMEM((PLANES, 2, count, PIECE), low),
            pltpu.VMEM((PLANES, count, PIECE), low),
            pltpu.VMEM((2, PLANES - 1, count, PIECE), low),
            pltpu.VMEM((D, D), low),
            pltpu.VMEM((4, D, PIECE), low),
            pltpu.VMEM((2, D, PIECE), low),
            pltpu.VMEM((D, PIECE), low),
            pltpu.VMEM((2, PLANES - 1, 256, PIECE), low),
            pltpu.VMEM((4, 768, PIECE), low),
            pltpu.VMEM((2, 768, PIECE), low),
            pltpu.VMEM((768, PIECE), low),
            pltpu.VMEM((PLANES, rows, D), low),
            pltpu.VMEM((2, PLANES - 1, rows, D), low),
            pltpu.VMEM((7, 24, PIECE), full),
            pltpu.SemaphoreType.DMA((CLOSE_COPIES,)),
            pltpu.SemaphoreType.DMA((CLOSE_COPIES,)),
            pltpu.SemaphoreType.DMA((24,)),
        ],
        compiler_params=pltpu.CompilerParams(
            vmem_limit_bytes=CLOSE_VMEM, collective_id=3, has_side_effects=True
        ),
        name="closing",
    )(made, low_ref, attended_own, *heads, normed, weight, *tables, *incoming, logs, begin_row, gains, gain_two, squares)


def middle_back_kernel(*refs):
    middle_ref, grad_ref, back_ref, weight_ref, gain_ref = refs[:5]
    low_ref, dm_ref, gain_grad_ref = refs[5:8]
    outs = refs[8:12]
    depth = lax.axis_index("mp")
    half = middle_ref.shape[0] // 2
    gain = gain_ref[1:2, :]
    gain_grad_ref[...] = jnp.zeros_like(gain_grad_ref)
    for tile in range(2):
        rows = pl.ds(tile * half, half)
        middle, incoming = middle_ref[rows, :], back_ref[rows, :]
        factor = lax.rsqrt(jnp.mean(middle * middle, axis=-1, keepdims=True) + 1e-06)
        scaled = incoming * gain
        mean = jnp.mean(scaled * middle, axis=-1, keepdims=True)
        total = grad_ref[rows, :].astype(jnp.float32) + factor * scaled - middle * (factor**3 * mean)
        gain_grad_ref[0:1, :] += jnp.sum(incoming * middle * factor, axis=0, keepdims=True)
        dm_ref[rows, :] = total
        low_ref[rows, :] = total.astype(jnp.bfloat16)
    for index, out in enumerate(outs):
        owner = lax.rem(depth + index, PLANES)
        rows = pl.ds(pl.multiple_of(owner * 256, 256), 256)
        out[...] = tokens_dot(low_ref[...], weight_ref[rows, :], 1, 1).astype(jnp.bfloat16)


def middle_back(middle, grad, back, weight, gains):
    rows = middle.shape[0]
    return pl.pallas_call(
        middle_back_kernel,
        out_shape=[
            jax.ShapeDtypeStruct((rows, D), jnp.bfloat16),
            jax.ShapeDtypeStruct((rows, D), jnp.float32),
            jax.ShapeDtypeStruct((8, D), jnp.float32),
        ]
        + [jax.ShapeDtypeStruct((rows, 256), jnp.bfloat16)] * PLANES,
        compiler_params=pltpu.CompilerParams(vmem_limit_bytes=VMEM_LIMIT),
        cost_estimate=cost(2 * rows * D * D, 12 << 20),
        name="middle_back",
    )(middle, grad, back, weight, gains)


def stepped(master, gradient, moment, square, step_rate, decay, outs, at):
    new = adamw(master[at], gradient, moment[at], square[at], step_rate, decay)
    for out, value in zip(outs, new):
        out[at] = value


def update_kernel(*refs):
    hidden_ref, dm_ref, back_ref, gain_ref, attn_ref, out_ref, feed_ref, small_ref = refs[:8]
    masters, moments, squares = refs[8:13], refs[13:18], refs[18:23]
    grad_ref, norm_ref = refs[23:25]
    outs = [refs[25 + index : 40 : 5] for index in range(5)]
    place = lax.axis_index("dp")
    hidden = hidden_ref[...].astype(jnp.float32)
    factor = rms_factor(hidden)
    grad_ref[...] = dm_ref[...] + norm_back(hidden, factor, gain_ref[0:1, :], back_ref[...])[0]
    tokens = 8.0 * hidden_ref.shape[0] * PLANES
    norm_ref[...] = jnp.sqrt(small_ref[4, 16:24, :] / (tokens * D))
    every = slice(None)
    rates = (D**-0.5, max(1, 8 * HEADS * HD // LEN) ** -0.5, D**-0.5, (FF // 3) ** -0.5)

    def weight(index, gradient, at):
        stepped(
            masters[index], gradient, moments[index], squares[index], rates[index], 0.1, outs[index], at
        )

    for which in range(3):
        weight(0, jnp.transpose(attn_ref[pl.ds(which * 256, 256), :]), which)
    weight(1, out_ref[...], (every, every))
    count = masters[3].shape[0]
    for which in range(2):
        weight(2, feed_ref[pl.ds(which * count, count), :], which)
    weight(3, feed_ref[pl.ds(2 * count, count), :], (every, every))
    for which in range(2):
        at = pl.ds(which, 1)
        stepped(
            masters[4],
            small_ref[4, pl.ds(8 * which + place, 1), :],
            moments[4],
            squares[4],
            0.2,
            0.0,
            outs[4],
            (at, every),
        )


def update(hidden, dm, back, gains, totals, small, masters, moments, squares):
    full = jnp.float32
    shape = jax.ShapeDtypeStruct
    return pl.pallas_call(
        update_kernel,
        out_shape=[shape(dm.shape, full), shape((8, PIECE), full)]
        + [shape(one.shape, full) for one in masters] * 3,
        compiler_params=pltpu.CompilerParams(vmem_limit_bytes=VMEM_LIMIT),
        cost_estimate=cost(0, 16 << 20),
        name="update",
    )(hidden, dm, back, gains, *totals, small, *masters, *moments, *squares)


def fast_shards(
    hidden_in,
    segment_ids,
    first_values,
    grad_out,
    input_proj,
    output_proj,
    expand_proj,
    reduce_proj,
    norm_gains,
    old_moment_input,
    old_moment_output,
    old_moment_expand,
    old_moment_reduce,
    old_moment_gains,
    old_square_input,
    old_square_output,
    old_square_expand,
    old_square_reduce,
    old_square_gains,
):
    place, depth = lax.axis_index("dp"), lax.axis_index("mp")
    low = jnp.bfloat16
    hidden, out_cotangent = hidden_in[0], grad_out[0]
    ffs = reduce_proj.shape[0]

    attn_piece = jnp.concatenate(
        [
            input_proj.astype(low).transpose(0, 2, 1).reshape(768, PIECE),
            norm_gains.astype(low),
            jnp.zeros((14, PIECE), low),
        ]
    )
    feed_piece = jnp.concatenate(
        [
            expand_proj.astype(low).transpose(0, 2, 1).reshape(2 * ffs, PIECE),
            reduce_proj.astype(low),
        ]
    )

    (
        queries,
        keys,
        values,
        attended,
        normed,
        attn_weight,
        out_weight,
        feed_all,
        cosine,
        sine_part,
        gains,
        squares,
        logs,
        middle,
        normed_two,
        attended_own,
        begin_row,
    ) = opening(hidden, attn_piece, output_proj.astype(low), feed_piece, first_values[0], segment_ids)
    normed_two_grad, layer_output, made = feed(normed_two, out_cotangent, middle, feed_all)
    layer_output = layer_output[None]
    branch_low, middle_grad, gain_two, *out_grads = middle_back(
        middle, out_cotangent, normed_two_grad, out_weight, gains
    )
    values_grad, normed_grad, feed_total, out_total, attn_total, small = closing(
        made,
        branch_low,
        attended_own,
        (queries, keys, values, attended),
        normed,
        attn_weight,
        (cosine, sine_part),
        out_grads,
        logs,
        begin_row,
        gains,
        gain_two,
        squares,
    )
    masters = [input_proj, output_proj, expand_proj, reduce_proj, norm_gains]
    moments = [
        old_moment_input,
        old_moment_output,
        old_moment_expand,
        old_moment_reduce,
        old_moment_gains,
    ]
    squares = [
        old_square_input,
        old_square_output,
        old_square_expand,
        old_square_reduce,
        old_square_gains,
    ]
    for group in (masters, moments, squares):
        group[2] = group[2].transpose(0, 2, 1)
    input_grad, norms, *updated = update(
        hidden,
        middle_grad,
        normed_grad,
        gains,
        (attn_total, out_total, feed_total),
        small,
        masters,
        moments,
        squares,
    )
    for index in (2, 7, 12):
        updated[index] = updated[index].transpose(0, 2, 1)
    return (layer_output, input_grad[None], values_grad[None], norms[:2, 0], *updated)


def solution(mesh):
    quick = mesh.shape["dp"] == 8 and mesh.shape["mp"] == PLANES
    return jax.shard_map(
        fast_shards if quick else shards,
        mesh=mesh,
        in_specs=(
            P("dp", "mp", None),
            P("dp", None),
            P("dp", None, "mp"),
            P("dp", "mp", None),
            P(None, "dp", "mp"),
            P("mp", "dp"),
            P(None, "dp", "mp"),
            P("mp", "dp"),
            P(None, "dp"),
            P(None, "dp", "mp"),
            P("mp", "dp"),
            P(None, "dp", "mp"),
            P("mp", "dp"),
            P(None, "dp"),
            P(None, "dp", "mp"),
            P("mp", "dp"),
            P(None, "dp", "mp"),
            P("mp", "dp"),
            P(None, "dp"),
        ),
        out_specs=(
            P("dp", "mp", None),
            P("dp", "mp", None),
            P("dp", None, "mp"),
            P(),
            P(None, "dp", "mp"),
            P("mp", "dp"),
            P(None, "dp", "mp"),
            P("mp", "dp"),
            P(None, "dp"),
            P(None, "dp", "mp"),
            P("mp", "dp"),
            P(None, "dp", "mp"),
            P("mp", "dp"),
            P(None, "dp"),
            P(None, "dp", "mp"),
            P("mp", "dp"),
            P(None, "dp", "mp"),
            P("mp", "dp"),
            P(None, "dp"),
        ),
        check_vma=False,
    )
```
